32 devices in a mesh: dp: 4 (over z), ctx: 4 (over x, core), fsdp: 2 (over y).
Axes of the slice: x: 2, y: 2, z: 4, core: 2. Of those that a mesh axis runs over, the one named last changes fastest.
Arguments:
- states: bfloat16 [32, 512, 1024], P(('dp', 'fsdp'), 'ctx'), may hold values from -6 to 6
- cotangent: bfloat16 [32, 512, 1024], P(('dp', 'fsdp'), 'ctx'), may hold values from -6 to 6
- lengths: int32 [32], replicated, may hold values from 128 to 512, as said below
- slot_source: int32 [32], replicated, may hold values from 0 to 31, as said below
- query_weight: bfloat16 [1024, 1024], P('fsdp'), may hold values from -0.1875 to 0.1875
- query_bias: bfloat16 [1024], P('fsdp'), may hold values from -3 to 3
- key_weight: bfloat16 [1024, 1024], P('fsdp'), may hold values from -0.1875 to 0.1875
- value_weight: bfloat16 [1024, 1024], P('fsdp'), may hold values from -0.1875 to 0.1875
- value_bias: bfloat16 [1024], P('fsdp'), may hold values from -3 to 3
- output_weight: bfloat16 [1024, 1024], P('fsdp'), may hold values from -0.5 to 0.5
- output_bias: bfloat16 [1024], P('fsdp'), may hold values from -3 to 3
- first_gain: bfloat16 [1024], P('fsdp'), may hold values from 0.5 to 1.5
- first_shift: bfloat16 [1024], P('fsdp'), may hold values from -3 to 3
- inner_weight: bfloat16 [1024, 4096], P('fsdp'), may hold values from -0.1875 to 0.1875
- inner_bias: bfloat16 [4096], P('fsdp'), may hold values from -3 to 3
- outer_weight: bfloat16 [4096, 1024], P('fsdp'), may hold values from -0.09375 to 0.09375
- outer_bias: bfloat16 [1024], P('fsdp'), may hold values from -3 to 3
- final_gain: bfloat16 [1024], P('fsdp'), may hold values from 0.5 to 1.5
- final_shift: bfloat16 [1024], P('fsdp'), may hold values from -3 to 3
Outputs:
- encoded: bfloat16 [32, 512, 1024], P(('dp', 'fsdp'), 'ctx')
- input_grad: bfloat16 [32, 512, 1024], P(('dp', 'fsdp'), 'ctx')
- query_weight_grad: float32 [1024, 1024], P(('dp', 'ctx', 'fsdp'))
- query_bias_grad: float32 [1024], P(('dp', 'ctx', 'fsdp'))
- key_weight_grad: float32 [1024, 1024], P(('dp', 'ctx', 'fsdp'))
- value_weight_grad: float32 [1024, 1024], P(('dp', 'ctx', 'fsdp'))
- value_bias_grad: float32 [1024], P(('dp', 'ctx', 'fsdp'))
- output_weight_grad: float32 [1024, 1024], P(('dp', 'ctx', 'fsdp'))
- output_bias_grad: float32 [1024], P(('dp', 'ctx', 'fsdp'))
- first_gain_grad: float32 [1024], P(('dp', 'ctx', 'fsdp'))
- first_shift_grad: float32 [1024], P(('dp', 'ctx', 'fsdp'))
- inner_weight_grad: float32 [1024, 4096], P(('dp', 'ctx', 'fsdp'))
- inner_bias_grad: float32 [4096], P(('dp', 'ctx', 'fsdp'))
- outer_weight_grad: float32 [4096, 1024], P(('dp', 'ctx', 'fsdp'))
- outer_bias_gradient: float32 [1024], P(('dp', 'ctx', 'fsdp'))
- final_gain_grad: float32 [1024], P(('dp', 'ctx', 'fsdp'))
- final_shift_grad: float32 [1024], P(('dp', 'ctx', 'fsdp'))
The draws below stay inside these ranges and needn't reach their ends.
Inputs may be any that keep to these rules, and one draw needn't show every extreme that they name: slot_source is a permutation of the 32 sequences. Slot t belongs to group t // 8; the 4 slots of one index of dp and fsdp (an aligned block) take their sequences from the devices of the same index of fsdp whose groups lie in the same aligned set of four groups, 1 from each of the four. `lengths`: every aligned block of 4 slots holds one sequence of 512 tokens, and the valid tokens of two such blocks differ by at most 192.
All inputs are finite; a program needn't handle non-finite values.
Results may differ from the reference program's by a relative error of at most 0.015.
Values may be sent and summed in bfloat16 or wider, within the bound.
A program may use at most 192 MiB of HBM per device.

```python
import math
import jax
import jax.numpy as jnp
from jax import lax

D = 1024
HEADS = 16
HEAD_DIM = 64
FF = 4096
LEN = 512
SEQ_DEV = 4
SEQ_GRP = 8
SEQS = 32
N_DP = 4
N_FSDP = 2


def permutations_of(rng, count, size):
    return jax.vmap(lambda single: jax.random.permutation(single, size))(jax.random.split(rng, count))


def deal_plan(key):
    base_key = jax.random.fold_in(key, 31)
    block_key, send_key, slot_key, jitter_key = jax.random.split(base_key, 4)
    set_count = N_DP // 4
    quarter = SEQ_DEV // 4
    rank_blocks = permutations_of(block_key, set_count * N_FSDP, 4).reshape(set_count, N_FSDP, 4)
    send_picks = permutations_of(send_key, set_count * 4 * N_FSDP, SEQ_DEV).reshape(set_count, 4, N_FSDP, SEQ_DEV)
    slot_picks = permutations_of(slot_key, set_count * 4 * N_FSDP, SEQ_DEV).reshape(set_count, 4, N_FSDP, SEQ_DEV)
    grid_shape = (set_count, 4, N_FSDP, 4, quarter)
    set_axis = jnp.broadcast_to(jnp.arange(set_count, dtype=jnp.int32).reshape(-1, 1, 1, 1, 1), grid_shape)
    target_axis = jnp.broadcast_to(jnp.arange(4, dtype=jnp.int32).reshape(1, -1, 1, 1, 1), grid_shape)
    fsdp_axis = jnp.broadcast_to(jnp.arange(N_FSDP, dtype=jnp.int32).reshape(1, 1, -1, 1, 1), grid_shape)
    source_axis = jnp.broadcast_to(jnp.arange(4, dtype=jnp.int32).reshape(1, 1, 1, -1, 1), grid_shape)
    quarter_axis = jnp.broadcast_to(jnp.arange(quarter, dtype=jnp.int32).reshape(1, 1, 1, 1, -1), grid_shape)
    source_local = send_picks[set_axis, source_axis, fsdp_axis, target_axis * quarter + quarter_axis]
    source_seq = (4 * set_axis + source_axis) * SEQ_GRP + fsdp_axis * SEQ_DEV + source_local
    slot_local = slot_picks[set_axis, target_axis, fsdp_axis, source_axis * quarter + quarter_axis]
    slot_index = (4 * set_axis + target_axis) * SEQ_GRP + fsdp_axis * SEQ_DEV + slot_local
    rank_index = rank_blocks[set_axis, fsdp_axis, source_axis] * quarter + quarter_axis
    step_size = (LEN - LEN // 4) // (SEQ_DEV - 1)
    jitter = jax.random.randint(jitter_key, grid_shape, 0, max(1, step_size // 2))
    slot_length = jnp.where(rank_index == SEQ_DEV - 1, LEN, LEN // 4 + rank_index * step_size + jitter)
    sources = jnp.zeros((SEQS,), jnp.int32).at[slot_index.reshape(-1)].set(source_seq.reshape(-1).astype(jnp.int32))
    lengths = jnp.zeros((SEQS,), jnp.int32).at[slot_index.reshape(-1)].set(slot_length.reshape(-1).astype(jnp.int32))
    return (sources, lengths)


def draw_slot_source(key, part):
    return deal_plan(key)[0]


def draw_lengths(key, part):
    return deal_plan(key)[1]


def levels(key, shape, pieces, least, largest):
    factor_of, own = 1.0, jax.random.fold_in(key, 6)
    for position, shards_of in pieces:
        steps = jnp.exp(jax.random.uniform(jax.random.fold_in(own, position), (shards_of,), jnp.float32, least / len(pieces), largest / len(pieces)))
        factor_of = factor_of * jnp.repeat(steps, shape[position] // shards_of).reshape([-1 if axis == position else 1 for axis in range(len(shape))])
    return factor_of


def normal_values(key, extent, spread, limit, cuts=(), kind=jnp.bfloat16):
    array = spread * jax.random.normal(key, extent, jnp.float32)
    if cuts:
        array = array * levels(key, extent, cuts, -0.22, 0.18)
    return jnp.clip(array, -limit, limit).astype(kind)


def setup_inputs(seed: int = 0) -> dict:
    splits = jax.random.split(jax.random.key(seed), 20)
    return {
        "states": normal_values(splits[0], (SEQS, LEN, D), 1.0, 6.0, ((0, 8), (1, 4))),
        "cotangent": normal_values(splits[1], (SEQS, LEN, D), 1.0, 6.0, ((0, 8), (1, 4))),
        "lengths": draw_lengths(jax.random.fold_in(splits[19], 71), 0),
        "slot_source": draw_slot_source(jax.random.fold_in(splits[19], 71), 0),
        "query_weight": normal_values(splits[4], (D, D), D ** -0.5, 0.1875, ((0, 2),)),
        "query_bias": normal_values(splits[5], (D,), 0.5, 3.0, ((0, 2),)),
        "key_weight": normal_values(splits[6], (D, D), D ** -0.5, 0.1875, ((0, 2),)),
        "value_weight": normal_values(splits[7], (D, D), D ** -0.5, 0.1875, ((0, 2),)),
        "value_bias": normal_values(splits[8], (D,), 0.5, 3.0, ((0, 2),)),
        "output_weight": normal_values(splits[9], (D, D), (D // 8) ** -0.5, 0.5, ((0, 2),)),
        "output_bias": normal_values(splits[10], (D,), 0.5, 3.0, ((0, 2),)),
        "first_gain": jnp.clip(1.0 + 0.1 * jax.random.normal(splits[11], (D,), jnp.float32), 0.5, 1.5).astype(jnp.bfloat16),
        "first_shift": normal_values(splits[12], (D,), 0.5, 3.0, ((0, 2),)),
        "inner_weight": normal_values(splits[13], (D, FF), D ** -0.5, 0.1875, ((0, 2),)),
        "inner_bias": normal_values(splits[14], (FF,), 0.5, 3.0, ((0, 2),)),
        "outer_weight": normal_values(splits[15], (FF, D), FF ** -0.5, 0.09375, ((0, 2),)),
        "outer_bias": normal_values(splits[16], (D,), 0.5, 3.0, ((0, 2),)),
        "final_gain": jnp.clip(1.0 + 0.1 * jax.random.normal(splits[17], (D,), jnp.float32), 0.5, 1.5).astype(jnp.bfloat16),
        "final_shift": normal_values(splits[18], (D,), 0.5, 3.0, ((0, 2),)),
    }


@jax.custom_vjp
def low(v):
    return lax.optimization_barrier(v.astype(jnp.bfloat16)).astype(jnp.float32)

@jax.custom_vjp
def low_back(v):
    return v

def low_keep(v):
    return (low(v), None)

def low_pass(kept, grad):
    return (grad,)

def backward_keep_mask(v):
    return (v, None)

def back_low(kept, grad):
    return (low(grad),)
low.defvjp(low_keep, low_pass)
low_back.defvjp(backward_keep_mask, back_low)
EPS = 1e-12
MASKED = -1e+30

def both_ways(v):
    return low(low_back(v))

def product(left_operand_matrix, right_operand_matrix):
    return jnp.einsum('ghp,pq->ghq', left_operand_matrix, right_operand_matrix, precision=lax.Precision.HIGHEST)

def norm_rows(summed, scale_vec, shift_vec):
    row_mean = lax.optimization_barrier(jnp.mean(summed, axis=-1, keepdims=True))
    centered = summed - row_mean
    inverse = lax.rsqrt(lax.optimization_barrier(jnp.mean(centered * centered, axis=-1, keepdims=True)) + EPS)
    return centered * inverse * scale_vec + shift_vec

def forward(states, valid_keys, query_weight, query_bias, key_weight, value_weight, value_bias, output_weight, output_bias, first_gain, first_shift, inner_weight, inner_bias, outer_weight, outer_bias, final_gain, final_shift):
    seq_count, length, model_width = states.shape
    query_rows = both_ways(product(states, query_weight) + query_bias)
    key_rows = both_ways(product(states, key_weight))
    value_rows = both_ways(product(states, value_weight) + value_bias)
    query_heads = query_rows.reshape(seq_count, length, HEADS, HEAD_DIM)
    key_heads = key_rows.reshape(seq_count, length, HEADS, HEAD_DIM)
    value_heads = value_rows.reshape(seq_count, length, HEADS, HEAD_DIM)
    scores = jnp.einsum('sqhe,skhe->shqk', query_heads, key_heads, precision=lax.Precision.HIGHEST)
    scores = low_back(scores * (1.0 / math.sqrt(HEAD_DIM)))
    scores = jnp.where(valid_keys[:, None, None, :] > 0.5, scores, MASKED)
    probability = low(jax.nn.softmax(scores, axis=-1))
    mixed_rows = jnp.einsum('shqk,skhe->sqhe', probability, value_heads, precision=lax.Precision.HIGHEST)
    attended = both_ways(mixed_rows.reshape(seq_count, length, model_width))
    first_sum = states + low_back(product(attended, output_weight) + output_bias)
    first_out = norm_rows(first_sum, first_gain, first_shift)
    hidden = low_back(product(low(first_out), inner_weight) + inner_bias)
    activated = low(jax.nn.gelu(hidden, approximate=False))
    second_sum = first_out + low_back(product(activated, outer_weight) + outer_bias)
    return norm_rows(second_sum, final_gain, final_shift) * valid_keys[..., None]

def reference(states, cotangent, lengths, slot_source, query_weight, query_bias, key_weight, value_weight, value_bias, output_weight, output_bias, first_gain, first_shift, inner_weight, inner_bias, outer_weight, outer_bias, final_gain, final_shift):
    seq_total = slot_source.shape[0]
    own_lengths = jnp.zeros((seq_total,), jnp.int32).at[slot_source.astype(jnp.int32)].set(lengths.astype(jnp.int32))
    places = jnp.arange(LEN, dtype=jnp.int32)
    valid_keys = (places[None, :] < own_lengths[:, None]).astype(jnp.float32)
    params = tuple((w.astype(jnp.float32) for w in (query_weight, query_bias, key_weight, value_weight, value_bias, output_weight, output_bias, first_gain, first_shift, inner_weight, inner_bias, outer_weight, outer_bias, final_gain, final_shift)))
    batch_size = min(seq_total, max(1, 4096 // LEN))
    batch_count = seq_total // batch_size

    def scan_step(running_total, block_item):
        batch_in, batch_cot, batch_valid = block_item

        def run_layer(layer_in, *weight_args):
            return forward(layer_in, batch_valid, *weight_args)
        encoded, pull = jax.vjp(run_layer, batch_in.astype(jnp.float32), *params)
        grads = pull(batch_cot.astype(jnp.float32))
        running_total = tuple((acc + new for acc, new in zip(running_total, grads[1:])))
        return (running_total, (encoded.astype(jnp.bfloat16), grads[0].astype(jnp.bfloat16)))
    empty_sums = tuple((jnp.zeros_like(p) for p in params))
    model_width = states.shape[-1]
    sums_all, outputs = lax.scan(scan_step, empty_sums, (states.reshape(batch_count, batch_size, LEN, model_width), cotangent.reshape(batch_count, batch_size, LEN, model_width), valid_keys.reshape(batch_count, batch_size, LEN)))
    encoded = outputs[0].reshape(states.shape)
    input_grad = outputs[1].reshape(states.shape)
    return (encoded, input_grad, sums_all[0], sums_all[1], sums_all[2], sums_all[3], sums_all[4], sums_all[5], sums_all[6], sums_all[7], sums_all[8], sums_all[9], sums_all[10], sums_all[11], sums_all[12], sums_all[13], sums_all[14])
```

```python
import functools
import math

import jax
import jax.numpy as jnp
from jax import lax
from jax.experimental import pallas as pl
from jax.experimental.pallas import tpu as pltpu
from jax.sharding import PartitionSpec as P

HEADS = 16
EPS = 1e-12
MASKED = -1e30
F32 = jnp.float32
BF16 = jnp.bfloat16
OWNERS = ("dp", "ctx", "fsdp")


def swap(value, axis, mask):
    pairs = [(source, source ^ mask) for source in range(lax.axis_size(axis))]
    return lax.ppermute(value, axis, pairs)


def pick(array, index, axis):
    return lax.dynamic_index_in_dim(array, index, axis, keepdims=False)


def add_low(left, right):
    return (left.astype(F32) + right.astype(F32)).astype(BF16)


def matmul(left, right):
    return jnp.dot(left, right, preferred_element_type=F32)


def matmul_tn(left, right):
    return lax.dot_general(left, right, (((0,), (0,)), ((), ())), preferred_element_type=F32)


def matmul_nt(left, right):
    return lax.dot_general(left, right, (((1,), (1,)), ((), ())), preferred_element_type=F32)


def col_sum(matrix):
    return jnp.sum(matrix.astype(F32), axis=0)


def norm_rows(summed, scale_vec, shift_vec):
    row_mean = jnp.mean(summed, axis=-1, keepdims=True)
    centered = summed - row_mean
    inverse = lax.rsqrt(jnp.mean(centered * centered, axis=-1, keepdims=True) + EPS)
    normed = centered * inverse
    return (normed * scale_vec + shift_vec, normed, inverse)


def norm_back(upstream, normed, inverse, scale_vec):
    scaled = upstream * scale_vec
    return inverse * (
        scaled
        - jnp.mean(scaled, axis=-1, keepdims=True)
        - normed * jnp.mean(scaled * normed, axis=-1, keepdims=True)
    )


def half_lanes(pair, which):
    lane = lax.broadcasted_iota(jnp.int32, pair.shape, 1)
    keep = lane < 64 if which == 0 else lane >= 64
    return jnp.where(keep, pair, jnp.zeros_like(pair))


def with_flag(pair, flag, which):
    lane = lax.broadcasted_iota(jnp.int32, pair.shape, 1)
    keep = lane < 64 if which == 0 else lane >= 64
    spot = lane == (64 if which == 0 else 0)
    return jnp.where(keep, pair, jnp.where(spot, flag, jnp.zeros_like(pair)))


def attend_kernel(qkv_ref, bias_ref, out_ref, lse_ref):
    width = out_ref.shape[-1]
    rows = out_ref.shape[0] * out_ref.shape[2]
    bias = bias_ref[0]
    lane = lax.broadcasted_iota(jnp.int32, (rows, 128), 1)
    one = jnp.ones((rows, 128), BF16)
    totals = jnp.zeros((rows, 128), F32)
    for pair_index in range(width // 128):
        first = pair_index * 128
        query = qkv_ref[:, 0, :, first : first + 128].reshape(rows, 128)
        key = qkv_ref[:, 0, :, width + first : width + first + 128].reshape(rows, 128)
        value = qkv_ref[:, 0, :, 2 * width + first : 2 * width + first + 128].reshape(rows, 128)
        query = (query.astype(F32) * 0.125).astype(BF16)
        mixed = []
        for which in range(2):
            scores = matmul_nt(with_flag(query, one, which), with_flag(key, bias, which))
            top = jnp.max(scores, axis=-1, keepdims=True)
            weight = jnp.exp(scores - top)
            total = jnp.sum(weight, axis=-1, keepdims=True)
            mixed.append(matmul(weight.astype(BF16), value) * (1.0 / total))
            totals = jnp.where(lane == 2 * pair_index + which, top + jnp.log(total), totals)
        joined = jnp.where(lane < 64, mixed[0], mixed[1]).astype(BF16)
        out_ref[:, 0, :, first : first + 128] = joined.reshape(out_ref.shape[0], out_ref.shape[2], 128)
    lse_ref[0] = jnp.transpose(totals)[:8]


def attend_back_kernel(qkv_ref, bias_ref, lse_ref, grad_ref, out_ref):
    width = grad_ref.shape[-1]
    shape = (grad_ref.shape[0], grad_ref.shape[2], 128)
    rows = shape[0] * shape[1]
    bias = bias_ref[0]
    lane = lax.broadcasted_iota(jnp.int32, (rows, 128), 1)
    one = jnp.ones((rows, 128), BF16)
    for pair_index in range(width // 128):
        first = pair_index * 128
        query = qkv_ref[:, 0, :, first : first + 128].reshape(rows, 128)
        key = qkv_ref[:, 0, :, width + first : width + first + 128].reshape(rows, 128)
        value = qkv_ref[:, 0, :, 2 * width + first : 2 * width + first + 128].reshape(rows, 128)
        grad = grad_ref[:, 0, :, first : first + 128].reshape(rows, 128)
        query = (query.astype(F32) * 0.125).astype(BF16)
        query_parts, key_parts, value_parts = [], [], []
        for which in range(2):
            spot = 2 * pair_index + which
            log_total = lse_ref[0, spot : spot + 1, :]
            scores = matmul_nt(with_flag(key, bias, which), with_flag(query, one, which))
            probs = jnp.exp(scores - log_total)
            probs_grad = matmul_nt(value, half_lanes(grad, which))
            value_parts.append(matmul(probs.astype(BF16), grad))
            row_dot = jnp.sum(probs * probs_grad, axis=0, keepdims=True)
            score_grad = (probs * (probs_grad - row_dot)).astype(BF16)
            key_parts.append(matmul(score_grad, query))
            query_parts.append(matmul_tn(score_grad, key) * 0.125)
        for place, parts in enumerate((query_parts, key_parts, value_parts)):
            joined = jnp.where(lane < 64, parts[0], parts[1]).astype(BF16)
            start = place * width + first
            out_ref[:, 0, :, start : start + 128] = joined.reshape(shape)


def attention_call(kernel, arrays, outs, flops):
    def whole(array):
        shape = array.shape
        if len(shape) == 4:
            return pl.BlockSpec((shape[0], 1) + shape[2:], lambda s: (0, s, 0, 0))
        return pl.BlockSpec((1,) + shape[1:], lambda s: (s, 0, 0))

    return pl.pallas_call(
        kernel,
        grid=(arrays[0].shape[1],),
        in_specs=[whole(array) for array in arrays],
        out_specs=[whole(out) for out in outs],
        out_shape=outs,
        compiler_params=pltpu.CompilerParams(vmem_limit_bytes=40 * 1024 * 1024),
        cost_estimate=pl.CostEstimate(flops=flops, bytes_accessed=8 << 20, transcendentals=0),
    )(*arrays)


def shards(
    states,
    cotangent,
    lengths,
    slot_source,
    query_weight,
    query_bias,
    key_weight,
    value_weight,
    value_bias,
    output_weight,
    output_bias,
    first_gain,
    first_shift,
    inner_weight,
    inner_bias,
    outer_weight,
    outer_bias,
    final_gain,
    final_shift,
):
    seq_dev, block_len, width = states.shape
    n_dp, n_ctx, n_fsdp = (lax.axis_size(name) for name in OWNERS)
    assert (n_ctx, n_fsdp) == (4, 2)
    head_size = width // HEADS
    units = inner_weight.shape[1]
    tokens = seq_dev * block_len
    d, me, y = (lax.axis_index(name) for name in OWNERS)
    x, c = me // 2, me % 2
    own_heads = HEADS // n_ctx
    cols = own_heads * head_size
    aligned = n_dp == own_heads

    def other_half(local):
        return swap(local, "fsdp", 1)

    def ordered(own, other, axis=0):
        return jnp.where(
            y == 0, jnp.concatenate((own, other), axis), jnp.concatenate((other, own), axis)
        )

    def gathered(local, axis=0):
        return ordered(local, other_half(local), axis)

    wide = (query_bias, value_bias, output_bias, first_gain, first_shift, outer_bias, final_gain, final_shift)
    packed = jnp.concatenate([v.reshape(1, -1) for v in wide] + [inner_bias.reshape(-1, width // 2)])
    other_packed = other_half(packed)
    both = jnp.where(y == 0, jnp.stack((packed, other_packed)), jnp.stack((other_packed, packed)))
    b_query, b_value, b_out, g_first, s_first, b_outer, g_final, s_final = (
        both[:, i].reshape(width).astype(F32) for i in range(8)
    )
    b_inner = both[:, 8:].reshape(2 * n_dp, 2, -1)
    b_inner = pick(b_inner, c, 1).reshape(-1).astype(F32)

    def head_cols(matrix):
        parts = matrix.reshape(matrix.shape[:-1] + (own_heads, n_ctx, head_size))
        return pick(parts, me, parts.ndim - 2).reshape(matrix.shape[:-1] + (cols,))

    w_qkv = gathered(
        jnp.concatenate((head_cols(query_weight), head_cols(key_weight), head_cols(value_weight)), 1)
    )
    b_qkv = jnp.concatenate((head_cols(b_query), jnp.zeros((cols,), F32), head_cols(b_value)))

    from_x = swap(states, "ctx", 2)
    from_core = swap(states, "ctx", 1)
    from_far = swap(from_x, "ctx", 1)
    states_all = jnp.stack((states, from_core, from_x, from_far))
    flat_all = states_all.reshape(-1, width)

    out_rows = output_weight.reshape(-1, 2, 2, head_size, width)
    out_rows = pick(out_rows, c, 2)
    w_out = gathered(out_rows)
    w_out = jnp.concatenate((pick(w_out, x, 1), pick(w_out, 1 - x, 1)), 0).reshape(-1, width)
    block = units // (4 * n_dp)
    w_inner = gathered(
        pick(inner_weight.reshape(width // 2, 2 * n_dp, 2, block), c, 2).reshape(width // 2, -1)
    )
    w_outer = gathered(pick(outer_weight.reshape(n_dp, 2, block, width), c, 1).reshape(-1, width))

    qkv = (matmul(flat_all, w_qkv) + b_qkv).astype(BF16)
    qkv = qkv.reshape(n_ctx, seq_dev, block_len, 3 * cols)

    my_seqs = (d * n_fsdp + y) * seq_dev + jnp.arange(seq_dev, dtype=jnp.int32)
    seq_len = jnp.sum(jnp.where(slot_source[None, :] == my_seqs[:, None], lengths[None, :], 0), axis=1)
    places = (me ^ jnp.arange(n_ctx, dtype=jnp.int32))[:, None] * block_len + jnp.arange(
        block_len, dtype=jnp.int32
    )
    key_ok = places.reshape(1, -1) < seq_len[:, None]
    key_bias = jnp.where(key_ok, 0.0, MASKED).astype(BF16)
    key_bias = jnp.broadcast_to(key_bias[:, :, None], key_bias.shape + (128,))
    valid_rows = (places[0][None, :] < seq_len[:, None]).astype(F32).reshape(-1, 1)

    full_len = n_ctx * block_len
    score_flops = 2 * seq_dev * own_heads * full_len * full_len * 128
    attended_all, log_total = attention_call(
        attend_kernel,
        (qkv, key_bias),
        (
            jax.ShapeDtypeStruct((n_ctx, seq_dev, block_len, cols), BF16),
            jax.ShapeDtypeStruct((seq_dev, 8, full_len), F32),
        ),
        2 * score_flops,
    )
    near = attended_all[:2].reshape(-1, cols)
    far = swap(attended_all[2:], "ctx", 2).reshape(-1, cols)
    attended = jnp.concatenate((near, far), axis=1)

    def share(own):
        return jnp.concatenate((own, swap(own, "ctx", 1)), axis=0)

    def collect(both_rows):
        return both_rows[:tokens] + swap(both_rows[tokens:].astype(BF16), "ctx", 1).astype(F32)

    flat_in = states.reshape(-1, width)
    first_sum = flat_in.astype(F32) + collect(matmul(attended, w_out)) + b_out
    first_out, first_norm, first_inverse = norm_rows(first_sum, g_first, s_first)
    first_low = share(first_out.astype(BF16))
    hidden = matmul(first_low, w_inner) + b_inner
    below = 0.5 * (1.0 + lax.erf(hidden * math.sqrt(0.5)))
    slope = (below + hidden * jnp.exp(-0.5 * hidden * hidden) * (1.0 / math.sqrt(2 * math.pi))).astype(BF16)
    activated = (hidden * below).astype(BF16)
    second_sum = first_out + collect(matmul(activated, w_outer)) + b_outer
    second_out, second_norm, second_inverse = norm_rows(second_sum, g_final, s_final)
    encoded = (second_out * valid_rows).astype(BF16).reshape(states.shape)

    out_grad = cotangent.reshape(-1, width).astype(F32) * valid_rows
    final_gain_part = jnp.sum(out_grad * second_norm, axis=0)
    final_shift_part = jnp.sum(out_grad, axis=0)
    second_grad = norm_back(out_grad, second_norm, second_inverse, g_final)
    outer_round_own = second_grad.astype(BF16)
    outer_bias_part = col_sum(outer_round_own)
    outer_round = share(outer_round_own)
    outer_weight_part = matmul_tn(activated, outer_round).astype(BF16)
    hidden_grad = (matmul_nt(outer_round, w_outer) * slope.astype(F32)).astype(BF16)
    inner_bias_part = col_sum(hidden_grad)
    inner_weight_part = matmul_tn(first_low, hidden_grad).astype(BF16)
    first_grad = second_grad + collect(matmul_nt(hidden_grad, w_inner))
    first_gain_part = jnp.sum(first_grad * first_norm, axis=0)
    first_shift_part = jnp.sum(first_grad, axis=0)
    sum_grad = norm_back(first_grad, first_norm, first_inverse, g_first)
    branch_own = sum_grad.astype(BF16)
    output_bias_part = col_sum(branch_own)
    branch_grad = share(branch_own)
    output_weight_part = matmul_tn(attended, branch_grad).astype(BF16)
    attended_grad = matmul_nt(branch_grad, w_out).astype(BF16)
    near_grad = attended_grad[:, :cols]
    far_grad = swap(attended_grad[:, cols:], "ctx", 2)
    attended_grad_all = jnp.concatenate((near_grad, far_grad), 0).reshape(attended_all.shape)
    (qkv_grad,) = attention_call(
        attend_back_kernel,
        (qkv, key_bias, log_total, attended_grad_all),
        (jax.ShapeDtypeStruct(qkv.shape, BF16),),
        5 * score_flops,
    )
    flat_grad = qkv_grad.reshape(-1, 3 * cols)
    bias_part = col_sum(flat_grad)
    qkv_weight_part = matmul_tn(flat_all, flat_grad).astype(BF16)
    input_part = matmul_nt(flat_grad, w_qkv).reshape(n_ctx, tokens, width)
    to_core = swap(jnp.stack((input_part[1], input_part[3])).astype(BF16), "ctx", 1)
    to_x = swap((input_part[2] + to_core[1].astype(F32)).astype(BF16), "ctx", 2)
    input_grad = sum_grad + input_part[0] + to_core[0].astype(F32) + to_x.astype(F32)
    input_grad = input_grad.astype(BF16).reshape(states.shape)

    token_sums = jnp.stack(
        (final_gain_part, final_shift_part, outer_bias_part, first_gain_part, first_shift_part, output_bias_part)
    )
    if not aligned:
        def placed_heads(part):
            whole = jnp.zeros(part.shape[:-1] + (own_heads, n_ctx, head_size), part.dtype)
            part = part.reshape(part.shape[:-1] + (own_heads, 1, head_size))
            return lax.dynamic_update_slice_in_dim(whole, part, me, part.ndim - 2).reshape(
                part.shape[:-3] + (width,)
            )

        def placed_units(part, axis):
            split = part.shape[:axis] + (2 * n_dp, 1, block) + part.shape[axis + 1 :]
            whole = jnp.zeros(split[: axis + 1] + (2,) + split[axis + 2 :], part.dtype)
            whole = lax.dynamic_update_slice_in_dim(whole, part.reshape(split), c, axis + 1)
            return whole.reshape(part.shape[:axis] + (units,) + part.shape[axis + 1 :])

        def placed_rows(part):
            part = part.reshape(2, own_heads, 1, 1, head_size, width)
            whole = jnp.zeros((own_heads, 2, 2, head_size, width), part.dtype)
            whole = lax.dynamic_update_slice(whole, part[0], (0, x, c, 0, 0))
            whole = lax.dynamic_update_slice(whole, part[1], (0, 1 - x, c, 0, 0))
            return whole.reshape(width, width)

        def owned(part):
            return lax.psum_scatter(part, OWNERS, scatter_dimension=0, tiled=True).astype(F32)

        qkv_weights = [owned(placed_heads(qkv_weight_part[:, i * cols : (i + 1) * cols])) for i in range(3)]
        query_bias_own = owned(placed_heads(bias_part[:cols]))
        value_bias_own = owned(placed_heads(bias_part[2 * cols :]))
        output_weight_own = owned(placed_rows(output_weight_part))
        inner_weight_own = owned(placed_units(inner_weight_part, 1))
        inner_bias_own = owned(placed_units(inner_bias_part, 0))
        outer_weight_own = owned(placed_units(outer_weight_part, 0))
        sums = [owned(token_sums[i]) for i in range(6)]
    else:

        def halved(part, index, axis, name, mask, kind=add_low):
            there = swap(pick(part, 1 - index, axis), name, mask)
            return kind(pick(part, index, axis), there)

        def over_z(part, kind):
            part = part.reshape((2, 2) + part.shape[1:])
            part = halved(part, d % 2, 1, "dp", 1, kind)
            return halved(part, d // 2, 0, "dp", 2, lambda a, b: a.astype(F32) + b.astype(F32))

        def scattered(part):
            half = n_dp // 2
            one, two = part[:half], part[half:]
            one = halved(one, x, 1, "ctx", 2)
            two = halved(two, y, 2, "fsdp", 1)
            one = halved(one, y, 1, "fsdp", 1)
            two = halved(two, x, 1, "ctx", 2)
            return over_z(jnp.concatenate((one, two)), add_low)

        rows = width // (8 * n_dp)
        outer_weight_own = scattered(outer_weight_part.reshape(n_dp, 2, 2, -1, width))
        inner_pieces = inner_weight_part.reshape(n_dp, 2, 2, 2, rows, units // 2)
        inner_pieces = jnp.swapaxes(inner_pieces, 2, 3).reshape(n_dp, 2, 2, 2 * rows, units // 2)
        inner_sum = scattered(inner_pieces).reshape(2, rows, units // 2)
        inner_there = swap(pick(inner_sum, 1 - c, 0), "ctx", 1)
        inner_here = pick(inner_sum, c, 0)
        inner_both = jnp.where(c == 0, jnp.stack((inner_here, inner_there)), jnp.stack((inner_there, inner_here)))
        inner_both = inner_both.reshape(2, rows, 2 * n_dp, block)
        inner_weight_own = jnp.transpose(inner_both, (1, 2, 0, 3)).reshape(rows, units)
        out_pieces = output_weight_part.reshape(2, n_dp, 2, rows, width)
        out_mine, out_there = out_pieces[0], swap(out_pieces[1], "ctx", 2)
        out_sum = halved(add_low(out_mine, out_there), y, 1, "fsdp", 1)
        output_weight_own = over_z(out_sum, add_low)
        qkv_pieces = qkv_weight_part.reshape(n_dp, n_ctx, 2, rows, 3 * cols)
        qkv_sum = over_z(halved(qkv_pieces, y, 2, "fsdp", 1), add_low)
        qkv_sum = lax.all_to_all(qkv_sum, "ctx", 0, 0)
        qkv_sum = qkv_sum.reshape(n_ctx, rows, 3, own_heads, head_size)
        qkv_sum = jnp.transpose(qkv_sum, (2, 1, 3, 0, 4)).reshape(3, rows, width)
        qkv_weights = [qkv_sum[0], qkv_sum[1], qkv_sum[2]]

        def add(a, b):
            return a + b

        pieces = token_sums.reshape(6, n_dp, 2, 2, 2, rows)
        pieces = halved(pieces, c, 3, "ctx", 1, add)
        pieces = jnp.transpose(pieces, (1, 2, 3, 0, 4)).reshape(n_dp, 2, 2, 6 * rows)
        pieces = jnp.concatenate((pieces, inner_bias_part.reshape(n_dp, 2, 2, -1)), -1)
        pieces = halved(pieces, x, 1, "ctx", 2, add)
        query_piece = bias_part[:cols].reshape(n_dp, 2, rows)
        value_piece = bias_part[2 * cols :].reshape(n_dp, 2, rows)
        pieces = jnp.concatenate((pieces, query_piece, value_piece), -1)
        pieces = over_z(halved(pieces, y, 1, "fsdp", 1, add), add)
        sums = [pieces[i * rows : (i + 1) * rows] for i in range(6)]
        spot = 6 * rows + units // (8 * n_dp)
        inner_bias_own = pieces[6 * rows : spot]
        query_bias_own = pieces[spot : spot + rows]
        value_bias_own = pieces[spot + rows : spot + 2 * rows]

    return (
        encoded,
        input_grad,
        qkv_weights[0],
        query_bias_own,
        qkv_weights[1],
        qkv_weights[2],
        value_bias_own,
        output_weight_own,
        sums[5],
        sums[3],
        sums[4],
        inner_weight_own,
        inner_bias_own,
        outer_weight_own,
        sums[2],
        sums[0],
        sums[1],
    )


def solution(mesh):
    tokens = P(("dp", "fsdp"), "ctx", None)
    matrix, vector = P("fsdp", None), P("fsdp")
    own_matrix, own_vector = P(OWNERS, None), P(OWNERS)
    return jax.shard_map(
        shards,
        mesh=mesh,
        in_specs=(
            tokens,
            tokens,
            P(),
            P(),
            matrix,
            vector,
            matrix,
            matrix,
            vector,
            matrix,
            vector,
            vector,
            vector,
            matrix,
            vector,
            matrix,
            vector,
            vector,
            vector,
        ),
        out_specs=(
            tokens,
            tokens,
            own_matrix,
            own_vector,
            own_matrix,
            own_matrix,
            own_vector,
            own_matrix,
            own_vector,
            own_vector,
            own_vector,
            own_matrix,
            own_vector,
            own_matrix,
            own_vector,
            own_vector,
            own_vector,
        ),
        check_vma=False,
    )
```

```python
import functools
import math

import jax
import jax.numpy as jnp
from jax import lax
from jax.experimental import pallas as pl
from jax.experimental.pallas import tpu as pltpu
from jax.sharding import PartitionSpec as P

HEADS = 16
EPS = 1e-12
MASKED = -1e30
F32 = jnp.float32
BF16 = jnp.bfloat16
OWNERS = ("dp", "ctx", "fsdp")


def swap(value, axis, mask):
    pairs = [(source, source ^ mask) for source in range(lax.axis_size(axis))]
    return lax.ppermute(value, axis, pairs)


def pick(array, index, axis):
    return lax.dynamic_index_in_dim(array, index, axis, keepdims=False)


def add_low(left, right):
    return (left.astype(F32) + right.astype(F32)).astype(BF16)


def matmul(left, right):
    return jnp.dot(left, right, preferred_element_type=F32)


def matmul_tn(left, right):
    return lax.dot_general(left, right, (((0,), (0,)), ((), ())), preferred_element_type=F32)


def matmul_nt(left, right):
    return lax.dot_general(left, right, (((1,), (1,)), ((), ())), preferred_element_type=F32)


def col_sum(matrix):
    return jnp.sum(matrix.astype(F32), axis=0)


def norm_rows(summed, scale_vec, shift_vec):
    row_mean = jnp.mean(summed, axis=-1, keepdims=True)
    centered = summed - row_mean
    inverse = lax.rsqrt(jnp.mean(centered * centered, axis=-1, keepdims=True) + EPS)
    normed = centered * inverse
    return (normed * scale_vec + shift_vec, normed, inverse)


def norm_back(upstream, normed, inverse, scale_vec):
    scaled = upstream * scale_vec
    return inverse * (
        scaled
        - jnp.mean(scaled, axis=-1, keepdims=True)
        - normed * jnp.mean(scaled * normed, axis=-1, keepdims=True)
    )


def half_lanes(pair, which):
    lane = lax.broadcasted_iota(jnp.int32, pair.shape, 1)
    keep = lane < 64 if which == 0 else lane >= 64
    return jnp.where(keep, pair, jnp.zeros_like(pair))


def with_flag(pair, flag, which):
    lane = lax.broadcasted_iota(jnp.int32, pair.shape, 1)
    keep = lane < 64 if which == 0 else lane >= 64
    spot = lane == (64 if which == 0 else 0)
    return jnp.where(keep, pair, jnp.where(spot, flag, jnp.zeros_like(pair)))


def attend_kernel(qkv_ref, bias_ref, out_ref, lse_ref):
    width = out_ref.shape[-1]
    rows = out_ref.shape[0] * out_ref.shape[2]
    bias = bias_ref[0]
    lane = lax.broadcasted_iota(jnp.int32, (rows, 128), 1)
    one = jnp.ones((rows, 128), BF16)
    totals = jnp.zeros((rows, 128), F32)
    for pair_index in range(width // 128):
        first = pair_index * 128
        query = qkv_ref[:, 0, :, first : first + 128].reshape(rows, 128)
        key = qkv_ref[:, 0, :, width + first : width + first + 128].reshape(rows, 128)
        value = qkv_ref[:, 0, :, 2 * width + first : 2 * width + first + 128].reshape(rows, 128)
        query = (query.astype(F32) * 0.125).astype(BF16)
        mixed = []
        for which in range(2):
            scores = matmul_nt(with_flag(query, one, which), with_flag(key, bias, which))
            top = jnp.max(scores, axis=-1, keepdims=True)
            weight = jnp.exp(scores - top)
            total = jnp.sum(weight, axis=-1, keepdims=True)
            mixed.append(matmul(weight.astype(BF16), value) * (1.0 / total))
            totals = jnp.where(lane == 2 * pair_index + which, top + jnp.log(total), totals)
        joined = jnp.where(lane < 64, mixed[0], mixed[1]).astype(BF16)
        out_ref[:, 0, :, first : first + 128] = joined.reshape(out_ref.shape[0], out_ref.shape[2], 128)
    lse_ref[0] = jnp.transpose(totals)[:8]


def attend_back_kernel(qkv_ref, bias_ref, lse_ref, grad_ref, out_ref):
    width = grad_ref.shape[-1]
    shape = (grad_ref.shape[0], grad_ref.shape[2], 128)
    rows = shape[0] * shape[1]
    bias = bias_ref[0]
    lane = lax.broadcasted_iota(jnp.int32, (rows, 128), 1)
    one = jnp.ones((rows, 128), BF16)
    for pair_index in range(width // 128):
        first = pair_index * 128
        query = qkv_ref[:, 0, :, first : first + 128].reshape(rows, 128)
        key = qkv_ref[:, 0, :, width + first : width + first + 128].reshape(rows, 128)
        value = qkv_ref[:, 0, :, 2 * width + first : 2 * width + first + 128].reshape(rows, 128)
        grad = grad_ref[:, 0, :, first : first + 128].reshape(rows, 128)
        query = (query.astype(F32) * 0.125).astype(BF16)
        query_parts, key_parts, value_parts = [], [], []
        for which in range(2):
            spot = 2 * pair_index + which
            log_total = lse_ref[0, spot : spot + 1, :]
            scores = matmul_nt(with_flag(key, bias, which), with_flag(query, one, which))
            probs = jnp.exp(scores - log_total)
            probs_grad = matmul_nt(value, half_lanes(grad, which))
            value_parts.append(matmul(probs.astype(BF16), grad))
            row_dot = jnp.sum(probs * probs_grad, axis=0, keepdims=True)
            score_grad = (probs * (probs_grad - row_dot)).astype(BF16)
            key_parts.append(matmul(score_grad, query))
            query_parts.append(matmul_tn(score_grad, key) * 0.125)
        for place, parts in enumerate((query_parts, key_parts, value_parts)):
            joined = jnp.where(lane < 64, parts[0], parts[1]).astype(BF16)
            start = place * width + first
            out_ref[:, 0, :, start : start + 128] = joined.reshape(shape)


def attention_call(kernel, arrays, outs, flops):
    def whole(array):
        shape = array.shape
        if len(shape) == 4:
            return pl.BlockSpec((shape[0], 1) + shape[2:], lambda s: (0, s, 0, 0))
        return pl.BlockSpec((1,) + shape[1:], lambda s: (s, 0, 0))

    return pl.pallas_call(
        kernel,
        grid=(arrays[0].shape[1],),
        in_specs=[whole(array) for array in arrays],
        out_specs=[whole(out) for out in outs],
        out_shape=outs,
        compiler_params=pltpu.CompilerParams(vmem_limit_bytes=40 * 1024 * 1024),
        cost_estimate=pl.CostEstimate(flops=flops, bytes_accessed=8 << 20, transcendentals=0),
    )(*arrays)


MESH = pl.DeviceIdType.MESH


def repeat(count, body):
    def step(index, carry):
        body(index)
        return carry

    lax.fori_loop(0, count, step, 0)


class Slots:
    def __init__(self):
        self.total = 0

    def take(self, count=1):
        first = self.total
        self.total += count
        return first


def layer_kernel(
    lens_ref,
    states,
    cotangent,
    wq_own,
    vec_own,
    wo_own,
    wi_own,
    wu_own,
    encoded_out,
    st_all,
    wq_all,
    vec_all,
    w_out,
    w_in,
    w_ou,
    vecs,
    qkv,
    lse,
    att,
    att_far,
    part_far,
    part_in,
    part_far2,
    part_in2,
    first_norm,
    first_inv,
    first_out,
    low2,
    act,
    slope,
    acc,
    send,
    recv,
    local,
):
    d, me, y = lax.axis_index("dp"), lax.axis_index("ctx"), lax.axis_index("fsdp")
    x, c = me // 2, me % 2
    to_core = {"ctx": me + 1 - 2 * c}
    to_x = {"ctx": (me + 2) % 4}
    to_y = {"fsdp": 1 - y}
    to_z = {"dp": d + 1 - 2 * (d % 2)}
    to_zz = {"dp": (d + 2) % 4}
    to_far = {"ctx": 3 - me}
    slots = Slots()
    pending = []

    def remote(src, dst, slot, device):
        return pltpu.make_async_remote_copy(
            src_ref=src,
            dst_ref=dst,
            send_sem=send.at[slot],
            recv_sem=recv.at[slot],
            device_id=device,
            device_id_type=MESH,
        )

    def at_end(count, make):
        pending.append((count, make))

    local_slots = Slots()

    def fetch(src, dst):
        copy = pltpu.make_async_copy(src, dst, local.at[local_slots.take()])
        copy.start()
        return copy

    barrier = pltpu.get_barrier_semaphore()
    for device in (to_core, to_x, to_y, to_z, to_zz, to_far):
        pl.semaphore_signal(barrier, inc=1, device_id=device, device_id_type=MESH)
    pl.semaphore_wait(barrier, 6)

    first = slots.take(4)
    state_x = lambda s: remote(states.at[s], st_all.at[2, s], first + s, to_x)
    second = slots.take(4)
    state_core = lambda s: remote(states.at[s], st_all.at[1, s], second + s, to_core)
    third = slots.take(4)
    state_far = lambda s: remote(st_all.at[2, s], st_all.at[3, s], third + s, to_core)
    wq_slot = slots.take()
    wq_copy = remote(wq_own, wq_all.at[pl.ds(pl.multiple_of(y * 512, 512), 512)], wq_slot, to_y)
    vec_slot = slots.take()
    vec_copy = remote(vec_own, vec_all.at[y], vec_slot, to_y)
    for s in range(4):
        state_x(s).start()
    wq_copy.start()
    vec_copy.start()
    for s in range(4):
        state_core(s).start()
    at_end(4, state_x)
    at_end(4, state_core)
    at_end(4, state_far)
    at_end(1, lambda _: wq_copy)
    at_end(1, lambda _: vec_copy)

    p = d % 2
    wo_slot = slots.take(2)

    def wo_copy(side):
        src = wo_own.at[pl.ds(pl.multiple_of(p * 256 + side * 128 + c * 64, 64), 64)]
        return remote(src, w_out.at[x if side == 0 else 1 - x, 2 * y + p], wo_slot + side, to_y)

    wo_pass_slot = slots.take(2)

    def wo_pass(side):
        here = w_out.at[x if side == 0 else 1 - x, 2 * (1 - y) + p]
        return remote(here, here, wo_pass_slot + side, to_z)

    wi_slot = slots.take(8)

    def wi_copy(b):
        src = wi_own.at[
            pl.ds(pl.multiple_of(x * 256, 256), 256), pl.ds(pl.multiple_of((2 * b + c) * 256, 256), 256)
        ]
        dst = w_in.at[
            pl.ds(pl.multiple_of(y * 512 + x * 256, 256), 256), pl.ds(pl.multiple_of(b * 256, 256), 256)
        ]
        return remote(src, dst, wi_slot + b, to_y)

    wi_pass_slot = slots.take(8)

    def wi_pass(b):
        here = w_in.at[
            pl.ds(pl.multiple_of((1 - y) * 512 + x * 256, 256), 256),
            pl.ds(pl.multiple_of(b * 256, 256), 256),
        ]
        return remote(here, here, wi_pass_slot + b, to_x)

    wu_slot = slots.take(4)

    def wu_copy(k):
        side, half = k // 2, k % 2
        src = wu_own.at[pl.ds(pl.multiple_of((p * 4 + side * 2 + c) * 256 + half * 128, 128), 128)]
        dst = w_ou.at[pl.ds(pl.multiple_of((4 * y + 2 * p + side) * 256 + half * 128, 128), 128)]
        return remote(src, dst, wu_slot + k, to_y)

    wu_pass_slot = slots.take(4)

    def wu_pass(k):
        side, half = k // 2, k % 2
        here = w_ou.at[
            pl.ds(pl.multiple_of((4 * (1 - y) + 2 * p + side) * 256 + half * 128, 128), 128)
        ]
        return remote(here, here, wu_pass_slot + k, to_z)

    for side in range(2):
        wo_copy(side).start()
    for b in range(8):
        wi_copy(b).start()
    for k in range(4):
        wu_copy(k).start()
    for count, make in ((2, wo_copy), (2, wo_pass), (8, wi_copy), (8, wi_pass), (4, wu_copy), (4, wu_pass)):
        at_end(count, make)

    own_early = [
        fetch(states, st_all.at[0]),
        fetch(wq_own, wq_all.at[pl.ds(pl.multiple_of(y * 512, 512), 512)]),
        fetch(vec_own, vec_all.at[y]),
    ]
    own_out = []
    for half in range(2):
        for side in range(2):
            src = wo_own.at[pl.ds(pl.multiple_of(half * 256 + side * 128 + c * 64, 64), 64)]
            own_out.append(fetch(src, w_out.at[x if side == 0 else 1 - x, 2 * y + half]))
    own_late = []
    for b in range(8):
        src = wi_own.at[:, pl.ds(pl.multiple_of((2 * b + c) * 256, 256), 256)]
        dst = w_in.at[pl.ds(pl.multiple_of(y * 512, 512), 512), pl.ds(b * 256, 256)]
        own_late.append(fetch(src, dst))
    for half in range(2):
        for side in range(2):
            src = wu_own.at[pl.ds(pl.multiple_of((half * 4 + side * 2 + c) * 256, 256), 256)]
            dst = w_ou.at[pl.ds(pl.multiple_of((4 * y + 2 * half + side) * 256, 256), 256)]
            own_late.append(fetch(src, dst))

    for s in range(2):
        state_x(s).wait_recv()
        state_far(s).start()
    for copy in own_early:
        copy.wait()
    vec_copy.wait_recv()
    vecs[:, :512] = vec_all[0].astype(F32)
    vecs[:, 512:] = vec_all[1].astype(F32)
    wq_copy.wait_recv()

    att_slot = slots.take(8)

    def att_copy(s, j):
        rows = pl.ds(pl.multiple_of(j * 512 + s * 128, 128), 128)
        return remote(att_far.at[j, s], att.at[rows, 256:512], att_slot + 2 * s + j, to_x)

    at_end(8, lambda k: att_copy(k // 2, k % 2))
    q_bias = jnp.concatenate((vecs[0:1, 0:128], vecs[0:1, 512:640]), 1)
    v_bias = jnp.concatenate((vecs[0:1, 128:256], vecs[0:1, 640:768]), 1)

    def key_flags(s):
        pieces = []
        for j in range(4):
            position = lax.broadcasted_iota(jnp.int32, (128, 128), 0)
            place = me + 1 - 2 * c if j == 1 else me
            place = (place + 2) % 4 if j == 2 else place
            place = 3 - me if j == 3 else place
            pieces.append(jnp.where(position + place * 128 < lens_ref[s], 0.0, MASKED))
        return jnp.concatenate(pieces, 0).astype(BF16)

    def attention(s):
        @pl.when(s < 2)
        def _():
            state_x(s + 2).wait_recv()
            state_far(s + 2).start()

        @pl.when(s == 3)
        def _():
            for side in range(2):
                wo_copy(side).wait_recv()
                wo_pass(side).start()

        state_core(s).wait_recv()
        state_far(s).wait_recv()
        rows = st_all[:, s].reshape(512, 1024)
        for place in range(3):
            made = matmul(rows, wq_all[:, place * 256 : place * 256 + 256])
            made = made + q_bias if place == 0 else made
            made = made + v_bias if place == 2 else made
            qkv[:, s, :, place * 256 : place * 256 + 256] = made.astype(BF16).reshape(4, 128, 256)
        bias = key_flags(s)
        lane = lax.broadcasted_iota(jnp.int32, (512, 128), 1)
        one = jnp.ones((512, 128), BF16)
        totals = jnp.zeros((512, 128), F32)
        for pair in range(2):
            base = pair * 128
            query = qkv[:, s, :, base : base + 128].reshape(512, 128)
            key = qkv[:, s, :, 256 + base : 384 + base].reshape(512, 128)
            value = qkv[:, s, :, 512 + base : 640 + base].reshape(512, 128)
            query = (query.astype(F32) * 0.125).astype(BF16)
            mixed = []
            for which in range(2):
                scores = matmul_nt(with_flag(query, one, which), with_flag(key, bias, which))
                top = jnp.max(scores, axis=-1, keepdims=True)
                weight = jnp.exp(scores - top)
                total = jnp.sum(weight, axis=-1, keepdims=True)
                mixed.append(matmul(weight.astype(BF16), value) * (1.0 / total))
                totals = jnp.where(lane == 2 * pair + which, top + jnp.log(total), totals)
            joined = jnp.where(lane < 64, mixed[0], mixed[1]).astype(BF16)
            for j in range(2):
                rows_j = pl.ds(pl.multiple_of(j * 512 + s * 128, 128), 128)
                att[rows_j, base : base + 128] = joined[j * 128 : j * 128 + 128]
                att_far[j, s, :, base : base + 128] = joined[256 + j * 128 : 384 + j * 128]
        for j in range(2):
            att_copy(s, j).start()
        lse[s] = jnp.transpose(totals)[:8]

    repeat(4, attention)

    def pass_inner(b):
        wi_copy(b).wait_recv()
        wi_pass(b).start()

    for b in range(4):
        pass_inner(b)
    for copy in own_out:
        copy.wait()
    for side in range(2):
        wo_pass(side).wait_recv()
    for s in range(4):
        for j in range(2):
            att_copy(s, j).wait_recv()
    out_slot = slots.take(4)

    def out_copy(n):
        return remote(part_far.at[n], part_in.at[n], out_slot + n, to_core)

    at_end(4, out_copy)
    for n in range(4):
        right = w_out[:, :, :, n * 256 : n * 256 + 256].reshape(512, 256)
        part_far[n] = matmul(att[512:], right).astype(BF16)
        out_copy(n).start()
    for b in range(4, 6):
        pass_inner(b)
    for n in range(4):
        right = w_out[:, :, :, n * 256 : n * 256 + 256].reshape(512, 256)
        made = matmul(att[:512], right) + vecs[1:2, n * 256 : n * 256 + 256]
        made = made + st_all[0, :, :, n * 256 : n * 256 + 256].astype(F32).reshape(512, 256)
        out_copy(n).wait_recv()
        first_norm[:, n * 256 : n * 256 + 256] = made + part_in[n].astype(F32)

    low_slot = slots.take(4)

    def low_copy(k):
        src = low2.at[pl.ds(pl.multiple_of(k * 128, 128), 128)]
        dst = low2.at[pl.ds(pl.multiple_of(512 + k * 128, 128), 128)]
        return remote(src, dst, low_slot + k, to_core)

    at_end(4, low_copy)

    def norm_first(k):
        for half in range(2):
            rows = pl.ds(pl.multiple_of(k * 128 + half * 64, 64), 64)
            made, normed, inverse = norm_rows(first_norm[rows, :], vecs[2:3, :], vecs[3:4, :])
            first_norm[rows, :] = normed
            first_inv[rows, :] = jnp.broadcast_to(inverse, (64, 128))
            first_out[rows, :] = made
            low2[rows, :] = made.astype(BF16)
        low_copy(k).start()

    repeat(4, norm_first)
    for b in range(6, 8):
        pass_inner(b)
    for k in range(4):
        low_copy(k).wait_recv()
    for copy in own_late:
        copy.wait()

    def unit_block(b):
        wi_pass(b).wait_recv()
        here = pl.ds(pl.multiple_of(b * 256, 256), 256)
        spot = pl.ds(pl.multiple_of((b // 4) * 512 + c * 256, 256), 256)
        row = vecs[pl.ds(8 + b % 4, 1), spot]
        for m in range(2):
            hidden = matmul(low2[m * 512 : m * 512 + 512, :], w_in[:, here]) + row
            below = 0.5 * (1.0 + lax.erf(hidden * math.sqrt(0.5)))
            bell = jnp.exp(-0.5 * hidden * hidden) * (1.0 / math.sqrt(2 * math.pi))
            act[m * 512 : m * 512 + 512, here] = (hidden * below).astype(BF16)
            slope[m * 512 : m * 512 + 512, here] = (below + hidden * bell).astype(BF16)

    repeat(8, unit_block)
    mine = pl.ds(pl.multiple_of(y * 1024, 1024), 1024)
    theirs = pl.ds(pl.multiple_of((1 - y) * 1024, 1024), 1024)
    for k in range(2):
        wu_copy(k).wait_recv()
        wu_pass(k).start()

    def outer_own(n):
        here = pl.ds(pl.multiple_of(n * 256, 256), 256)
        for m in range(2):
            acc[m * 512 : m * 512 + 512, here] = matmul(
                act[m * 512 : m * 512 + 512, mine], w_ou[mine, here]
            )

    repeat(4, outer_own)
    for k in range(2, 4):
        wu_copy(k).wait_recv()
        wu_pass(k).start()
    for k in range(4):
        wu_pass(k).wait_recv()
    sum_slot = slots.take(4)

    def sum_copy(n):
        return remote(part_far2.at[n], part_in2.at[n], sum_slot + n, to_core)

    at_end(4, sum_copy)

    def outer_far(n):
        here = pl.ds(pl.multiple_of(n * 256, 256), 256)
        made = acc[512:, here] + matmul(act[512:, theirs], w_ou[theirs, here])
        part_far2[n] = made.astype(BF16)
        sum_copy(n).start()

    repeat(4, outer_far)

    def outer_near(n):
        here = pl.ds(pl.multiple_of(n * 256, 256), 256)
        made = acc[:512, here] + matmul(act[:512, theirs], w_ou[theirs, here])
        made = made + first_out[:, here] + vecs[4:5, here]
        sum_copy(n).wait_recv()
        acc[:512, here] = made + part_in2[n].astype(F32)

    repeat(4, outer_near)

    def norm_second(k):
        valid_place = lax.broadcasted_iota(jnp.int32, (128, 1), 0) + me * 128
        valid = jnp.where(valid_place < lens_ref[k], 1.0, 0.0)
        for half in range(2):
            rows = pl.ds(pl.multiple_of(k * 128 + half * 64, 64), 64)
            made, normed, inverse = norm_rows(acc[rows, :], vecs[5:6, :], vecs[6:7, :])
            encoded_out[rows, :] = (made * valid[half * 64 : half * 64 + 64]).astype(BF16)

    repeat(4, norm_second)
    for count, make in pending:
        for k in range(count):
            make(k).wait_send()


def layer_call(arrays):
    any_space = pl.BlockSpec(memory_space=pl.ANY)
    v = pltpu.VMEM
    return pl.pallas_call(
        layer_kernel,
        in_specs=[pl.BlockSpec(memory_space=pltpu.SMEM)] + [any_space] * 7,
        out_specs=pl.BlockSpec(memory_space=pltpu.VMEM),
        out_shape=jax.ShapeDtypeStruct((512, 1024), BF16),
        scratch_shapes=[
            v((4, 4, 128, 1024), BF16),
            v((1024, 768), BF16),
            v((2, 16, 512), BF16),
            v((2, 4, 64, 1024), BF16),
            v((1024, 2048), BF16),
            v((2048, 1024), BF16),
            v((16, 1024), F32),
            v((4, 4, 128, 768), BF16),
            v((4, 8, 512), F32),
            v((1024, 512), BF16),
            v((2, 4, 128, 256), BF16),
            v((4, 512, 256), BF16),
            v((4, 512, 256), BF16),
            v((4, 512, 256), BF16),
            v((4, 512, 256), BF16),
            v((512, 1024), F32),
            v((512, 128), F32),
            v((512, 1024), F32),
            v((1024, 1024), BF16),
            v((1024, 2048), BF16),
            v((1024, 2048), BF16),
            v((1024, 1024), F32),
            pltpu.SemaphoreType.DMA((80,)),
            pltpu.SemaphoreType.DMA((80,)),
            pltpu.SemaphoreType.DMA((40,)),
        ],
        compiler_params=pltpu.CompilerParams(
            collective_id=0, has_side_effects=True, vmem_limit_bytes=64 * 1024 * 1024 - 65536
        ),
    )(*arrays)


def shards(
    states,
    cotangent,
    lengths,
    slot_source,
    query_weight,
    query_bias,
    key_weight,
    value_weight,
    value_bias,
    output_weight,
    output_bias,
    first_gain,
    first_shift,
    inner_weight,
    inner_bias,
    outer_weight,
    outer_bias,
    final_gain,
    final_shift,
):
    seq_dev, block_len, width = states.shape
    n_dp, n_ctx, n_fsdp = (lax.axis_size(name) for name in OWNERS)
    assert (n_ctx, n_fsdp) == (4, 2)
    head_size = width // HEADS
    units = inner_weight.shape[1]
    tokens = seq_dev * block_len
    d, me, y = (lax.axis_index(name) for name in OWNERS)
    x, c = me // 2, me % 2
    own_heads = HEADS // n_ctx
    cols = own_heads * head_size
    aligned = n_dp == own_heads

    def other_half(local):
        return swap(local, "fsdp", 1)

    def ordered(own, other, axis=0):
        return jnp.where(
            y == 0, jnp.concatenate((own, other), axis), jnp.concatenate((other, own), axis)
        )

    def gathered(local, axis=0):
        return ordered(local, other_half(local), axis)

    wide = (query_bias, value_bias, output_bias, first_gain, first_shift, outer_bias, final_gain, final_shift)
    packed = jnp.concatenate([v.reshape(1, -1) for v in wide] + [inner_bias.reshape(-1, width // 2)])
    other_packed = other_half(packed)
    both = jnp.where(y == 0, jnp.stack((packed, other_packed)), jnp.stack((other_packed, packed)))
    b_query, b_value, b_out, g_first, s_first, b_outer, g_final, s_final = (
        both[:, i].reshape(width).astype(F32) for i in range(8)
    )
    b_inner = both[:, 8:].reshape(2 * n_dp, 2, -1)
    b_inner = pick(b_inner, c, 1).reshape(-1).astype(F32)

    def head_cols(matrix):
        parts = matrix.reshape(matrix.shape[:-1] + (own_heads, n_ctx, head_size))
        return pick(parts, me, parts.ndim - 2).reshape(matrix.shape[:-1] + (cols,))

    w_qkv = gathered(
        jnp.concatenate((head_cols(query_weight), head_cols(key_weight), head_cols(value_weight)), 1)
    )
    b_qkv = jnp.concatenate((head_cols(b_query), jnp.zeros((cols,), F32), head_cols(b_value)))

    from_x = swap(states, "ctx", 2)
    from_core = swap(states, "ctx", 1)
    from_far = swap(from_x, "ctx", 1)
    states_all = jnp.stack((states, from_core, from_x, from_far))
    flat_all = states_all.reshape(-1, width)

    out_rows = output_weight.reshape(-1, 2, 2, head_size, width)
    out_rows = pick(out_rows, c, 2)
    w_out = gathered(out_rows)
    w_out = jnp.concatenate((pick(w_out, x, 1), pick(w_out, 1 - x, 1)), 0).reshape(-1, width)
    block = units // (4 * n_dp)
    w_inner = gathered(
        pick(inner_weight.reshape(width // 2, 2 * n_dp, 2, block), c, 2).reshape(width // 2, -1)
    )
    w_outer = gathered(pick(outer_weight.reshape(n_dp, 2, block, width), c, 1).reshape(-1, width))

    qkv = (matmul(flat_all, w_qkv) + b_qkv).astype(BF16)
    qkv = qkv.reshape(n_ctx, seq_dev, block_len, 3 * cols)

    my_seqs = (d * n_fsdp + y) * seq_dev + jnp.arange(seq_dev, dtype=jnp.int32)
    seq_len = jnp.sum(jnp.where(slot_source[None, :] == my_seqs[:, None], lengths[None, :], 0), axis=1)
    places = (me ^ jnp.arange(n_ctx, dtype=jnp.int32))[:, None] * block_len + jnp.arange(
        block_len, dtype=jnp.int32
    )
    key_ok = places.reshape(1, -1) < seq_len[:, None]
    key_bias = jnp.where(key_ok, 0.0, MASKED).astype(BF16)
    key_bias = jnp.broadcast_to(key_bias[:, :, None], key_bias.shape + (128,))
    valid_rows = (places[0][None, :] < seq_len[:, None]).astype(F32).reshape(-1, 1)

    full_len = n_ctx * block_len
    score_flops = 2 * seq_dev * own_heads * full_len * full_len * 128
    attended_all, log_total = attention_call(
        attend_kernel,
        (qkv, key_bias),
        (
            jax.ShapeDtypeStruct((n_ctx, seq_dev, block_len, cols), BF16),
            jax.ShapeDtypeStruct((seq_dev, 8, full_len), F32),
        ),
        2 * score_flops,
    )
    near = attended_all[:2].reshape(-1, cols)
    far = swap(attended_all[2:], "ctx", 2).reshape(-1, cols)
    attended = jnp.concatenate((near, far), axis=1)

    def share(own):
        return jnp.concatenate((own, swap(own, "ctx", 1)), axis=0)

    def collect(both_rows):
        return both_rows[:tokens] + swap(both_rows[tokens:].astype(BF16), "ctx", 1).astype(F32)

    if aligned:
        half_bias = lambda v: pick(v.reshape(2, n_ctx, head_size), me, 1).reshape(1, -1)
        top = jnp.concatenate((half_bias(query_bias), half_bias(value_bias), jnp.zeros((1, 256), BF16)), 1)
        rows16 = [top] + [v.reshape(1, -1) for v in (output_bias, first_gain, first_shift, outer_bias, final_gain, final_shift)]
        rows16 += [jnp.zeros((1, 512), BF16), inner_bias.reshape(4, 512), jnp.zeros((4, 512), BF16)]
        vec_own = jnp.concatenate(rows16, 0)
        wq_own = jnp.concatenate((head_cols(query_weight), head_cols(key_weight), head_cols(value_weight)), 1)
        encoded_new = layer_call((seq_len, states, cotangent, wq_own, vec_own, output_weight, inner_weight, outer_weight))
    flat_in = states.reshape(-1, width)
    first_sum = flat_in.astype(F32) + collect(matmul(attended, w_out)) + b_out
    first_out, first_norm, first_inverse = norm_rows(first_sum, g_first, s_first)
    first_low = share(first_out.astype(BF16))
    hidden = matmul(first_low, w_inner) + b_inner
    below = 0.5 * (1.0 + lax.erf(hidden * math.sqrt(0.5)))
    slope = (below + hidden * jnp.exp(-0.5 * hidden * hidden) * (1.0 / math.sqrt(2 * math.pi))).astype(BF16)
    activated = (hidden * below).astype(BF16)
    second_sum = first_out + collect(matmul(activated, w_outer)) + b_outer
    second_out, second_norm, second_inverse = norm_rows(second_sum, g_final, s_final)
    encoded = (second_out * valid_rows).astype(BF16).reshape(states.shape)
    if aligned:
        encoded = encoded_new.reshape(states.shape)

    out_grad = cotangent.reshape(-1, width).astype(F32) * valid_rows
    final_gain_part = jnp.sum(out_grad * second_norm, axis=0)
    final_shift_part = jnp.sum(out_grad, axis=0)
    second_grad = norm_back(out_grad, second_norm, second_inverse, g_final)
    outer_round_own = second_grad.astype(BF16)
    outer_bias_part = col_sum(outer_round_own)
    outer_round = share(outer_round_own)
    outer_weight_part = matmul_tn(activated, outer_round).astype(BF16)
    hidden_grad = (matmul_nt(outer_round, w_outer) * slope.astype(F32)).astype(BF16)
    inner_bias_part = col_sum(hidden_grad)
    inner_weight_part = matmul_tn(first_low, hidden_grad).astype(BF16)
    first_grad = second_grad + collect(matmul_nt(hidden_grad, w_inner))
    first_gain_part = jnp.sum(first_grad * first_norm, axis=0)
    first_shift_part = jnp.sum(first_grad, axis=0)
    sum_grad = norm_back(first_grad, first_norm, first_inverse, g_first)
    branch_own = sum_grad.astype(BF16)
    output_bias_part = col_sum(branch_own)
    branch_grad = share(branch_own)
    output_weight_part = matmul_tn(attended, branch_grad).astype(BF16)
    attended_grad = matmul_nt(branch_grad, w_out).astype(BF16)
    near_grad = attended_grad[:, :cols]
    far_grad = swap(attended_grad[:, cols:], "ctx", 2)
    attended_grad_all = jnp.concatenate((near_grad, far_grad), 0).reshape(attended_all.shape)
    (qkv_grad,) = attention_call(
        attend_back_kernel,
        (qkv, key_bias, log_total, attended_grad_all),
        (jax.ShapeDtypeStruct(qkv.shape, BF16),),
        5 * score_flops,
    )
    flat_grad = qkv_grad.reshape(-1, 3 * cols)
    bias_part = col_sum(flat_grad)
    qkv_weight_part = matmul_tn(flat_all, flat_grad).astype(BF16)
    input_part = matmul_nt(flat_grad, w_qkv).reshape(n_ctx, tokens, width)
    to_core = swap(jnp.stack((input_part[1], input_part[3])).astype(BF16), "ctx", 1)
    to_x = swap((input_part[2] + to_core[1].astype(F32)).astype(BF16), "ctx", 2)
    input_grad = sum_grad + input_part[0] + to_core[0].astype(F32) + to_x.astype(F32)
    input_grad = input_grad.astype(BF16).reshape(states.shape)

    token_sums = jnp.stack(
        (final_gain_part, final_shift_part, outer_bias_part, first_gain_part, first_shift_part, output_bias_part)
    )
    if not aligned:
        def placed_heads(part):
            whole = jnp.zeros(part.shape[:-1] + (own_heads, n_ctx, head_size), part.dtype)
            part = part.reshape(part.shape[:-1] + (own_heads, 1, head_size))
            return lax.dynamic_update_slice_in_dim(whole, part, me, part.ndim - 2).reshape(
                part.shape[:-3] + (width,)
            )

        def placed_units(part, axis):
            split = part.shape[:axis] + (2 * n_dp, 1, block) + part.shape[axis + 1 :]
            whole = jnp.zeros(split[: axis + 1] + (2,) + split[axis + 2 :], part.dtype)
            whole = lax.dynamic_update_slice_in_dim(whole, part.reshape(split), c, axis + 1)
            return whole.reshape(part.shape[:axis] + (units,) + part.shape[axis + 1 :])

        def placed_rows(part):
            part = part.reshape(2, own_heads, 1, 1, head_size, width)
            whole = jnp.zeros((own_heads, 2, 2, head_size, width), part.dtype)
            whole = lax.dynamic_update_slice(whole, part[0], (0, x, c, 0, 0))
            whole = lax.dynamic_update_slice(whole, part[1], (0, 1 - x, c, 0, 0))
            return whole.reshape(width, width)

        def owned(part):
            return lax.psum_scatter(part, OWNERS, scatter_dimension=0, tiled=True).astype(F32)

        qkv_weights = [owned(placed_heads(qkv_weight_part[:, i * cols : (i + 1) * cols])) for i in range(3)]
        query_bias_own = owned(placed_heads(bias_part[:cols]))
        value_bias_own = owned(placed_heads(bias_part[2 * cols :]))
        output_weight_own = owned(placed_rows(output_weight_part))
        inner_weight_own = owned(placed_units(inner_weight_part, 1))
        inner_bias_own = owned(placed_units(inner_bias_part, 0))
        outer_weight_own = owned(placed_units(outer_weight_part, 0))
        sums = [owned(token_sums[i]) for i in range(6)]
    else:

        def halved(part, index, axis, name, mask, kind=add_low):
            there = swap(pick(part, 1 - index, axis), name, mask)
            return kind(pick(part, index, axis), there)

        def over_z(part, kind):
            part = part.reshape((2, 2) + part.shape[1:])
            part = halved(part, d % 2, 1, "dp", 1, kind)
            return halved(part, d // 2, 0, "dp", 2, lambda a, b: a.astype(F32) + b.astype(F32))

        def scattered(part):
            half = n_dp // 2
            one, two = part[:half], part[half:]
            one = halved(one, x, 1, "ctx", 2)
            two = halved(two, y, 2, "fsdp", 1)
            one = halved(one, y, 1, "fsdp", 1)
            two = halved(two, x, 1, "ctx", 2)
            return over_z(jnp.concatenate((one, two)), add_low)

        rows = width // (8 * n_dp)
        outer_weight_own = scattered(outer_weight_part.reshape(n_dp, 2, 2, -1, width))
        inner_pieces = inner_weight_part.reshape(n_dp, 2, 2, 2, rows, units // 2)
        inner_pieces = jnp.swapaxes(inner_pieces, 2, 3).reshape(n_dp, 2, 2, 2 * rows, units // 2)
        inner_sum = scattered(inner_pieces).reshape(2, rows, units // 2)
        inner_there = swap(pick(inner_sum, 1 - c, 0), "ctx", 1)
        inner_here = pick(inner_sum, c, 0)
        inner_both = jnp.where(c == 0, jnp.stack((inner_here, inner_there)), jnp.stack((inner_there, inner_here)))
        inner_both = inner_both.reshape(2, rows, 2 * n_dp, block)
        inner_weight_own = jnp.transpose(inner_both, (1, 2, 0, 3)).reshape(rows, units)
        out_pieces = output_weight_part.reshape(2, n_dp, 2, rows, width)
        out_mine, out_there = out_pieces[0], swap(out_pieces[1], "ctx", 2)
        out_sum = halved(add_low(out_mine, out_there), y, 1, "fsdp", 1)
        output_weight_own = over_z(out_sum, add_low)
        qkv_pieces = qkv_weight_part.reshape(n_dp, n_ctx, 2, rows, 3 * cols)
        qkv_sum = over_z(halved(qkv_pieces, y, 2, "fsdp", 1), add_low)
        qkv_sum = lax.all_to_all(qkv_sum, "ctx", 0, 0)
        qkv_sum = qkv_sum.reshape(n_ctx, rows, 3, own_heads, head_size)
        qkv_sum = jnp.transpose(qkv_sum, (2, 1, 3, 0, 4)).reshape(3, rows, width)
        qkv_weights = [qkv_sum[0], qkv_sum[1], qkv_sum[2]]

        def add(a, b):
            return a + b

        pieces = token_sums.reshape(6, n_dp, 2, 2, 2, rows)
        pieces = halved(pieces, c, 3, "ctx", 1, add)
        pieces = jnp.transpose(pieces, (1, 2, 3, 0, 4)).reshape(n_dp, 2, 2, 6 * rows)
        pieces = jnp.concatenate((pieces, inner_bias_part.reshape(n_dp, 2, 2, -1)), -1)
        pieces = halved(pieces, x, 1, "ctx", 2, add)
        query_piece = bias_part[:cols].reshape(n_dp, 2, rows)
        value_piece = bias_part[2 * cols :].reshape(n_dp, 2, rows)
        pieces = jnp.concatenate((pieces, query_piece, value_piece), -1)
        pieces = over_z(halved(pieces, y, 1, "fsdp", 1, add), add)
        sums = [pieces[i * rows : (i + 1) * rows] for i in range(6)]
        spot = 6 * rows + units // (8 * n_dp)
        inner_bias_own = pieces[6 * rows : spot]
        query_bias_own = pieces[spot : spot + rows]
        value_bias_own = pieces[spot + rows : spot + 2 * rows]

    return (
        encoded,
        input_grad,
        qkv_weights[0],
        query_bias_own,
        qkv_weights[1],
        qkv_weights[2],
        value_bias_own,
        output_weight_own,
        sums[5],
        sums[3],
        sums[4],
        inner_weight_own,
        inner_bias_own,
        outer_weight_own,
        sums[2],
        sums[0],
        sums[1],
    )


def solution(mesh):
    tokens = P(("dp", "fsdp"), "ctx", None)
    matrix, vector = P("fsdp", None), P("fsdp")
    own_matrix, own_vector = P(OWNERS, None), P(OWNERS)
    return jax.shard_map(
        shards,
        mesh=mesh,
        in_specs=(
            tokens,
            tokens,
            P(),
            P(),
            matrix,
            vector,
            matrix,
            matrix,
            vector,
            matrix,
            vector,
            vector,
            vector,
            matrix,
            vector,
            matrix,
            vector,
            vector,
            vector,
        ),
        out_specs=(
            tokens,
            tokens,
            own_matrix,
            own_vector,
            own_matrix,
            own_matrix,
            own_vector,
            own_matrix,
            own_vector,
            own_vector,
            own_vector,
            own_matrix,
            own_vector,
            own_matrix,
            own_vector,
            own_vector,
            own_vector,
        ),
        check_vma=False,
    )
```

```python
import functools
import math

import jax
import jax.numpy as jnp
from jax import lax
from jax.experimental import pallas as pl
from jax.experimental.pallas import tpu as pltpu
from jax.sharding import PartitionSpec as P

HEADS = 16
EPS = 1e-12
MASKED = -1e30
F32 = jnp.float32
BF16 = jnp.bfloat16
OWNERS = ("dp", "ctx", "fsdp")


def swap(value, axis, mask):
    pairs = [(source, source ^ mask) for source in range(lax.axis_size(axis))]
    return lax.ppermute(value, axis, pairs)


def pick(array, index, axis):
    return lax.dynamic_index_in_dim(array, index, axis, keepdims=False)


def add_low(left, right):
    return (left.astype(F32) + right.astype(F32)).astype(BF16)


def matmul(left, right):
    return jnp.dot(left, right, preferred_element_type=F32)


def matmul_tn(left, right):
    return lax.dot_general(left, right, (((0,), (0,)), ((), ())), preferred_element_type=F32)


def matmul_nt(left, right):
    return lax.dot_general(left, right, (((1,), (1,)), ((), ())), preferred_element_type=F32)


def col_sum(matrix):
    return jnp.sum(matrix.astype(F32), axis=0)


def norm_rows(summed, scale_vec, shift_vec):
    row_mean = jnp.mean(summed, axis=-1, keepdims=True)
    centered = summed - row_mean
    inverse = lax.rsqrt(jnp.mean(centered * centered, axis=-1, keepdims=True) + EPS)
    normed = centered * inverse
    return (normed * scale_vec + shift_vec, normed, inverse)


def norm_back(upstream, normed, inverse, scale_vec):
    scaled = upstream * scale_vec
    return inverse * (
        scaled
        - jnp.mean(scaled, axis=-1, keepdims=True)
        - normed * jnp.mean(scaled * normed, axis=-1, keepdims=True)
    )


def half_lanes(pair, which):
    lane = lax.broadcasted_iota(jnp.int32, pair.shape, 1)
    keep = lane < 64 if which == 0 else lane >= 64
    return jnp.where(keep, pair, jnp.zeros_like(pair))


def with_flag(pair, flag, which):
    lane = lax.broadcasted_iota(jnp.int32, pair.shape, 1)
    keep = lane < 64 if which == 0 else lane >= 64
    spot = lane == (64 if which == 0 else 0)
    return jnp.where(keep, pair, jnp.where(spot, flag, jnp.zeros_like(pair)))


def attend_kernel(qkv_ref, bias_ref, out_ref, lse_ref):
    width = out_ref.shape[-1]
    rows = out_ref.shape[0] * out_ref.shape[2]
    bias = bias_ref[0]
    lane = lax.broadcasted_iota(jnp.int32, (rows, 128), 1)
    one = jnp.ones((rows, 128), BF16)
    totals = jnp.zeros((rows, 128), F32)
    for pair_index in range(width // 128):
        first = pair_index * 128
        query = qkv_ref[:, 0, :, first : first + 128].reshape(rows, 128)
        key = qkv_ref[:, 0, :, width + first : width + first + 128].reshape(rows, 128)
        value = qkv_ref[:, 0, :, 2 * width + first : 2 * width + first + 128].reshape(rows, 128)
        query = (query.astype(F32) * 0.125).astype(BF16)
        mixed = []
        for which in range(2):
            scores = matmul_nt(with_flag(query, one, which), with_flag(key, bias, which))
            top = jnp.max(scores, axis=-1, keepdims=True)
            weight = jnp.exp(scores - top)
            total = jnp.sum(weight, axis=-1, keepdims=True)
            mixed.append(matmul(weight.astype(BF16), value) * (1.0 / total))
            totals = jnp.where(lane == 2 * pair_index + which, top + jnp.log(total), totals)
        joined = jnp.where(lane < 64, mixed[0], mixed[1]).astype(BF16)
        out_ref[:, 0, :, first : first + 128] = joined.reshape(out_ref.shape[0], out_ref.shape[2], 128)
    lse_ref[0] = jnp.transpose(totals)[:8]


def attend_back_kernel(qkv_ref, bias_ref, lse_ref, grad_ref, out_ref):
    width = grad_ref.shape[-1]
    shape = (grad_ref.shape[0], grad_ref.shape[2], 128)
    rows = shape[0] * shape[1]
    bias = bias_ref[0]
    lane = lax.broadcasted_iota(jnp.int32, (rows, 128), 1)
    one = jnp.ones((rows, 128), BF16)
    for pair_index in range(width // 128):
        first = pair_index * 128
        query = qkv_ref[:, 0, :, first : first + 128].reshape(rows, 128)
        key = qkv_ref[:, 0, :, width + first : width + first + 128].reshape(rows, 128)
        value = qkv_ref[:, 0, :, 2 * width + first : 2 * width + first + 128].reshape(rows, 128)
        grad = grad_ref[:, 0, :, first : first + 128].reshape(rows, 128)
        query = (query.astype(F32) * 0.125).astype(BF16)
        query_parts, key_parts, value_parts = [], [], []
        for which in range(2):
            spot = 2 * pair_index + which
            log_total = lse_ref[0, spot : spot + 1, :]
            scores = matmul_nt(with_flag(key, bias, which), with_flag(query, one, which))
            probs = jnp.exp(scores - log_total)
            probs_grad = matmul_nt(value, half_lanes(grad, which))
            value_parts.append(matmul(probs.astype(BF16), grad))
            row_dot = jnp.sum(probs * probs_grad, axis=0, keepdims=True)
            score_grad = (probs * (probs_grad - row_dot)).astype(BF16)
            key_parts.append(matmul(score_grad, query))
            query_parts.append(matmul_tn(score_grad, key) * 0.125)
        for place, parts in enumerate((query_parts, key_parts, value_parts)):
            joined = jnp.where(lane < 64, parts[0], parts[1]).astype(BF16)
            start = place * width + first
            out_ref[:, 0, :, start : start + 128] = joined.reshape(shape)


def attention_call(kernel, arrays, outs, flops):
    def whole(array):
        shape = array.shape
        if len(shape) == 4:
            return pl.BlockSpec((shape[0], 1) + shape[2:], lambda s: (0, s, 0, 0))
        return pl.BlockSpec((1,) + shape[1:], lambda s: (s, 0, 0))

    return pl.pallas_call(
        kernel,
        grid=(arrays[0].shape[1],),
        in_specs=[whole(array) for array in arrays],
        out_specs=[whole(out) for out in outs],
        out_shape=outs,
        compiler_params=pltpu.CompilerParams(vmem_limit_bytes=40 * 1024 * 1024),
        cost_estimate=pl.CostEstimate(flops=flops, bytes_accessed=8 << 20, transcendentals=0),
    )(*arrays)


MESH = pl.DeviceIdType.MESH


def repeat(count, body):
    def step(index, carry):
        body(index)
        return carry

    lax.fori_loop(0, count, step, 0)


class Slots:
    def __init__(self):
        self.total = 0

    def take(self, count=1):
        first = self.total
        self.total += count
        return first


def layer_kernel(
    lens_ref,
    states,
    wq_own,
    vec_own,
    wo_own,
    wi_own,
    wu_own,
    encoded_out,
    o_states,
    o_wq,
    o_wout,
    o_win,
    o_wou,
    o_vecs,
    o_qkv,
    o_lse,
    o_att,
    o_norm,
    o_inv,
    o_low,
    o_act,
    o_slope,
    o_norm2,
    o_inv2,
    st_all,
    wq_all,
    vec_all,
    w_out,
    w_in,
    w_ou,
    vecs,
    qkv,
    lse,
    att,
    att_far,
    part_far,
    part_in,
    part_far2,
    part_in2,
    first_norm,
    first_inv,
    first_out,
    low2,
    act,
    slope,
    acc,
    second_inv,
    send,
    recv,
    local,
):
    d, me, y = lax.axis_index("dp"), lax.axis_index("ctx"), lax.axis_index("fsdp")
    x, c = me // 2, me % 2
    to_core = {"ctx": me + 1 - 2 * c}
    to_x = {"ctx": (me + 2) % 4}
    to_y = {"fsdp": 1 - y}
    to_z = {"dp": d + 1 - 2 * (d % 2)}
    to_zz = {"dp": (d + 2) % 4}
    to_far = {"ctx": 3 - me}
    slots = Slots()
    pending = []

    def remote(src, dst, slot, device):
        return pltpu.make_async_remote_copy(
            src_ref=src,
            dst_ref=dst,
            send_sem=send.at[slot],
            recv_sem=recv.at[slot],
            device_id=device,
            device_id_type=MESH,
        )

    def at_end(count, make):
        pending.append((count, make))

    local_slots = Slots()

    def fetch(src, dst):
        copy = pltpu.make_async_copy(src, dst, local.at[local_slots.take()])
        copy.start()
        return copy

    kept = []

    def keep(src, dst):
        kept.append(fetch(src, dst))

    barrier = pltpu.get_barrier_semaphore()
    for device in (to_core, to_x, to_y, to_z, to_zz, to_far):
        pl.semaphore_signal(barrier, inc=1, device_id=device, device_id_type=MESH)
    pl.semaphore_wait(barrier, 6)

    first = slots.take(4)
    state_x = lambda s: remote(states.at[s], st_all.at[2, s], first + s, to_x)
    second = slots.take(4)
    state_core = lambda s: remote(states.at[s], st_all.at[1, s], second + s, to_core)
    third = slots.take(4)
    state_far = lambda s: remote(st_all.at[2, s], st_all.at[3, s], third + s, to_core)
    wq_slot = slots.take()
    wq_copy = remote(wq_own, wq_all.at[pl.ds(pl.multiple_of(y * 512, 512), 512)], wq_slot, to_y)
    vec_slot = slots.take()
    vec_copy = remote(vec_own, vec_all.at[y], vec_slot, to_y)
    for s in range(4):
        state_x(s).start()
    wq_copy.start()
    vec_copy.start()
    for s in range(4):
        state_core(s).start()
    at_end(4, state_x)
    at_end(4, state_core)
    at_end(4, state_far)
    at_end(1, lambda _: wq_copy)
    at_end(1, lambda _: vec_copy)

    p = d % 2
    wo_slot = slots.take(2)

    def wo_copy(side):
        src = wo_own.at[pl.ds(pl.multiple_of(p * 256 + side * 128 + c * 64, 64), 64)]
        return remote(src, w_out.at[x if side == 0 else 1 - x, 2 * y + p], wo_slot + side, to_y)

    wo_pass_slot = slots.take(2)

    def wo_pass(side):
        here = w_out.at[x if side == 0 else 1 - x, 2 * (1 - y) + p]
        return remote(here, here, wo_pass_slot + side, to_z)

    wi_slot = slots.take(8)

    def wi_copy(b):
        src = wi_own.at[
            pl.ds(pl.multiple_of(x * 256, 256), 256), pl.ds(pl.multiple_of((2 * b + c) * 256, 256), 256)
        ]
        dst = w_in.at[
            pl.ds(pl.multiple_of(y * 512 + x * 256, 256), 256), pl.ds(pl.multiple_of(b * 256, 256), 256)
        ]
        return remote(src, dst, wi_slot + b, to_y)

    wi_pass_slot = slots.take(8)

    def wi_pass(b):
        here = w_in.at[
            pl.ds(pl.multiple_of((1 - y) * 512 + x * 256, 256), 256),
            pl.ds(pl.multiple_of(b * 256, 256), 256),
        ]
        return remote(here, here, wi_pass_slot + b, to_x)

    wu_slot = slots.take(4)

    def wu_copy(k):
        side, half = k // 2, k % 2
        src = wu_own.at[pl.ds(pl.multiple_of((p * 4 + side * 2 + c) * 256 + half * 128, 128), 128)]
        dst = w_ou.at[pl.ds(pl.multiple_of((4 * y + 2 * p + side) * 256 + half * 128, 128), 128)]
        return remote(src, dst, wu_slot + k, to_y)

    wu_pass_slot = slots.take(4)

    def wu_pass(k):
        side, half = k // 2, k % 2
        here = w_ou.at[
            pl.ds(pl.multiple_of((4 * (1 - y) + 2 * p + side) * 256 + half * 128, 128), 128)
        ]
        return remote(here, here, wu_pass_slot + k, to_z)

    for side in range(2):
        wo_copy(side).start()
    for b in range(8):
        wi_copy(b).start()
    for k in range(4):
        wu_copy(k).start()
    for count, make in ((2, wo_copy), (2, wo_pass), (8, wi_copy), (8, wi_pass), (4, wu_copy), (4, wu_pass)):
        at_end(count, make)

    own_early = [
        fetch(states, st_all.at[0]),
        fetch(wq_own, wq_all.at[pl.ds(pl.multiple_of(y * 512, 512), 512)]),
        fetch(vec_own, vec_all.at[y]),
    ]
    own_out = []
    for half in range(2):
        for side in range(2):
            src = wo_own.at[pl.ds(pl.multiple_of(half * 256 + side * 128 + c * 64, 64), 64)]
            own_out.append(fetch(src, w_out.at[x if side == 0 else 1 - x, 2 * y + half]))
    own_late = []
    for b in range(8):
        src = wi_own.at[:, pl.ds(pl.multiple_of((2 * b + c) * 256, 256), 256)]
        dst = w_in.at[pl.ds(pl.multiple_of(y * 512, 512), 512), pl.ds(b * 256, 256)]
        own_late.append(fetch(src, dst))
    for half in range(2):
        for side in range(2):
            src = wu_own.at[pl.ds(pl.multiple_of((half * 4 + side * 2 + c) * 256, 256), 256)]
            dst = w_ou.at[pl.ds(pl.multiple_of((4 * y + 2 * half + side) * 256, 256), 256)]
            own_late.append(fetch(src, dst))

    for s in range(2):
        state_x(s).wait_recv()
        state_far(s).start()
    for copy in own_early:
        copy.wait()
    vec_copy.wait_recv()
    vecs[:, :512] = vec_all[0].astype(F32)
    vecs[:, 512:] = vec_all[1].astype(F32)
    wq_copy.wait_recv()

    att_slot = slots.take(8)

    def att_copy(s, j):
        rows = pl.ds(pl.multiple_of(j * 512 + s * 128, 128), 128)
        return remote(att_far.at[j, s], att.at[rows, 256:512], att_slot + 2 * s + j, to_x)

    at_end(8, lambda k: att_copy(k // 2, k % 2))
    q_bias = jnp.concatenate((vecs[0:1, 0:128], vecs[0:1, 512:640]), 1)
    v_bias = jnp.concatenate((vecs[0:1, 128:256], vecs[0:1, 640:768]), 1)

    def key_flags(s):
        pieces = []
        for j in range(4):
            position = lax.broadcasted_iota(jnp.int32, (128, 128), 0)
            place = me + 1 - 2 * c if j == 1 else me
            place = (place + 2) % 4 if j == 2 else place
            place = 3 - me if j == 3 else place
            pieces.append(jnp.where(position + place * 128 < lens_ref[s], 0.0, MASKED))
        return jnp.concatenate(pieces, 0).astype(BF16)

    def attention(s):
        @pl.when(s < 2)
        def _():
            state_x(s + 2).wait_recv()
            state_far(s + 2).start()

        @pl.when(s == 3)
        def _():
            for side in range(2):
                wo_copy(side).wait_recv()
                wo_pass(side).start()

        state_core(s).wait_recv()
        state_far(s).wait_recv()
        rows = st_all[:, s].reshape(512, 1024)
        for place in range(3):
            made = matmul(rows, wq_all[:, place * 256 : place * 256 + 256])
            made = made + q_bias if place == 0 else made
            made = made + v_bias if place == 2 else made
            qkv[:, s, :, place * 256 : place * 256 + 256] = made.astype(BF16).reshape(4, 128, 256)
        bias = key_flags(s)
        lane = lax.broadcasted_iota(jnp.int32, (512, 128), 1)
        one = jnp.ones((512, 128), BF16)
        totals = jnp.zeros((512, 128), F32)
        for pair in range(2):
            base = pair * 128
            query = qkv[:, s, :, base : base + 128].reshape(512, 128)
            key = qkv[:, s, :, 256 + base : 384 + base].reshape(512, 128)
            value = qkv[:, s, :, 512 + base : 640 + base].reshape(512, 128)
            query = (query.astype(F32) * 0.125).astype(BF16)
            mixed = []
            for which in range(2):
                scores = matmul_nt(with_flag(query, one, which), with_flag(key, bias, which))
                top = jnp.max(scores, axis=-1, keepdims=True)
                weight = jnp.exp(scores - top)
                total = jnp.sum(weight, axis=-1, keepdims=True)
                mixed.append(matmul(weight.astype(BF16), value) * (1.0 / total))
                totals = jnp.where(lane == 2 * pair + which, top + jnp.log(total), totals)
            joined = jnp.where(lane < 64, mixed[0], mixed[1]).astype(BF16)
            for j in range(2):
                rows_j = pl.ds(pl.multiple_of(j * 512 + s * 128, 128), 128)
                att[rows_j, base : base + 128] = joined[j * 128 : j * 128 + 128]
                att_far[j, s, :, base : base + 128] = joined[256 + j * 128 : 384 + j * 128]
        for j in range(2):
            att_copy(s, j).start()
        lse[s] = jnp.transpose(totals)[:8]

    repeat(4, attention)
    for src, dst in ((st_all, o_states), (wq_all, o_wq), (vecs, o_vecs), (qkv, o_qkv), (lse, o_lse)):
        keep(src, dst)

    def pass_inner(b):
        wi_copy(b).wait_recv()
        wi_pass(b).start()

    for b in range(4):
        pass_inner(b)
    for copy in own_out:
        copy.wait()
    for side in range(2):
        wo_pass(side).wait_recv()
    for s in range(4):
        for j in range(2):
            att_copy(s, j).wait_recv()
    keep(att, o_att)
    keep(w_out, o_wout)
    out_slot = slots.take(4)

    def out_copy(n):
        return remote(part_far.at[n], part_in.at[n], out_slot + n, to_core)

    at_end(4, out_copy)
    for n in range(4):
        right = w_out[:, :, :, n * 256 : n * 256 + 256].reshape(512, 256)
        part_far[n] = matmul(att[512:], right).astype(BF16)
        out_copy(n).start()
    for b in range(4, 6):
        pass_inner(b)
    for n in range(4):
        right = w_out[:, :, :, n * 256 : n * 256 + 256].reshape(512, 256)
        made = matmul(att[:512], right) + vecs[1:2, n * 256 : n * 256 + 256]
        made = made + st_all[0, :, :, n * 256 : n * 256 + 256].astype(F32).reshape(512, 256)
        out_copy(n).wait_recv()
        first_norm[:, n * 256 : n * 256 + 256] = made + part_in[n].astype(F32)

    low_slot = slots.take(4)

    def low_copy(k):
        src = low2.at[pl.ds(pl.multiple_of(k * 128, 128), 128)]
        dst = low2.at[pl.ds(pl.multiple_of(512 + k * 128, 128), 128)]
        return remote(src, dst, low_slot + k, to_core)

    at_end(4, low_copy)

    def norm_first(k):
        for half in range(2):
            rows = pl.ds(pl.multiple_of(k * 128 + half * 64, 64), 64)
            made, normed, inverse = norm_rows(first_norm[rows, :], vecs[2:3, :], vecs[3:4, :])
            first_norm[rows, :] = normed
            first_inv[rows, :] = jnp.broadcast_to(inverse, (64, 128))
            first_out[rows, :] = made
            low2[rows, :] = made.astype(BF16)
        low_copy(k).start()

    repeat(4, norm_first)
    for b in range(6, 8):
        pass_inner(b)
    for k in range(4):
        low_copy(k).wait_recv()
    for copy in own_late:
        copy.wait()
    for src, dst in ((first_norm, o_norm), (first_inv, o_inv), (low2, o_low)):
        keep(src, dst)

    def unit_block(b):
        wi_pass(b).wait_recv()
        here = pl.ds(pl.multiple_of(b * 256, 256), 256)
        spot = pl.ds(pl.multiple_of((b // 4) * 512 + c * 256, 256), 256)
        row = vecs[pl.ds(8 + b % 4, 1), spot]
        for m in range(2):
            hidden = matmul(low2[m * 512 : m * 512 + 512, :], w_in[:, here]) + row
            below = 0.5 * (1.0 + lax.erf(hidden * math.sqrt(0.5)))
            bell = jnp.exp(-0.5 * hidden * hidden) * (1.0 / math.sqrt(2 * math.pi))
            act[m * 512 : m * 512 + 512, here] = (hidden * below).astype(BF16)
            slope[m * 512 : m * 512 + 512, here] = (below + hidden * bell).astype(BF16)

    repeat(8, unit_block)
    for src, dst in ((act, o_act), (slope, o_slope), (w_in, o_win)):
        keep(src, dst)
    mine = pl.ds(pl.multiple_of(y * 1024, 1024), 1024)
    theirs = pl.ds(pl.multiple_of((1 - y) * 1024, 1024), 1024)
    for k in range(2):
        wu_copy(k).wait_recv()
        wu_pass(k).start()

    def outer_own(n):
        here = pl.ds(pl.multiple_of(n * 256, 256), 256)
        for m in range(2):
            acc[m * 512 : m * 512 + 512, here] = matmul(
                act[m * 512 : m * 512 + 512, mine], w_ou[mine, here]
            )

    repeat(4, outer_own)
    for k in range(2, 4):
        wu_copy(k).wait_recv()
        wu_pass(k).start()
    for k in range(4):
        wu_pass(k).wait_recv()
    keep(w_ou, o_wou)
    sum_slot = slots.take(4)

    def sum_copy(n):
        return remote(part_far2.at[n], part_in2.at[n], sum_slot + n, to_core)

    at_end(4, sum_copy)

    def outer_far(n):
        here = pl.ds(pl.multiple_of(n * 256, 256), 256)
        made = acc[512:, here] + matmul(act[512:, theirs], w_ou[theirs, here])
        part_far2[n] = made.astype(BF16)
        sum_copy(n).start()

    repeat(4, outer_far)

    def outer_near(n):
        here = pl.ds(pl.multiple_of(n * 256, 256), 256)
        made = acc[:512, here] + matmul(act[:512, theirs], w_ou[theirs, here])
        made = made + first_out[:, here] + vecs[4:5, here]
        sum_copy(n).wait_recv()
        acc[:512, here] = made + part_in2[n].astype(F32)

    repeat(4, outer_near)

    def norm_second(k):
        valid_place = lax.broadcasted_iota(jnp.int32, (128, 1), 0) + me * 128
        valid = jnp.where(valid_place < lens_ref[k], 1.0, 0.0)
        for half in range(2):
            rows = pl.ds(pl.multiple_of(k * 128 + half * 64, 64), 64)
            made, normed, inverse = norm_rows(acc[rows, :], vecs[5:6, :], vecs[6:7, :])
            encoded_out[rows, :] = (made * valid[half * 64 : half * 64 + 64]).astype(BF16)
            acc[rows, :] = normed
            second_inv[rows, :] = jnp.broadcast_to(inverse, (64, 128))

    repeat(4, norm_second)
    keep(acc.at[:512], o_norm2)
    keep(second_inv, o_inv2)
    for copy in kept:
        copy.wait()
    for count, make in pending:
        for k in range(count):
            make(k).wait_send()


def layer_call(arrays):
    any_space = pl.BlockSpec(memory_space=pl.ANY)
    v = pltpu.VMEM
    return pl.pallas_call(
        layer_kernel,
        in_specs=[pl.BlockSpec(memory_space=pltpu.SMEM)] + [any_space] * 6,
        out_specs=[pl.BlockSpec(memory_space=pltpu.VMEM)] + [any_space] * 16,
        out_shape=[
            jax.ShapeDtypeStruct(shape, kind)
            for shape, kind in (
                ((512, 1024), BF16),
                ((4, 4, 128, 1024), BF16),
                ((1024, 768), BF16),
                ((2, 4, 64, 1024), BF16),
                ((1024, 2048), BF16),
                ((2048, 1024), BF16),
                ((16, 1024), F32),
                ((4, 4, 128, 768), BF16),
                ((4, 8, 512), F32),
                ((1024, 512), BF16),
                ((512, 1024), F32),
                ((512, 128), F32),
                ((1024, 1024), BF16),
                ((1024, 2048), BF16),
                ((1024, 2048), BF16),
                ((512, 1024), F32),
                ((512, 128), F32),
            )
        ],
        scratch_shapes=[
            v((4, 4, 128, 1024), BF16),
            v((1024, 768), BF16),
            v((2, 16, 512), BF16),
            v((2, 4, 64, 1024), BF16),
            v((1024, 2048), BF16),
            v((2048, 1024), BF16),
            v((16, 1024), F32),
            v((4, 4, 128, 768), BF16),
            v((4, 8, 512), F32),
            v((1024, 512), BF16),
            v((2, 4, 128, 256), BF16),
            v((4, 512, 256), BF16),
            v((4, 512, 256), BF16),
            v((4, 512, 256), BF16),
            v((4, 512, 256), BF16),
            v((512, 1024), F32),
            v((512, 128), F32),
            v((512, 1024), F32),
            v((1024, 1024), BF16),
            v((1024, 2048), BF16),
            v((1024, 2048), BF16),
            v((1024, 1024), F32),
            v((512, 128), F32),
            pltpu.SemaphoreType.DMA((80,)),
            pltpu.SemaphoreType.DMA((80,)),
            pltpu.SemaphoreType.DMA((64,)),
        ],
        compiler_params=pltpu.CompilerParams(
            collective_id=0, has_side_effects=True, vmem_limit_bytes=64 * 1024 * 1024 - 65536
        ),
    )(*arrays)


def shards(
    states,
    cotangent,
    lengths,
    slot_source,
    query_weight,
    query_bias,
    key_weight,
    value_weight,
    value_bias,
    output_weight,
    output_bias,
    first_gain,
    first_shift,
    inner_weight,
    inner_bias,
    outer_weight,
    outer_bias,
    final_gain,
    final_shift,
):
    seq_dev, block_len, width = states.shape
    n_dp, n_ctx, n_fsdp = (lax.axis_size(name) for name in OWNERS)
    assert (n_ctx, n_fsdp) == (4, 2)
    head_size = width // HEADS
    units = inner_weight.shape[1]
    tokens = seq_dev * block_len
    d, me, y = (lax.axis_index(name) for name in OWNERS)
    x, c = me // 2, me % 2
    own_heads = HEADS // n_ctx
    cols = own_heads * head_size
    aligned = n_dp == own_heads

    def other_half(local):
        return swap(local, "fsdp", 1)

    def ordered(own, other, axis=0):
        return jnp.where(
            y == 0, jnp.concatenate((own, other), axis), jnp.concatenate((other, own), axis)
        )

    def gathered(local, axis=0):
        return ordered(local, other_half(local), axis)

    def head_cols(matrix):
        parts = matrix.reshape(matrix.shape[:-1] + (own_heads, n_ctx, head_size))
        return pick(parts, me, parts.ndim - 2).reshape(matrix.shape[:-1] + (cols,))

    my_seqs = (d * n_fsdp + y) * seq_dev + jnp.arange(seq_dev, dtype=jnp.int32)
    seq_len = jnp.sum(jnp.where(slot_source[None, :] == my_seqs[:, None], lengths[None, :], 0), axis=1)
    places = (me ^ jnp.arange(n_ctx, dtype=jnp.int32))[:, None] * block_len + jnp.arange(
        block_len, dtype=jnp.int32
    )
    key_ok = places.reshape(1, -1) < seq_len[:, None]
    key_bias = jnp.where(key_ok, 0.0, MASKED).astype(BF16)
    key_bias = jnp.broadcast_to(key_bias[:, :, None], key_bias.shape + (128,))
    valid_rows = (places[0][None, :] < seq_len[:, None]).astype(F32).reshape(-1, 1)
    full_len = n_ctx * block_len
    score_flops = 2 * seq_dev * own_heads * full_len * full_len * 128
    block = units // (4 * n_dp)
    wq_own = jnp.concatenate((head_cols(query_weight), head_cols(key_weight), head_cols(value_weight)), 1)

    def share(own):
        return jnp.concatenate((own, swap(own, "ctx", 1)), axis=0)

    def collect(both_rows):
        return both_rows[:tokens] + swap(both_rows[tokens:].astype(BF16), "ctx", 1).astype(F32)

    if aligned:
        half_bias = lambda v: pick(v.reshape(2, n_ctx, head_size), me, 1).reshape(1, -1)
        top = jnp.concatenate((half_bias(query_bias), half_bias(value_bias), jnp.zeros((1, 256), BF16)), 1)
        rows16 = [top] + [
            v.reshape(1, -1)
            for v in (output_bias, first_gain, first_shift, outer_bias, final_gain, final_shift)
        ]
        rows16 += [jnp.zeros((1, 512), BF16), inner_bias.reshape(4, 512), jnp.zeros((4, 512), BF16)]
        vec_own = jnp.concatenate(rows16, 0)
        (
            encoded,
            flat_all,
            w_qkv,
            w_out,
            w_inner,
            w_outer,
            vecs,
            qkv,
            log_total,
            attended,
            first_norm,
            first_inverse,
            first_low,
            activated,
            slope,
            second_norm,
            second_inverse,
        ) = layer_call((seq_len, states, wq_own, vec_own, output_weight, inner_weight, outer_weight))
        encoded = encoded.reshape(states.shape)
        flat_all = flat_all.reshape(-1, width)
        w_out = w_out.reshape(-1, width)
        g_first, g_final = vecs[2], vecs[5]
        first_inverse, second_inverse = first_inverse[:, :1], second_inverse[:, :1]
    else:

        def other_half(local):
            return swap(local, "fsdp", 1)

        def ordered(own, other, axis=0):
            return jnp.where(
                y == 0, jnp.concatenate((own, other), axis), jnp.concatenate((other, own), axis)
            )

        def gathered(local, axis=0):
            return ordered(local, other_half(local), axis)

        wide = (query_bias, value_bias, output_bias, first_gain, first_shift, outer_bias, final_gain, final_shift)
        packed = jnp.concatenate([v.reshape(1, -1) for v in wide] + [inner_bias.reshape(-1, width // 2)])
        other_packed = other_half(packed)
        both = jnp.where(y == 0, jnp.stack((packed, other_packed)), jnp.stack((other_packed, packed)))
        b_query, b_value, b_out, g_first, s_first, b_outer, g_final, s_final = (
            both[:, i].reshape(width).astype(F32) for i in range(8)
        )
        b_inner = both[:, 8:].reshape(2 * n_dp, 2, -1)
        b_inner = pick(b_inner, c, 1).reshape(-1).astype(F32)
        w_qkv = gathered(wq_own)
        b_qkv = jnp.concatenate((head_cols(b_query), jnp.zeros((cols,), F32), head_cols(b_value)))

        from_x = swap(states, "ctx", 2)
        from_core = swap(states, "ctx", 1)
        from_far = swap(from_x, "ctx", 1)
        flat_all = jnp.stack((states, from_core, from_x, from_far)).reshape(-1, width)

        w_out = gathered(pick(output_weight.reshape(-1, 2, 2, head_size, width), c, 2))
        w_out = jnp.concatenate((pick(w_out, x, 1), pick(w_out, 1 - x, 1)), 0).reshape(-1, width)
        w_inner = gathered(
            pick(inner_weight.reshape(width // 2, 2 * n_dp, 2, block), c, 2).reshape(width // 2, -1)
        )
        w_outer = gathered(pick(outer_weight.reshape(n_dp, 2, block, width), c, 1).reshape(-1, width))

        qkv = (matmul(flat_all, w_qkv) + b_qkv).astype(BF16)
        qkv = qkv.reshape(n_ctx, seq_dev, block_len, 3 * cols)
        attended_all, log_total = attention_call(
            attend_kernel,
            (qkv, key_bias),
            (
                jax.ShapeDtypeStruct((n_ctx, seq_dev, block_len, cols), BF16),
                jax.ShapeDtypeStruct((seq_dev, 8, full_len), F32),
            ),
            2 * score_flops,
        )
        near = attended_all[:2].reshape(-1, cols)
        far = swap(attended_all[2:], "ctx", 2).reshape(-1, cols)
        attended = jnp.concatenate((near, far), axis=1)
        first_sum = states.reshape(-1, width).astype(F32) + collect(matmul(attended, w_out)) + b_out
        first_out, first_norm, first_inverse = norm_rows(first_sum, g_first, s_first)
        first_low = share(first_out.astype(BF16))
        hidden = matmul(first_low, w_inner) + b_inner
        below = 0.5 * (1.0 + lax.erf(hidden * math.sqrt(0.5)))
        bell = jnp.exp(-0.5 * hidden * hidden) * (1.0 / math.sqrt(2 * math.pi))
        slope = (below + hidden * bell).astype(BF16)
        activated = (hidden * below).astype(BF16)
        second_sum = first_out + collect(matmul(activated, w_outer)) + b_outer
        second_out, second_norm, second_inverse = norm_rows(second_sum, g_final, s_final)
        encoded = (second_out * valid_rows).astype(BF16).reshape(states.shape)

    out_grad = cotangent.reshape(-1, width).astype(F32) * valid_rows
    final_gain_part = jnp.sum(out_grad * second_norm, axis=0)
    final_shift_part = jnp.sum(out_grad, axis=0)
    second_grad = norm_back(out_grad, second_norm, second_inverse, g_final)
    outer_round_own = second_grad.astype(BF16)
    outer_bias_part = col_sum(outer_round_own)
    outer_round = share(outer_round_own)
    outer_weight_part = matmul_tn(activated, outer_round).astype(BF16)
    hidden_grad = (matmul_nt(outer_round, w_outer) * slope.astype(F32)).astype(BF16)
    inner_bias_part = col_sum(hidden_grad)
    inner_weight_part = matmul_tn(first_low, hidden_grad).astype(BF16)
    first_grad = second_grad + collect(matmul_nt(hidden_grad, w_inner))
    first_gain_part = jnp.sum(first_grad * first_norm, axis=0)
    first_shift_part = jnp.sum(first_grad, axis=0)
    sum_grad = norm_back(first_grad, first_norm, first_inverse, g_first)
    branch_own = sum_grad.astype(BF16)
    output_bias_part = col_sum(branch_own)
    branch_grad = share(branch_own)
    output_weight_part = matmul_tn(attended, branch_grad).astype(BF16)
    attended_grad = matmul_nt(branch_grad, w_out).astype(BF16)
    near_grad = attended_grad[:, :cols]
    far_grad = swap(attended_grad[:, cols:], "ctx", 2)
    attended_grad_all = jnp.concatenate((near_grad, far_grad), 0).reshape(n_ctx, seq_dev, block_len, cols)
    (qkv_grad,) = attention_call(
        attend_back_kernel,
        (qkv, key_bias, log_total, attended_grad_all),
        (jax.ShapeDtypeStruct(qkv.shape, BF16),),
        5 * score_flops,
    )
    flat_grad = qkv_grad.reshape(-1, 3 * cols)
    bias_part = col_sum(flat_grad)
    qkv_weight_part = matmul_tn(flat_all, flat_grad).astype(BF16)
    input_part = matmul_nt(flat_grad, w_qkv).reshape(n_ctx, tokens, width)
    to_core = swap(jnp.stack((input_part[1], input_part[3])).astype(BF16), "ctx", 1)
    to_x = swap((input_part[2] + to_core[1].astype(F32)).astype(BF16), "ctx", 2)
    input_grad = sum_grad + input_part[0] + to_core[0].astype(F32) + to_x.astype(F32)
    input_grad = input_grad.astype(BF16).reshape(states.shape)

    token_sums = jnp.stack(
        (final_gain_part, final_shift_part, outer_bias_part, first_gain_part, first_shift_part, output_bias_part)
    )
    if not aligned:
        def placed_heads(part):
            whole = jnp.zeros(part.shape[:-1] + (own_heads, n_ctx, head_size), part.dtype)
            part = part.reshape(part.shape[:-1] + (own_heads, 1, head_size))
            return lax.dynamic_update_slice_in_dim(whole, part, me, part.ndim - 2).reshape(
                part.shape[:-3] + (width,)
            )

        def placed_units(part, axis):
            split = part.shape[:axis] + (2 * n_dp, 1, block) + part.shape[axis + 1 :]
            whole = jnp.zeros(split[: axis + 1] + (2,) + split[axis + 2 :], part.dtype)
            whole = lax.dynamic_update_slice_in_dim(whole, part.reshape(split), c, axis + 1)
            return whole.reshape(part.shape[:axis] + (units,) + part.shape[axis + 1 :])

        def placed_rows(part):
            part = part.reshape(2, own_heads, 1, 1, head_size, width)
            whole = jnp.zeros((own_heads, 2, 2, head_size, width), part.dtype)
            whole = lax.dynamic_update_slice(whole, part[0], (0, x, c, 0, 0))
            whole = lax.dynamic_update_slice(whole, part[1], (0, 1 - x, c, 0, 0))
            return whole.reshape(width, width)

        def owned(part):
            return lax.psum_scatter(part, OWNERS, scatter_dimension=0, tiled=True).astype(F32)

        qkv_weights = [owned(placed_heads(qkv_weight_part[:, i * cols : (i + 1) * cols])) for i in range(3)]
        query_bias_own = owned(placed_heads(bias_part[:cols]))
        value_bias_own = owned(placed_heads(bias_part[2 * cols :]))
        output_weight_own = owned(placed_rows(output_weight_part))
        inner_weight_own = owned(placed_units(inner_weight_part, 1))
        inner_bias_own = owned(placed_units(inner_bias_part, 0))
        outer_weight_own = owned(placed_units(outer_weight_part, 0))
        sums = [owned(token_sums[i]) for i in range(6)]
    else:

        def halved(part, index, axis, name, mask, kind=add_low):
            there = swap(pick(part, 1 - index, axis), name, mask)
            return kind(pick(part, index, axis), there)

        def over_z(part, kind):
            part = part.reshape((2, 2) + part.shape[1:])
            part = halved(part, d % 2, 1, "dp", 1, kind)
            return halved(part, d // 2, 0, "dp", 2, lambda a, b: a.astype(F32) + b.astype(F32))

        def scattered(part):
            half = n_dp // 2
            one, two = part[:half], part[half:]
            one = halved(one, x, 1, "ctx", 2)
            two = halved(two, y, 2, "fsdp", 1)
            one = halved(one, y, 1, "fsdp", 1)
            two = halved(two, x, 1, "ctx", 2)
            return over_z(jnp.concatenate((one, two)), add_low)

        rows = width // (8 * n_dp)
        outer_weight_own = scattered(outer_weight_part.reshape(n_dp, 2, 2, -1, width))
        inner_pieces = inner_weight_part.reshape(n_dp, 2, 2, 2, rows, units // 2)
        inner_pieces = jnp.swapaxes(inner_pieces, 2, 3).reshape(n_dp, 2, 2, 2 * rows, units // 2)
        inner_sum = scattered(inner_pieces).reshape(2, rows, units // 2)
        inner_there = swap(pick(inner_sum, 1 - c, 0), "ctx", 1)
        inner_here = pick(inner_sum, c, 0)
        inner_both = jnp.where(c == 0, jnp.stack((inner_here, inner_there)), jnp.stack((inner_there, inner_here)))
        inner_both = inner_both.reshape(2, rows, 2 * n_dp, block)
        inner_weight_own = jnp.transpose(inner_both, (1, 2, 0, 3)).reshape(rows, units)
        out_pieces = output_weight_part.reshape(2, n_dp, 2, rows, width)
        out_mine, out_there = out_pieces[0], swap(out_pieces[1], "ctx", 2)
        out_sum = halved(add_low(out_mine, out_there), y, 1, "fsdp", 1)
        output_weight_own = over_z(out_sum, add_low)
        qkv_pieces = qkv_weight_part.reshape(n_dp, n_ctx, 2, rows, 3 * cols)
        qkv_sum = over_z(halved(qkv_pieces, y, 2, "fsdp", 1), add_low)
        qkv_sum = lax.all_to_all(qkv_sum, "ctx", 0, 0)
        qkv_sum = qkv_sum.reshape(n_ctx, rows, 3, own_heads, head_size)
        qkv_sum = jnp.transpose(qkv_sum, (2, 1, 3, 0, 4)).reshape(3, rows, width)
        qkv_weights = [qkv_sum[0], qkv_sum[1], qkv_sum[2]]

        def add(a, b):
            return a + b

        pieces = token_sums.reshape(6, n_dp, 2, 2, 2, rows)
        pieces = halved(pieces, c, 3, "ctx", 1, add)
        pieces = jnp.transpose(pieces, (1, 2, 3, 0, 4)).reshape(n_dp, 2, 2, 6 * rows)
        pieces = jnp.concatenate((pieces, inner_bias_part.reshape(n_dp, 2, 2, -1)), -1)
        pieces = halved(pieces, x, 1, "ctx", 2, add)
        query_piece = bias_part[:cols].reshape(n_dp, 2, rows)
        value_piece = bias_part[2 * cols :].reshape(n_dp, 2, rows)
        pieces = jnp.concatenate((pieces, query_piece, value_piece), -1)
        pieces = over_z(halved(pieces, y, 1, "fsdp", 1, add), add)
        sums = [pieces[i * rows : (i + 1) * rows] for i in range(6)]
        spot = 6 * rows + units // (8 * n_dp)
        inner_bias_own = pieces[6 * rows : spot]
        query_bias_own = pieces[spot : spot + rows]
        value_bias_own = pieces[spot + rows : spot + 2 * rows]

    return (
        encoded,
        input_grad,
        qkv_weights[0],
        query_bias_own,
        qkv_weights[1],
        qkv_weights[2],
        value_bias_own,
        output_weight_own,
        sums[5],
        sums[3],
        sums[4],
        inner_weight_own,
        inner_bias_own,
        outer_weight_own,
        sums[2],
        sums[0],
        sums[1],
    )


def solution(mesh):
    tokens = P(("dp", "fsdp"), "ctx", None)
    matrix, vector = P("fsdp", None), P("fsdp")
    own_matrix, own_vector = P(OWNERS, None), P(OWNERS)
    return jax.shard_map(
        shards,
        mesh=mesh,
        in_specs=(
            tokens,
            tokens,
            P(),
            P(),
            matrix,
            vector,
            matrix,
            matrix,
            vector,
            matrix,
            vector,
            vector,
            vector,
            matrix,
            vector,
            matrix,
            vector,
            vector,
            vector,
        ),
        out_specs=(
            tokens,
            tokens,
            own_matrix,
            own_vector,
            own_matrix,
            own_matrix,
            own_vector,
            own_matrix,
            own_vector,
            own_vector,
            own_vector,
            own_matrix,
            own_vector,
            own_matrix,
            own_vector,
            own_vector,
            own_vector,
        ),
        check_vma=False,
    )
```

```python
import functools
import math

import jax
import jax.numpy as jnp
from jax import lax
from jax.experimental import pallas as pl
from jax.experimental.pallas import tpu as pltpu
from jax.sharding import PartitionSpec as P

HEADS = 16
EPS = 1e-12
MASKED = -1e30
F32 = jnp.float32
BF16 = jnp.bfloat16
OWNERS = ("dp", "ctx", "fsdp")


def swap(value, axis, mask):
    pairs = [(source, source ^ mask) for source in range(lax.axis_size(axis))]
    return lax.ppermute(value, axis, pairs)


def pick(array, index, axis):
    return lax.dynamic_index_in_dim(array, index, axis, keepdims=False)


def add_low(left, right):
    return (left.astype(F32) + right.astype(F32)).astype(BF16)


def matmul(left, right):
    return jnp.dot(left, right, preferred_element_type=F32)


def matmul_tn(left, right):
    return lax.dot_general(left, right, (((0,), (0,)), ((), ())), preferred_element_type=F32)


def matmul_nt(left, right):
    return lax.dot_general(left, right, (((1,), (1,)), ((), ())), preferred_element_type=F32)


def col_sum(matrix):
    return jnp.sum(matrix.astype(F32), axis=0)


def norm_rows(summed, scale_vec, shift_vec):
    row_mean = jnp.mean(summed, axis=-1, keepdims=True)
    centered = summed - row_mean
    inverse = lax.rsqrt(jnp.mean(centered * centered, axis=-1, keepdims=True) + EPS)
    normed = centered * inverse
    return (normed * scale_vec + shift_vec, normed, inverse)


def norm_back(upstream, normed, inverse, scale_vec):
    scaled = upstream * scale_vec
    return inverse * (
        scaled
        - jnp.mean(scaled, axis=-1, keepdims=True)
        - normed * jnp.mean(scaled * normed, axis=-1, keepdims=True)
    )


def half_lanes(pair, which):
    lane = lax.broadcasted_iota(jnp.int32, pair.shape, 1)
    keep = lane < 64 if which == 0 else lane >= 64
    return jnp.where(keep, pair, jnp.zeros_like(pair))


def with_flag(pair, flag, which):
    lane = lax.broadcasted_iota(jnp.int32, pair.shape, 1)
    keep = lane < 64 if which == 0 else lane >= 64
    spot = lane == (64 if which == 0 else 0)
    return jnp.where(keep, pair, jnp.where(spot, flag, jnp.zeros_like(pair)))


def attend_kernel(qkv_ref, bias_ref, out_ref, lse_ref):
    width = out_ref.shape[-1]
    rows = out_ref.shape[0] * out_ref.shape[2]
    bias = bias_ref[0]
    lane = lax.broadcasted_iota(jnp.int32, (rows, 128), 1)
    one = jnp.ones((rows, 128), BF16)
    totals = jnp.zeros((rows, 128), F32)
    for pair_index in range(width // 128):
        first = pair_index * 128
        query = qkv_ref[:, 0, :, first : first + 128].reshape(rows, 128)
        key = qkv_ref[:, 0, :, width + first : width + first + 128].reshape(rows, 128)
        value = qkv_ref[:, 0, :, 2 * width + first : 2 * width + first + 128].reshape(rows, 128)
        query = (query.astype(F32) * 0.125).astype(BF16)
        mixed = []
        for which in range(2):
            scores = matmul_nt(with_flag(query, one, which), with_flag(key, bias, which))
            top = jnp.max(scores, axis=-1, keepdims=True)
            weight = jnp.exp(scores - top)
            total = jnp.sum(weight, axis=-1, keepdims=True)
            mixed.append(matmul(weight.astype(BF16), value) * (1.0 / total))
            totals = jnp.where(lane == 2 * pair_index + which, top + jnp.log(total), totals)
        joined = jnp.where(lane < 64, mixed[0], mixed[1]).astype(BF16)
        out_ref[:, 0, :, first : first + 128] = joined.reshape(out_ref.shape[0], out_ref.shape[2], 128)
    lse_ref[0] = jnp.transpose(totals)[:8]


def attend_back_kernel(qkv_ref, bias_ref, lse_ref, grad_ref, out_ref):
    width = grad_ref.shape[-1]
    shape = (grad_ref.shape[0], grad_ref.shape[2], 128)
    rows = shape[0] * shape[1]
    bias = bias_ref[0]
    lane = lax.broadcasted_iota(jnp.int32, (rows, 128), 1)
    one = jnp.ones((rows, 128), BF16)
    for pair_index in range(width // 128):
        first = pair_index * 128
        query = qkv_ref[:, 0, :, first : first + 128].reshape(rows, 128)
        key = qkv_ref[:, 0, :, width + first : width + first + 128].reshape(rows, 128)
        value = qkv_ref[:, 0, :, 2 * width + first : 2 * width + first + 128].reshape(rows, 128)
        grad = grad_ref[:, 0, :, first : first + 128].reshape(rows, 128)
        query = (query.astype(F32) * 0.125).astype(BF16)
        query_parts, key_parts, value_parts = [], [], []
        for which in range(2):
            spot = 2 * pair_index + which
            log_total = lse_ref[0, spot : spot + 1, :]
            scores = matmul_nt(with_flag(key, bias, which), with_flag(query, one, which))
            probs = jnp.exp(scores - log_total)
            probs_grad = matmul_nt(value, half_lanes(grad, which))
            value_parts.append(matmul(probs.astype(BF16), grad))
            row_dot = jnp.sum(probs * probs_grad, axis=0, keepdims=True)
            score_grad = (probs * (probs_grad - row_dot)).astype(BF16)
            key_parts.append(matmul(score_grad, query))
            query_parts.append(matmul_tn(score_grad, key) * 0.125)
        for place, parts in enumerate((query_parts, key_parts, value_parts)):
            joined = jnp.where(lane < 64, parts[0], parts[1]).astype(BF16)
            start = place * width + first
            out_ref[:, 0, :, start : start + 128] = joined.reshape(shape)


def attention_call(kernel, arrays, outs, flops):
    def whole(array):
        shape = array.shape
        if len(shape) == 4:
            return pl.BlockSpec((shape[0], 1) + shape[2:], lambda s: (0, s, 0, 0))
        return pl.BlockSpec((1,) + shape[1:], lambda s: (s, 0, 0))

    return pl.pallas_call(
        kernel,
        grid=(arrays[0].shape[1],),
        in_specs=[whole(array) for array in arrays],
        out_specs=[whole(out) for out in outs],
        out_shape=outs,
        compiler_params=pltpu.CompilerParams(vmem_limit_bytes=40 * 1024 * 1024),
        cost_estimate=pl.CostEstimate(flops=flops, bytes_accessed=8 << 20, transcendentals=0),
    )(*arrays)


MESH = pl.DeviceIdType.MESH


def repeat(count, body):
    def step(index, carry):
        body(index)
        return carry

    lax.fori_loop(0, count, step, 0)


class Slots:
    def __init__(self):
        self.total = 0

    def take(self, count=1):
        first = self.total
        self.total += count
        return first


def layer_kernel(
    lens_ref,
    states,
    wq_own,
    vec_own,
    wo_own,
    wi_own,
    wu_own,
    encoded_out,
    o_states,
    o_wq,
    o_wout,
    o_win,
    o_wou,
    o_vecs,
    o_qkv,
    o_lse,
    o_att,
    o_norm,
    o_inv,
    o_low,
    o_act,
    o_slope,
    o_norm2,
    o_inv2,
    st_all,
    wq_all,
    vec_all,
    w_out,
    w_in,
    w_ou,
    vecs,
    qkv,
    lse,
    att,
    att_far,
    part_far,
    part_in,
    part_far2,
    part_in2,
    first_norm,
    first_inv,
    first_out,
    low2,
    act,
    slope,
    acc,
    second_inv,
    send,
    recv,
    local,
):
    d, me, y = lax.axis_index("dp"), lax.axis_index("ctx"), lax.axis_index("fsdp")
    x, c = me // 2, me % 2
    to_core = {"ctx": me + 1 - 2 * c}
    to_x = {"ctx": (me + 2) % 4}
    to_y = {"fsdp": 1 - y}
    to_z = {"dp": d + 1 - 2 * (d % 2)}
    to_zz = {"dp": (d + 2) % 4}
    to_far = {"ctx": 3 - me}
    slots = Slots()
    pending = []

    def remote(src, dst, slot, device):
        return pltpu.make_async_remote_copy(
            src_ref=src,
            dst_ref=dst,
            send_sem=send.at[slot],
            recv_sem=recv.at[slot],
            device_id=device,
            device_id_type=MESH,
        )

    def at_end(count, make):
        pending.append((count, make))

    local_slots = Slots()

    def fetch(src, dst):
        copy = pltpu.make_async_copy(src, dst, local.at[local_slots.take()])
        copy.start()
        return copy

    kept = []

    def keep(src, dst):
        kept.append(fetch(src, dst))

    barrier = pltpu.get_barrier_semaphore()
    for device in (to_core, to_x, to_y, to_z, to_zz, to_far):
        pl.semaphore_signal(barrier, inc=1, device_id=device, device_id_type=MESH)
    pl.semaphore_wait(barrier, 6)

    first = slots.take(4)
    state_x = lambda s: remote(states.at[s], st_all.at[2, s], first + s, to_x)
    second = slots.take(4)
    state_core = lambda s: remote(states.at[s], st_all.at[1, s], second + s, to_core)
    third = slots.take(4)
    state_far = lambda s: remote(st_all.at[2, s], st_all.at[3, s], third + s, to_core)
    wq_slot = slots.take()
    wq_copy = remote(wq_own, wq_all.at[pl.ds(pl.multiple_of(y * 512, 512), 512)], wq_slot, to_y)
    vec_slot = slots.take()
    vec_copy = remote(vec_own, vec_all.at[y], vec_slot, to_y)
    for s in range(4):
        state_x(s).start()
    wq_copy.start()
    vec_copy.start()
    for s in range(4):
        state_core(s).start()
    at_end(4, state_x)
    at_end(4, state_core)
    at_end(4, state_far)
    at_end(1, lambda _: wq_copy)
    at_end(1, lambda _: vec_copy)

    p = d % 2
    wo_slot = slots.take(2)

    def wo_copy(side):
        src = wo_own.at[pl.ds(pl.multiple_of(p * 256 + side * 128 + c * 64, 64), 64)]
        return remote(src, w_out.at[x if side == 0 else 1 - x, 2 * y + p], wo_slot + side, to_y)

    wo_pass_slot = slots.take(2)

    def wo_pass(side):
        here = w_out.at[x if side == 0 else 1 - x, 2 * (1 - y) + p]
        return remote(here, here, wo_pass_slot + side, to_z)

    wi_slot = slots.take(8)

    def wi_copy(b):
        src = wi_own.at[
            pl.ds(pl.multiple_of(x * 256, 256), 256), pl.ds(pl.multiple_of((2 * b + c) * 256, 256), 256)
        ]
        dst = w_in.at[
            pl.ds(pl.multiple_of(y * 512 + x * 256, 256), 256), pl.ds(pl.multiple_of(b * 256, 256), 256)
        ]
        return remote(src, dst, wi_slot + b, to_y)

    wi_pass_slot = slots.take(8)

    def wi_pass(b):
        here = w_in.at[
            pl.ds(pl.multiple_of((1 - y) * 512 + x * 256, 256), 256),
            pl.ds(pl.multiple_of(b * 256, 256), 256),
        ]
        return remote(here, here, wi_pass_slot + b, to_x)

    wu_slot = slots.take(4)

    def wu_copy(k):
        side, half = k // 2, k % 2
        src = wu_own.at[pl.ds(pl.multiple_of((p * 4 + side * 2 + c) * 256 + half * 128, 128), 128)]
        dst = w_ou.at[pl.ds(pl.multiple_of((4 * y + 2 * p + side) * 256 + half * 128, 128), 128)]
        return remote(src, dst, wu_slot + k, to_y)

    wu_pass_slot = slots.take(4)

    def wu_pass(k):
        side, half = k // 2, k % 2
        here = w_ou.at[
            pl.ds(pl.multiple_of((4 * (1 - y) + 2 * p + side) * 256 + half * 128, 128), 128)
        ]
        return remote(here, here, wu_pass_slot + k, to_z)

    for side in range(2):
        wo_copy(side).start()
    for b in range(8):
        wi_copy(b).start()
    for k in range(4):
        wu_copy(k).start()
    for count, make in ((2, wo_copy), (2, wo_pass), (8, wi_copy), (8, wi_pass), (4, wu_copy), (4, wu_pass)):
        at_end(count, make)

    own_early = [
        fetch(states, st_all.at[0]),
        fetch(wq_own, wq_all.at[pl.ds(pl.multiple_of(y * 512, 512), 512)]),
        fetch(vec_own, vec_all.at[y]),
    ]
    own_out = []
    for half in range(2):
        for side in range(2):
            src = wo_own.at[pl.ds(pl.multiple_of(half * 256 + side * 128 + c * 64, 64), 64)]
            own_out.append(fetch(src, w_out.at[x if side == 0 else 1 - x, 2 * y + half]))
    own_late = []
    for b in range(8):
        src = wi_own.at[:, pl.ds(pl.multiple_of((2 * b + c) * 256, 256), 256)]
        dst = w_in.at[pl.ds(pl.multiple_of(y * 512, 512), 512), pl.ds(b * 256, 256)]
        own_late.append(fetch(src, dst))
    for half in range(2):
        for side in range(2):
            src = wu_own.at[pl.ds(pl.multiple_of((half * 4 + side * 2 + c) * 256, 256), 256)]
            dst = w_ou.at[pl.ds(pl.multiple_of((4 * y + 2 * half + side) * 256, 256), 256)]
            own_late.append(fetch(src, dst))

    for s in range(2):
        state_x(s).wait_recv()
        state_far(s).start()
    for copy in own_early:
        copy.wait()
    vec_copy.wait_recv()
    vecs[:, :512] = vec_all[0].astype(F32)
    vecs[:, 512:] = vec_all[1].astype(F32)
    wq_copy.wait_recv()

    att_slot = slots.take(8)

    def att_copy(s, j):
        rows = pl.ds(pl.multiple_of(j * 512 + s * 128, 128), 128)
        return remote(att_far.at[j, s], att.at[rows, 256:512], att_slot + 2 * s + j, to_x)

    at_end(8, lambda k: att_copy(k // 2, k % 2))
    q_bias = jnp.concatenate((vecs[0:1, 0:128], vecs[0:1, 512:640]), 1)
    v_bias = jnp.concatenate((vecs[0:1, 128:256], vecs[0:1, 640:768]), 1)

    def key_flags(s):
        pieces = []
        for j in range(4):
            position = lax.broadcasted_iota(jnp.int32, (128, 128), 0)
            place = me + 1 - 2 * c if j == 1 else me
            place = (place + 2) % 4 if j == 2 else place
            place = 3 - me if j == 3 else place
            pieces.append(jnp.where(position + place * 128 < lens_ref[s], 0.0, MASKED))
        return jnp.concatenate(pieces, 0).astype(BF16)

    def attention(s):
        @pl.when(s < 2)
        def _():
            state_x(s + 2).wait_recv()
            state_far(s + 2).start()

        @pl.when(s == 3)
        def _():
            for side in range(2):
                wo_copy(side).wait_recv()
                wo_pass(side).start()

        state_core(s).wait_recv()
        state_far(s).wait_recv()
        rows = st_all[:, s].reshape(512, 1024)
        for place in range(3):
            made = matmul(rows, wq_all[:, place * 256 : place * 256 + 256])
            made = made + q_bias if place == 0 else made
            made = made + v_bias if place == 2 else made
            qkv[:, s, :, place * 256 : place * 256 + 256] = made.astype(BF16).reshape(4, 128, 256)
        bias = key_flags(s)
        lane = lax.broadcasted_iota(jnp.int32, (512, 128), 1)
        one = jnp.ones((512, 128), BF16)
        totals = jnp.zeros((512, 128), F32)
        for pair in range(2):
            base = pair * 128
            query = qkv[:, s, :, base : base + 128].reshape(512, 128)
            key = qkv[:, s, :, 256 + base : 384 + base].reshape(512, 128)
            value = qkv[:, s, :, 512 + base : 640 + base].reshape(512, 128)
            query = (query.astype(F32) * 0.125).astype(BF16)
            mixed = []
            for which in range(2):
                scores = matmul_nt(with_flag(query, one, which), with_flag(key, bias, which))
                top = jnp.max(scores, axis=-1, keepdims=True)
                weight = jnp.exp(scores - top)
                total = jnp.sum(weight, axis=-1, keepdims=True)
                mixed.append(matmul(weight.astype(BF16), value) * (1.0 / total))
                totals = jnp.where(lane == 2 * pair + which, top + jnp.log(total), totals)
            joined = jnp.where(lane < 64, mixed[0], mixed[1]).astype(BF16)
            for j in range(2):
                rows_j = pl.ds(pl.multiple_of(j * 512 + s * 128, 128), 128)
                att[rows_j, base : base + 128] = joined[j * 128 : j * 128 + 128]
                att_far[j, s, :, base : base + 128] = joined[256 + j * 128 : 384 + j * 128]
        for j in range(2):
            att_copy(s, j).start()
        lse[s] = jnp.transpose(totals)[:8]

    repeat(4, attention)
    for src, dst in ((st_all, o_states), (wq_all, o_wq), (vecs, o_vecs), (qkv, o_qkv), (lse, o_lse)):
        keep(src, dst)

    def pass_inner(b):
        wi_copy(b).wait_recv()
        wi_pass(b).start()

    for b in range(4):
        pass_inner(b)
    for copy in own_out:
        copy.wait()
    for side in range(2):
        wo_pass(side).wait_recv()
    for s in range(4):
        for j in range(2):
            att_copy(s, j).wait_recv()
    keep(att, o_att)
    keep(w_out, o_wout)
    out_slot = slots.take(4)

    def out_copy(n):
        return remote(part_far.at[n], part_in.at[n], out_slot + n, to_core)

    at_end(4, out_copy)
    for n in range(4):
        right = w_out[:, :, :, n * 256 : n * 256 + 256].reshape(512, 256)
        part_far[n] = matmul(att[512:], right).astype(BF16)
        out_copy(n).start()
    for b in range(4, 6):
        pass_inner(b)
    for n in range(4):
        right = w_out[:, :, :, n * 256 : n * 256 + 256].reshape(512, 256)
        made = matmul(att[:512], right) + vecs[1:2, n * 256 : n * 256 + 256]
        made = made + st_all[0, :, :, n * 256 : n * 256 + 256].astype(F32).reshape(512, 256)
        out_copy(n).wait_recv()
        first_norm[:, n * 256 : n * 256 + 256] = made + part_in[n].astype(F32)

    low_slot = slots.take(4)

    def low_copy(k):
        src = low2.at[pl.ds(pl.multiple_of(k * 128, 128), 128)]
        dst = low2.at[pl.ds(pl.multiple_of(512 + k * 128, 128), 128)]
        return remote(src, dst, low_slot + k, to_core)

    at_end(4, low_copy)

    def norm_first(k):
        for half in range(2):
            rows = pl.ds(pl.multiple_of(k * 128 + half * 64, 64), 64)
            made, normed, inverse = norm_rows(first_norm[rows, :], vecs[2:3, :], vecs[3:4, :])
            first_norm[rows, :] = normed
            first_inv[rows, :] = jnp.broadcast_to(inverse, (64, 128))
            first_out[rows, :] = made
            low2[rows, :] = made.astype(BF16)
        low_copy(k).start()

    repeat(4, norm_first)
    for b in range(6, 8):
        pass_inner(b)
    for k in range(4):
        low_copy(k).wait_recv()
    for copy in own_late:
        copy.wait()
    for src, dst in ((first_norm, o_norm), (first_inv, o_inv), (low2, o_low)):
        keep(src, dst)

    def unit_block(b):
        wi_pass(b).wait_recv()
        here = pl.ds(pl.multiple_of(b * 256, 256), 256)
        spot = pl.ds(pl.multiple_of((b // 4) * 512 + c * 256, 256), 256)
        row = vecs[pl.ds(8 + b % 4, 1), spot]
        for m in range(2):
            hidden = matmul(low2[m * 512 : m * 512 + 512, :], w_in[:, here]) + row
            below = 0.5 * (1.0 + lax.erf(hidden * math.sqrt(0.5)))
            bell = jnp.exp(-0.5 * hidden * hidden) * (1.0 / math.sqrt(2 * math.pi))
            act[m * 512 : m * 512 + 512, here] = (hidden * below).astype(BF16)
            slope[m * 512 : m * 512 + 512, here] = (below + hidden * bell).astype(BF16)

    repeat(8, unit_block)
    for src, dst in ((act, o_act), (slope, o_slope), (w_in, o_win)):
        keep(src, dst)
    mine = pl.ds(pl.multiple_of(y * 1024, 1024), 1024)
    theirs = pl.ds(pl.multiple_of((1 - y) * 1024, 1024), 1024)
    for k in range(2):
        wu_copy(k).wait_recv()
        wu_pass(k).start()

    def outer_own(n):
        here = pl.ds(pl.multiple_of(n * 256, 256), 256)
        for m in range(2):
            acc[m * 512 : m * 512 + 512, here] = matmul(
                act[m * 512 : m * 512 + 512, mine], w_ou[mine, here]
            )

    repeat(4, outer_own)
    for k in range(2, 4):
        wu_copy(k).wait_recv()
        wu_pass(k).start()
    for k in range(4):
        wu_pass(k).wait_recv()
    keep(w_ou, o_wou)
    sum_slot = slots.take(4)

    def sum_copy(n):
        return remote(part_far2.at[n], part_in2.at[n], sum_slot + n, to_core)

    at_end(4, sum_copy)

    def outer_far(n):
        here = pl.ds(pl.multiple_of(n * 256, 256), 256)
        made = acc[512:, here] + matmul(act[512:, theirs], w_ou[theirs, here])
        part_far2[n] = made.astype(BF16)
        sum_copy(n).start()

    repeat(4, outer_far)

    def outer_near(n):
        here = pl.ds(pl.multiple_of(n * 256, 256), 256)
        made = acc[:512, here] + matmul(act[:512, theirs], w_ou[theirs, here])
        made = made + first_out[:, here] + vecs[4:5, here]
        sum_copy(n).wait_recv()
        acc[:512, here] = made + part_in2[n].astype(F32)

    repeat(4, outer_near)

    def norm_second(k):
        valid_place = lax.broadcasted_iota(jnp.int32, (128, 1), 0) + me * 128
        valid = jnp.where(valid_place < lens_ref[k], 1.0, 0.0)
        for half in range(2):
            rows = pl.ds(pl.multiple_of(k * 128 + half * 64, 64), 64)
            made, normed, inverse = norm_rows(acc[rows, :], vecs[5:6, :], vecs[6:7, :])
            encoded_out[rows, :] = (made * valid[half * 64 : half * 64 + 64]).astype(BF16)
            acc[rows, :] = normed
            second_inv[rows, :] = jnp.broadcast_to(inverse, (64, 128))

    repeat(4, norm_second)
    keep(acc.at[:512], o_norm2)
    keep(second_inv, o_inv2)
    for copy in kept:
        copy.wait()
    for count, make in pending:
        for k in range(count):
            make(k).wait_send()


def layer_call(arrays):
    any_space = pl.BlockSpec(memory_space=pl.ANY)
    v = pltpu.VMEM
    return pl.pallas_call(
        layer_kernel,
        in_specs=[pl.BlockSpec(memory_space=pltpu.SMEM)] + [any_space] * 6,
        out_specs=[pl.BlockSpec(memory_space=pltpu.VMEM)] + [any_space] * 16,
        out_shape=[
            jax.ShapeDtypeStruct(shape, kind)
            for shape, kind in (
                ((512, 1024), BF16),
                ((4, 4, 128, 1024), BF16),
                ((1024, 768), BF16),
                ((2, 4, 64, 1024), BF16),
                ((1024, 2048), BF16),
                ((2048, 1024), BF16),
                ((16, 1024), F32),
                ((4, 4, 128, 768), BF16),
                ((4, 8, 512), F32),
                ((1024, 512), BF16),
                ((512, 1024), F32),
                ((512, 128), F32),
                ((1024, 1024), BF16),
                ((1024, 2048), BF16),
                ((1024, 2048), BF16),
                ((512, 1024), F32),
                ((512, 128), F32),
            )
        ],
        scratch_shapes=[
            v((4, 4, 128, 1024), BF16),
            v((1024, 768), BF16),
            v((2, 16, 512), BF16),
            v((2, 4, 64, 1024), BF16),
            v((1024, 2048), BF16),
            v((2048, 1024), BF16),
            v((16, 1024), F32),
            v((4, 4, 128, 768), BF16),
            v((4, 8, 512), F32),
            v((1024, 512), BF16),
            v((2, 4, 128, 256), BF16),
            v((4, 512, 256), BF16),
            v((4, 512, 256), BF16),
            v((4, 512, 256), BF16),
            v((4, 512, 256), BF16),
            v((512, 1024), F32),
            v((512, 128), F32),
            v((512, 1024), F32),
            v((1024, 1024), BF16),
            v((1024, 2048), BF16),
            v((1024, 2048), BF16),
            v((1024, 1024), F32),
            v((512, 128), F32),
            pltpu.SemaphoreType.DMA((80,)),
            pltpu.SemaphoreType.DMA((80,)),
            pltpu.SemaphoreType.DMA((64,)),
        ],
        compiler_params=pltpu.CompilerParams(
            collective_id=0, has_side_effects=True, vmem_limit_bytes=64 * 1024 * 1024 - 65536
        ),
    )(*arrays)


def accumulate(dst, src, lead, rows):
    steps = rows // 32
    total = math.prod(lead) * steps

    def body(index):
        place = []
        rest = index // steps
        for size in reversed(lead):
            place.insert(0, rest % size)
            rest = rest // size
        here = tuple(place) + (pl.ds(pl.multiple_of((index % steps) * 32, 32), 32),)
        dst[here] = add_low(dst[here], src[here])

    repeat(total, body)


def back_kernel(
    lens_ref,
    i_cot,
    i_n2,
    i_i2,
    i_vecs,
    i_w_ou,
    i_act,
    i_slope,
    i_low,
    i_w_in,
    i_n1,
    i_i1,
    i_att,
    i_w_out,
    i_qkv,
    i_lse,
    i_wq,
    i_states,
    grad_out,
    ou_out,
    in_out,
    out_out,
    qkv_out,
    vec_out,
    cot,
    n2,
    i2,
    vecs,
    w_ou,
    act,
    slope,
    low,
    w_in,
    n1,
    i1,
    att,
    w_out,
    qkv,
    lse,
    wq,
    outer2,
    part_in,
    branch2,
    mix_all,
    mix_far,
    g_ou,
    a_ou,
    b_ou,
    z_ou,
    zz_ou,
    a_in,
    b_in,
    z_in,
    zz_in,
    f_in,
    c_in,
    g_o,
    z_o,
    zz_o,
    x_o,
    y_o,
    g_q,
    y_q,
    z_q,
    zz_q,
    s_q,
    r_q,
    bias_q,
    vb,
    vr,
    send,
    recv,
    local,
):
    d, me, y = lax.axis_index("dp"), lax.axis_index("ctx"), lax.axis_index("fsdp")
    x, c = me // 2, me % 2
    p, q = d % 2, d // 2
    to_core = {"ctx": me + 1 - 2 * c}
    to_x = {"ctx": (me + 2) % 4}
    to_y = {"fsdp": 1 - y}
    to_z = {"dp": d + 1 - 2 * (d % 2)}
    to_zz = {"dp": (d + 2) % 4}
    to_far = {"ctx": 3 - me}
    slots = Slots()
    local_slots = Slots()
    pending = []

    def remotes(count, parts):
        first = slots.take(count)

        def make(k):
            src, dst, device = parts(k)
            return pltpu.make_async_remote_copy(
                src_ref=src,
                dst_ref=dst,
                send_sem=send.at[first + k],
                recv_sem=recv.at[first + k],
                device_id=device,
                device_id_type=MESH,
            )

        pending.append((count, make))
        return make

    def fetch(src, dst):
        copy = pltpu.make_async_copy(src, dst, local.at[local_slots.take()])
        copy.start()
        return copy

    early = [fetch(i_cot, cot), fetch(i_n2, n2), fetch(i_i2, i2), fetch(i_vecs, vecs)]
    barrier = pltpu.get_barrier_semaphore()
    for device in (to_core, to_x, to_y, to_z, to_zz, to_far):
        pl.semaphore_signal(barrier, inc=1, device_id=device, device_id_type=MESH)
    vb[0] = jnp.zeros((24, 1024), F32)
    bias_q[...] = jnp.zeros((8, 768), F32)
    for copy in early:
        copy.wait()
    got_act, got_w_ou = fetch(i_act, act), fetch(i_w_ou, w_ou)
    pl.semaphore_wait(barrier, 6)

    def chunk_of(buffer):
        def parts(k):
            src = buffer.at[pl.ds(pl.multiple_of(k * 128, 128), 128)]
            dst = buffer.at[pl.ds(pl.multiple_of(512 + k * 128, 128), 128)]
            return src, dst, to_core

        return parts

    outer_copy = remotes(4, chunk_of(outer2))
    branch_copy = remotes(4, chunk_of(branch2))

    def count_in(row, values):
        vb[0, row : row + 1, :] += jnp.sum(values, axis=0, keepdims=True)

    def norm_second(k):
        place = lax.broadcasted_iota(jnp.int32, (128, 1), 0) + me * 128
        valid = jnp.where(place < lens_ref[k], 1.0, 0.0)
        for half in range(2):
            rows = pl.ds(pl.multiple_of(k * 128 + half * 64, 64), 64)
            upstream = cot[k, half * 64 : half * 64 + 64].astype(F32) * valid[half * 64 : half * 64 + 64]
            normed = n2[rows, :]
            count_in(0, upstream * normed)
            count_in(1, upstream)
            made = norm_back(upstream, normed, i2[rows, 0:1], vecs[5:6, :])
            n2[rows, :] = made
            made = made.astype(BF16)
            outer2[rows, :] = made
            count_in(2, made.astype(F32))
        outer_copy(k).start()

    repeat(4, norm_second)
    late = [fetch(i_slope, slope), fetch(i_w_in, w_in)]
    got_act.wait()
    for k in range(4):
        outer_copy(k).wait_recv()

    def ou_first(k, x_first):
        if x_first:
            return g_ou.at[k, 1 - x], a_ou.at[k], to_x
        return g_ou.at[k, :, 1 - y], a_ou.at[k], to_y

    ou_a_x = remotes(2, lambda k: ou_first(k, True))
    ou_a_y = remotes(2, lambda k: ou_first(k + 2, False))
    ou_b_y = remotes(2, lambda k: (a_ou.at[k, 1 - y], b_ou.at[k], to_y))
    ou_b_x = remotes(2, lambda k: (a_ou.at[k + 2, 1 - x], b_ou.at[k + 2], to_x))
    ou_z = remotes(2, lambda k: (b_ou.at[2 * k + 1 - p], z_ou.at[k], to_z))
    ou_zz = remotes(1, lambda k: (z_ou.at[1 - q], zz_ou, to_zz))

    def ou_add_a(k):
        if k < 2:
            ou_a_x(k).wait_recv()
            accumulate(a_ou.at[k], g_ou.at[k, x], (2,), 128)
            ou_b_y(k).start()
        else:
            ou_a_y(k - 2).wait_recv()
            accumulate(a_ou.at[k], g_ou.at[k, :, y], (2,), 128)
            ou_b_x(k - 2).start()

    def ou_add_b(k):
        if k < 2:
            ou_b_y(k).wait_recv()
            accumulate(b_ou.at[k], a_ou.at[k, y], (), 128)
        else:
            ou_b_x(k - 2).wait_recv()
            accumulate(b_ou.at[k], a_ou.at[k, x], (), 128)

    def ou_add_z():
        for k in range(2):
            ou_z(k).wait_recv()
            accumulate(z_ou.at[k], b_ou.at[2 * k + p], (), 128)
        ou_zz(0).start()

    def ou_last():
        ou_zz(0).wait_recv()

        def body(i):
            rows = pl.ds(pl.multiple_of(i * 32, 32), 32)
            ou_out[rows, :] = z_ou[q, rows, :].astype(F32) + zz_ou[rows, :].astype(F32)

        repeat(4, body)

    in_a_x = remotes(1, lambda k: (act.at[0, 1 - x], a_in.at[0], to_x))
    in_a_y = remotes(3, lambda k: (act.at[k + 1, :, :, 1 - y], a_in.at[k + 1], to_y))
    in_b_y = remotes(1, lambda k: (a_in.at[0, :, 1 - y], b_in.at[0], to_y))
    in_b_x = remotes(3, lambda k: (a_in.at[k + 1, 1 - x], b_in.at[k + 1], to_x))
    in_z = remotes(2, lambda k: (b_in.at[2 * k + 1 - p], z_in.at[k], to_z))
    in_zz = remotes(1, lambda k: (z_in.at[1 - q], zz_in, to_zz))
    in_core = remotes(1, lambda k: (f_in.at[1 - c], c_in, to_core))

    def in_add_a(k):
        if k < 1:
            in_a_x(0).wait_recv()
            accumulate(a_in.at[0], act.at[0, x], (2, 2), 32)
            in_b_y(0).start()
        else:
            in_a_y(k - 1).wait_recv()
            accumulate(a_in.at[k], act.at[k, :, :, y], (2, 2), 32)
            in_b_x(k - 1).start()

    def in_add_b(k):
        if k < 1:
            in_b_y(0).wait_recv()
            accumulate(b_in.at[0], a_in.at[0, :, y], (2,), 32)
        else:
            in_b_x(k - 1).wait_recv()
            accumulate(b_in.at[k], a_in.at[k, x], (2,), 32)

    def in_add_z():
        for k in range(2):
            in_z(k).wait_recv()
            accumulate(z_in.at[k], b_in.at[2 * k + p], (2,), 32)
        in_zz(0).start()

    def in_sum():
        in_zz(0).wait_recv()
        for k in range(2):
            f_in[k] = z_in[q, k].astype(F32) + zz_in[k].astype(F32)
        in_core(0).start()

    def in_last():
        def place(b, own):
            return pl.ds(pl.multiple_of((2 * b + (c if own else 1 - c)) * 256, 256), 256)

        for b in range(8):
            in_out[:, place(b, True)] = f_in[c, :, b * 256 : b * 256 + 256]
        in_core(0).wait_recv()
        for b in range(8):
            in_out[:, place(b, False)] = c_in[:, b * 256 : b * 256 + 256]

    o_z = remotes(1, lambda k: (g_o.at[:, :, 1 - p], z_o, to_z))
    o_zz = remotes(1, lambda k: (z_o.at[:, 1 - q], zz_o, to_zz))
    o_x = remotes(1, lambda k: (zz_o.at[1], x_o, to_x))
    o_y = remotes(1, lambda k: (x_o.at[1 - y], y_o, to_y))

    def o_add_z():
        o_z(0).wait_recv()
        accumulate(z_o, g_o.at[:, :, p], (2, 2, 2), 32)
        o_zz(0).start()

    def o_add_zz():
        o_zz(0).wait_recv()
        accumulate(zz_o, z_o.at[:, q], (2, 2), 32)
        o_x(0).start()

    def o_add_x():
        o_x(0).wait_recv()
        accumulate(x_o, zz_o.at[0], (2,), 32)
        o_y(0).start()

    def o_last():
        o_y(0).wait_recv()
        out_out[...] = x_o[y].astype(F32) + y_o[...].astype(F32)

    q_y = remotes(4, lambda k: (g_q.at[k, :, 1 - y], y_q.at[k], to_y))
    q_z = remotes(2, lambda k: (y_q.at[2 * k + 1 - p], z_q.at[k], to_z))
    q_zz = remotes(1, lambda k: (z_q.at[1 - q], zz_q, to_zz))
    others = ((me + 1 - 2 * c, to_core), ((me + 2) % 4, to_x), (3 - me, to_far))
    q_all = [
        remotes(1, lambda k, j=j: (s_q.at[others[j][0]], r_q.at[j], others[j][1])) for j in range(3)
    ]

    def q_add_y(k):
        q_y(k).wait_recv()
        accumulate(y_q.at[k], g_q.at[k, :, y], (4,), 32)

    def q_add_z():
        for k in range(2):
            q_z(k).wait_recv()
            accumulate(z_q.at[k], y_q.at[2 * k + p], (4,), 32)
        q_zz(0).start()

    def q_sum():
        q_zz(0).wait_recv()
        for k in range(4):
            s_q[k] = z_q[q, k].astype(F32) + zz_q[k].astype(F32)
        for j in range(3):
            q_all[j](0).start()

    def q_last():
        qkv_out[me] = s_q[me]
        for j in range(3):
            q_all[j](0).wait_recv()
            qkv_out[others[j][0]] = r_q[j]

    v_core = remotes(1, lambda k: (vb.at[0, pl.ds(0, 8)], vr.at[0, pl.ds(0, 8)], to_core))
    v_x = remotes(1, lambda k: (vb.at[1, pl.ds(0, 16)], vr.at[1, pl.ds(0, 16)], to_x))
    v_y = remotes(1, lambda k: (vb.at[2], vr.at[2], to_y))
    v_z = remotes(1, lambda k: (vb.at[3], vr.at[3], to_z))
    v_zz = remotes(1, lambda k: (vb.at[4], vr.at[4], to_zz))

    def outer_grad(i):
        k = (i % 2) * 2 + i // 2
        for half in range(2):
            spot = pl.ds(pl.multiple_of((2 * k + half) * 256, 256), 256)
            left = act[:, :, :, :, :, spot].reshape(1024, 256)
            made = matmul_tn(left, outer2[...])
            g_ou[k, half] = made.astype(BF16).reshape(2, 128, 1024)

        @pl.when(i % 2 == 0)
        def _():
            ou_a_x(k).start()

        @pl.when(i % 2 == 1)
        def _():
            ou_a_y(k - 2).start()

    repeat(4, outer_grad)
    got_w_ou.wait()
    for copy in late:
        copy.wait()
    late = [fetch(i_n1, n1), fetch(i_i1, i1), fetch(i_low, low), fetch(i_att, att), fetch(i_w_out, w_out)]
    late += [fetch(i_qkv, qkv), fetch(i_lse, lse), fetch(i_wq, wq)]

    def hidden_grad(b):
        here = pl.ds(pl.multiple_of(b * 256, 256), 256)
        total = jnp.zeros((1, 256), F32)
        for m in range(2):
            made = matmul_nt(outer2[m * 512 : m * 512 + 512, :], w_ou[here, :])
            made = (made * slope[m * 512 : m * 512 + 512, here].astype(F32)).astype(BF16)
            slope[m * 512 : m * 512 + 512, here] = made
            total = total + jnp.sum(made.astype(F32), axis=0, keepdims=True)
        vb[0, pl.ds(8 + b, 1), 0:256] = total

    repeat(8, hidden_grad)

    def part_copy_parts(n):
        spot = pl.ds(pl.multiple_of(n * 256, 256), 256)
        return w_ou.at[pl.ds(1536, 512), spot], part_in.at[n], to_core

    part_copy = remotes(4, part_copy_parts)

    def first_far(n):
        here = pl.ds(pl.multiple_of(n * 256, 256), 256)
        w_ou[1536:2048, here] = matmul_nt(slope[512:, :], w_in[here, :]).astype(BF16)
        part_copy(n).start()

    repeat(4, first_far)
    ou_add_a(0)
    ou_add_a(2)

    def first_near(n):
        here = pl.ds(pl.multiple_of(n * 256, 256), 256)
        made = n2[:, here] + matmul_nt(slope[:512, :], w_in[here, :])
        part_copy(n).wait_recv()
        n2[:, here] = made + part_in[n].astype(F32)

    repeat(4, first_near)
    for copy in late:
        copy.wait()

    def norm_first(k):
        for half in range(2):
            rows = pl.ds(pl.multiple_of(k * 128 + half * 64, 64), 64)
            upstream = n2[rows, :]
            normed = n1[rows, :]
            count_in(3, upstream * normed)
            count_in(4, upstream)
            made = norm_back(upstream, normed, i1[rows, 0:1], vecs[2:3, :])
            n2[rows, :] = made
            made = made.astype(BF16)
            branch2[rows, :] = made
            count_in(5, made.astype(F32))
        branch_copy(k).start()

    repeat(4, norm_first)
    v_core(0).start()
    for k in range(4):
        branch_copy(k).wait_recv()

    mix_copy = remotes(4, lambda s: (mix_far.at[:, s], mix_all.at[pl.ds(2, 2), s], to_x))
    mix_far[...] = matmul_nt(branch2[...], w_out[1].reshape(256, 1024)).astype(BF16).reshape(2, 4, 128, 256)
    for s in range(4):
        mix_copy(s).start()
    mix_all[0:2] = matmul_nt(branch2[...], w_out[0].reshape(256, 1024)).astype(BF16).reshape(2, 4, 128, 256)

    for half in range(2):
        made = matmul_tn(att[:, half * 256 : half * 256 + 256], branch2[...])
        g_o[half] = made.astype(BF16).reshape(2, 2, 2, 32, 1024)
    o_z(0).start()
    v_core(0).wait_recv()
    vb[1, 0:8] = vb[0, 0:8] + vr[0, 0:8]
    vb[1, 8:16] = vb[0, 8:16]
    v_x(0).start()
    ou_add_a(1)
    ou_add_a(3)

    def inner_grad(k):
        left = low[:, pl.ds(pl.multiple_of(k * 256, 256), 256)]
        for half in range(4):
            made = matmul_tn(left, slope[:, half * 512 : half * 512 + 512]).astype(BF16)
            act[k, :, :, :, :, half * 512 : half * 512 + 512] = made.reshape(2, 2, 2, 32, 512)

        @pl.when(k == 0)
        def _():
            in_a_x(0).start()

        @pl.when(k > 0)
        def _():
            in_a_y(k - 1).start()

    repeat(4, inner_grad)
    got_states = []
    for j in range(4):
        for s in range(4):
            rows = pl.ds((j // 2) * 512 + s * 128, 128)
            got_states.append(fetch(i_states.at[j, s], slope.at[rows, pl.ds((j % 2) * 1024, 1024)]))

    def key_flags(s):
        pieces = []
        for j in range(4):
            position = lax.broadcasted_iota(jnp.int32, (128, 128), 0)
            place = me + 1 - 2 * c if j == 1 else me
            place = (place + 2) % 4 if j == 2 else place
            place = 3 - me if j == 3 else place
            pieces.append(jnp.where(position + place * 128 < lens_ref[s], 0.0, MASKED))
        return jnp.concatenate(pieces, 0).astype(BF16)

    hooks = {
        0: [o_add_z],
        1: [lambda: ou_add_b(0), lambda: ou_add_b(2)],
        2: [o_add_zz, lambda: ou_add_b(1), lambda: ou_z(0).start()],
        3: [lambda: ou_add_b(3), lambda: ou_z(1).start()],
    }

    def attention(s):
        for step, actions in hooks.items():

            @pl.when(s == step)
            def _():
                for action in actions:
                    action()

        mix_copy(s).wait_recv()
        bias = key_flags(s)
        lane = lax.broadcasted_iota(jnp.int32, (512, 128), 1)
        one = jnp.ones((512, 128), BF16)
        for pair in range(2):
            base = pair * 128
            query = qkv[:, s, :, base : base + 128].reshape(512, 128)
            key = qkv[:, s, :, 256 + base : 384 + base].reshape(512, 128)
            value = qkv[:, s, :, 512 + base : 640 + base].reshape(512, 128)
            grad = mix_all[:, s, :, base : base + 128].reshape(512, 128)
            query = (query.astype(F32) * 0.125).astype(BF16)
            query_parts, key_parts, value_parts = [], [], []
            for which in range(2):
                spot = 2 * pair + which
                log_total = lse[s, spot : spot + 1, :]
                scores = matmul_nt(with_flag(key, bias, which), with_flag(query, one, which))
                probs = jnp.exp(scores - log_total)
                probs_grad = matmul_nt(value, half_lanes(grad, which))
                value_parts.append(matmul(probs.astype(BF16), grad))
                row_dot = jnp.sum(probs * probs_grad, axis=0, keepdims=True)
                score_grad = (probs * (probs_grad - row_dot)).astype(BF16)
                key_parts.append(matmul(score_grad, query))
                query_parts.append(matmul_tn(score_grad, key) * 0.125)
            for place, parts in enumerate((query_parts, key_parts, value_parts)):
                joined = jnp.where(lane < 64, parts[0], parts[1]).astype(BF16)
                start = place * 256 + base
                qkv[:, s, :, start : start + 128] = joined.reshape(4, 128, 128)
                bias_q[0:1, start : start + 128] += jnp.sum(joined.astype(F32), axis=0, keepdims=True)

    repeat(4, attention)

    def piece_copy_parts(k):
        rows = pl.ds(pl.multiple_of((k % 2) * 512, 512), 512)
        spot = pl.ds(pl.multiple_of((k // 2) * 256, 256), 256)
        return w_ou.at[rows, spot], w_in.at[rows, spot], to_core

    piece_copy = remotes(8, piece_copy_parts)

    def pass_copy_parts(n):
        src = w_ou.at[pl.ds(1024, 512), pl.ds(pl.multiple_of(n * 256, 256), 256)]
        dst = w_in.at[pl.ds(0, 512), pl.ds(pl.multiple_of(1024 + n * 256, 256), 256)]
        return src, dst, to_x

    pass_copy = remotes(4, pass_copy_parts)

    def piece(j, n):
        rows = wq[pl.ds(pl.multiple_of(n * 256, 256), 256), :]
        return matmul_nt(qkv[j].reshape(512, 768), rows)

    def far_pieces(n):
        spot = pl.ds(pl.multiple_of(n * 256, 256), 256)
        w_ou[512:1024, spot] = piece(3, n).astype(BF16)
        piece_copy(2 * n + 1).start()
        w_ou[0:512, spot] = piece(1, n).astype(BF16)
        piece_copy(2 * n).start()

    repeat(4, far_pieces)

    def passed(n):
        spot = pl.ds(pl.multiple_of(n * 256, 256), 256)
        made = piece(2, n)
        piece_copy(2 * n + 1).wait_recv()
        w_ou[1024:1536, spot] = (made + w_in[512:1024, spot].astype(F32)).astype(BF16)
        pass_copy(n).start()

    repeat(4, passed)
    v_x(0).wait_recv()
    vb[2, 0:16] = vb[1, 0:16] + vr[1, 0:16]
    vb[2, 16:24] = jnp.concatenate((bias_q[...], jnp.zeros((8, 256), F32)), 1)
    v_y(0).start()
    for copy in got_states:
        copy.wait()

    def projection_grad(k):
        made = jnp.zeros((256, 768), F32)
        for j in range(4):
            spot = pl.ds(pl.multiple_of((j % 2) * 1024 + k * 256, 256), 256)
            left = slope[(j // 2) * 512 : (j // 2) * 512 + 512, spot]
            made = made + matmul_tn(left, qkv[j].reshape(512, 768))
        g_q[k] = made.astype(BF16).reshape(4, 2, 32, 768)
        q_y(k).start()

    repeat(4, projection_grad)
    in_add_a(0)
    in_add_a(1)
    v_y(0).wait_recv()
    vb[3] = vb[2] + vr[2]
    v_z(0).start()
    o_add_x()
    ou_add_z()
    in_add_a(2)
    in_add_a(3)
    v_z(0).wait_recv()
    vb[4] = vb[3] + vr[3]
    v_zz(0).start()
    in_add_b(0)
    in_add_b(1)
    in_z(0).start()

    def near_piece(n):
        spot = pl.ds(pl.multiple_of(n * 256, 256), 256)
        made = n2[:, spot] + piece(0, n)
        piece_copy(2 * n).wait_recv()
        n2[:, spot] = made + w_in[0:512, spot].astype(F32)

    repeat(4, near_piece)
    ou_last()
    o_last()
    for k in range(2):
        q_add_y(k)
    q_z(0).start()
    in_add_b(2)
    in_add_b(3)
    in_z(1).start()
    for k in range(2, 4):
        q_add_y(k)
    q_z(1).start()
    in_add_z()
    q_add_z()
    v_zz(0).wait_recv()
    vec_out[...] = vb[4] + vr[4]
    in_sum()
    q_sum()

    def last_piece(n):
        spot = pl.ds(pl.multiple_of(n * 256, 256), 256)
        far = pl.ds(pl.multiple_of(1024 + n * 256, 256), 256)
        pass_copy(n).wait_recv()
        grad_out[:, spot] = (n2[:, spot] + w_in[0:512, far].astype(F32)).astype(BF16)

    repeat(4, last_piece)
    in_last()
    q_last()
    for count, make in pending:
        for k in range(count):
            make(k).wait_send()


def back_call(arrays):
    any_space = pl.BlockSpec(memory_space=pl.ANY)
    outs = (
        ((512, 1024), BF16),
        ((128, 1024), F32),
        ((32, 4096), F32),
        ((32, 1024), F32),
        ((4, 32, 768), F32),
        ((24, 1024), F32),
    )
    scratch = (
        ((4, 128, 1024), BF16),
        ((512, 1024), F32),
        ((512, 128), F32),
        ((16, 1024), F32),
        ((2048, 1024), BF16),
        ((4, 2, 2, 2, 32, 2048), BF16),
        ((1024, 2048), BF16),
        ((1024, 1024), BF16),
        ((1024, 2048), BF16),
        ((512, 1024), F32),
        ((512, 128), F32),
        ((1024, 512), BF16),
        ((2, 4, 64, 1024), BF16),
        ((4, 4, 128, 768), BF16),
        ((4, 8, 512), F32),
        ((1024, 768), BF16),
        ((1024, 1024), BF16),
        ((4, 512, 256), BF16),
        ((1024, 1024), BF16),
        ((4, 4, 128, 256), BF16),
        ((2, 4, 128, 256), BF16),
        ((4, 2, 2, 128, 1024), BF16),
        ((4, 2, 128, 1024), BF16),
        ((4, 128, 1024), BF16),
        ((2, 128, 1024), BF16),
        ((128, 1024), BF16),
        ((4, 2, 2, 32, 2048), BF16),
        ((4, 2, 32, 2048), BF16),
        ((2, 2, 32, 2048), BF16),
        ((2, 32, 2048), BF16),
        ((2, 32, 2048), F32),
        ((32, 2048), F32),
        ((2, 2, 2, 2, 32, 1024), BF16),
        ((2, 2, 2, 32, 1024), BF16),
        ((2, 2, 32, 1024), BF16),
        ((2, 32, 1024), BF16),
        ((32, 1024), BF16),
        ((4, 4, 2, 32, 768), BF16),
        ((4, 4, 32, 768), BF16),
        ((2, 4, 32, 768), BF16),
        ((4, 32, 768), BF16),
        ((4, 32, 768), F32),
        ((3, 32, 768), F32),
        ((8, 768), F32),
        ((5, 24, 1024), F32),
        ((5, 24, 1024), F32),
    )
    return pl.pallas_call(
        back_kernel,
        in_specs=[pl.BlockSpec(memory_space=pltpu.SMEM)] + [any_space] * 17,
        out_specs=[pl.BlockSpec(memory_space=pltpu.VMEM)] * len(outs),
        out_shape=[jax.ShapeDtypeStruct(shape, kind) for shape, kind in outs],
        scratch_shapes=[pltpu.VMEM(shape, kind) for shape, kind in scratch]
        + [
            pltpu.SemaphoreType.DMA((96,)),
            pltpu.SemaphoreType.DMA((96,)),
            pltpu.SemaphoreType.DMA((48,)),
        ],
        compiler_params=pltpu.CompilerParams(
            collective_id=1, has_side_effects=True, vmem_limit_bytes=64 * 1024 * 1024 - 65536
        ),
    )(*arrays)


def shards(
    states,
    cotangent,
    lengths,
    slot_source,
    query_weight,
    query_bias,
    key_weight,
    value_weight,
    value_bias,
    output_weight,
    output_bias,
    first_gain,
    first_shift,
    inner_weight,
    inner_bias,
    outer_weight,
    outer_bias,
    final_gain,
    final_shift,
):
    seq_dev, block_len, width = states.shape
    n_dp, n_ctx, n_fsdp = (lax.axis_size(name) for name in OWNERS)
    assert (n_ctx, n_fsdp) == (4, 2)
    head_size = width // HEADS
    units = inner_weight.shape[1]
    tokens = seq_dev * block_len
    d, me, y = (lax.axis_index(name) for name in OWNERS)
    x, c = me // 2, me % 2
    own_heads = HEADS // n_ctx
    cols = own_heads * head_size
    aligned = n_dp == own_heads

    def other_half(local):
        return swap(local, "fsdp", 1)

    def ordered(own, other, axis=0):
        return jnp.where(
            y == 0, jnp.concatenate((own, other), axis), jnp.concatenate((other, own), axis)
        )

    def gathered(local, axis=0):
        return ordered(local, other_half(local), axis)

    def head_cols(matrix):
        parts = matrix.reshape(matrix.shape[:-1] + (own_heads, n_ctx, head_size))
        return pick(parts, me, parts.ndim - 2).reshape(matrix.shape[:-1] + (cols,))

    my_seqs = (d * n_fsdp + y) * seq_dev + jnp.arange(seq_dev, dtype=jnp.int32)
    seq_len = jnp.sum(jnp.where(slot_source[None, :] == my_seqs[:, None], lengths[None, :], 0), axis=1)
    places = (me ^ jnp.arange(n_ctx, dtype=jnp.int32))[:, None] * block_len + jnp.arange(
        block_len, dtype=jnp.int32
    )
    key_ok = places.reshape(1, -1) < seq_len[:, None]
    key_bias = jnp.where(key_ok, 0.0, MASKED).astype(BF16)
    key_bias = jnp.broadcast_to(key_bias[:, :, None], key_bias.shape + (128,))
    valid_rows = (places[0][None, :] < seq_len[:, None]).astype(F32).reshape(-1, 1)
    full_len = n_ctx * block_len
    score_flops = 2 * seq_dev * own_heads * full_len * full_len * 128
    block = units // (4 * n_dp)
    wq_own = jnp.concatenate((head_cols(query_weight), head_cols(key_weight), head_cols(value_weight)), 1)

    def share(own):
        return jnp.concatenate((own, swap(own, "ctx", 1)), axis=0)

    def collect(both_rows):
        return both_rows[:tokens] + swap(both_rows[tokens:].astype(BF16), "ctx", 1).astype(F32)

    if aligned:
        half_bias = lambda v: pick(v.reshape(2, n_ctx, head_size), me, 1).reshape(1, -1)
        top = jnp.concatenate((half_bias(query_bias), half_bias(value_bias), jnp.zeros((1, 256), BF16)), 1)
        rows16 = [top] + [
            v.reshape(1, -1)
            for v in (output_bias, first_gain, first_shift, outer_bias, final_gain, final_shift)
        ]
        rows16 += [jnp.zeros((1, 512), BF16), inner_bias.reshape(4, 512), jnp.zeros((4, 512), BF16)]
        vec_own = jnp.concatenate(rows16, 0)
        (
            encoded,
            flat_all,
            w_qkv,
            w_out,
            w_inner,
            w_outer,
            vecs,
            qkv,
            log_total,
            attended,
            first_norm,
            first_inverse,
            first_low,
            activated,
            slope,
            second_norm,
            second_inverse,
        ) = layer_call((seq_len, states, wq_own, vec_own, output_weight, inner_weight, outer_weight))
        input_grad, outer_weight_own, inner_weight_own, output_weight_own, qkv_sum, sums = back_call(
            (
                seq_len,
                cotangent,
                second_norm,
                second_inverse,
                vecs,
                w_outer,
                activated.reshape(4, 2, 2, 2, 32, units // 2),
                slope,
                first_low,
                w_inner,
                first_norm,
                first_inverse,
                attended,
                w_out,
                qkv,
                log_total,
                w_qkv,
                flat_all,
            )
        )
        rows = width // (8 * n_dp)
        qkv_sum = qkv_sum.reshape(n_ctx, rows, 3, own_heads, head_size)
        qkv_sum = jnp.transpose(qkv_sum, (2, 1, 3, 0, 4)).reshape(3, rows, width)
        spot = ((d * n_ctx + me) * n_fsdp + y) * rows
        token_sums = lax.dynamic_slice(sums, (0, spot), (6, rows))
        inner_bias_own = lax.dynamic_slice(sums, (8 + 2 * d + x, y * block // 2), (1, block // 2)).reshape(-1)
        own_bias = [
            lax.dynamic_slice(sums, (16, i * cols + d * head_size + y * rows), (1, rows)).reshape(-1) for i in (0, 2)
        ]
        return (
            encoded.reshape(states.shape),
            input_grad.reshape(states.shape),
            qkv_sum[0],
            own_bias[0],
            qkv_sum[1],
            qkv_sum[2],
            own_bias[1],
            output_weight_own,
            token_sums[5],
            token_sums[3],
            token_sums[4],
            inner_weight_own,
            inner_bias_own,
            outer_weight_own,
            token_sums[2],
            token_sums[0],
            token_sums[1],
        )

    def other_half(local):
        return swap(local, "fsdp", 1)

    def ordered(own, other, axis=0):
        return jnp.where(
            y == 0, jnp.concatenate((own, other), axis), jnp.concatenate((other, own), axis)
        )

    def gathered(local, axis=0):
        return ordered(local, other_half(local), axis)

    wide = (query_bias, value_bias, output_bias, first_gain, first_shift, outer_bias, final_gain, final_shift)
    packed = jnp.concatenate([v.reshape(1, -1) for v in wide] + [inner_bias.reshape(-1, width // 2)])
    other_packed = other_half(packed)
    both = jnp.where(y == 0, jnp.stack((packed, other_packed)), jnp.stack((other_packed, packed)))
    b_query, b_value, b_out, g_first, s_first, b_outer, g_final, s_final = (
        both[:, i].reshape(width).astype(F32) for i in range(8)
    )
    b_inner = both[:, 8:].reshape(2 * n_dp, 2, -1)
    b_inner = pick(b_inner, c, 1).reshape(-1).astype(F32)
    w_qkv = gathered(wq_own)
    b_qkv = jnp.concatenate((head_cols(b_query), jnp.zeros((cols,), F32), head_cols(b_value)))

    from_x = swap(states, "ctx", 2)
    from_core = swap(states, "ctx", 1)
    from_far = swap(from_x, "ctx", 1)
    flat_all = jnp.stack((states, from_core, from_x, from_far)).reshape(-1, width)

    w_out = gathered(pick(output_weight.reshape(-1, 2, 2, head_size, width), c, 2))
    w_out = jnp.concatenate((pick(w_out, x, 1), pick(w_out, 1 - x, 1)), 0).reshape(-1, width)
    w_inner = gathered(
        pick(inner_weight.reshape(width // 2, 2 * n_dp, 2, block), c, 2).reshape(width // 2, -1)
    )
    w_outer = gathered(pick(outer_weight.reshape(n_dp, 2, block, width), c, 1).reshape(-1, width))

    qkv = (matmul(flat_all, w_qkv) + b_qkv).astype(BF16)
    qkv = qkv.reshape(n_ctx, seq_dev, block_len, 3 * cols)
    attended_all, log_total = attention_call(
        attend_kernel,
        (qkv, key_bias),
        (
            jax.ShapeDtypeStruct((n_ctx, seq_dev, block_len, cols), BF16),
            jax.ShapeDtypeStruct((seq_dev, 8, full_len), F32),
        ),
        2 * score_flops,
    )
    near = attended_all[:2].reshape(-1, cols)
    far = swap(attended_all[2:], "ctx", 2).reshape(-1, cols)
    attended = jnp.concatenate((near, far), axis=1)
    first_sum = states.reshape(-1, width).astype(F32) + collect(matmul(attended, w_out)) + b_out
    first_out, first_norm, first_inverse = norm_rows(first_sum, g_first, s_first)
    first_low = share(first_out.astype(BF16))
    hidden = matmul(first_low, w_inner) + b_inner
    below = 0.5 * (1.0 + lax.erf(hidden * math.sqrt(0.5)))
    bell = jnp.exp(-0.5 * hidden * hidden) * (1.0 / math.sqrt(2 * math.pi))
    slope = (below + hidden * bell).astype(BF16)
    activated = (hidden * below).astype(BF16)
    second_sum = first_out + collect(matmul(activated, w_outer)) + b_outer
    second_out, second_norm, second_inverse = norm_rows(second_sum, g_final, s_final)
    encoded = (second_out * valid_rows).astype(BF16).reshape(states.shape)

    out_grad = cotangent.reshape(-1, width).astype(F32) * valid_rows
    final_gain_part = jnp.sum(out_grad * second_norm, axis=0)
    final_shift_part = jnp.sum(out_grad, axis=0)
    second_grad = norm_back(out_grad, second_norm, second_inverse, g_final)
    outer_round_own = second_grad.astype(BF16)
    outer_bias_part = col_sum(outer_round_own)
    outer_round = share(outer_round_own)
    outer_weight_part = matmul_tn(activated, outer_round).astype(BF16)
    hidden_grad = (matmul_nt(outer_round, w_outer) * slope.astype(F32)).astype(BF16)
    inner_bias_part = col_sum(hidden_grad)
    inner_weight_part = matmul_tn(first_low, hidden_grad).astype(BF16)
    first_grad = second_grad + collect(matmul_nt(hidden_grad, w_inner))
    first_gain_part = jnp.sum(first_grad * first_norm, axis=0)
    first_shift_part = jnp.sum(first_grad, axis=0)
    sum_grad = norm_back(first_grad, first_norm, first_inverse, g_first)
    branch_own = sum_grad.astype(BF16)
    output_bias_part = col_sum(branch_own)
    branch_grad = share(branch_own)
    output_weight_part = matmul_tn(attended, branch_grad).astype(BF16)
    attended_grad = matmul_nt(branch_grad, w_out).astype(BF16)
    near_grad = attended_grad[:, :cols]
    far_grad = swap(attended_grad[:, cols:], "ctx", 2)
    attended_grad_all = jnp.concatenate((near_grad, far_grad), 0).reshape(n_ctx, seq_dev, block_len, cols)
    (qkv_grad,) = attention_call(
        attend_back_kernel,
        (qkv, key_bias, log_total, attended_grad_all),
        (jax.ShapeDtypeStruct(qkv.shape, BF16),),
        5 * score_flops,
    )
    flat_grad = qkv_grad.reshape(-1, 3 * cols)
    bias_part = col_sum(flat_grad)
    qkv_weight_part = matmul_tn(flat_all, flat_grad).astype(BF16)
    input_part = matmul_nt(flat_grad, w_qkv).reshape(n_ctx, tokens, width)
    to_core = swap(jnp.stack((input_part[1], input_part[3])).astype(BF16), "ctx", 1)
    to_x = swap((input_part[2] + to_core[1].astype(F32)).astype(BF16), "ctx", 2)
    input_grad = sum_grad + input_part[0] + to_core[0].astype(F32) + to_x.astype(F32)
    input_grad = input_grad.astype(BF16).reshape(states.shape)

    token_sums = jnp.stack(
        (final_gain_part, final_shift_part, outer_bias_part, first_gain_part, first_shift_part, output_bias_part)
    )
    def placed_heads(part):
        whole = jnp.zeros(part.shape[:-1] + (own_heads, n_ctx, head_size), part.dtype)
        part = part.reshape(part.shape[:-1] + (own_heads, 1, head_size))
        return lax.dynamic_update_slice_in_dim(whole, part, me, part.ndim - 2).reshape(
            part.shape[:-3] + (width,)
        )

    def placed_units(part, axis):
        split = part.shape[:axis] + (2 * n_dp, 1, block) + part.shape[axis + 1 :]
        whole = jnp.zeros(split[: axis + 1] + (2,) + split[axis + 2 :], part.dtype)
        whole = lax.dynamic_update_slice_in_dim(whole, part.reshape(split), c, axis + 1)
        return whole.reshape(part.shape[:axis] + (units,) + part.shape[axis + 1 :])

    def placed_rows(part):
        part = part.reshape(2, own_heads, 1, 1, head_size, width)
        whole = jnp.zeros((own_heads, 2, 2, head_size, width), part.dtype)
        whole = lax.dynamic_update_slice(whole, part[0], (0, x, c, 0, 0))
        whole = lax.dynamic_update_slice(whole, part[1], (0, 1 - x, c, 0, 0))
        return whole.reshape(width, width)

    def owned(part):
        return lax.psum_scatter(part, OWNERS, scatter_dimension=0, tiled=True).astype(F32)

    qkv_weights = [owned(placed_heads(qkv_weight_part[:, i * cols : (i + 1) * cols])) for i in range(3)]
    query_bias_own = owned(placed_heads(bias_part[:cols]))
    value_bias_own = owned(placed_heads(bias_part[2 * cols :]))
    output_weight_own = owned(placed_rows(output_weight_part))
    inner_weight_own = owned(placed_units(inner_weight_part, 1))
    inner_bias_own = owned(placed_units(inner_bias_part, 0))
    outer_weight_own = owned(placed_units(outer_weight_part, 0))
    sums = [owned(token_sums[i]) for i in range(6)]

    return (
        encoded,
        input_grad,
        qkv_weights[0],
        query_bias_own,
        qkv_weights[1],
        qkv_weights[2],
        value_bias_own,
        output_weight_own,
        sums[5],
        sums[3],
        sums[4],
        inner_weight_own,
        inner_bias_own,
        outer_weight_own,
        sums[2],
        sums[0],
        sums[1],
    )


def solution(mesh):
    tokens = P(("dp", "fsdp"), "ctx", None)
    matrix, vector = P("fsdp", None), P("fsdp")
    own_matrix, own_vector = P(OWNERS, None), P(OWNERS)
    return jax.shard_map(
        shards,
        mesh=mesh,
        in_specs=(
            tokens,
            tokens,
            P(),
            P(),
            matrix,
            vector,
            matrix,
            matrix,
            vector,
            matrix,
            vector,
            vector,
            vector,
            matrix,
            vector,
            matrix,
            vector,
            vector,
            vector,
        ),
        out_specs=(
            tokens,
            tokens,
            own_matrix,
            own_vector,
            own_matrix,
            own_matrix,
            own_vector,
            own_matrix,
            own_vector,
            own_vector,
            own_vector,
            own_matrix,
            own_vector,
            own_matrix,
            own_vector,
            own_vector,
            own_vector,
        ),
        check_vma=False,
    )
```

```python
import functools
import math

import jax
import jax.numpy as jnp
from jax import lax
from jax.experimental import pallas as pl
from jax.experimental.pallas import tpu as pltpu
from jax.sharding import PartitionSpec as P

HEADS = 16
EPS = 1e-12
MASKED = -1e30
F32 = jnp.float32
BF16 = jnp.bfloat16
OWNERS = ("dp", "ctx", "fsdp")


def swap(value, axis, mask):
    pairs = [(source, source ^ mask) for source in range(lax.axis_size(axis))]
    return lax.ppermute(value, axis, pairs)


def pick(array, index, axis):
    return lax.dynamic_index_in_dim(array, index, axis, keepdims=False)


def add_low(left, right):
    return (left.astype(F32) + right.astype(F32)).astype(BF16)


def matmul(left, right):
    return jnp.dot(left, right, preferred_element_type=F32)


def matmul_tn(left, right):
    return lax.dot_general(left, right, (((0,), (0,)), ((), ())), preferred_element_type=F32)


def matmul_nt(left, right):
    return lax.dot_general(left, right, (((1,), (1,)), ((), ())), preferred_element_type=F32)


def col_sum(matrix):
    return jnp.sum(matrix.astype(F32), axis=0)


def norm_rows(summed, scale_vec, shift_vec):
    row_mean = jnp.mean(summed, axis=-1, keepdims=True)
    centered = summed - row_mean
    inverse = lax.rsqrt(jnp.mean(centered * centered, axis=-1, keepdims=True) + EPS)
    normed = centered * inverse
    return (normed * scale_vec + shift_vec, normed, inverse)


def norm_back(upstream, normed, inverse, scale_vec):
    scaled = upstream * scale_vec
    return inverse * (
        scaled
        - jnp.mean(scaled, axis=-1, keepdims=True)
        - normed * jnp.mean(scaled * normed, axis=-1, keepdims=True)
    )


def half_lanes(pair, which):
    lane = lax.broadcasted_iota(jnp.int32, pair.shape, 1)
    keep = lane < 64 if which == 0 else lane >= 64
    return jnp.where(keep, pair, jnp.zeros_like(pair))


def with_flag(pair, flag, which):
    lane = lax.broadcasted_iota(jnp.int32, pair.shape, 1)
    keep = lane < 64 if which == 0 else lane >= 64
    spot = lane == (64 if which == 0 else 0)
    return jnp.where(keep, pair, jnp.where(spot, flag, jnp.zeros_like(pair)))


def attend_kernel(qkv_ref, bias_ref, out_ref, lse_ref):
    width = out_ref.shape[-1]
    rows = out_ref.shape[0] * out_ref.shape[2]
    bias = bias_ref[0]
    lane = lax.broadcasted_iota(jnp.int32, (rows, 128), 1)
    one = jnp.ones((rows, 128), BF16)
    totals = jnp.zeros((rows, 128), F32)
    for pair_index in range(width // 128):
        first = pair_index * 128
        query = qkv_ref[:, 0, :, first : first + 128].reshape(rows, 128)
        key = qkv_ref[:, 0, :, width + first : width + first + 128].reshape(rows, 128)
        value = qkv_ref[:, 0, :, 2 * width + first : 2 * width + first + 128].reshape(rows, 128)
        query = (query.astype(F32) * 0.125).astype(BF16)
        mixed = []
        for which in range(2):
            scores = matmul_nt(with_flag(query, one, which), with_flag(key, bias, which))
            top = jnp.max(scores, axis=-1, keepdims=True)
            weight = jnp.exp(scores - top)
            total = jnp.sum(weight, axis=-1, keepdims=True)
            mixed.append(matmul(weight.astype(BF16), value) * (1.0 / total))
            totals = jnp.where(lane == 2 * pair_index + which, top + jnp.log(total), totals)
        joined = jnp.where(lane < 64, mixed[0], mixed[1]).astype(BF16)
        out_ref[:, 0, :, first : first + 128] = joined.reshape(out_ref.shape[0], out_ref.shape[2], 128)
    lse_ref[0] = jnp.transpose(totals)[:8]


def attend_back_kernel(qkv_ref, bias_ref, lse_ref, grad_ref, out_ref):
    width = grad_ref.shape[-1]
    shape = (grad_ref.shape[0], grad_ref.shape[2], 128)
    rows = shape[0] * shape[1]
    bias = bias_ref[0]
    lane = lax.broadcasted_iota(jnp.int32, (rows, 128), 1)
    one = jnp.ones((rows, 128), BF16)
    for pair_index in range(width // 128):
        first = pair_index * 128
        query = qkv_ref[:, 0, :, first : first + 128].reshape(rows, 128)
        key = qkv_ref[:, 0, :, width + first : width + first + 128].reshape(rows, 128)
        value = qkv_ref[:, 0, :, 2 * width + first : 2 * width + first + 128].reshape(rows, 128)
        grad = grad_ref[:, 0, :, first : first + 128].reshape(rows, 128)
        query = (query.astype(F32) * 0.125).astype(BF16)
        query_parts, key_parts, value_parts = [], [], []
        for which in range(2):
            spot = 2 * pair_index + which
            log_total = lse_ref[0, spot : spot + 1, :]
            scores = matmul_nt(with_flag(key, bias, which), with_flag(query, one, which))
            probs = jnp.exp(scores - log_total)
            probs_grad = matmul_nt(value, half_lanes(grad, which))
            value_parts.append(matmul(probs.astype(BF16), grad))
            row_dot = jnp.sum(probs * probs_grad, axis=0, keepdims=True)
            score_grad = (probs * (probs_grad - row_dot)).astype(BF16)
            key_parts.append(matmul(score_grad, query))
            query_parts.append(matmul_tn(score_grad, key) * 0.125)
        for place, parts in enumerate((query_parts, key_parts, value_parts)):
            joined = jnp.where(lane < 64, parts[0], parts[1]).astype(BF16)
            start = place * width + first
            out_ref[:, 0, :, start : start + 128] = joined.reshape(shape)


def attention_call(kernel, arrays, outs, flops):
    def whole(array):
        shape = array.shape
        if len(shape) == 4:
            return pl.BlockSpec((shape[0], 1) + shape[2:], lambda s: (0, s, 0, 0))
        return pl.BlockSpec((1,) + shape[1:], lambda s: (s, 0, 0))

    return pl.pallas_call(
        kernel,
        grid=(arrays[0].shape[1],),
        in_specs=[whole(array) for array in arrays],
        out_specs=[whole(out) for out in outs],
        out_shape=outs,
        compiler_params=pltpu.CompilerParams(vmem_limit_bytes=40 * 1024 * 1024),
        cost_estimate=pl.CostEstimate(flops=flops, bytes_accessed=8 << 20, transcendentals=0),
    )(*arrays)


MESH = pl.DeviceIdType.MESH


def repeat(count, body):
    def step(index, carry):
        body(index)
        return carry

    lax.fori_loop(0, count, step, 0)


class Slots:
    def __init__(self):
        self.total = 0

    def take(self, count=1):
        first = self.total
        self.total += count
        return first


def layer_kernel(
    lens_ref,
    states,
    wq_own,
    vec_own,
    wo_own,
    wi_own,
    wu_own,
    encoded_out,
    o_states,
    o_wq,
    o_wout,
    o_win,
    o_wou,
    o_vecs,
    o_qkv,
    o_lse,
    o_att,
    o_norm,
    o_inv,
    o_low,
    o_act,
    o_slope,
    o_norm2,
    o_inv2,
    st_all,
    wq_all,
    vec_all,
    w_out,
    w_in,
    w_ou,
    vecs,
    qkv,
    lse,
    att,
    att_far,
    part_far,
    part_in,
    part_far2,
    part_in2,
    first_norm,
    first_inv,
    first_out,
    low2,
    act,
    slope,
    acc,
    second_inv,
    send,
    recv,
    local,
):
    d, me, y = lax.axis_index("dp"), lax.axis_index("ctx"), lax.axis_index("fsdp")
    x, c = me // 2, me % 2
    to_core = {"ctx": me + 1 - 2 * c}
    to_x = {"ctx": (me + 2) % 4}
    to_y = {"fsdp": 1 - y}
    to_z = {"dp": d + 1 - 2 * (d % 2)}
    to_zz = {"dp": (d + 2) % 4}
    to_far = {"ctx": 3 - me}
    slots = Slots()
    pending = []

    def remote(src, dst, slot, device):
        return pltpu.make_async_remote_copy(
            src_ref=src,
            dst_ref=dst,
            send_sem=send.at[slot],
            recv_sem=recv.at[slot],
            device_id=device,
            device_id_type=MESH,
        )

    def at_end(count, make):
        pending.append((count, make))

    local_slots = Slots()

    def fetch(src, dst):
        copy = pltpu.make_async_copy(src, dst, local.at[local_slots.take()])
        copy.start()
        return copy

    kept = []

    def keep(src, dst):
        kept.append(fetch(src, dst))

    barrier = pltpu.get_barrier_semaphore()
    for device in (to_core, to_x, to_y, to_z, to_zz, to_far):
        pl.semaphore_signal(barrier, inc=1, device_id=device, device_id_type=MESH)
    pl.semaphore_wait(barrier, 6)

    first = slots.take(4)
    state_x = lambda s: remote(states.at[s], st_all.at[2, s], first + s, to_x)
    second = slots.take(4)
    state_core = lambda s: remote(states.at[s], st_all.at[1, s], second + s, to_core)
    third = slots.take(4)
    state_far = lambda s: remote(st_all.at[2, s], st_all.at[3, s], third + s, to_core)
    p = d % 2
    wq_slot = slots.take(2)

    def wq_copy(k):
        src = wq_own.at[pl.ds(pl.multiple_of(p * 256 + k * 128, 128), 128)]
        dst = wq_all.at[pl.ds(pl.multiple_of(y * 512 + p * 256 + k * 128, 128), 128)]
        return remote(src, dst, wq_slot + k, to_y)

    wq_pass_slot = slots.take(2)

    def wq_pass(k):
        here = wq_all.at[pl.ds(pl.multiple_of((1 - y) * 512 + p * 256 + k * 128, 128), 128)]
        return remote(here, here, wq_pass_slot + k, to_z)

    vec_slot = slots.take()
    vec_copy = remote(vec_own, vec_all.at[y], vec_slot, to_y)
    for s in range(4):
        state_x(s).start()
    vec_copy.start()
    for k in range(2):
        wq_copy(k).start()
    for s in range(4):
        state_core(s).start()
    at_end(4, state_x)
    at_end(4, state_core)
    at_end(4, state_far)
    at_end(2, wq_copy)
    at_end(2, wq_pass)
    at_end(1, lambda _: vec_copy)

    wo_slot = slots.take(2)

    def wo_copy(side):
        src = wo_own.at[pl.ds(pl.multiple_of(p * 256 + side * 128 + c * 64, 64), 64)]
        return remote(src, w_out.at[x if side == 0 else 1 - x, 2 * y + p], wo_slot + side, to_y)

    wo_pass_slot = slots.take(2)

    def wo_pass(side):
        here = w_out.at[x if side == 0 else 1 - x, 2 * (1 - y) + p]
        return remote(here, here, wo_pass_slot + side, to_z)

    wi_slot = slots.take(8)

    def wi_copy(b):
        src = wi_own.at[
            pl.ds(pl.multiple_of(x * 256, 256), 256), pl.ds(pl.multiple_of((2 * b + c) * 256, 256), 256)
        ]
        dst = w_in.at[
            pl.ds(pl.multiple_of(y * 512 + x * 256, 256), 256), pl.ds(pl.multiple_of(b * 256, 256), 256)
        ]
        return remote(src, dst, wi_slot + b, to_y)

    wi_pass_slot = slots.take(8)

    def wi_pass(b):
        here = w_in.at[
            pl.ds(pl.multiple_of((1 - y) * 512 + x * 256, 256), 256),
            pl.ds(pl.multiple_of(b * 256, 256), 256),
        ]
        return remote(here, here, wi_pass_slot + b, to_x)

    wu_slot = slots.take(4)

    def wu_copy(k):
        side, half = k // 2, k % 2
        src = wu_own.at[pl.ds(pl.multiple_of((p * 4 + side * 2 + c) * 256 + half * 128, 128), 128)]
        dst = w_ou.at[pl.ds(pl.multiple_of((4 * y + 2 * p + side) * 256 + half * 128, 128), 128)]
        return remote(src, dst, wu_slot + k, to_y)

    wu_pass_slot = slots.take(4)

    def wu_pass(k):
        side, half = k // 2, k % 2
        here = w_ou.at[
            pl.ds(pl.multiple_of((4 * (1 - y) + 2 * p + side) * 256 + half * 128, 128), 128)
        ]
        return remote(here, here, wu_pass_slot + k, to_z)

    for side in range(2):
        wo_copy(side).start()
    for b in range(8):
        wi_copy(b).start()
    for k in range(4):
        wu_copy(k).start()
    for count, make in ((2, wo_copy), (2, wo_pass), (8, wi_copy), (8, wi_pass), (4, wu_copy), (4, wu_pass)):
        at_end(count, make)

    own_early = [
        fetch(states, st_all.at[0]),
        fetch(wq_own, wq_all.at[pl.ds(pl.multiple_of(y * 512, 512), 512)]),
        fetch(vec_own, vec_all.at[y]),
    ]
    own_out = []
    for half in range(2):
        for side in range(2):
            src = wo_own.at[pl.ds(pl.multiple_of(half * 256 + side * 128 + c * 64, 64), 64)]
            own_out.append(fetch(src, w_out.at[x if side == 0 else 1 - x, 2 * y + half]))
    own_late = []
    for b in range(8):
        src = wi_own.at[:, pl.ds(pl.multiple_of((2 * b + c) * 256, 256), 256)]
        dst = w_in.at[pl.ds(pl.multiple_of(y * 512, 512), 512), pl.ds(b * 256, 256)]
        own_late.append(fetch(src, dst))
    for half in range(2):
        for side in range(2):
            src = wu_own.at[pl.ds(pl.multiple_of((half * 4 + side * 2 + c) * 256, 256), 256)]
            dst = w_ou.at[pl.ds(pl.multiple_of((4 * y + 2 * half + side) * 256, 256), 256)]
            own_late.append(fetch(src, dst))

    state_x(0).wait_recv()
    state_far(0).start()
    for k in range(2):
        wq_copy(k).wait_recv()
        wq_pass(k).start()
    state_x(1).wait_recv()
    state_far(1).start()
    for copy in own_early:
        copy.wait()
    vec_copy.wait_recv()
    vecs[:, :512] = vec_all[0].astype(F32)
    vecs[:, 512:] = vec_all[1].astype(F32)
    for side in range(2):
        wo_copy(side).wait_recv()
        wo_pass(side).start()
    for k in range(2):
        wq_pass(k).wait_recv()

    att_slot = slots.take(8)

    def att_copy(s, j):
        rows = pl.ds(pl.multiple_of(j * 512 + s * 128, 128), 128)
        return remote(att_far.at[j, s], att.at[rows, 256:512], att_slot + 2 * s + j, to_x)

    at_end(8, lambda k: att_copy(k // 2, k % 2))
    q_bias = jnp.concatenate((vecs[0:1, 0:128], vecs[0:1, 512:640]), 1)
    v_bias = jnp.concatenate((vecs[0:1, 128:256], vecs[0:1, 640:768]), 1)

    def key_flags(s):
        pieces = []
        for j in range(4):
            position = lax.broadcasted_iota(jnp.int32, (128, 128), 0)
            place = me + 1 - 2 * c if j == 1 else me
            place = (place + 2) % 4 if j == 2 else place
            place = 3 - me if j == 3 else place
            pieces.append(jnp.where(position + place * 128 < lens_ref[s], 0.0, MASKED))
        return jnp.concatenate(pieces, 0).astype(BF16)

    def pass_inner(b):
        wi_copy(b).wait_recv()
        wi_pass(b).start()

    def attention(s):
        @pl.when(s < 2)
        def _():
            state_x(s + 2).wait_recv()
            state_far(s + 2).start()

        @pl.when((s == 1) | (s == 2))
        def _():
            for k in range(2):
                pass_inner(2 * (s - 1) + k)

        @pl.when(s == 3)
        def _():
            pass_inner(4)

        state_core(s).wait_recv()
        state_far(s).wait_recv()
        rows = st_all[:, s].reshape(512, 1024)
        for place in range(3):
            made = matmul(rows, wq_all[:, place * 256 : place * 256 + 256])
            made = made + q_bias if place == 0 else made
            made = made + v_bias if place == 2 else made
            qkv[:, s, :, place * 256 : place * 256 + 256] = made.astype(BF16).reshape(4, 128, 256)
        bias = key_flags(s)
        lane = lax.broadcasted_iota(jnp.int32, (512, 128), 1)
        one = jnp.ones((512, 128), BF16)
        totals = jnp.zeros((512, 128), F32)
        for pair in range(2):
            base = pair * 128
            query = qkv[:, s, :, base : base + 128].reshape(512, 128)
            key = qkv[:, s, :, 256 + base : 384 + base].reshape(512, 128)
            value = qkv[:, s, :, 512 + base : 640 + base].reshape(512, 128)
            query = (query.astype(F32) * 0.125).astype(BF16)
            mixed = []
            for which in range(2):
                scores = matmul_nt(with_flag(query, one, which), with_flag(key, bias, which))
                top = jnp.max(scores, axis=-1, keepdims=True)
                weight = jnp.exp(scores - top)
                total = jnp.sum(weight, axis=-1, keepdims=True)
                mixed.append(matmul(weight.astype(BF16), value) * (1.0 / total))
                totals = jnp.where(lane == 2 * pair + which, top + jnp.log(total), totals)
            joined = jnp.where(lane < 64, mixed[0], mixed[1]).astype(BF16)
            for j in range(2):
                rows_j = pl.ds(pl.multiple_of(j * 512 + s * 128, 128), 128)
                att[rows_j, base : base + 128] = joined[j * 128 : j * 128 + 128]
                att_far[j, s, :, base : base + 128] = joined[256 + j * 128 : 384 + j * 128]
        for j in range(2):
            att_copy(s, j).start()
        lse[s] = jnp.transpose(totals)[:8]

    repeat(4, attention)
    for src, dst in ((st_all, o_states), (wq_all, o_wq), (vecs, o_vecs), (qkv, o_qkv), (lse, o_lse)):
        keep(src, dst)

    for b in range(5, 7):
        pass_inner(b)
    for copy in own_out:
        copy.wait()
    for side in range(2):
        wo_pass(side).wait_recv()
    for s in range(4):
        for j in range(2):
            att_copy(s, j).wait_recv()
    keep(att, o_att)
    keep(w_out, o_wout)
    out_slot = slots.take(4)

    def out_copy(n):
        return remote(part_far.at[n], part_in.at[n], out_slot + n, to_core)

    at_end(4, out_copy)
    for n in range(4):
        right = w_out[:, :, :, n * 256 : n * 256 + 256].reshape(512, 256)
        part_far[n] = matmul(att[512:], right).astype(BF16)
        out_copy(n).start()
    pass_inner(7)
    for n in range(4):
        right = w_out[:, :, :, n * 256 : n * 256 + 256].reshape(512, 256)
        made = matmul(att[:512], right) + vecs[1:2, n * 256 : n * 256 + 256]
        made = made + st_all[0, :, :, n * 256 : n * 256 + 256].astype(F32).reshape(512, 256)
        out_copy(n).wait_recv()
        first_norm[:, n * 256 : n * 256 + 256] = made + part_in[n].astype(F32)

    low_slot = slots.take(4)

    def low_copy(k):
        src = low2.at[pl.ds(pl.multiple_of(k * 128, 128), 128)]
        dst = low2.at[pl.ds(pl.multiple_of(512 + k * 128, 128), 128)]
        return remote(src, dst, low_slot + k, to_core)

    at_end(4, low_copy)

    def norm_first(k):
        for half in range(2):
            rows = pl.ds(pl.multiple_of(k * 128 + half * 64, 64), 64)
            made, normed, inverse = norm_rows(first_norm[rows, :], vecs[2:3, :], vecs[3:4, :])
            first_norm[rows, :] = normed
            first_inv[rows, :] = jnp.broadcast_to(inverse, (64, 128))
            first_out[rows, :] = made
            low2[rows, :] = made.astype(BF16)
        low_copy(k).start()

    repeat(4, norm_first)

    def pass_outer(k):
        wu_copy(k).wait_recv()
        wu_pass(k).start()

    pass_outer(0)
    for k in range(4):
        low_copy(k).wait_recv()
    for copy in own_late:
        copy.wait()
    for src, dst in ((first_norm, o_norm), (first_inv, o_inv), (low2, o_low)):
        keep(src, dst)

    def unit_block(b):
        @pl.when((b == 2) | (b == 5))
        def _():
            pass_outer(1 + b // 4)

        wi_pass(b).wait_recv()
        here = pl.ds(pl.multiple_of(b * 256, 256), 256)
        spot = pl.ds(pl.multiple_of((b // 4) * 512 + c * 256, 256), 256)
        row = vecs[pl.ds(8 + b % 4, 1), spot]
        for m in range(2):
            hidden = matmul(low2[m * 512 : m * 512 + 512, :], w_in[:, here]) + row
            below = 0.5 * (1.0 + lax.erf(hidden * math.sqrt(0.5)))
            bell = jnp.exp(-0.5 * hidden * hidden) * (1.0 / math.sqrt(2 * math.pi))
            act[m * 512 : m * 512 + 512, here] = (hidden * below).astype(BF16)
            slope[m * 512 : m * 512 + 512, here] = (below + hidden * bell).astype(BF16)

    repeat(8, unit_block)
    for src, dst in ((act, o_act), (slope, o_slope), (w_in, o_win)):
        keep(src, dst)
    mine = pl.ds(pl.multiple_of(y * 1024, 1024), 1024)
    theirs = pl.ds(pl.multiple_of((1 - y) * 1024, 1024), 1024)
    pass_outer(3)

    def outer_own(n):
        here = pl.ds(pl.multiple_of(n * 256, 256), 256)
        for m in range(2):
            acc[m * 512 : m * 512 + 512, here] = matmul(
                act[m * 512 : m * 512 + 512, mine], w_ou[mine, here]
            )

    repeat(4, outer_own)
    for k in range(4):
        wu_pass(k).wait_recv()
    keep(w_ou, o_wou)
    sum_slot = slots.take(4)

    def sum_copy(n):
        return remote(part_far2.at[n], part_in2.at[n], sum_slot + n, to_core)

    at_end(4, sum_copy)

    def outer_far(n):
        here = pl.ds(pl.multiple_of(n * 256, 256), 256)
        made = acc[512:, here] + matmul(act[512:, theirs], w_ou[theirs, here])
        part_far2[n] = made.astype(BF16)
        sum_copy(n).start()

    repeat(4, outer_far)

    def outer_near(n):
        here = pl.ds(pl.multiple_of(n * 256, 256), 256)
        made = acc[:512, here] + matmul(act[:512, theirs], w_ou[theirs, here])
        made = made + first_out[:, here] + vecs[4:5, here]
        sum_copy(n).wait_recv()
        acc[:512, here] = made + part_in2[n].astype(F32)

    repeat(4, outer_near)

    def norm_second(k):
        valid_place = lax.broadcasted_iota(jnp.int32, (128, 1), 0) + me * 128
        valid = jnp.where(valid_place < lens_ref[k], 1.0, 0.0)
        for half in range(2):
            rows = pl.ds(pl.multiple_of(k * 128 + half * 64, 64), 64)
            made, normed, inverse = norm_rows(acc[rows, :], vecs[5:6, :], vecs[6:7, :])
            encoded_out[rows, :] = (made * valid[half * 64 : half * 64 + 64]).astype(BF16)
            acc[rows, :] = normed
            second_inv[rows, :] = jnp.broadcast_to(inverse, (64, 128))

    repeat(4, norm_second)
    keep(acc.at[:512], o_norm2)
    keep(second_inv, o_inv2)
    for copy in kept:
        copy.wait()
    for count, make in pending:
        for k in range(count):
            make(k).wait_send()


def layer_call(arrays):
    any_space = pl.BlockSpec(memory_space=pl.ANY)
    v = pltpu.VMEM
    return pl.pallas_call(
        layer_kernel,
        in_specs=[pl.BlockSpec(memory_space=pltpu.SMEM)] + [any_space] * 6,
        out_specs=[pl.BlockSpec(memory_space=pltpu.VMEM)] + [any_space] * 16,
        out_shape=[
            jax.ShapeDtypeStruct(shape, kind)
            for shape, kind in (
                ((512, 1024), BF16),
                ((4, 4, 128, 1024), BF16),
                ((1024, 768), BF16),
                ((2, 4, 64, 1024), BF16),
                ((1024, 2048), BF16),
                ((2048, 1024), BF16),
                ((16, 1024), F32),
                ((4, 4, 128, 768), BF16),
                ((4, 8, 512), F32),
                ((1024, 512), BF16),
                ((512, 1024), F32),
                ((512, 128), F32),
                ((1024, 1024), BF16),
                ((1024, 2048), BF16),
                ((1024, 2048), BF16),
                ((512, 1024), F32),
                ((512, 128), F32),
            )
        ],
        scratch_shapes=[
            v((4, 4, 128, 1024), BF16),
            v((1024, 768), BF16),
            v((2, 16, 512), BF16),
            v((2, 4, 64, 1024), BF16),
            v((1024, 2048), BF16),
            v((2048, 1024), BF16),
            v((16, 1024), F32),
            v((4, 4, 128, 768), BF16),
            v((4, 8, 512), F32),
            v((1024, 512), BF16),
            v((2, 4, 128, 256), BF16),
            v((4, 512, 256), BF16),
            v((4, 512, 256), BF16),
            v((4, 512, 256), BF16),
            v((4, 512, 256), BF16),
            v((512, 1024), F32),
            v((512, 128), F32),
            v((512, 1024), F32),
            v((1024, 1024), BF16),
            v((1024, 2048), BF16),
            v((1024, 2048), BF16),
            v((1024, 1024), F32),
            v((512, 128), F32),
            pltpu.SemaphoreType.DMA((80,)),
            pltpu.SemaphoreType.DMA((80,)),
            pltpu.SemaphoreType.DMA((64,)),
        ],
        compiler_params=pltpu.CompilerParams(
            collective_id=0, has_side_effects=True, vmem_limit_bytes=64 * 1024 * 1024 - 65536
        ),
    )(*arrays)


def accumulate(dst, src, lead, rows):
    steps = rows // 32
    total = math.prod(lead) * steps

    def body(index):
        place = []
        rest = index // steps
        for size in reversed(lead):
            place.insert(0, rest % size)
            rest = rest // size
        here = tuple(place) + (pl.ds(pl.multiple_of((index % steps) * 32, 32), 32),)
        dst[here] = add_low(dst[here], src[here])

    repeat(total, body)


def back_kernel(
    lens_ref,
    i_cot,
    i_n2,
    i_i2,
    i_vecs,
    i_w_ou,
    i_act,
    i_slope,
    i_low,
    i_w_in,
    i_n1,
    i_i1,
    i_att,
    i_w_out,
    i_qkv,
    i_lse,
    i_wq,
    i_states,
    grad_out,
    ou_out,
    in_out,
    out_out,
    qkv_out,
    vec_out,
    cot,
    n2,
    i2,
    vecs,
    w_ou,
    act,
    slope,
    low,
    w_in,
    n1,
    i1,
    att,
    w_out,
    qkv,
    lse,
    wq,
    outer2,
    part_in,
    branch2,
    mix_all,
    mix_far,
    g_ou,
    a_ou,
    b_ou,
    z_ou,
    zz_ou,
    az_ou,
    azz_ou,
    ax_ou,
    ay_ou,
    a_in,
    b_in,
    z_in,
    zz_in,
    az_in,
    azz_in,
    ax_in,
    ay_in,
    f_in,
    c_in,
    g_o,
    z_o,
    zz_o,
    x_o,
    y_o,
    g_q,
    y_q,
    z_q,
    zz_q,
    s_q,
    r_q,
    bias_q,
    vb,
    vr,
    send,
    recv,
    local,
):
    d, me, y = lax.axis_index("dp"), lax.axis_index("ctx"), lax.axis_index("fsdp")
    x, c = me // 2, me % 2
    p, q = d % 2, d // 2
    to_core = {"ctx": me + 1 - 2 * c}
    to_x = {"ctx": (me + 2) % 4}
    to_y = {"fsdp": 1 - y}
    to_z = {"dp": d + 1 - 2 * (d % 2)}
    to_zz = {"dp": (d + 2) % 4}
    to_far = {"ctx": 3 - me}
    slots = Slots()
    local_slots = Slots()
    pending = []

    def remotes(count, parts):
        first = slots.take(count)

        def make(k):
            src, dst, device = parts(k)
            return pltpu.make_async_remote_copy(
                src_ref=src,
                dst_ref=dst,
                send_sem=send.at[first + k],
                recv_sem=recv.at[first + k],
                device_id=device,
                device_id_type=MESH,
            )

        pending.append((count, make))
        return make

    def fetch(src, dst):
        copy = pltpu.make_async_copy(src, dst, local.at[local_slots.take()])
        copy.start()
        return copy

    early = [fetch(i_cot, cot), fetch(i_n2, n2), fetch(i_i2, i2), fetch(i_vecs, vecs)]
    barrier = pltpu.get_barrier_semaphore()
    for device in (to_core, to_x, to_y, to_z, to_zz, to_far):
        pl.semaphore_signal(barrier, inc=1, device_id=device, device_id_type=MESH)
    vb[0] = jnp.zeros((24, 1024), F32)
    bias_q[...] = jnp.zeros((8, 768), F32)
    for copy in early:
        copy.wait()
    got_act, got_w_ou = fetch(i_act, act), fetch(i_w_ou, w_ou)
    pl.semaphore_wait(barrier, 6)

    def chunk_of(buffer):
        def parts(k):
            src = buffer.at[pl.ds(pl.multiple_of(k * 128, 128), 128)]
            dst = buffer.at[pl.ds(pl.multiple_of(512 + k * 128, 128), 128)]
            return src, dst, to_core

        return parts

    outer_copy = remotes(4, chunk_of(outer2))
    branch_copy = remotes(4, chunk_of(branch2))

    def count_in(row, values):
        vb[0, row : row + 1, :] += jnp.sum(values, axis=0, keepdims=True)

    def norm_second(k):
        place = lax.broadcasted_iota(jnp.int32, (128, 1), 0) + me * 128
        valid = jnp.where(place < lens_ref[k], 1.0, 0.0)
        for half in range(2):
            rows = pl.ds(pl.multiple_of(k * 128 + half * 64, 64), 64)
            upstream = cot[k, half * 64 : half * 64 + 64].astype(F32) * valid[half * 64 : half * 64 + 64]
            normed = n2[rows, :]
            count_in(0, upstream * normed)
            count_in(1, upstream)
            made = norm_back(upstream, normed, i2[rows, 0:1], vecs[5:6, :])
            n2[rows, :] = made
            made = made.astype(BF16)
            outer2[rows, :] = made
            count_in(2, made.astype(F32))
        outer_copy(k).start()

    repeat(4, norm_second)
    late = [fetch(i_slope, slope), fetch(i_w_in, w_in)]
    got_act.wait()
    for k in range(4):
        outer_copy(k).wait_recv()

    low_ou, top_ou = pl.ds(0, 256), pl.ds(256, 768)
    low_in, top_in = pl.ds(0, 512), pl.ds(512, 1536)

    def ou_first(k, x_first):
        if x_first:
            return g_ou.at[k, 1 - x, :, :, top_ou], a_ou.at[k], to_x
        return g_ou.at[k, :, 1 - y, :, top_ou], a_ou.at[k], to_y

    ou_a_x = remotes(2, lambda k: ou_first(k, True))
    ou_a_y = remotes(2, lambda k: ou_first(k + 2, False))
    ou_b_y = remotes(2, lambda k: (a_ou.at[k, 1 - y], b_ou.at[k], to_y))
    ou_b_x = remotes(2, lambda k: (a_ou.at[k + 2, 1 - x], b_ou.at[k + 2], to_x))
    ou_z = remotes(2, lambda k: (b_ou.at[2 * k + 1 - p], z_ou.at[k], to_z))
    ou_zz = remotes(1, lambda k: (z_ou.at[1 - q], zz_ou, to_zz))
    low_ou_z = remotes(2, lambda k: (g_ou.at[2 * k + 1 - p, :, :, :, low_ou], az_ou.at[k], to_z))
    low_ou_zz = remotes(1, lambda k: (az_ou.at[1 - q], azz_ou, to_zz))
    low_ou_x = remotes(1, lambda k: (azz_ou.at[1 - x], ax_ou, to_x))
    low_ou_y = remotes(1, lambda k: (ax_ou.at[1 - y], ay_ou, to_y))

    def ou_add_a(k):
        if k < 2:
            ou_a_x(k).wait_recv()
            accumulate(a_ou.at[k], g_ou.at[k, x, :, :, top_ou], (2,), 128)
            ou_b_y(k).start()
        else:
            ou_a_y(k - 2).wait_recv()
            accumulate(a_ou.at[k], g_ou.at[k, :, y, :, top_ou], (2,), 128)
            ou_b_x(k - 2).start()

    def ou_add_b(k):
        if k < 2:
            ou_b_y(k).wait_recv()
            accumulate(b_ou.at[k], a_ou.at[k, y], (), 128)
        else:
            ou_b_x(k - 2).wait_recv()
            accumulate(b_ou.at[k], a_ou.at[k, x], (), 128)

    def ou_add_z():
        for k in range(2):
            ou_z(k).wait_recv()
            accumulate(z_ou.at[k], b_ou.at[2 * k + p], (), 128)
        ou_zz(0).start()

    def low_ou_add_z():
        for k in range(2):
            low_ou_z(k).wait_recv()
            accumulate(az_ou.at[k], g_ou.at[2 * k + p, :, :, :, low_ou], (2, 2), 128)
        low_ou_zz(0).start()

    def low_ou_add_zz():
        low_ou_zz(0).wait_recv()
        accumulate(azz_ou, az_ou.at[q], (2, 2), 128)
        low_ou_x(0).start()

    def low_ou_add_x():
        low_ou_x(0).wait_recv()
        accumulate(ax_ou, azz_ou.at[x], (2,), 128)
        low_ou_y(0).start()

    def ou_last():
        ou_zz(0).wait_recv()
        low_ou_y(0).wait_recv()

        def body(i):
            rows = pl.ds(pl.multiple_of(i * 32, 32), 32)
            ou_out[rows, 256:] = z_ou[q, rows, :].astype(F32) + zz_ou[rows, :].astype(F32)
            ou_out[rows, :256] = ax_ou[y, rows, :].astype(F32) + ay_ou[rows, :].astype(F32)

        repeat(4, body)

    in_a = remotes(4, lambda k: (act.at[k, :, :, 1 - y, :, top_in], a_in.at[k], to_y))
    in_b = remotes(4, lambda k: (a_in.at[k, 1 - x], b_in.at[k], to_x))
    in_z = remotes(2, lambda k: (b_in.at[2 * k + 1 - p], z_in.at[k], to_z))
    in_zz = remotes(1, lambda k: (z_in.at[1 - q], zz_in, to_zz))
    in_core = remotes(1, lambda k: (f_in.at[1 - c], c_in, to_core))
    low_in_z = remotes(2, lambda k: (act.at[2 * k + 1 - p, :, :, :, :, low_in], az_in.at[k], to_z))
    low_in_zz = remotes(1, lambda k: (az_in.at[1 - q], azz_in, to_zz))
    low_in_x = remotes(1, lambda k: (azz_in.at[1 - x], ax_in, to_x))
    low_in_y = remotes(1, lambda k: (ax_in.at[:, 1 - y], ay_in, to_y))

    def in_add_a(k):
        in_a(k).wait_recv()
        accumulate(a_in.at[k], act.at[k, :, :, y, :, top_in], (2, 2), 32)
        in_b(k).start()

    def in_add_b(k):
        in_b(k).wait_recv()
        accumulate(b_in.at[k], a_in.at[k, x], (2,), 32)

    def in_add_z():
        for k in range(2):
            in_z(k).wait_recv()
            accumulate(z_in.at[k], b_in.at[2 * k + p], (2,), 32)
        in_zz(0).start()

    def low_in_add_z():
        for k in range(2):
            low_in_z(k).wait_recv()
            accumulate(az_in.at[k], act.at[2 * k + p, :, :, :, :, low_in], (2, 2, 2), 32)
        low_in_zz(0).start()

    def low_in_add_zz():
        low_in_zz(0).wait_recv()
        accumulate(azz_in, az_in.at[q], (2, 2, 2), 32)
        low_in_x(0).start()

    def low_in_add_x():
        low_in_x(0).wait_recv()
        accumulate(ax_in, azz_in.at[x], (2, 2), 32)
        low_in_y(0).start()

    def in_sum():
        in_zz(0).wait_recv()
        low_in_y(0).wait_recv()
        for k in range(2):
            f_in[k, :, 512:] = z_in[q, k].astype(F32) + zz_in[k].astype(F32)
            f_in[k, :, :512] = ax_in[k, y].astype(F32) + ay_in[k].astype(F32)
        in_core(0).start()

    def in_last():
        def place(b, own):
            return pl.ds(pl.multiple_of((2 * b + (c if own else 1 - c)) * 256, 256), 256)

        for b in range(8):
            in_out[:, place(b, True)] = f_in[c, :, b * 256 : b * 256 + 256]
        in_core(0).wait_recv()
        for b in range(8):
            in_out[:, place(b, False)] = c_in[:, b * 256 : b * 256 + 256]

    o_z = remotes(1, lambda k: (g_o.at[:, :, 1 - p], z_o, to_z))
    o_zz = remotes(1, lambda k: (z_o.at[:, 1 - q], zz_o, to_zz))
    o_x = remotes(1, lambda k: (zz_o.at[1], x_o, to_x))
    o_y = remotes(1, lambda k: (x_o.at[1 - y], y_o, to_y))

    def o_add_z():
        o_z(0).wait_recv()
        accumulate(z_o, g_o.at[:, :, p], (2, 2, 2), 32)
        o_zz(0).start()

    def o_add_zz():
        o_zz(0).wait_recv()
        accumulate(zz_o, z_o.at[:, q], (2, 2), 32)
        o_x(0).start()

    def o_add_x():
        o_x(0).wait_recv()
        accumulate(x_o, zz_o.at[0], (2,), 32)
        o_y(0).start()

    def o_last():
        o_y(0).wait_recv()
        out_out[...] = x_o[y].astype(F32) + y_o[...].astype(F32)

    q_y = remotes(4, lambda k: (g_q.at[k, :, 1 - y], y_q.at[k], to_y))
    q_z = remotes(2, lambda k: (y_q.at[2 * k + 1 - p], z_q.at[k], to_z))
    q_zz = remotes(1, lambda k: (z_q.at[1 - q], zz_q, to_zz))
    others = ((me + 1 - 2 * c, to_core), ((me + 2) % 4, to_x), (3 - me, to_far))
    q_all = [
        remotes(1, lambda k, j=j: (s_q.at[others[j][0]], r_q.at[j], others[j][1])) for j in range(3)
    ]

    def q_add_y(k):
        q_y(k).wait_recv()
        accumulate(y_q.at[k], g_q.at[k, :, y], (4,), 32)

    def q_add_z():
        for k in range(2):
            q_z(k).wait_recv()
            accumulate(z_q.at[k], y_q.at[2 * k + p], (4,), 32)
        q_zz(0).start()

    def q_sum():
        q_zz(0).wait_recv()
        for k in range(4):
            s_q[k] = z_q[q, k].astype(F32) + zz_q[k].astype(F32)
        for j in range(3):
            q_all[j](0).start()

    def q_last():
        qkv_out[me] = s_q[me]
        for j in range(3):
            q_all[j](0).wait_recv()
            qkv_out[others[j][0]] = r_q[j]

    v_core = remotes(1, lambda k: (vb.at[0, pl.ds(0, 8)], vr.at[0, pl.ds(0, 8)], to_core))
    v_x = remotes(1, lambda k: (vb.at[1, pl.ds(0, 16)], vr.at[1, pl.ds(0, 16)], to_x))
    v_y = remotes(1, lambda k: (vb.at[2], vr.at[2], to_y))
    v_z = remotes(1, lambda k: (vb.at[3], vr.at[3], to_z))
    v_zz = remotes(1, lambda k: (vb.at[4], vr.at[4], to_zz))

    def outer_grad(i):
        k = (i % 2) * 2 + i // 2
        for half in range(2):
            spot = pl.ds(pl.multiple_of((2 * k + half) * 256, 256), 256)
            left = act[:, :, :, :, :, spot].reshape(1024, 256)
            made = matmul_tn(left, outer2[...])
            g_ou[k, half] = made.astype(BF16).reshape(2, 128, 1024)

        @pl.when(i % 2 == 0)
        def _():
            ou_a_x(k).start()

        @pl.when(i % 2 == 1)
        def _():
            ou_a_y(k - 2).start()

        @pl.when(i >= 2)
        def _():
            low_ou_z(i - 2).start()

    repeat(4, outer_grad)
    got_w_ou.wait()
    for copy in late:
        copy.wait()
    late = [fetch(i_n1, n1), fetch(i_i1, i1), fetch(i_low, low), fetch(i_att, att), fetch(i_w_out, w_out)]
    late += [fetch(i_qkv, qkv), fetch(i_lse, lse), fetch(i_wq, wq)]

    def hidden_grad(b):
        here = pl.ds(pl.multiple_of(b * 256, 256), 256)
        total = jnp.zeros((1, 256), F32)
        for m in range(2):
            made = matmul_nt(outer2[m * 512 : m * 512 + 512, :], w_ou[here, :])
            made = (made * slope[m * 512 : m * 512 + 512, here].astype(F32)).astype(BF16)
            slope[m * 512 : m * 512 + 512, here] = made
            total = total + jnp.sum(made.astype(F32), axis=0, keepdims=True)
        vb[0, pl.ds(8 + b, 1), 0:256] = total

    repeat(8, hidden_grad)

    def part_copy_parts(n):
        spot = pl.ds(pl.multiple_of(n * 256, 256), 256)
        return w_ou.at[pl.ds(1536, 512), spot], part_in.at[n], to_core

    part_copy = remotes(4, part_copy_parts)

    def first_far(n):
        here = pl.ds(pl.multiple_of(n * 256, 256), 256)
        w_ou[1536:2048, here] = matmul_nt(slope[512:, :], w_in[here, :]).astype(BF16)
        part_copy(n).start()

    repeat(4, first_far)
    ou_add_a(0)
    ou_add_a(2)
    low_ou_add_z()

    def first_near(n):
        here = pl.ds(pl.multiple_of(n * 256, 256), 256)
        made = n2[:, here] + matmul_nt(slope[:512, :], w_in[here, :])
        part_copy(n).wait_recv()
        n2[:, here] = made + part_in[n].astype(F32)

    repeat(4, first_near)
    for copy in late:
        copy.wait()

    def norm_first(k):
        for half in range(2):
            rows = pl.ds(pl.multiple_of(k * 128 + half * 64, 64), 64)
            upstream = n2[rows, :]
            normed = n1[rows, :]
            count_in(3, upstream * normed)
            count_in(4, upstream)
            made = norm_back(upstream, normed, i1[rows, 0:1], vecs[2:3, :])
            n2[rows, :] = made
            made = made.astype(BF16)
            branch2[rows, :] = made
            count_in(5, made.astype(F32))
        branch_copy(k).start()

    repeat(4, norm_first)
    v_core(0).start()
    ou_add_a(1)
    ou_add_a(3)
    for k in range(4):
        branch_copy(k).wait_recv()

    mix_copy = remotes(4, lambda s: (mix_far.at[:, s], mix_all.at[pl.ds(2, 2), s], to_x))
    mix_far[...] = matmul_nt(branch2[...], w_out[1].reshape(256, 1024)).astype(BF16).reshape(2, 4, 128, 256)
    for s in range(4):
        mix_copy(s).start()
    mix_all[0:2] = matmul_nt(branch2[...], w_out[0].reshape(256, 1024)).astype(BF16).reshape(2, 4, 128, 256)

    for half in range(2):
        made = matmul_tn(att[:, half * 256 : half * 256 + 256], branch2[...])
        g_o[half] = made.astype(BF16).reshape(2, 2, 2, 32, 1024)
    o_z(0).start()
    v_core(0).wait_recv()
    vb[1, 0:8] = vb[0, 0:8] + vr[0, 0:8]
    vb[1, 8:16] = vb[0, 8:16]
    v_x(0).start()

    def inner_grad(k):
        left = low[:, pl.ds(pl.multiple_of(k * 256, 256), 256)]
        for half in range(4):
            made = matmul_tn(left, slope[:, half * 512 : half * 512 + 512]).astype(BF16)
            act[k, :, :, :, :, half * 512 : half * 512 + 512] = made.reshape(2, 2, 2, 32, 512)

        in_a(k).start()

        @pl.when(k % 2 == 1)
        def _():
            low_in_z(k // 2).start()

    repeat(4, inner_grad)
    got_states = []
    for j in range(4):
        for s in range(4):
            rows = pl.ds((j // 2) * 512 + s * 128, 128)
            got_states.append(fetch(i_states.at[j, s], slope.at[rows, pl.ds((j % 2) * 1024, 1024)]))

    def key_flags(s):
        pieces = []
        for j in range(4):
            position = lax.broadcasted_iota(jnp.int32, (128, 128), 0)
            place = me + 1 - 2 * c if j == 1 else me
            place = (place + 2) % 4 if j == 2 else place
            place = 3 - me if j == 3 else place
            pieces.append(jnp.where(position + place * 128 < lens_ref[s], 0.0, MASKED))
        return jnp.concatenate(pieces, 0).astype(BF16)

    def piece_copy_parts(k):
        rows = pl.ds(pl.multiple_of((k % 2) * 512 + (k // 2) * 128, 128), 128)
        return w_ou.at[rows], w_in.at[rows, pl.ds(0, 1024)], to_core

    piece_copy = remotes(8, piece_copy_parts)

    def pass_copy_parts(s):
        src = w_ou.at[pl.ds(pl.multiple_of(1024 + s * 128, 128), 128)]
        dst = w_in.at[pl.ds(pl.multiple_of(s * 128, 128), 128), pl.ds(1024, 1024)]
        return src, dst, to_x

    pass_copy = remotes(4, pass_copy_parts)

    def far_pieces(s):
        for which in range(2):
            rows = pl.ds(pl.multiple_of(512 * which + s * 128, 128), 128)
            w_ou[rows, :] = matmul_nt(qkv[1 + 2 * which, s], wq[...]).astype(BF16)
        for which in range(2):
            piece_copy(2 * s + which).start()

    def passed(s):
        made = matmul_nt(qkv[2, s], wq[...])
        piece_copy(2 * s + 1).wait_recv()
        rows = pl.ds(pl.multiple_of(512 + s * 128, 128), 128)
        made = made + w_in[rows, 0:1024].astype(F32)
        w_ou[pl.ds(pl.multiple_of(1024 + s * 128, 128), 128), :] = made.astype(BF16)
        pass_copy(s).start()

    hooks = {
        0: [lambda: ou_add_b(0), lambda: ou_add_b(2), low_ou_add_zz],
        1: [lambda: ou_add_b(1), lambda: ou_add_b(3), lambda: ou_z(0).start(), lambda: ou_z(1).start(), o_add_z],
        2: [lambda: in_add_a(0)],
        3: [lambda: in_add_a(1)],
    }

    def attention(s):
        for step, actions in hooks.items():

            @pl.when(s == step)
            def _():
                for action in actions:
                    action()

        mix_copy(s).wait_recv()
        bias = key_flags(s)
        lane = lax.broadcasted_iota(jnp.int32, (512, 128), 1)
        one = jnp.ones((512, 128), BF16)
        for pair in range(2):
            base = pair * 128
            query = qkv[:, s, :, base : base + 128].reshape(512, 128)
            key = qkv[:, s, :, 256 + base : 384 + base].reshape(512, 128)
            value = qkv[:, s, :, 512 + base : 640 + base].reshape(512, 128)
            grad = mix_all[:, s, :, base : base + 128].reshape(512, 128)
            query = (query.astype(F32) * 0.125).astype(BF16)
            query_parts, key_parts, value_parts = [], [], []
            for which in range(2):
                spot = 2 * pair + which
                log_total = lse[s, spot : spot + 1, :]
                scores = matmul_nt(with_flag(key, bias, which), with_flag(query, one, which))
                probs = jnp.exp(scores - log_total)
                probs_grad = matmul_nt(value, half_lanes(grad, which))
                value_parts.append(matmul(probs.astype(BF16), grad))
                row_dot = jnp.sum(probs * probs_grad, axis=0, keepdims=True)
                score_grad = (probs * (probs_grad - row_dot)).astype(BF16)
                key_parts.append(matmul(score_grad, query))
                query_parts.append(matmul_tn(score_grad, key) * 0.125)
            for place, parts in enumerate((query_parts, key_parts, value_parts)):
                joined = jnp.where(lane < 64, parts[0], parts[1]).astype(BF16)
                start = place * 256 + base
                qkv[:, s, :, start : start + 128] = joined.reshape(4, 128, 128)
                bias_q[0:1, start : start + 128] += jnp.sum(joined.astype(F32), axis=0, keepdims=True)
        far_pieces(s)

        @pl.when(s > 0)
        def _():
            passed(s - 1)

    repeat(4, attention)
    passed(3)

    v_x(0).wait_recv()
    vb[2, 0:16] = vb[1, 0:16] + vr[1, 0:16]
    vb[2, 16:24] = jnp.concatenate((bias_q[...], jnp.zeros((8, 256), F32)), 1)
    v_y(0).start()
    for copy in got_states:
        copy.wait()

    def projection_grad(k):
        made = jnp.zeros((256, 768), F32)
        for j in range(4):
            spot = pl.ds(pl.multiple_of((j % 2) * 1024 + k * 256, 256), 256)
            left = slope[(j // 2) * 512 : (j // 2) * 512 + 512, spot]
            made = made + matmul_tn(left, qkv[j].reshape(512, 768))
        g_q[k] = made.astype(BF16).reshape(4, 2, 32, 768)
        q_y(k).start()

    repeat(4, projection_grad)
    in_add_a(2)
    low_in_add_z()
    ou_add_z()
    v_y(0).wait_recv()
    vb[3] = vb[2] + vr[2]
    v_z(0).start()
    o_add_zz()
    in_add_a(3)
    for k in range(2):
        in_add_b(k)
    in_z(0).start()

    def near_piece(s):
        rows = pl.ds(pl.multiple_of(s * 128, 128), 128)
        made = n2[rows, :] + matmul_nt(qkv[0, s], wq[...])
        piece_copy(2 * s).wait_recv()
        n2[rows, :] = made + w_in[rows, 0:1024].astype(F32)

    repeat(4, near_piece)
    low_ou_add_x()
    for k in range(2):
        q_add_y(k)
    q_z(0).start()
    low_in_add_zz()
    for k in range(2, 4):
        q_add_y(k)
    q_z(1).start()
    v_z(0).wait_recv()
    vb[4] = vb[3] + vr[3]
    v_zz(0).start()
    for k in range(2, 4):
        in_add_b(k)
    in_z(1).start()
    q_add_z()
    o_add_x()
    low_in_add_x()
    in_add_z()

    def last_piece(s):
        rows = pl.ds(pl.multiple_of(s * 128, 128), 128)
        pass_copy(s).wait_recv()
        grad_out[rows, :] = (n2[rows, :] + w_in[rows, 1024:2048].astype(F32)).astype(BF16)

    repeat(4, last_piece)
    ou_last()
    o_last()
    v_zz(0).wait_recv()
    vec_out[...] = vb[4] + vr[4]
    q_sum()
    in_sum()
    q_last()
    in_last()
    for count, make in pending:
        for k in range(count):
            make(k).wait_send()


def back_call(arrays):
    any_space = pl.BlockSpec(memory_space=pl.ANY)
    outs = (
        ((512, 1024), BF16),
        ((128, 1024), F32),
        ((32, 4096), F32),
        ((32, 1024), F32),
        ((4, 32, 768), F32),
        ((24, 1024), F32),
    )
    scratch = (
        ((4, 128, 1024), BF16),
        ((512, 1024), F32),
        ((512, 128), F32),
        ((16, 1024), F32),
        ((2048, 1024), BF16),
        ((4, 2, 2, 2, 32, 2048), BF16),
        ((1024, 2048), BF16),
        ((1024, 1024), BF16),
        ((1024, 2048), BF16),
        ((512, 1024), F32),
        ((512, 128), F32),
        ((1024, 512), BF16),
        ((2, 4, 64, 1024), BF16),
        ((4, 4, 128, 768), BF16),
        ((4, 8, 512), F32),
        ((1024, 768), BF16),
        ((1024, 1024), BF16),
        ((4, 512, 256), BF16),
        ((1024, 1024), BF16),
        ((4, 4, 128, 256), BF16),
        ((2, 4, 128, 256), BF16),
        ((4, 2, 2, 128, 1024), BF16),
        ((4, 2, 128, 768), BF16),
        ((4, 128, 768), BF16),
        ((2, 128, 768), BF16),
        ((128, 768), BF16),
        ((2, 2, 2, 128, 256), BF16),
        ((2, 2, 128, 256), BF16),
        ((2, 128, 256), BF16),
        ((128, 256), BF16),
        ((4, 2, 2, 32, 1536), BF16),
        ((4, 2, 32, 1536), BF16),
        ((2, 2, 32, 1536), BF16),
        ((2, 32, 1536), BF16),
        ((2, 2, 2, 2, 32, 512), BF16),
        ((2, 2, 2, 32, 512), BF16),
        ((2, 2, 32, 512), BF16),
        ((2, 32, 512), BF16),
        ((2, 32, 2048), F32),
        ((32, 2048), F32),
        ((2, 2, 2, 2, 32, 1024), BF16),
        ((2, 2, 2, 32, 1024), BF16),
        ((2, 2, 32, 1024), BF16),
        ((2, 32, 1024), BF16),
        ((32, 1024), BF16),
        ((4, 4, 2, 32, 768), BF16),
        ((4, 4, 32, 768), BF16),
        ((2, 4, 32, 768), BF16),
        ((4, 32, 768), BF16),
        ((4, 32, 768), F32),
        ((3, 32, 768), F32),
        ((8, 768), F32),
        ((5, 24, 1024), F32),
        ((5, 24, 1024), F32),
    )
    return pl.pallas_call(
        back_kernel,
        in_specs=[pl.BlockSpec(memory_space=pltpu.SMEM)] + [any_space] * 17,
        out_specs=[pl.BlockSpec(memory_space=pltpu.VMEM)] * len(outs),
        out_shape=[jax.ShapeDtypeStruct(shape, kind) for shape, kind in outs],
        scratch_shapes=[pltpu.VMEM(shape, kind) for shape, kind in scratch]
        + [
            pltpu.SemaphoreType.DMA((96,)),
            pltpu.SemaphoreType.DMA((96,)),
            pltpu.SemaphoreType.DMA((48,)),
        ],
        compiler_params=pltpu.CompilerParams(
            collective_id=1, has_side_effects=True, vmem_limit_bytes=64 * 1024 * 1024 - 65536
        ),
    )(*arrays)


def shards(
    states,
    cotangent,
    lengths,
    slot_source,
    query_weight,
    query_bias,
    key_weight,
    value_weight,
    value_bias,
    output_weight,
    output_bias,
    first_gain,
    first_shift,
    inner_weight,
    inner_bias,
    outer_weight,
    outer_bias,
    final_gain,
    final_shift,
):
    seq_dev, block_len, width = states.shape
    n_dp, n_ctx, n_fsdp = (lax.axis_size(name) for name in OWNERS)
    assert (n_ctx, n_fsdp) == (4, 2)
    head_size = width // HEADS
    units = inner_weight.shape[1]
    tokens = seq_dev * block_len
    d, me, y = (lax.axis_index(name) for name in OWNERS)
    x, c = me // 2, me % 2
    own_heads = HEADS // n_ctx
    cols = own_heads * head_size
    aligned = n_dp == own_heads

    def other_half(local):
        return swap(local, "fsdp", 1)

    def ordered(own, other, axis=0):
        return jnp.where(
            y == 0, jnp.concatenate((own, other), axis), jnp.concatenate((other, own), axis)
        )

    def gathered(local, axis=0):
        return ordered(local, other_half(local), axis)

    def head_cols(matrix):
        parts = matrix.reshape(matrix.shape[:-1] + (own_heads, n_ctx, head_size))
        return pick(parts, me, parts.ndim - 2).reshape(matrix.shape[:-1] + (cols,))

    my_seqs = (d * n_fsdp + y) * seq_dev + jnp.arange(seq_dev, dtype=jnp.int32)
    seq_len = jnp.sum(jnp.where(slot_source[None, :] == my_seqs[:, None], lengths[None, :], 0), axis=1)
    places = (me ^ jnp.arange(n_ctx, dtype=jnp.int32))[:, None] * block_len + jnp.arange(
        block_len, dtype=jnp.int32
    )
    key_ok = places.reshape(1, -1) < seq_len[:, None]
    key_bias = jnp.where(key_ok, 0.0, MASKED).astype(BF16)
    key_bias = jnp.broadcast_to(key_bias[:, :, None], key_bias.shape + (128,))
    valid_rows = (places[0][None, :] < seq_len[:, None]).astype(F32).reshape(-1, 1)
    full_len = n_ctx * block_len
    score_flops = 2 * seq_dev * own_heads * full_len * full_len * 128
    block = units // (4 * n_dp)
    wq_own = jnp.concatenate((head_cols(query_weight), head_cols(key_weight), head_cols(value_weight)), 1)

    def share(own):
        return jnp.concatenate((own, swap(own, "ctx", 1)), axis=0)

    def collect(both_rows):
        return both_rows[:tokens] + swap(both_rows[tokens:].astype(BF16), "ctx", 1).astype(F32)

    if aligned:
        half_bias = lambda v: pick(v.reshape(2, n_ctx, head_size), me, 1).reshape(1, -1)
        top = jnp.concatenate((half_bias(query_bias), half_bias(value_bias), jnp.zeros((1, 256), BF16)), 1)
        rows16 = [top] + [
            v.reshape(1, -1)
            for v in (output_bias, first_gain, first_shift, outer_bias, final_gain, final_shift)
        ]
        rows16 += [jnp.zeros((1, 512), BF16), inner_bias.reshape(4, 512), jnp.zeros((4, 512), BF16)]
        vec_own = jnp.concatenate(rows16, 0)
        (
            encoded,
            flat_all,
            w_qkv,
            w_out,
            w_inner,
            w_outer,
            vecs,
            qkv,
            log_total,
            attended,
            first_norm,
            first_inverse,
            first_low,
            activated,
            slope,
            second_norm,
            second_inverse,
        ) = layer_call((seq_len, states, wq_own, vec_own, output_weight, inner_weight, outer_weight))
        input_grad, outer_weight_own, inner_weight_own, output_weight_own, qkv_sum, sums = back_call(
            (
                seq_len,
                cotangent,
                second_norm,
                second_inverse,
                vecs,
                w_outer,
                activated.reshape(4, 2, 2, 2, 32, units // 2),
                slope,
                first_low,
                w_inner,
                first_norm,
                first_inverse,
                attended,
                w_out,
                qkv,
                log_total,
                w_qkv,
                flat_all,
            )
        )
        rows = width // (8 * n_dp)
        qkv_sum = qkv_sum.reshape(n_ctx, rows, 3, own_heads, head_size)
        qkv_sum = jnp.transpose(qkv_sum, (2, 1, 3, 0, 4)).reshape(3, rows, width)
        spot = ((d * n_ctx + me) * n_fsdp + y) * rows
        token_sums = lax.dynamic_slice(sums, (0, spot), (6, rows))
        inner_bias_own = lax.dynamic_slice(sums, (8 + 2 * d + x, y * block // 2), (1, block // 2)).reshape(-1)
        own_bias = [
            lax.dynamic_slice(sums, (16, i * cols + d * head_size + y * rows), (1, rows)).reshape(-1) for i in (0, 2)
        ]
        return (
            encoded.reshape(states.shape),
            input_grad.reshape(states.shape),
            qkv_sum[0],
            own_bias[0],
            qkv_sum[1],
            qkv_sum[2],
            own_bias[1],
            output_weight_own,
            token_sums[5],
            token_sums[3],
            token_sums[4],
            inner_weight_own,
            inner_bias_own,
            outer_weight_own,
            token_sums[2],
            token_sums[0],
            token_sums[1],
        )

    def other_half(local):
        return swap(local, "fsdp", 1)

    def ordered(own, other, axis=0):
        return jnp.where(
            y == 0, jnp.concatenate((own, other), axis), jnp.concatenate((other, own), axis)
        )

    def gathered(local, axis=0):
        return ordered(local, other_half(local), axis)

    wide = (query_bias, value_bias, output_bias, first_gain, first_shift, outer_bias, final_gain, final_shift)
    packed = jnp.concatenate([v.reshape(1, -1) for v in wide] + [inner_bias.reshape(-1, width // 2)])
    other_packed = other_half(packed)
    both = jnp.where(y == 0, jnp.stack((packed, other_packed)), jnp.stack((other_packed, packed)))
    b_query, b_value, b_out, g_first, s_first, b_outer, g_final, s_final = (
        both[:, i].reshape(width).astype(F32) for i in range(8)
    )
    b_inner = both[:, 8:].reshape(2 * n_dp, 2, -1)
    b_inner = pick(b_inner, c, 1).reshape(-1).astype(F32)
    w_qkv = gathered(wq_own)
    b_qkv = jnp.concatenate((head_cols(b_query), jnp.zeros((cols,), F32), head_cols(b_value)))

    from_x = swap(states, "ctx", 2)
    from_core = swap(states, "ctx", 1)
    from_far = swap(from_x, "ctx", 1)
    flat_all = jnp.stack((states, from_core, from_x, from_far)).reshape(-1, width)

    w_out = gathered(pick(output_weight.reshape(-1, 2, 2, head_size, width), c, 2))
    w_out = jnp.concatenate((pick(w_out, x, 1), pick(w_out, 1 - x, 1)), 0).reshape(-1, width)
    w_inner = gathered(
        pick(inner_weight.reshape(width // 2, 2 * n_dp, 2, block), c, 2).reshape(width // 2, -1)
    )
    w_outer = gathered(pick(outer_weight.reshape(n_dp, 2, block, width), c, 1).reshape(-1, width))

    qkv = (matmul(flat_all, w_qkv) + b_qkv).astype(BF16)
    qkv = qkv.reshape(n_ctx, seq_dev, block_len, 3 * cols)
    attended_all, log_total = attention_call(
        attend_kernel,
        (qkv, key_bias),
        (
            jax.ShapeDtypeStruct((n_ctx, seq_dev, block_len, cols), BF16),
            jax.ShapeDtypeStruct((seq_dev, 8, full_len), F32),
        ),
        2 * score_flops,
    )
    near = attended_all[:2].reshape(-1, cols)
    far = swap(attended_all[2:], "ctx", 2).reshape(-1, cols)
    attended = jnp.concatenate((near, far), axis=1)
    first_sum = states.reshape(-1, width).astype(F32) + collect(matmul(attended, w_out)) + b_out
    first_out, first_norm, first_inverse = norm_rows(first_sum, g_first, s_first)
    first_low = share(first_out.astype(BF16))
    hidden = matmul(first_low, w_inner) + b_inner
    below = 0.5 * (1.0 + lax.erf(hidden * math.sqrt(0.5)))
    bell = jnp.exp(-0.5 * hidden * hidden) * (1.0 / math.sqrt(2 * math.pi))
    slope = (below + hidden * bell).astype(BF16)
    activated = (hidden * below).astype(BF16)
    second_sum = first_out + collect(matmul(activated, w_outer)) + b_outer
    second_out, second_norm, second_inverse = norm_rows(second_sum, g_final, s_final)
    encoded = (second_out * valid_rows).astype(BF16).reshape(states.shape)

    out_grad = cotangent.reshape(-1, width).astype(F32) * valid_rows
    final_gain_part = jnp.sum(out_grad * second_norm, axis=0)
    final_shift_part = jnp.sum(out_grad, axis=0)
    second_grad = norm_back(out_grad, second_norm, second_inverse, g_final)
    outer_round_own = second_grad.astype(BF16)
    outer_bias_part = col_sum(outer_round_own)
    outer_round = share(outer_round_own)
    outer_weight_part = matmul_tn(activated, outer_round).astype(BF16)
    hidden_grad = (matmul_nt(outer_round, w_outer) * slope.astype(F32)).astype(BF16)
    inner_bias_part = col_sum(hidden_grad)
    inner_weight_part = matmul_tn(first_low, hidden_grad).astype(BF16)
    first_grad = second_grad + collect(matmul_nt(hidden_grad, w_inner))
    first_gain_part = jnp.sum(first_grad * first_norm, axis=0)
    first_shift_part = jnp.sum(first_grad, axis=0)
    sum_grad = norm_back(first_grad, first_norm, first_inverse, g_first)
    branch_own = sum_grad.astype(BF16)
    output_bias_part = col_sum(branch_own)
    branch_grad = share(branch_own)
    output_weight_part = matmul_tn(attended, branch_grad).astype(BF16)
    attended_grad = matmul_nt(branch_grad, w_out).astype(BF16)
    near_grad = attended_grad[:, :cols]
    far_grad = swap(attended_grad[:, cols:], "ctx", 2)
    attended_grad_all = jnp.concatenate((near_grad, far_grad), 0).reshape(n_ctx, seq_dev, block_len, cols)
    (qkv_grad,) = attention_call(
        attend_back_kernel,
        (qkv, key_bias, log_total, attended_grad_all),
        (jax.ShapeDtypeStruct(qkv.shape, BF16),),
        5 * score_flops,
    )
    flat_grad = qkv_grad.reshape(-1, 3 * cols)
    bias_part = col_sum(flat_grad)
    qkv_weight_part = matmul_tn(flat_all, flat_grad).astype(BF16)
    input_part = matmul_nt(flat_grad, w_qkv).reshape(n_ctx, tokens, width)
    to_core = swap(jnp.stack((input_part[1], input_part[3])).astype(BF16), "ctx", 1)
    to_x = swap((input_part[2] + to_core[1].astype(F32)).astype(BF16), "ctx", 2)
    input_grad = sum_grad + input_part[0] + to_core[0].astype(F32) + to_x.astype(F32)
    input_grad = input_grad.astype(BF16).reshape(states.shape)

    token_sums = jnp.stack(
        (final_gain_part, final_shift_part, outer_bias_part, first_gain_part, first_shift_part, output_bias_part)
    )
    def placed_heads(part):
        whole = jnp.zeros(part.shape[:-1] + (own_heads, n_ctx, head_size), part.dtype)
        part = part.reshape(part.shape[:-1] + (own_heads, 1, head_size))
        return lax.dynamic_update_slice_in_dim(whole, part, me, part.ndim - 2).reshape(
            part.shape[:-3] + (width,)
        )

    def placed_units(part, axis):
        split = part.shape[:axis] + (2 * n_dp, 1, block) + part.shape[axis + 1 :]
        whole = jnp.zeros(split[: axis + 1] + (2,) + split[axis + 2 :], part.dtype)
        whole = lax.dynamic_update_slice_in_dim(whole, part.reshape(split), c, axis + 1)
        return whole.reshape(part.shape[:axis] + (units,) + part.shape[axis + 1 :])

    def placed_rows(part):
        part = part.reshape(2, own_heads, 1, 1, head_size, width)
        whole = jnp.zeros((own_heads, 2, 2, head_size, width), part.dtype)
        whole = lax.dynamic_update_slice(whole, part[0], (0, x, c, 0, 0))
        whole = lax.dynamic_update_slice(whole, part[1], (0, 1 - x, c, 0, 0))
        return whole.reshape(width, width)

    def owned(part):
        return lax.psum_scatter(part, OWNERS, scatter_dimension=0, tiled=True).astype(F32)

    qkv_weights = [owned(placed_heads(qkv_weight_part[:, i * cols : (i + 1) * cols])) for i in range(3)]
    query_bias_own = owned(placed_heads(bias_part[:cols]))
    value_bias_own = owned(placed_heads(bias_part[2 * cols :]))
    output_weight_own = owned(placed_rows(output_weight_part))
    inner_weight_own = owned(placed_units(inner_weight_part, 1))
    inner_bias_own = owned(placed_units(inner_bias_part, 0))
    outer_weight_own = owned(placed_units(outer_weight_part, 0))
    sums = [owned(token_sums[i]) for i in range(6)]

    return (
        encoded,
        input_grad,
        qkv_weights[0],
        query_bias_own,
        qkv_weights[1],
        qkv_weights[2],
        value_bias_own,
        output_weight_own,
        sums[5],
        sums[3],
        sums[4],
        inner_weight_own,
        inner_bias_own,
        outer_weight_own,
        sums[2],
        sums[0],
        sums[1],
    )


def solution(mesh):
    tokens = P(("dp", "fsdp"), "ctx", None)
    matrix, vector = P("fsdp", None), P("fsdp")
    own_matrix, own_vector = P(OWNERS, None), P(OWNERS)
    return jax.shard_map(
        shards,
        mesh=mesh,
        in_specs=(
            tokens,
            tokens,
            P(),
            P(),
            matrix,
            vector,
            matrix,
            matrix,
            vector,
            matrix,
            vector,
            vector,
            vector,
            matrix,
            vector,
            matrix,
            vector,
            vector,
            vector,
        ),
        out_specs=(
            tokens,
            tokens,
            own_matrix,
            own_vector,
            own_matrix,
            own_matrix,
            own_vector,
            own_matrix,
            own_vector,
            own_vector,
            own_vector,
            own_matrix,
            own_vector,
            own_matrix,
            own_vector,
            own_vector,
            own_vector,
        ),
        check_vma=False,
    )
```

```python
import functools
import math

import jax
import jax.numpy as jnp
from jax import lax
from jax.experimental import pallas as pl
from jax.experimental.pallas import tpu as pltpu
from jax.sharding import PartitionSpec as P

HEADS = 16
EPS = 1e-12
MASKED = -1e30
F32 = jnp.float32
BF16 = jnp.bfloat16
OWNERS = ("dp", "ctx", "fsdp")


def swap(value, axis, mask):
    pairs = [(source, source ^ mask) for source in range(lax.axis_size(axis))]
    return lax.ppermute(value, axis, pairs)


def pick(array, index, axis):
    return lax.dynamic_index_in_dim(array, index, axis, keepdims=False)


def add_low(left, right):
    return (left.astype(F32) + right.astype(F32)).astype(BF16)


def matmul(left, right):
    return jnp.dot(left, right, preferred_element_type=F32)


def matmul_tn(left, right):
    return lax.dot_general(left, right, (((0,), (0,)), ((), ())), preferred_element_type=F32)


def matmul_nt(left, right):
    return lax.dot_general(left, right, (((1,), (1,)), ((), ())), preferred_element_type=F32)


def col_sum(matrix):
    return jnp.sum(matrix.astype(F32), axis=0)


def norm_rows(summed, scale_vec, shift_vec):
    row_mean = jnp.mean(summed, axis=-1, keepdims=True)
    centered = summed - row_mean
    inverse = lax.rsqrt(jnp.mean(centered * centered, axis=-1, keepdims=True) + EPS)
    normed = centered * inverse
    return (normed * scale_vec + shift_vec, normed, inverse)


def norm_back(upstream, normed, inverse, scale_vec):
    scaled = upstream * scale_vec
    return inverse * (
        scaled
        - jnp.mean(scaled, axis=-1, keepdims=True)
        - normed * jnp.mean(scaled * normed, axis=-1, keepdims=True)
    )


def half_lanes(pair, which):
    lane = lax.broadcasted_iota(jnp.int32, pair.shape, 1)
    keep = lane < 64 if which == 0 else lane >= 64
    return jnp.where(keep, pair, jnp.zeros_like(pair))


def with_flag(pair, flag, which):
    lane = lax.broadcasted_iota(jnp.int32, pair.shape, 1)
    keep = lane < 64 if which == 0 else lane >= 64
    spot = lane == (64 if which == 0 else 0)
    return jnp.where(keep, pair, jnp.where(spot, flag, jnp.zeros_like(pair)))


def attend_kernel(qkv_ref, bias_ref, out_ref, lse_ref):
    width = out_ref.shape[-1]
    rows = out_ref.shape[0] * out_ref.shape[2]
    bias = bias_ref[0]
    lane = lax.broadcasted_iota(jnp.int32, (rows, 128), 1)
    one = jnp.ones((rows, 128), BF16)
    totals = jnp.zeros((rows, 128), F32)
    for pair_index in range(width // 128):
        first = pair_index * 128
        query = qkv_ref[:, 0, :, first : first + 128].reshape(rows, 128)
        key = qkv_ref[:, 0, :, width + first : width + first + 128].reshape(rows, 128)
        value = qkv_ref[:, 0, :, 2 * width + first : 2 * width + first + 128].reshape(rows, 128)
        query = (query.astype(F32) * 0.125).astype(BF16)
        mixed = []
        for which in range(2):
            scores = matmul_nt(with_flag(query, one, which), with_flag(key, bias, which))
            top = jnp.max(scores, axis=-1, keepdims=True)
            weight = jnp.exp(scores - top)
            total = jnp.sum(weight, axis=-1, keepdims=True)
            mixed.append(matmul(weight.astype(BF16), value) * (1.0 / total))
            totals = jnp.where(lane == 2 * pair_index + which, top + jnp.log(total), totals)
        joined = jnp.where(lane < 64, mixed[0], mixed[1]).astype(BF16)
        out_ref[:, 0, :, first : first + 128] = joined.reshape(out_ref.shape[0], out_ref.shape[2], 128)
    lse_ref[0] = jnp.transpose(totals)[:8]


def attend_back_kernel(qkv_ref, bias_ref, lse_ref, grad_ref, out_ref):
    width = grad_ref.shape[-1]
    shape = (grad_ref.shape[0], grad_ref.shape[2], 128)
    rows = shape[0] * shape[1]
    bias = bias_ref[0]
    lane = lax.broadcasted_iota(jnp.int32, (rows, 128), 1)
    one = jnp.ones((rows, 128), BF16)
    for pair_index in range(width // 128):
        first = pair_index * 128
        query = qkv_ref[:, 0, :, first : first + 128].reshape(rows, 128)
        key = qkv_ref[:, 0, :, width + first : width + first + 128].reshape(rows, 128)
        value = qkv_ref[:, 0, :, 2 * width + first : 2 * width + first + 128].reshape(rows, 128)
        grad = grad_ref[:, 0, :, first : first + 128].reshape(rows, 128)
        query = (query.astype(F32) * 0.125).astype(BF16)
        query_parts, key_parts, value_parts = [], [], []
        for which in range(2):
            spot = 2 * pair_index + which
            log_total = lse_ref[0, spot : spot + 1, :]
            scores = matmul_nt(with_flag(key, bias, which), with_flag(query, one, which))
            probs = jnp.exp(scores - log_total)
            probs_grad = matmul_nt(value, half_lanes(grad, which))
            value_parts.append(matmul(probs.astype(BF16), grad))
            row_dot = jnp.sum(probs * probs_grad, axis=0, keepdims=True)
            score_grad = (probs * (probs_grad - row_dot)).astype(BF16)
            key_parts.append(matmul(score_grad, query))
            query_parts.append(matmul_tn(score_grad, key) * 0.125)
        for place, parts in enumerate((query_parts, key_parts, value_parts)):
            joined = jnp.where(lane < 64, parts[0], parts[1]).astype(BF16)
            start = place * width + first
            out_ref[:, 0, :, start : start + 128] = joined.reshape(shape)


def attention_call(kernel, arrays, outs, flops):
    def whole(array):
        shape = array.shape
        if len(shape) == 4:
            return pl.BlockSpec((shape[0], 1) + shape[2:], lambda s: (0, s, 0, 0))
        return pl.BlockSpec((1,) + shape[1:], lambda s: (s, 0, 0))

    return pl.pallas_call(
        kernel,
        grid=(arrays[0].shape[1],),
        in_specs=[whole(array) for array in arrays],
        out_specs=[whole(out) for out in outs],
        out_shape=outs,
        compiler_params=pltpu.CompilerParams(vmem_limit_bytes=40 * 1024 * 1024),
        cost_estimate=pl.CostEstimate(flops=flops, bytes_accessed=8 << 20, transcendentals=0),
    )(*arrays)


MESH = pl.DeviceIdType.MESH


def repeat(count, body):
    def step(index, carry):
        body(index)
        return carry

    lax.fori_loop(0, count, step, 0)


class Slots:
    def __init__(self):
        self.total = 0

    def take(self, count=1):
        first = self.total
        self.total += count
        return first


def read_lengths(slot_ref, length_ref, lens_ref, first):
    def step(t, totals):
        source, count = slot_ref[t], length_ref[t]
        return tuple(total + jnp.where(source == first + i, count, 0) for i, total in enumerate(totals))

    totals = lax.fori_loop(0, slot_ref.shape[0], step, (jnp.int32(0),) * 4)
    for i in range(4):
        lens_ref[i] = totals[i]


def layer_kernel(
    length_ref,
    slot_ref,
    states,
    query_own,
    key_own,
    value_own,
    vec_query,
    vec_out,
    vec_gain,
    vec_shift,
    vec_outer,
    vec_gain2,
    vec_shift2,
    vec_value,
    vec_inner,
    wo_own,
    wi_own,
    wu_own,
    encoded_out,
    o_states,
    o_wq,
    o_wout,
    o_win,
    o_wou,
    o_vecs,
    o_qkv,
    o_lse,
    o_att,
    o_norm,
    o_inv,
    o_low,
    o_act,
    o_slope,
    o_norm2,
    o_inv2,
    lens_ref,
    st_all,
    wq_all,
    vec_all,
    w_out,
    w_in,
    w_ou,
    vecs,
    qkv,
    lse,
    att,
    att_far,
    part_far,
    part_in,
    part_far2,
    part_in2,
    first_norm,
    first_inv,
    first_out,
    low2,
    act,
    slope,
    acc,
    second_inv,
    chosen,
    own_three,
    send,
    recv,
    local,
):
    d, me, y = lax.axis_index("dp"), lax.axis_index("ctx"), lax.axis_index("fsdp")
    x, c = me // 2, me % 2
    to_core = {"ctx": me + 1 - 2 * c}
    to_x = {"ctx": (me + 2) % 4}
    to_y = {"fsdp": 1 - y}
    to_z = {"dp": d + 1 - 2 * (d % 2)}
    to_zz = {"dp": (d + 2) % 4}
    to_far = {"ctx": 3 - me}
    slots = Slots()
    pending = []

    def remote(src, dst, slot, device):
        return pltpu.make_async_remote_copy(
            src_ref=src,
            dst_ref=dst,
            send_sem=send.at[slot],
            recv_sem=recv.at[slot],
            device_id=device,
            device_id_type=MESH,
        )

    def at_end(count, make):
        pending.append((count, make))

    local_slots = Slots()

    def fetch(src, dst):
        copy = pltpu.make_async_copy(src, dst, local.at[local_slots.take()])
        copy.start()
        return copy

    kept = []

    def keep(src, dst):
        kept.append(fetch(src, dst))

    three = [fetch(src, own_three.at[i]) for i, src in enumerate((query_own, key_own, value_own))]
    barrier = pltpu.get_barrier_semaphore()
    for device in (to_core, to_x, to_y, to_z, to_zz, to_far):
        pl.semaphore_signal(barrier, inc=1, device_id=device, device_id_type=MESH)
    row = lax.broadcasted_iota(jnp.int32, (1024, 256), 0)
    col = lax.broadcasted_iota(jnp.int32, (1024, 256), 1)
    chosen[...] = jnp.where(row == (col // 64) * 256 + me * 64 + col % 64, 1.0, 0.0).astype(BF16)
    read_lengths(slot_ref, length_ref, lens_ref, (2 * d + y) * 4)
    singles = (vec_query, vec_out, vec_gain, vec_shift, vec_outer, vec_gain2, vec_shift2, vec_value)
    vec_all[y, 0:8] = jnp.concatenate([single[...].astype(F32).reshape(1, 512) for single in singles], 0)
    inner_rows = vec_inner[...].astype(F32).reshape(4, 512)
    vec_all[y, 8:16] = jnp.concatenate((inner_rows, jnp.zeros((4, 512), F32)), 0)
    pl.semaphore_wait(barrier, 6)

    first = slots.take(4)
    state_x = lambda s: remote(states.at[s], st_all.at[2, s], first + s, to_x)
    second = slots.take(4)
    state_core = lambda s: remote(states.at[s], st_all.at[1, s], second + s, to_core)
    third = slots.take(4)
    state_far = lambda s: remote(st_all.at[2, s], st_all.at[3, s], third + s, to_core)
    p = d % 2
    wq_slot = slots.take(2)

    def wq_copy(k):
        here = wq_all.at[pl.ds(pl.multiple_of(y * 512 + p * 256 + k * 128, 128), 128)]
        return remote(here, here, wq_slot + k, to_y)

    wq_pass_slot = slots.take(2)

    def wq_pass(k):
        here = wq_all.at[pl.ds(pl.multiple_of((1 - y) * 512 + p * 256 + k * 128, 128), 128)]
        return remote(here, here, wq_pass_slot + k, to_z)

    vec_slot = slots.take()
    vec_copy = remote(vec_all.at[y], vec_all.at[y], vec_slot, to_y)
    for s in range(4):
        state_x(s).start()
    vec_copy.start()
    for s in range(4):
        state_core(s).start()
    at_end(4, state_x)
    at_end(4, state_core)
    at_end(4, state_far)
    at_end(2, wq_copy)
    at_end(2, wq_pass)
    at_end(1, lambda _: vec_copy)

    wo_slot = slots.take(2)

    def wo_copy(side):
        src = wo_own.at[pl.ds(pl.multiple_of(p * 256 + side * 128 + c * 64, 64), 64)]
        return remote(src, w_out.at[x if side == 0 else 1 - x, 2 * y + p], wo_slot + side, to_y)

    wo_pass_slot = slots.take(2)

    def wo_pass(side):
        here = w_out.at[x if side == 0 else 1 - x, 2 * (1 - y) + p]
        return remote(here, here, wo_pass_slot + side, to_z)

    wi_slot = slots.take(8)

    def wi_copy(b):
        src = wi_own.at[
            pl.ds(pl.multiple_of(x * 256, 256), 256), pl.ds(pl.multiple_of((2 * b + c) * 256, 256), 256)
        ]
        dst = w_in.at[
            pl.ds(pl.multiple_of(y * 512 + x * 256, 256), 256), pl.ds(pl.multiple_of(b * 256, 256), 256)
        ]
        return remote(src, dst, wi_slot + b, to_y)

    wi_pass_slot = slots.take(8)

    def wi_pass(b):
        here = w_in.at[
            pl.ds(pl.multiple_of((1 - y) * 512 + x * 256, 256), 256),
            pl.ds(pl.multiple_of(b * 256, 256), 256),
        ]
        return remote(here, here, wi_pass_slot + b, to_x)

    wu_slot = slots.take(4)

    def wu_copy(k):
        side, half = k // 2, k % 2
        src = wu_own.at[pl.ds(pl.multiple_of((p * 4 + side * 2 + c) * 256 + half * 128, 128), 128)]
        dst = w_ou.at[pl.ds(pl.multiple_of((4 * y + 2 * p + side) * 256 + half * 128, 128), 128)]
        return remote(src, dst, wu_slot + k, to_y)

    wu_pass_slot = slots.take(4)

    def wu_pass(k):
        side, half = k // 2, k % 2
        here = w_ou.at[
            pl.ds(pl.multiple_of((4 * (1 - y) + 2 * p + side) * 256 + half * 128, 128), 128)
        ]
        return remote(here, here, wu_pass_slot + k, to_z)

    for side in range(2):
        wo_copy(side).start()
    for place in range(3):
        three[place].wait()
        made = matmul(own_three[place], chosen[...]).astype(BF16)
        wq_all[pl.ds(pl.multiple_of(y * 512, 512), 512), place * 256 : place * 256 + 256] = made
    for k in range(2):
        wq_copy(k).start()
    for b in range(8):
        wi_copy(b).start()
    for k in range(4):
        wu_copy(k).start()
    for count, make in ((2, wo_copy), (2, wo_pass), (8, wi_copy), (8, wi_pass), (4, wu_copy), (4, wu_pass)):
        at_end(count, make)

    own_early = [
        fetch(states, st_all.at[0]),
    ]
    own_out = []
    for half in range(2):
        for side in range(2):
            src = wo_own.at[pl.ds(pl.multiple_of(half * 256 + side * 128 + c * 64, 64), 64)]
            own_out.append(fetch(src, w_out.at[x if side == 0 else 1 - x, 2 * y + half]))
    own_late = []
    for b in range(8):
        src = wi_own.at[:, pl.ds(pl.multiple_of((2 * b + c) * 256, 256), 256)]
        dst = w_in.at[pl.ds(pl.multiple_of(y * 512, 512), 512), pl.ds(b * 256, 256)]
        own_late.append(fetch(src, dst))
    for half in range(2):
        for side in range(2):
            src = wu_own.at[pl.ds(pl.multiple_of((half * 4 + side * 2 + c) * 256, 256), 256)]
            dst = w_ou.at[pl.ds(pl.multiple_of((4 * y + 2 * half + side) * 256, 256), 256)]
            own_late.append(fetch(src, dst))

    state_x(0).wait_recv()
    state_far(0).start()
    for k in range(2):
        wq_copy(k).wait_recv()
        wq_pass(k).start()
    state_x(1).wait_recv()
    state_far(1).start()
    for copy in own_early:
        copy.wait()
    vec_copy.wait_recv()
    vecs[:, :512] = vec_all[0]
    vecs[:, 512:] = vec_all[1]
    for side in range(2):
        wo_copy(side).wait_recv()
        wo_pass(side).start()
    for k in range(2):
        wq_pass(k).wait_recv()

    att_slot = slots.take(8)

    def att_copy(s, j):
        rows = pl.ds(pl.multiple_of(j * 512 + s * 128, 128), 128)
        return remote(att_far.at[j, s], att.at[rows, 256:512], att_slot + 2 * s + j, to_x)

    at_end(8, lambda k: att_copy(k // 2, k % 2))
    biases = matmul(vecs[0:8, :].astype(BF16), chosen[...])
    q_bias, v_bias = biases[0:1], biases[7:8]

    def key_flags(s):
        pieces = []
        for j in range(4):
            position = lax.broadcasted_iota(jnp.int32, (128, 128), 0)
            place = me + 1 - 2 * c if j == 1 else me
            place = (place + 2) % 4 if j == 2 else place
            place = 3 - me if j == 3 else place
            pieces.append(jnp.where(position + place * 128 < lens_ref[s], 0.0, MASKED))
        return jnp.concatenate(pieces, 0).astype(BF16)

    def pass_inner(b):
        wi_copy(b).wait_recv()
        wi_pass(b).start()

    def attention(s):
        @pl.when(s < 2)
        def _():
            state_x(s + 2).wait_recv()
            state_far(s + 2).start()

        @pl.when((s == 1) | (s == 2))
        def _():
            for k in range(2):
                pass_inner(2 * (s - 1) + k)

        @pl.when(s == 3)
        def _():
            pass_inner(4)

        state_core(s).wait_recv()
        state_far(s).wait_recv()
        rows = st_all[:, s].reshape(512, 1024)
        for place in range(3):
            made = matmul(rows, wq_all[:, place * 256 : place * 256 + 256])
            made = made + q_bias if place == 0 else made
            made = made + v_bias if place == 2 else made
            qkv[:, s, :, place * 256 : place * 256 + 256] = made.astype(BF16).reshape(4, 128, 256)
        bias = key_flags(s)
        lane = lax.broadcasted_iota(jnp.int32, (512, 128), 1)
        one = jnp.ones((512, 128), BF16)
        totals = jnp.zeros((512, 128), F32)
        for pair in range(2):
            base = pair * 128
            query = qkv[:, s, :, base : base + 128].reshape(512, 128)
            key = qkv[:, s, :, 256 + base : 384 + base].reshape(512, 128)
            value = qkv[:, s, :, 512 + base : 640 + base].reshape(512, 128)
            query = (query.astype(F32) * 0.125).astype(BF16)
            mixed = []
            for which in range(2):
                scores = matmul_nt(with_flag(query, one, which), with_flag(key, bias, which))
                top = jnp.max(scores, axis=-1, keepdims=True)
                weight = jnp.exp(scores - top)
                total = jnp.sum(weight, axis=-1, keepdims=True)
                mixed.append(matmul(weight.astype(BF16), value) * (1.0 / total))
                totals = jnp.where(lane == 2 * pair + which, top + jnp.log(total), totals)
            joined = jnp.where(lane < 64, mixed[0], mixed[1]).astype(BF16)
            for j in range(2):
                rows_j = pl.ds(pl.multiple_of(j * 512 + s * 128, 128), 128)
                att[rows_j, base : base + 128] = joined[j * 128 : j * 128 + 128]
                att_far[j, s, :, base : base + 128] = joined[256 + j * 128 : 384 + j * 128]
        for j in range(2):
            att_copy(s, j).start()
        lse[s] = jnp.transpose(totals)[:8]

    repeat(4, attention)
    for src, dst in ((st_all, o_states), (wq_all, o_wq), (vecs, o_vecs), (qkv, o_qkv), (lse, o_lse)):
        keep(src, dst)

    for b in range(5, 7):
        pass_inner(b)
    for copy in own_out:
        copy.wait()
    for side in range(2):
        wo_pass(side).wait_recv()
    for s in range(4):
        for j in range(2):
            att_copy(s, j).wait_recv()
    keep(att, o_att)
    keep(w_out, o_wout)
    out_slot = slots.take(4)

    def out_copy(n):
        return remote(part_far.at[n], part_in.at[n], out_slot + n, to_core)

    at_end(4, out_copy)
    for n in range(4):
        right = w_out[:, :, :, n * 256 : n * 256 + 256].reshape(512, 256)
        part_far[n] = matmul(att[512:], right).astype(BF16)
        out_copy(n).start()
    pass_inner(7)
    for n in range(4):
        right = w_out[:, :, :, n * 256 : n * 256 + 256].reshape(512, 256)
        made = matmul(att[:512], right) + vecs[1:2, n * 256 : n * 256 + 256]
        made = made + st_all[0, :, :, n * 256 : n * 256 + 256].astype(F32).reshape(512, 256)
        out_copy(n).wait_recv()
        first_norm[:, n * 256 : n * 256 + 256] = made + part_in[n].astype(F32)

    low_slot = slots.take(4)

    def low_copy(k):
        src = low2.at[pl.ds(pl.multiple_of(k * 128, 128), 128)]
        dst = low2.at[pl.ds(pl.multiple_of(512 + k * 128, 128), 128)]
        return remote(src, dst, low_slot + k, to_core)

    at_end(4, low_copy)

    def norm_first(k):
        for half in range(2):
            rows = pl.ds(pl.multiple_of(k * 128 + half * 64, 64), 64)
            made, normed, inverse = norm_rows(first_norm[rows, :], vecs[2:3, :], vecs[3:4, :])
            first_norm[rows, :] = normed
            first_inv[rows, :] = jnp.broadcast_to(inverse, (64, 128))
            first_out[rows, :] = made
            low2[rows, :] = made.astype(BF16)
        low_copy(k).start()

    repeat(4, norm_first)

    def pass_outer(k):
        wu_copy(k).wait_recv()
        wu_pass(k).start()

    pass_outer(0)
    for k in range(4):
        low_copy(k).wait_recv()
    for copy in own_late:
        copy.wait()
    for src, dst in ((first_norm, o_norm), (first_inv, o_inv), (low2, o_low)):
        keep(src, dst)

    def unit_block(b):
        @pl.when((b == 2) | (b == 5))
        def _():
            pass_outer(1 + b // 4)

        wi_pass(b).wait_recv()
        here = pl.ds(pl.multiple_of(b * 256, 256), 256)
        spot = pl.ds(pl.multiple_of((b // 4) * 512 + c * 256, 256), 256)
        row = vecs[pl.ds(8 + b % 4, 1), spot]
        for m in range(2):
            hidden = matmul(low2[m * 512 : m * 512 + 512, :], w_in[:, here]) + row
            below = 0.5 * (1.0 + lax.erf(hidden * math.sqrt(0.5)))
            bell = jnp.exp(-0.5 * hidden * hidden) * (1.0 / math.sqrt(2 * math.pi))
            act[m * 512 : m * 512 + 512, here] = (hidden * below).astype(BF16)
            slope[m * 512 : m * 512 + 512, here] = (below + hidden * bell).astype(BF16)

    repeat(8, unit_block)
    for src, dst in ((act, o_act), (slope, o_slope), (w_in, o_win)):
        keep(src, dst)
    mine = pl.ds(pl.multiple_of(y * 1024, 1024), 1024)
    theirs = pl.ds(pl.multiple_of((1 - y) * 1024, 1024), 1024)
    pass_outer(3)

    def outer_own(n):
        here = pl.ds(pl.multiple_of(n * 256, 256), 256)
        for m in range(2):
            acc[m * 512 : m * 512 + 512, here] = matmul(
                act[m * 512 : m * 512 + 512, mine], w_ou[mine, here]
            )

    repeat(4, outer_own)
    for k in range(4):
        wu_pass(k).wait_recv()
    keep(w_ou, o_wou)
    sum_slot = slots.take(4)

    def sum_copy(n):
        return remote(part_far2.at[n], part_in2.at[n], sum_slot + n, to_core)

    at_end(4, sum_copy)

    def outer_far(n):
        here = pl.ds(pl.multiple_of(n * 256, 256), 256)
        made = acc[512:, here] + matmul(act[512:, theirs], w_ou[theirs, here])
        part_far2[n] = made.astype(BF16)
        sum_copy(n).start()

    repeat(4, outer_far)

    def outer_near(n):
        here = pl.ds(pl.multiple_of(n * 256, 256), 256)
        made = acc[:512, here] + matmul(act[:512, theirs], w_ou[theirs, here])
        made = made + first_out[:, here] + vecs[4:5, here]
        sum_copy(n).wait_recv()
        acc[:512, here] = made + part_in2[n].astype(F32)

    repeat(4, outer_near)

    def norm_second(k):
        valid_place = lax.broadcasted_iota(jnp.int32, (128, 1), 0) + me * 128
        valid = jnp.where(valid_place < lens_ref[k], 1.0, 0.0)
        for half in range(2):
            rows = pl.ds(pl.multiple_of(k * 128 + half * 64, 64), 64)
            made, normed, inverse = norm_rows(acc[rows, :], vecs[5:6, :], vecs[6:7, :])
            encoded_out[rows, :] = (made * valid[half * 64 : half * 64 + 64]).astype(BF16)
            acc[rows, :] = normed
            second_inv[rows, :] = jnp.broadcast_to(inverse, (64, 128))

    repeat(4, norm_second)
    keep(acc.at[:512], o_norm2)
    keep(second_inv, o_inv2)
    for copy in kept:
        copy.wait()
    for count, make in pending:
        for k in range(count):
            make(k).wait_send()


def layer_call(arrays):
    any_space = pl.BlockSpec(memory_space=pl.ANY)
    v = pltpu.VMEM
    return pl.pallas_call(
        layer_kernel,
        in_specs=[pl.BlockSpec(memory_space=pltpu.SMEM)] * 2
        + [any_space] * 4
        + [pl.BlockSpec(memory_space=pltpu.VMEM)] * 9
        + [any_space] * 3,
        out_specs=[pl.BlockSpec(memory_space=pltpu.VMEM)] + [any_space] * 16 + [pl.BlockSpec(memory_space=pltpu.SMEM)],
        out_shape=[
            jax.ShapeDtypeStruct(shape, kind)
            for shape, kind in (
                ((512, 1024), BF16),
                ((4, 4, 128, 1024), BF16),
                ((1024, 768), BF16),
                ((2, 4, 64, 1024), BF16),
                ((1024, 2048), BF16),
                ((2048, 1024), BF16),
                ((16, 1024), F32),
                ((4, 4, 128, 768), BF16),
                ((4, 8, 512), F32),
                ((1024, 512), BF16),
                ((512, 1024), F32),
                ((512, 128), F32),
                ((1024, 1024), BF16),
                ((1024, 2048), BF16),
                ((1024, 2048), BF16),
                ((512, 1024), F32),
                ((512, 128), F32),
                ((4,), jnp.int32),
            )
        ],
        scratch_shapes=[
            v((4, 4, 128, 1024), BF16),
            v((1024, 768), BF16),
            v((2, 16, 512), F32),
            v((2, 4, 64, 1024), BF16),
            v((1024, 2048), BF16),
            v((2048, 1024), BF16),
            v((16, 1024), F32),
            v((4, 4, 128, 768), BF16),
            v((4, 8, 512), F32),
            v((1024, 512), BF16),
            v((2, 4, 128, 256), BF16),
            v((4, 512, 256), BF16),
            v((4, 512, 256), BF16),
            v((4, 512, 256), BF16),
            v((4, 512, 256), BF16),
            v((512, 1024), F32),
            v((512, 128), F32),
            v((512, 1024), F32),
            v((1024, 1024), BF16),
            v((1024, 2048), BF16),
            v((1024, 2048), BF16),
            v((1024, 1024), F32),
            v((512, 128), F32),
            v((1024, 256), BF16),
            v((3, 512, 1024), BF16),
            pltpu.SemaphoreType.DMA((80,)),
            pltpu.SemaphoreType.DMA((80,)),
            pltpu.SemaphoreType.DMA((64,)),
        ],
        compiler_params=pltpu.CompilerParams(
            collective_id=0, has_side_effects=True, vmem_limit_bytes=64 * 1024 * 1024 - 65536
        ),
    )(*arrays)


def accumulate(dst, src, lead, rows):
    steps = rows // 32
    total = math.prod(lead) * steps

    def body(index):
        place = []
        rest = index // steps
        for size in reversed(lead):
            place.insert(0, rest % size)
            rest = rest // size
        here = tuple(place) + (pl.ds(pl.multiple_of((index % steps) * 32, 32), 32),)
        dst[here] = add_low(dst[here], src[here])

    repeat(total, body)


def back_kernel(
    lens_ref,
    i_cot,
    i_n2,
    i_i2,
    i_vecs,
    i_w_ou,
    i_act,
    i_slope,
    i_low,
    i_w_in,
    i_n1,
    i_i1,
    i_att,
    i_w_out,
    i_qkv,
    i_lse,
    i_wq,
    i_states,
    grad_out,
    ou_out,
    in_out,
    out_out,
    qkv_out,
    vec_out,
    cot,
    n2,
    i2,
    vecs,
    w_ou,
    act,
    slope,
    low,
    w_in,
    n1,
    i1,
    att,
    w_out,
    qkv,
    lse,
    wq,
    outer2,
    part_in,
    branch2,
    mix_all,
    mix_far,
    g_ou,
    a_ou,
    b_ou,
    z_ou,
    zz_ou,
    az_ou,
    azz_ou,
    ax_ou,
    ay_ou,
    a_in,
    b_in,
    z_in,
    zz_in,
    az_in,
    azz_in,
    ax_in,
    ay_in,
    f_in,
    c_in,
    g_o,
    z_o,
    zz_o,
    x_o,
    y_o,
    g_q,
    y_q,
    z_q,
    zz_q,
    s_q,
    r_q,
    bias_q,
    vb,
    vr,
    send,
    recv,
    local,
):
    d, me, y = lax.axis_index("dp"), lax.axis_index("ctx"), lax.axis_index("fsdp")
    x, c = me // 2, me % 2
    p, q = d % 2, d // 2
    to_core = {"ctx": me + 1 - 2 * c}
    to_x = {"ctx": (me + 2) % 4}
    to_y = {"fsdp": 1 - y}
    to_z = {"dp": d + 1 - 2 * (d % 2)}
    to_zz = {"dp": (d + 2) % 4}
    to_far = {"ctx": 3 - me}
    slots = Slots()
    local_slots = Slots()
    pending = []

    def remotes(count, parts):
        first = slots.take(count)

        def make(k):
            src, dst, device = parts(k)
            return pltpu.make_async_remote_copy(
                src_ref=src,
                dst_ref=dst,
                send_sem=send.at[first + k],
                recv_sem=recv.at[first + k],
                device_id=device,
                device_id_type=MESH,
            )

        pending.append((count, make))
        return make

    def fetch(src, dst):
        copy = pltpu.make_async_copy(src, dst, local.at[local_slots.take()])
        copy.start()
        return copy

    early = [fetch(i_cot, cot), fetch(i_n2, n2), fetch(i_i2, i2), fetch(i_vecs, vecs)]
    barrier = pltpu.get_barrier_semaphore()
    for device in (to_core, to_x, to_y, to_z, to_zz, to_far):
        pl.semaphore_signal(barrier, inc=1, device_id=device, device_id_type=MESH)
    vb[0] = jnp.zeros((24, 1024), F32)
    bias_q[...] = jnp.zeros((8, 768), F32)
    for copy in early:
        copy.wait()
    got_act, got_w_ou = fetch(i_act, act), fetch(i_w_ou, w_ou)
    pl.semaphore_wait(barrier, 6)

    def chunk_of(buffer):
        def parts(k):
            src = buffer.at[pl.ds(pl.multiple_of(k * 128, 128), 128)]
            dst = buffer.at[pl.ds(pl.multiple_of(512 + k * 128, 128), 128)]
            return src, dst, to_core

        return parts

    outer_copy = remotes(4, chunk_of(outer2))
    branch_copy = remotes(4, chunk_of(branch2))

    def count_in(row, values):
        vb[0, row : row + 1, :] += jnp.sum(values, axis=0, keepdims=True)

    def norm_second(k):
        place = lax.broadcasted_iota(jnp.int32, (128, 1), 0) + me * 128
        valid = jnp.where(place < lens_ref[k], 1.0, 0.0)
        for half in range(2):
            rows = pl.ds(pl.multiple_of(k * 128 + half * 64, 64), 64)
            upstream = cot[k, half * 64 : half * 64 + 64].astype(F32) * valid[half * 64 : half * 64 + 64]
            normed = n2[rows, :]
            count_in(0, upstream * normed)
            count_in(1, upstream)
            made = norm_back(upstream, normed, i2[rows, 0:1], vecs[5:6, :])
            n2[rows, :] = made
            made = made.astype(BF16)
            outer2[rows, :] = made
            count_in(2, made.astype(F32))
        outer_copy(k).start()

    repeat(4, norm_second)
    late = [fetch(i_slope, slope), fetch(i_w_in, w_in)]
    got_act.wait()
    for k in range(4):
        outer_copy(k).wait_recv()

    low_ou, top_ou = pl.ds(0, 256), pl.ds(256, 768)
    low_in, top_in = pl.ds(0, 512), pl.ds(512, 1536)

    def ou_first(k, x_first):
        if x_first:
            return g_ou.at[k, 1 - x, :, :, top_ou], a_ou.at[k], to_x
        return g_ou.at[k, :, 1 - y, :, top_ou], a_ou.at[k], to_y

    ou_a_x = remotes(2, lambda k: ou_first(k, True))
    ou_a_y = remotes(2, lambda k: ou_first(k + 2, False))
    ou_b_y = remotes(2, lambda k: (a_ou.at[k, 1 - y], b_ou.at[k], to_y))
    ou_b_x = remotes(2, lambda k: (a_ou.at[k + 2, 1 - x], b_ou.at[k + 2], to_x))
    ou_z = remotes(2, lambda k: (b_ou.at[2 * k + 1 - p], z_ou.at[k], to_z))
    ou_zz = remotes(1, lambda k: (z_ou.at[1 - q], zz_ou, to_zz))
    low_ou_z = remotes(2, lambda k: (g_ou.at[2 * k + 1 - p, :, :, :, low_ou], az_ou.at[k], to_z))
    low_ou_zz = remotes(1, lambda k: (az_ou.at[1 - q], azz_ou, to_zz))
    low_ou_x = remotes(1, lambda k: (azz_ou.at[1 - x], ax_ou, to_x))
    low_ou_y = remotes(1, lambda k: (ax_ou.at[1 - y], ay_ou, to_y))

    def ou_add_a(k):
        if k < 2:
            ou_a_x(k).wait_recv()
            accumulate(a_ou.at[k], g_ou.at[k, x, :, :, top_ou], (2,), 128)
            ou_b_y(k).start()
        else:
            ou_a_y(k - 2).wait_recv()
            accumulate(a_ou.at[k], g_ou.at[k, :, y, :, top_ou], (2,), 128)
            ou_b_x(k - 2).start()

    def ou_add_b(k):
        if k < 2:
            ou_b_y(k).wait_recv()
            accumulate(b_ou.at[k], a_ou.at[k, y], (), 128)
        else:
            ou_b_x(k - 2).wait_recv()
            accumulate(b_ou.at[k], a_ou.at[k, x], (), 128)

    def ou_add_z():
        for k in range(2):
            ou_z(k).wait_recv()
            accumulate(z_ou.at[k], b_ou.at[2 * k + p], (), 128)
        ou_zz(0).start()

    def low_ou_add_z():
        for k in range(2):
            low_ou_z(k).wait_recv()
            accumulate(az_ou.at[k], g_ou.at[2 * k + p, :, :, :, low_ou], (2, 2), 128)
        low_ou_zz(0).start()

    def low_ou_add_zz():
        low_ou_zz(0).wait_recv()
        accumulate(azz_ou, az_ou.at[q], (2, 2), 128)
        low_ou_x(0).start()

    def low_ou_add_x():
        low_ou_x(0).wait_recv()
        accumulate(ax_ou, azz_ou.at[x], (2,), 128)
        low_ou_y(0).start()

    def ou_last():
        ou_zz(0).wait_recv()
        low_ou_y(0).wait_recv()

        def body(i):
            rows = pl.ds(pl.multiple_of(i * 32, 32), 32)
            ou_out[rows, 256:] = z_ou[q, rows, :].astype(F32) + zz_ou[rows, :].astype(F32)
            ou_out[rows, :256] = ax_ou[y, rows, :].astype(F32) + ay_ou[rows, :].astype(F32)

        repeat(4, body)

    in_a = remotes(4, lambda k: (act.at[k, :, :, 1 - y, :, top_in], a_in.at[k], to_y))
    in_b = remotes(4, lambda k: (a_in.at[k, 1 - x], b_in.at[k], to_x))
    in_z = remotes(2, lambda k: (b_in.at[2 * k + 1 - p], z_in.at[k], to_z))
    in_zz = remotes(1, lambda k: (z_in.at[1 - q], zz_in, to_zz))
    in_core = remotes(1, lambda k: (f_in.at[1 - c], c_in, to_core))
    low_in_z = remotes(2, lambda k: (act.at[2 * k + 1 - p, :, :, :, :, low_in], az_in.at[k], to_z))
    low_in_zz = remotes(1, lambda k: (az_in.at[1 - q], azz_in, to_zz))
    low_in_x = remotes(1, lambda k: (azz_in.at[1 - x], ax_in, to_x))
    low_in_y = remotes(1, lambda k: (ax_in.at[:, 1 - y], ay_in, to_y))

    def in_add_a(k):
        in_a(k).wait_recv()
        accumulate(a_in.at[k], act.at[k, :, :, y, :, top_in], (2, 2), 32)
        in_b(k).start()

    def in_add_b(k):
        in_b(k).wait_recv()
        accumulate(b_in.at[k], a_in.at[k, x], (2,), 32)

    def in_add_z():
        for k in range(2):
            in_z(k).wait_recv()
            accumulate(z_in.at[k], b_in.at[2 * k + p], (2,), 32)
        in_zz(0).start()

    def low_in_add_z():
        for k in range(2):
            low_in_z(k).wait_recv()
            accumulate(az_in.at[k], act.at[2 * k + p, :, :, :, :, low_in], (2, 2, 2), 32)
        low_in_zz(0).start()

    def low_in_add_zz():
        low_in_zz(0).wait_recv()
        accumulate(azz_in, az_in.at[q], (2, 2, 2), 32)
        low_in_x(0).start()

    def low_in_add_x():
        low_in_x(0).wait_recv()
        accumulate(ax_in, azz_in.at[x], (2, 2), 32)
        low_in_y(0).start()

    def in_sum():
        in_zz(0).wait_recv()
        low_in_y(0).wait_recv()
        for k in range(2):
            f_in[k, :, 512:] = z_in[q, k].astype(F32) + zz_in[k].astype(F32)
            f_in[k, :, :512] = ax_in[k, y].astype(F32) + ay_in[k].astype(F32)
        in_core(0).start()

    def in_last():
        def place(b, own):
            return pl.ds(pl.multiple_of((2 * b + (c if own else 1 - c)) * 256, 256), 256)

        for b in range(8):
            in_out[:, place(b, True)] = f_in[c, :, b * 256 : b * 256 + 256]
        in_core(0).wait_recv()
        for b in range(8):
            in_out[:, place(b, False)] = c_in[:, b * 256 : b * 256 + 256]

    o_z = remotes(1, lambda k: (g_o.at[:, :, 1 - p], z_o, to_z))
    o_zz = remotes(1, lambda k: (z_o.at[:, 1 - q], zz_o, to_zz))
    o_x = remotes(1, lambda k: (zz_o.at[1], x_o, to_x))
    o_y = remotes(1, lambda k: (x_o.at[1 - y], y_o, to_y))

    def o_add_z():
        o_z(0).wait_recv()
        accumulate(z_o, g_o.at[:, :, p], (2, 2, 2), 32)
        o_zz(0).start()

    def o_add_zz():
        o_zz(0).wait_recv()
        accumulate(zz_o, z_o.at[:, q], (2, 2), 32)
        o_x(0).start()

    def o_add_x():
        o_x(0).wait_recv()
        accumulate(x_o, zz_o.at[0], (2,), 32)
        o_y(0).start()

    def o_last():
        o_y(0).wait_recv()
        out_out[...] = x_o[y].astype(F32) + y_o[...].astype(F32)

    q_y = remotes(4, lambda k: (g_q.at[k, :, 1 - y], y_q.at[k], to_y))
    q_z = remotes(2, lambda k: (y_q.at[2 * k + 1 - p], z_q.at[k], to_z))
    q_zz = remotes(1, lambda k: (z_q.at[1 - q], zz_q, to_zz))
    others = ((me + 1 - 2 * c, to_core), ((me + 2) % 4, to_x), (3 - me, to_far))
    q_all = [
        remotes(1, lambda k, j=j: (s_q.at[others[j][0]], r_q.at[j], others[j][1])) for j in range(3)
    ]

    def q_add_y(k):
        q_y(k).wait_recv()
        accumulate(y_q.at[k], g_q.at[k, :, y], (4,), 32)

    def q_add_z():
        for k in range(2):
            q_z(k).wait_recv()
            accumulate(z_q.at[k], y_q.at[2 * k + p], (4,), 32)
        q_zz(0).start()

    def q_sum():
        q_zz(0).wait_recv()
        for k in range(4):
            s_q[k] = z_q[q, k].astype(F32) + zz_q[k].astype(F32)
        for j in range(3):
            q_all[j](0).start()

    def q_last():
        qkv_out[me] = s_q[me]
        for j in range(3):
            q_all[j](0).wait_recv()
            qkv_out[others[j][0]] = r_q[j]

    v_core = remotes(1, lambda k: (vb.at[0, pl.ds(0, 8)], vr.at[0, pl.ds(0, 8)], to_core))
    v_x = remotes(1, lambda k: (vb.at[1, pl.ds(0, 16)], vr.at[1, pl.ds(0, 16)], to_x))
    v_y = remotes(1, lambda k: (vb.at[2], vr.at[2], to_y))
    v_z = remotes(1, lambda k: (vb.at[3], vr.at[3], to_z))
    v_zz = remotes(1, lambda k: (vb.at[4], vr.at[4], to_zz))

    def outer_grad(i):
        k = (i % 2) * 2 + i // 2
        for half in range(2):
            spot = pl.ds(pl.multiple_of((2 * k + half) * 256, 256), 256)
            left = act[:, :, :, :, :, spot].reshape(1024, 256)
            made = matmul_tn(left, outer2[...])
            g_ou[k, half] = made.astype(BF16).reshape(2, 128, 1024)

        @pl.when(i % 2 == 0)
        def _():
            ou_a_x(k).start()

        @pl.when(i % 2 == 1)
        def _():
            ou_a_y(k - 2).start()

        @pl.when(i >= 2)
        def _():
            low_ou_z(i - 2).start()

    repeat(4, outer_grad)
    got_w_ou.wait()
    for copy in late:
        copy.wait()
    late = [fetch(i_n1, n1), fetch(i_i1, i1), fetch(i_low, low), fetch(i_att, att), fetch(i_w_out, w_out)]
    late += [fetch(i_qkv, qkv), fetch(i_lse, lse), fetch(i_wq, wq)]

    def hidden_grad(b):
        here = pl.ds(pl.multiple_of(b * 256, 256), 256)
        total = jnp.zeros((1, 256), F32)
        for m in range(2):
            made = matmul_nt(outer2[m * 512 : m * 512 + 512, :], w_ou[here, :])
            made = (made * slope[m * 512 : m * 512 + 512, here].astype(F32)).astype(BF16)
            slope[m * 512 : m * 512 + 512, here] = made
            total = total + jnp.sum(made.astype(F32), axis=0, keepdims=True)
        vb[0, pl.ds(8 + b, 1), 0:256] = total

    repeat(8, hidden_grad)

    def part_copy_parts(n):
        spot = pl.ds(pl.multiple_of(n * 256, 256), 256)
        return w_ou.at[pl.ds(1536, 512), spot], part_in.at[n], to_core

    part_copy = remotes(4, part_copy_parts)

    def first_far(n):
        here = pl.ds(pl.multiple_of(n * 256, 256), 256)
        w_ou[1536:2048, here] = matmul_nt(slope[512:, :], w_in[here, :]).astype(BF16)
        part_copy(n).start()

    repeat(4, first_far)
    ou_add_a(0)
    ou_add_a(2)
    low_ou_add_z()

    def first_near(n):
        here = pl.ds(pl.multiple_of(n * 256, 256), 256)
        made = n2[:, here] + matmul_nt(slope[:512, :], w_in[here, :])
        part_copy(n).wait_recv()
        n2[:, here] = made + part_in[n].astype(F32)

    repeat(4, first_near)
    for copy in late:
        copy.wait()

    def norm_first(k):
        for half in range(2):
            rows = pl.ds(pl.multiple_of(k * 128 + half * 64, 64), 64)
            upstream = n2[rows, :]
            normed = n1[rows, :]
            count_in(3, upstream * normed)
            count_in(4, upstream)
            made = norm_back(upstream, normed, i1[rows, 0:1], vecs[2:3, :])
            n2[rows, :] = made
            made = made.astype(BF16)
            branch2[rows, :] = made
            count_in(5, made.astype(F32))
        branch_copy(k).start()

    repeat(4, norm_first)
    v_core(0).start()
    ou_add_a(1)
    ou_add_a(3)
    for k in range(4):
        branch_copy(k).wait_recv()

    mix_copy = remotes(4, lambda s: (mix_far.at[:, s], mix_all.at[pl.ds(2, 2), s], to_x))
    mix_far[...] = matmul_nt(branch2[...], w_out[1].reshape(256, 1024)).astype(BF16).reshape(2, 4, 128, 256)
    for s in range(4):
        mix_copy(s).start()
    mix_all[0:2] = matmul_nt(branch2[...], w_out[0].reshape(256, 1024)).astype(BF16).reshape(2, 4, 128, 256)

    for half in range(2):
        made = matmul_tn(att[:, half * 256 : half * 256 + 256], branch2[...])
        g_o[half] = made.astype(BF16).reshape(2, 2, 2, 32, 1024)
    o_z(0).start()
    v_core(0).wait_recv()
    vb[1, 0:8] = vb[0, 0:8] + vr[0, 0:8]
    vb[1, 8:16] = vb[0, 8:16]
    v_x(0).start()

    def inner_grad(k):
        left = low[:, pl.ds(pl.multiple_of(k * 256, 256), 256)]
        for half in range(4):
            made = matmul_tn(left, slope[:, half * 512 : half * 512 + 512]).astype(BF16)
            act[k, :, :, :, :, half * 512 : half * 512 + 512] = made.reshape(2, 2, 2, 32, 512)

        in_a(k).start()

        @pl.when(k % 2 == 1)
        def _():
            low_in_z(k // 2).start()

    repeat(4, inner_grad)
    got_states = []
    for j in range(4):
        for s in range(4):
            rows = pl.ds((j // 2) * 512 + s * 128, 128)
            got_states.append(fetch(i_states.at[j, s], slope.at[rows, pl.ds((j % 2) * 1024, 1024)]))

    def key_flags(s):
        pieces = []
        for j in range(4):
            position = lax.broadcasted_iota(jnp.int32, (128, 128), 0)
            place = me + 1 - 2 * c if j == 1 else me
            place = (place + 2) % 4 if j == 2 else place
            place = 3 - me if j == 3 else place
            pieces.append(jnp.where(position + place * 128 < lens_ref[s], 0.0, MASKED))
        return jnp.concatenate(pieces, 0).astype(BF16)

    def piece_copy_parts(k):
        rows = pl.ds(pl.multiple_of((k % 2) * 512 + (k // 2) * 128, 128), 128)
        return w_ou.at[rows], w_in.at[rows, pl.ds(0, 1024)], to_core

    piece_copy = remotes(8, piece_copy_parts)

    def pass_copy_parts(s):
        src = w_ou.at[pl.ds(pl.multiple_of(1024 + s * 128, 128), 128)]
        dst = w_in.at[pl.ds(pl.multiple_of(s * 128, 128), 128), pl.ds(1024, 1024)]
        return src, dst, to_x

    pass_copy = remotes(4, pass_copy_parts)

    def far_pieces(s):
        for which in range(2):
            rows = pl.ds(pl.multiple_of(512 * which + s * 128, 128), 128)
            w_ou[rows, :] = matmul_nt(qkv[1 + 2 * which, s], wq[...]).astype(BF16)
        for which in range(2):
            piece_copy(2 * s + which).start()

    def passed(s):
        made = matmul_nt(qkv[2, s], wq[...])
        piece_copy(2 * s + 1).wait_recv()
        rows = pl.ds(pl.multiple_of(512 + s * 128, 128), 128)
        made = made + w_in[rows, 0:1024].astype(F32)
        w_ou[pl.ds(pl.multiple_of(1024 + s * 128, 128), 128), :] = made.astype(BF16)
        pass_copy(s).start()

    hooks = {
        0: [lambda: ou_add_b(0), lambda: ou_add_b(2), low_ou_add_zz],
        1: [lambda: ou_add_b(1), lambda: ou_add_b(3), lambda: ou_z(0).start(), lambda: ou_z(1).start(), o_add_z],
        2: [lambda: in_add_a(0)],
        3: [lambda: in_add_a(1)],
    }

    def attention(s):
        for step, actions in hooks.items():

            @pl.when(s == step)
            def _():
                for action in actions:
                    action()

        mix_copy(s).wait_recv()
        bias = key_flags(s)
        lane = lax.broadcasted_iota(jnp.int32, (512, 128), 1)
        one = jnp.ones((512, 128), BF16)
        for pair in range(2):
            base = pair * 128
            query = qkv[:, s, :, base : base + 128].reshape(512, 128)
            key = qkv[:, s, :, 256 + base : 384 + base].reshape(512, 128)
            value = qkv[:, s, :, 512 + base : 640 + base].reshape(512, 128)
            grad = mix_all[:, s, :, base : base + 128].reshape(512, 128)
            query = (query.astype(F32) * 0.125).astype(BF16)
            query_parts, key_parts, value_parts = [], [], []
            for which in range(2):
                spot = 2 * pair + which
                log_total = lse[s, spot : spot + 1, :]
                scores = matmul_nt(with_flag(key, bias, which), with_flag(query, one, which))
                probs = jnp.exp(scores - log_total)
                probs_grad = matmul_nt(value, half_lanes(grad, which))
                value_parts.append(matmul(probs.astype(BF16), grad))
                row_dot = jnp.sum(probs * probs_grad, axis=0, keepdims=True)
                score_grad = (probs * (probs_grad - row_dot)).astype(BF16)
                key_parts.append(matmul(score_grad, query))
                query_parts.append(matmul_tn(score_grad, key) * 0.125)
            for place, parts in enumerate((query_parts, key_parts, value_parts)):
                joined = jnp.where(lane < 64, parts[0], parts[1]).astype(BF16)
                start = place * 256 + base
                qkv[:, s, :, start : start + 128] = joined.reshape(4, 128, 128)
                bias_q[0:1, start : start + 128] += jnp.sum(joined.astype(F32), axis=0, keepdims=True)
        far_pieces(s)

        @pl.when(s > 0)
        def _():
            passed(s - 1)

    repeat(4, attention)
    passed(3)

    v_x(0).wait_recv()
    vb[2, 0:16] = vb[1, 0:16] + vr[1, 0:16]
    vb[2, 16:24] = jnp.concatenate((bias_q[...], jnp.zeros((8, 256), F32)), 1)
    v_y(0).start()
    for copy in got_states:
        copy.wait()

    def projection_grad(k):
        made = jnp.zeros((256, 768), F32)
        for j in range(4):
            spot = pl.ds(pl.multiple_of((j % 2) * 1024 + k * 256, 256), 256)
            left = slope[(j // 2) * 512 : (j // 2) * 512 + 512, spot]
            made = made + matmul_tn(left, qkv[j].reshape(512, 768))
        g_q[k] = made.astype(BF16).reshape(4, 2, 32, 768)
        q_y(k).start()

    repeat(4, projection_grad)
    in_add_a(2)
    low_in_add_z()
    ou_add_z()
    v_y(0).wait_recv()
    vb[3] = vb[2] + vr[2]
    v_z(0).start()
    o_add_zz()
    in_add_a(3)
    for k in range(2):
        in_add_b(k)
    in_z(0).start()

    def near_piece(s):
        rows = pl.ds(pl.multiple_of(s * 128, 128), 128)
        made = n2[rows, :] + matmul_nt(qkv[0, s], wq[...])
        piece_copy(2 * s).wait_recv()
        n2[rows, :] = made + w_in[rows, 0:1024].astype(F32)

    repeat(4, near_piece)
    low_ou_add_x()
    for k in range(2):
        q_add_y(k)
    q_z(0).start()
    low_in_add_zz()
    for k in range(2, 4):
        q_add_y(k)
    q_z(1).start()
    v_z(0).wait_recv()
    vb[4] = vb[3] + vr[3]
    v_zz(0).start()
    for k in range(2, 4):
        in_add_b(k)
    in_z(1).start()
    q_add_z()
    o_add_x()
    low_in_add_x()
    in_add_z()

    def last_piece(s):
        rows = pl.ds(pl.multiple_of(s * 128, 128), 128)
        pass_copy(s).wait_recv()
        grad_out[rows, :] = (n2[rows, :] + w_in[rows, 1024:2048].astype(F32)).astype(BF16)

    repeat(4, last_piece)
    ou_last()
    o_last()
    v_zz(0).wait_recv()
    vec_out[...] = vb[4] + vr[4]
    q_sum()
    in_sum()
    q_last()
    in_last()
    for count, make in pending:
        for k in range(count):
            make(k).wait_send()


def back_call(arrays):
    any_space = pl.BlockSpec(memory_space=pl.ANY)
    outs = (
        ((512, 1024), BF16),
        ((128, 1024), F32),
        ((32, 4096), F32),
        ((32, 1024), F32),
        ((4, 32, 768), F32),
        ((24, 1024), F32),
    )
    scratch = (
        ((4, 128, 1024), BF16),
        ((512, 1024), F32),
        ((512, 128), F32),
        ((16, 1024), F32),
        ((2048, 1024), BF16),
        ((4, 2, 2, 2, 32, 2048), BF16),
        ((1024, 2048), BF16),
        ((1024, 1024), BF16),
        ((1024, 2048), BF16),
        ((512, 1024), F32),
        ((512, 128), F32),
        ((1024, 512), BF16),
        ((2, 4, 64, 1024), BF16),
        ((4, 4, 128, 768), BF16),
        ((4, 8, 512), F32),
        ((1024, 768), BF16),
        ((1024, 1024), BF16),
        ((4, 512, 256), BF16),
        ((1024, 1024), BF16),
        ((4, 4, 128, 256), BF16),
        ((2, 4, 128, 256), BF16),
        ((4, 2, 2, 128, 1024), BF16),
        ((4, 2, 128, 768), BF16),
        ((4, 128, 768), BF16),
        ((2, 128, 768), BF16),
        ((128, 768), BF16),
        ((2, 2, 2, 128, 256), BF16),
        ((2, 2, 128, 256), BF16),
        ((2, 128, 256), BF16),
        ((128, 256), BF16),
        ((4, 2, 2, 32, 1536), BF16),
        ((4, 2, 32, 1536), BF16),
        ((2, 2, 32, 1536), BF16),
        ((2, 32, 1536), BF16),
        ((2, 2, 2, 2, 32, 512), BF16),
        ((2, 2, 2, 32, 512), BF16),
        ((2, 2, 32, 512), BF16),
        ((2, 32, 512), BF16),
        ((2, 32, 2048), F32),
        ((32, 2048), F32),
        ((2, 2, 2, 2, 32, 1024), BF16),
        ((2, 2, 2, 32, 1024), BF16),
        ((2, 2, 32, 1024), BF16),
        ((2, 32, 1024), BF16),
        ((32, 1024), BF16),
        ((4, 4, 2, 32, 768), BF16),
        ((4, 4, 32, 768), BF16),
        ((2, 4, 32, 768), BF16),
        ((4, 32, 768), BF16),
        ((4, 32, 768), F32),
        ((3, 32, 768), F32),
        ((8, 768), F32),
        ((5, 24, 1024), F32),
        ((5, 24, 1024), F32),
    )
    return pl.pallas_call(
        back_kernel,
        in_specs=[pl.BlockSpec(memory_space=pltpu.SMEM)] + [any_space] * 17,
        out_specs=[pl.BlockSpec(memory_space=pltpu.VMEM)] * len(outs),
        out_shape=[jax.ShapeDtypeStruct(shape, kind) for shape, kind in outs],
        scratch_shapes=[pltpu.VMEM(shape, kind) for shape, kind in scratch]
        + [
            pltpu.SemaphoreType.DMA((96,)),
            pltpu.SemaphoreType.DMA((96,)),
            pltpu.SemaphoreType.DMA((48,)),
        ],
        compiler_params=pltpu.CompilerParams(
            collective_id=1, has_side_effects=True, vmem_limit_bytes=64 * 1024 * 1024 - 65536
        ),
    )(*arrays)


def finish_kernel(sums_ref, qkv_ref, *refs):
    count = 5
    sources, targets = refs[:count], refs[count : 2 * count]
    rows_out, inner_out, query_out, value_out = refs[2 * count : 2 * count + 6], *refs[2 * count + 6 : 2 * count + 9]
    projections = refs[2 * count + 9 : 2 * count + 12]
    stages, sems = refs[2 * count + 12 : 3 * count + 12], refs[3 * count + 12]
    d, me, y = lax.axis_index("dp"), lax.axis_index("ctx"), lax.axis_index("fsdp")
    copies_in = [pltpu.make_async_copy(sources[i], stages[i], sems.at[i]) for i in range(count)]
    copies_out = [pltpu.make_async_copy(stages[i], targets[i], sems.at[count + i]) for i in range(count)]
    for copy in copies_in:
        copy.start()

    def from_lane(values, lane):
        return pltpu.roll(values, (1024 - lane) % 1024, 1)

    own = from_lane(sums_ref[0:8, :], ((d * 4 + me) * 2 + y) * 32)
    for i in range(6):
        rows_out[i][...] = own[i, 0:32]
    row = lax.broadcasted_iota(jnp.int32, (8, 256), 0)
    inner = jnp.sum(jnp.where(row == 2 * d + me // 2, sums_ref[8:16, 0:256], 0.0), axis=0, keepdims=True)
    inner_out[...] = jnp.where(y == 0, inner[:, 0:128], inner[:, 128:256])[0]
    for start, out in ((0, query_out), (512, value_out)):
        out[...] = from_lane(sums_ref[16:24, :], start + d * 64 + y * 32)[0, 0:32]
    for place, out in enumerate(projections):
        for g in range(4):
            start = place * 256 + g * 64
            parts = [qkv_ref[i, :, start : start + 64] for i in range(4)]
            out[:, g * 256 : g * 256 + 256] = jnp.concatenate(parts, 1)
    for i in range(count):
        copies_in[i].wait()
        copies_out[i].start()
    for copy in copies_out:
        copy.wait()


def finish_call(sums, qkv_sum, arrays):
    any_space = pl.BlockSpec(memory_space=pl.ANY)
    vmem = pl.BlockSpec(memory_space=pltpu.VMEM)
    short = jax.ShapeDtypeStruct((32,), F32)
    return pl.pallas_call(
        finish_kernel,
        in_specs=[vmem] * 2 + [any_space] * 5,
        out_specs=[any_space] * 5 + [vmem] * 12,
        out_shape=[jax.ShapeDtypeStruct(a.shape, a.dtype) for a in arrays]
        + [short] * 6
        + [jax.ShapeDtypeStruct((128,), F32), short, short]
        + [jax.ShapeDtypeStruct((32, 1024), F32)] * 3,
        scratch_shapes=[pltpu.VMEM(a.shape, a.dtype) for a in arrays] + [pltpu.SemaphoreType.DMA((16,))],
    )(sums, qkv_sum, *arrays)


def shards(
    states,
    cotangent,
    lengths,
    slot_source,
    query_weight,
    query_bias,
    key_weight,
    value_weight,
    value_bias,
    output_weight,
    output_bias,
    first_gain,
    first_shift,
    inner_weight,
    inner_bias,
    outer_weight,
    outer_bias,
    final_gain,
    final_shift,
):
    seq_dev, block_len, width = states.shape
    n_dp, n_ctx, n_fsdp = (lax.axis_size(name) for name in OWNERS)
    assert (n_ctx, n_fsdp) == (4, 2)
    head_size = width // HEADS
    units = inner_weight.shape[1]
    tokens = seq_dev * block_len
    d, me, y = (lax.axis_index(name) for name in OWNERS)
    x, c = me // 2, me % 2
    own_heads = HEADS // n_ctx
    cols = own_heads * head_size
    aligned = n_dp == own_heads

    def other_half(local):
        return swap(local, "fsdp", 1)

    def ordered(own, other, axis=0):
        return jnp.where(
            y == 0, jnp.concatenate((own, other), axis), jnp.concatenate((other, own), axis)
        )

    def gathered(local, axis=0):
        return ordered(local, other_half(local), axis)

    def head_cols(matrix):
        parts = matrix.reshape(matrix.shape[:-1] + (own_heads, n_ctx, head_size))
        return pick(parts, me, parts.ndim - 2).reshape(matrix.shape[:-1] + (cols,))

    my_seqs = (d * n_fsdp + y) * seq_dev + jnp.arange(seq_dev, dtype=jnp.int32)
    seq_len = jnp.sum(jnp.where(slot_source[None, :] == my_seqs[:, None], lengths[None, :], 0), axis=1)
    places = (me ^ jnp.arange(n_ctx, dtype=jnp.int32))[:, None] * block_len + jnp.arange(
        block_len, dtype=jnp.int32
    )
    key_ok = places.reshape(1, -1) < seq_len[:, None]
    key_bias = jnp.where(key_ok, 0.0, MASKED).astype(BF16)
    key_bias = jnp.broadcast_to(key_bias[:, :, None], key_bias.shape + (128,))
    valid_rows = (places[0][None, :] < seq_len[:, None]).astype(F32).reshape(-1, 1)
    full_len = n_ctx * block_len
    score_flops = 2 * seq_dev * own_heads * full_len * full_len * 128
    block = units // (4 * n_dp)
    wq_own = jnp.concatenate((head_cols(query_weight), head_cols(key_weight), head_cols(value_weight)), 1)

    def share(own):
        return jnp.concatenate((own, swap(own, "ctx", 1)), axis=0)

    def collect(both_rows):
        return both_rows[:tokens] + swap(both_rows[tokens:].astype(BF16), "ctx", 1).astype(F32)

    if aligned:
        (
            encoded,
            flat_all,
            w_qkv,
            w_out,
            w_inner,
            w_outer,
            vecs,
            qkv,
            log_total,
            attended,
            first_norm,
            first_inverse,
            first_low,
            activated,
            slope,
            second_norm,
            second_inverse,
            own_lengths,
        ) = layer_call(
            (
                lengths,
                slot_source,
                states,
                query_weight,
                key_weight,
                value_weight,
                query_bias,
                output_bias,
                first_gain,
                first_shift,
                outer_bias,
                final_gain,
                final_shift,
                value_bias,
                inner_bias,
                output_weight,
                inner_weight,
                outer_weight,
            )
        )
        input_grad, outer_weight_own, inner_weight_own, output_weight_own, qkv_sum, sums = back_call(
            (
                own_lengths,
                cotangent,
                second_norm,
                second_inverse,
                vecs,
                w_outer,
                activated.reshape(4, 2, 2, 2, 32, units // 2),
                slope,
                first_low,
                w_inner,
                first_norm,
                first_inverse,
                attended,
                w_out,
                qkv,
                log_total,
                w_qkv,
                flat_all,
            )
        )
        finished = finish_call(
            sums, qkv_sum, (encoded, input_grad, outer_weight_own, inner_weight_own, output_weight_own)
        )
        encoded, input_grad, outer_weight_own, inner_weight_own, output_weight_own = finished[:5]
        final_gain_own, final_shift_own, outer_bias_own, first_gain_own, first_shift_own, output_bias_own = finished[5:11]
        inner_bias_own, query_bias_own, value_bias_own, query_own, key_own, value_own = finished[11:]
        return (
            encoded.reshape(states.shape),
            input_grad.reshape(states.shape),
            query_own,
            query_bias_own,
            key_own,
            value_own,
            value_bias_own,
            output_weight_own,
            output_bias_own,
            first_gain_own,
            first_shift_own,
            inner_weight_own,
            inner_bias_own,
            outer_weight_own,
            outer_bias_own,
            final_gain_own,
            final_shift_own,
        )

    def other_half(local):
        return swap(local, "fsdp", 1)

    def ordered(own, other, axis=0):
        return jnp.where(
            y == 0, jnp.concatenate((own, other), axis), jnp.concatenate((other, own), axis)
        )

    def gathered(local, axis=0):
        return ordered(local, other_half(local), axis)

    wide = (query_bias, value_bias, output_bias, first_gain, first_shift, outer_bias, final_gain, final_shift)
    packed = jnp.concatenate([v.reshape(1, -1) for v in wide] + [inner_bias.reshape(-1, width // 2)])
    other_packed = other_half(packed)
    both = jnp.where(y == 0, jnp.stack((packed, other_packed)), jnp.stack((other_packed, packed)))
    b_query, b_value, b_out, g_first, s_first, b_outer, g_final, s_final = (
        both[:, i].reshape(width).astype(F32) for i in range(8)
    )
    b_inner = both[:, 8:].reshape(2 * n_dp, 2, -1)
    b_inner = pick(b_inner, c, 1).reshape(-1).astype(F32)
    w_qkv = gathered(wq_own)
    b_qkv = jnp.concatenate((head_cols(b_query), jnp.zeros((cols,), F32), head_cols(b_value)))

    from_x = swap(states, "ctx", 2)
    from_core = swap(states, "ctx", 1)
    from_far = swap(from_x, "ctx", 1)
    flat_all = jnp.stack((states, from_core, from_x, from_far)).reshape(-1, width)

    w_out = gathered(pick(output_weight.reshape(-1, 2, 2, head_size, width), c, 2))
    w_out = jnp.concatenate((pick(w_out, x, 1), pick(w_out, 1 - x, 1)), 0).reshape(-1, width)
    w_inner = gathered(
        pick(inner_weight.reshape(width // 2, 2 * n_dp, 2, block), c, 2).reshape(width // 2, -1)
    )
    w_outer = gathered(pick(outer_weight.reshape(n_dp, 2, block, width), c, 1).reshape(-1, width))

    qkv = (matmul(flat_all, w_qkv) + b_qkv).astype(BF16)
    qkv = qkv.reshape(n_ctx, seq_dev, block_len, 3 * cols)
    attended_all, log_total = attention_call(
        attend_kernel,
        (qkv, key_bias),
        (
            jax.ShapeDtypeStruct((n_ctx, seq_dev, block_len, cols), BF16),
            jax.ShapeDtypeStruct((seq_dev, 8, full_len), F32),
        ),
        2 * score_flops,
    )
    near = attended_all[:2].reshape(-1, cols)
    far = swap(attended_all[2:], "ctx", 2).reshape(-1, cols)
    attended = jnp.concatenate((near, far), axis=1)
    first_sum = states.reshape(-1, width).astype(F32) + collect(matmul(attended, w_out)) + b_out
    first_out, first_norm, first_inverse = norm_rows(first_sum, g_first, s_first)
    first_low = share(first_out.astype(BF16))
    hidden = matmul(first_low, w_inner) + b_inner
    below = 0.5 * (1.0 + lax.erf(hidden * math.sqrt(0.5)))
    bell = jnp.exp(-0.5 * hidden * hidden) * (1.0 / math.sqrt(2 * math.pi))
    slope = (below + hidden * bell).astype(BF16)
    activated = (hidden * below).astype(BF16)
    second_sum = first_out + collect(matmul(activated, w_outer)) + b_outer
    second_out, second_norm, second_inverse = norm_rows(second_sum, g_final, s_final)
    encoded = (second_out * valid_rows).astype(BF16).reshape(states.shape)

    out_grad = cotangent.reshape(-1, width).astype(F32) * valid_rows
    final_gain_part = jnp.sum(out_grad * second_norm, axis=0)
    final_shift_part = jnp.sum(out_grad, axis=0)
    second_grad = norm_back(out_grad, second_norm, second_inverse, g_final)
    outer_round_own = second_grad.astype(BF16)
    outer_bias_part = col_sum(outer_round_own)
    outer_round = share(outer_round_own)
    outer_weight_part = matmul_tn(activated, outer_round).astype(BF16)
    hidden_grad = (matmul_nt(outer_round, w_outer) * slope.astype(F32)).astype(BF16)
    inner_bias_part = col_sum(hidden_grad)
    inner_weight_part = matmul_tn(first_low, hidden_grad).astype(BF16)
    first_grad = second_grad + collect(matmul_nt(hidden_grad, w_inner))
    first_gain_part = jnp.sum(first_grad * first_norm, axis=0)
    first_shift_part = jnp.sum(first_grad, axis=0)
    sum_grad = norm_back(first_grad, first_norm, first_inverse, g_first)
    branch_own = sum_grad.astype(BF16)
    output_bias_part = col_sum(branch_own)
    branch_grad = share(branch_own)
    output_weight_part = matmul_tn(attended, branch_grad).astype(BF16)
    attended_grad = matmul_nt(branch_grad, w_out).astype(BF16)
    near_grad = attended_grad[:, :cols]
    far_grad = swap(attended_grad[:, cols:], "ctx", 2)
    attended_grad_all = jnp.concatenate((near_grad, far_grad), 0).reshape(n_ctx, seq_dev, block_len, cols)
    (qkv_grad,) = attention_call(
        attend_back_kernel,
        (qkv, key_bias, log_total, attended_grad_all),
        (jax.ShapeDtypeStruct(qkv.shape, BF16),),
        5 * score_flops,
    )
    flat_grad = qkv_grad.reshape(-1, 3 * cols)
    bias_part = col_sum(flat_grad)
    qkv_weight_part = matmul_tn(flat_all, flat_grad).astype(BF16)
    input_part = matmul_nt(flat_grad, w_qkv).reshape(n_ctx, tokens, width)
    to_core = swap(jnp.stack((input_part[1], input_part[3])).astype(BF16), "ctx", 1)
    to_x = swap((input_part[2] + to_core[1].astype(F32)).astype(BF16), "ctx", 2)
    input_grad = sum_grad + input_part[0] + to_core[0].astype(F32) + to_x.astype(F32)
    input_grad = input_grad.astype(BF16).reshape(states.shape)

    token_sums = jnp.stack(
        (final_gain_part, final_shift_part, outer_bias_part, first_gain_part, first_shift_part, output_bias_part)
    )
    def placed_heads(part):
        whole = jnp.zeros(part.shape[:-1] + (own_heads, n_ctx, head_size), part.dtype)
        part = part.reshape(part.shape[:-1] + (own_heads, 1, head_size))
        return lax.dynamic_update_slice_in_dim(whole, part, me, part.ndim - 2).reshape(
            part.shape[:-3] + (width,)
        )

    def placed_units(part, axis):
        split = part.shape[:axis] + (2 * n_dp, 1, block) + part.shape[axis + 1 :]
        whole = jnp.zeros(split[: axis + 1] + (2,) + split[axis + 2 :], part.dtype)
        whole = lax.dynamic_update_slice_in_dim(whole, part.reshape(split), c, axis + 1)
        return whole.reshape(part.shape[:axis] + (units,) + part.shape[axis + 1 :])

    def placed_rows(part):
        part = part.reshape(2, own_heads, 1, 1, head_size, width)
        whole = jnp.zeros((own_heads, 2, 2, head_size, width), part.dtype)
        whole = lax.dynamic_update_slice(whole, part[0], (0, x, c, 0, 0))
        whole = lax.dynamic_update_slice(whole, part[1], (0, 1 - x, c, 0, 0))
        return whole.reshape(width, width)

    def owned(part):
        return lax.psum_scatter(part, OWNERS, scatter_dimension=0, tiled=True).astype(F32)

    qkv_weights = [owned(placed_heads(qkv_weight_part[:, i * cols : (i + 1) * cols])) for i in range(3)]
    query_bias_own = owned(placed_heads(bias_part[:cols]))
    value_bias_own = owned(placed_heads(bias_part[2 * cols :]))
    output_weight_own = owned(placed_rows(output_weight_part))
    inner_weight_own = owned(placed_units(inner_weight_part, 1))
    inner_bias_own = owned(placed_units(inner_bias_part, 0))
    outer_weight_own = owned(placed_units(outer_weight_part, 0))
    sums = [owned(token_sums[i]) for i in range(6)]

    return (
        encoded,
        input_grad,
        qkv_weights[0],
        query_bias_own,
        qkv_weights[1],
        qkv_weights[2],
        value_bias_own,
        output_weight_own,
        sums[5],
        sums[3],
        sums[4],
        inner_weight_own,
        inner_bias_own,
        outer_weight_own,
        sums[2],
        sums[0],
        sums[1],
    )


def solution(mesh):
    tokens = P(("dp", "fsdp"), "ctx", None)
    matrix, vector = P("fsdp", None), P("fsdp")
    own_matrix, own_vector = P(OWNERS, None), P(OWNERS)
    return jax.shard_map(
        shards,
        mesh=mesh,
        in_specs=(
            tokens,
            tokens,
            P(),
            P(),
            matrix,
            vector,
            matrix,
            matrix,
            vector,
            matrix,
            vector,
            vector,
            vector,
            matrix,
            vector,
            matrix,
            vector,
            vector,
            vector,
        ),
        out_specs=(
            tokens,
            tokens,
            own_matrix,
            own_vector,
            own_matrix,
            own_matrix,
            own_vector,
            own_matrix,
            own_vector,
            own_vector,
            own_vector,
            own_matrix,
            own_vector,
            own_matrix,
            own_vector,
            own_vector,
            own_vector,
        ),
        check_vma=False,
    )
```

```python
import functools
import math

import jax
import jax.numpy as jnp
from jax import lax
from jax.experimental import pallas as pl
from jax.experimental.pallas import tpu as pltpu
from jax.sharding import PartitionSpec as P

HEADS = 16
EPS = 1e-12
MASKED = -1e30
F32 = jnp.float32
BF16 = jnp.bfloat16
OWNERS = ("dp", "ctx", "fsdp")


def swap(value, axis, mask):
    pairs = [(source, source ^ mask) for source in range(lax.axis_size(axis))]
    return lax.ppermute(value, axis, pairs)


def pick(array, index, axis):
    return lax.dynamic_index_in_dim(array, index, axis, keepdims=False)


def add_low(left, right):
    return (left.astype(F32) + right.astype(F32)).astype(BF16)


def matmul(left, right):
    return jnp.dot(left, right, preferred_element_type=F32)


def matmul_tn(left, right):
    return lax.dot_general(left, right, (((0,), (0,)), ((), ())), preferred_element_type=F32)


def matmul_nt(left, right):
    return lax.dot_general(left, right, (((1,), (1,)), ((), ())), preferred_element_type=F32)


def col_sum(matrix):
    return jnp.sum(matrix.astype(F32), axis=0)


def norm_rows(summed, scale_vec, shift_vec):
    row_mean = jnp.mean(summed, axis=-1, keepdims=True)
    centered = summed - row_mean
    inverse = lax.rsqrt(jnp.mean(centered * centered, axis=-1, keepdims=True) + EPS)
    normed = centered * inverse
    return (normed * scale_vec + shift_vec, normed, inverse)


def norm_back(upstream, normed, inverse, scale_vec):
    scaled = upstream * scale_vec
    return inverse * (
        scaled
        - jnp.mean(scaled, axis=-1, keepdims=True)
        - normed * jnp.mean(scaled * normed, axis=-1, keepdims=True)
    )


def half_lanes(pair, which):
    lane = lax.broadcasted_iota(jnp.int32, pair.shape, 1)
    keep = lane < 64 if which == 0 else lane >= 64
    return jnp.where(keep, pair, jnp.zeros_like(pair))


def with_flag(pair, flag, which):
    lane = lax.broadcasted_iota(jnp.int32, pair.shape, 1)
    keep = lane < 64 if which == 0 else lane >= 64
    spot = lane == (64 if which == 0 else 0)
    return jnp.where(keep, pair, jnp.where(spot, flag, jnp.zeros_like(pair)))


def attend_kernel(qkv_ref, bias_ref, out_ref, lse_ref):
    width = out_ref.shape[-1]
    rows = out_ref.shape[0] * out_ref.shape[2]
    bias = bias_ref[0]
    lane = lax.broadcasted_iota(jnp.int32, (rows, 128), 1)
    one = jnp.ones((rows, 128), BF16)
    totals = jnp.zeros((rows, 128), F32)
    for pair_index in range(width // 128):
        first = pair_index * 128
        query = qkv_ref[:, 0, :, first : first + 128].reshape(rows, 128)
        key = qkv_ref[:, 0, :, width + first : width + first + 128].reshape(rows, 128)
        value = qkv_ref[:, 0, :, 2 * width + first : 2 * width + first + 128].reshape(rows, 128)
        query = (query.astype(F32) * 0.125).astype(BF16)
        mixed = []
        for which in range(2):
            scores = matmul_nt(with_flag(query, one, which), with_flag(key, bias, which))
            top = jnp.max(scores, axis=-1, keepdims=True)
            weight = jnp.exp(scores - top)
            total = jnp.sum(weight, axis=-1, keepdims=True)
            mixed.append(matmul(weight.astype(BF16), value) * (1.0 / total))
            totals = jnp.where(lane == 2 * pair_index + which, top + jnp.log(total), totals)
        joined = jnp.where(lane < 64, mixed[0], mixed[1]).astype(BF16)
        out_ref[:, 0, :, first : first + 128] = joined.reshape(out_ref.shape[0], out_ref.shape[2], 128)
    lse_ref[0] = jnp.transpose(totals)[:8]


def attend_back_kernel(qkv_ref, bias_ref, lse_ref, grad_ref, out_ref):
    width = grad_ref.shape[-1]
    shape = (grad_ref.shape[0], grad_ref.shape[2], 128)
    rows = shape[0] * shape[1]
    bias = bias_ref[0]
    lane = lax.broadcasted_iota(jnp.int32, (rows, 128), 1)
    one = jnp.ones((rows, 128), BF16)
    for pair_index in range(width // 128):
        first = pair_index * 128
        query = qkv_ref[:, 0, :, first : first + 128].reshape(rows, 128)
        key = qkv_ref[:, 0, :, width + first : width + first + 128].reshape(rows, 128)
        value = qkv_ref[:, 0, :, 2 * width + first : 2 * width + first + 128].reshape(rows, 128)
        grad = grad_ref[:, 0, :, first : first + 128].reshape(rows, 128)
        query = (query.astype(F32) * 0.125).astype(BF16)
        query_parts, key_parts, value_parts = [], [], []
        for which in range(2):
            spot = 2 * pair_index + which
            log_total = lse_ref[0, spot : spot + 1, :]
            scores = matmul_nt(with_flag(key, bias, which), with_flag(query, one, which))
            probs = jnp.exp(scores - log_total)
            probs_grad = matmul_nt(value, half_lanes(grad, which))
            value_parts.append(matmul(probs.astype(BF16), grad))
            row_dot = jnp.sum(probs * probs_grad, axis=0, keepdims=True)
            score_grad = (probs * (probs_grad - row_dot)).astype(BF16)
            key_parts.append(matmul(score_grad, query))
            query_parts.append(matmul_tn(score_grad, key) * 0.125)
        for place, parts in enumerate((query_parts, key_parts, value_parts)):
            joined = jnp.where(lane < 64, parts[0], parts[1]).astype(BF16)
            start = place * width + first
            out_ref[:, 0, :, start : start + 128] = joined.reshape(shape)


def attention_call(kernel, arrays, outs, flops):
    def whole(array):
        shape = array.shape
        if len(shape) == 4:
            return pl.BlockSpec((shape[0], 1) + shape[2:], lambda s: (0, s, 0, 0))
        return pl.BlockSpec((1,) + shape[1:], lambda s: (s, 0, 0))

    return pl.pallas_call(
        kernel,
        grid=(arrays[0].shape[1],),
        in_specs=[whole(array) for array in arrays],
        out_specs=[whole(out) for out in outs],
        out_shape=outs,
        compiler_params=pltpu.CompilerParams(vmem_limit_bytes=40 * 1024 * 1024),
        cost_estimate=pl.CostEstimate(flops=flops, bytes_accessed=8 << 20, transcendentals=0),
    )(*arrays)


MESH = pl.DeviceIdType.MESH


def repeat(count, body):
    def step(index, carry):
        body(index)
        return carry

    lax.fori_loop(0, count, step, 0)


class Slots:
    def __init__(self):
        self.total = 0

    def take(self, count=1):
        first = self.total
        self.total += count
        return first


def read_lengths(slot_ref, length_ref, lens_ref, first):
    def step(t, totals):
        source, count = slot_ref[t], length_ref[t]
        return tuple(total + jnp.where(source == first + i, count, 0) for i, total in enumerate(totals))

    totals = lax.fori_loop(0, slot_ref.shape[0], step, (jnp.int32(0),) * 4)
    for i in range(4):
        lens_ref[i] = totals[i]


def layer_kernel(
    length_ref,
    slot_ref,
    states,
    query_own,
    key_own,
    value_own,
    vec_query,
    vec_out,
    vec_gain,
    vec_shift,
    vec_outer,
    vec_gain2,
    vec_shift2,
    vec_value,
    vec_inner,
    wo_own,
    wi_own,
    wu_own,
    encoded_out,
    o_states,
    o_wq,
    o_wout,
    o_win,
    o_wou,
    o_vecs,
    o_qkv,
    o_lse,
    o_att,
    o_norm,
    o_inv,
    o_low,
    o_act,
    o_slope,
    o_norm2,
    o_inv2,
    lens_ref,
    st_all,
    wq_all,
    vec_all,
    w_out,
    w_in,
    w_ou,
    vecs,
    qkv,
    lse,
    att,
    att_far,
    part_far,
    part_in,
    part_far2,
    part_in2,
    first_norm,
    first_inv,
    first_out,
    low2,
    act,
    slope,
    acc,
    second_inv,
    chosen,
    own_three,
    send,
    recv,
    local,
):
    d, me, y = lax.axis_index("dp"), lax.axis_index("ctx"), lax.axis_index("fsdp")
    x, c = me // 2, me % 2
    to_core = {"ctx": me + 1 - 2 * c}
    to_x = {"ctx": (me + 2) % 4}
    to_y = {"fsdp": 1 - y}
    to_z = {"dp": d + 1 - 2 * (d % 2)}
    to_zz = {"dp": (d + 2) % 4}
    to_far = {"ctx": 3 - me}
    slots = Slots()
    pending = []

    def remote(src, dst, slot, device):
        return pltpu.make_async_remote_copy(
            src_ref=src,
            dst_ref=dst,
            send_sem=send.at[slot],
            recv_sem=recv.at[slot],
            device_id=device,
            device_id_type=MESH,
        )

    def at_end(count, make):
        pending.append((count, make))

    local_slots = Slots()

    def fetch(src, dst):
        copy = pltpu.make_async_copy(src, dst, local.at[local_slots.take()])
        copy.start()
        return copy

    kept = []

    def keep(src, dst):
        kept.append(fetch(src, dst))

    three = [fetch(src, own_three.at[i]) for i, src in enumerate((query_own, key_own, value_own))]
    barrier = pltpu.get_barrier_semaphore()
    for device in (to_core, to_x, to_y, to_z, to_zz, to_far):
        pl.semaphore_signal(barrier, inc=1, device_id=device, device_id_type=MESH)
    row = lax.broadcasted_iota(jnp.int32, (1024, 256), 0)
    col = lax.broadcasted_iota(jnp.int32, (1024, 256), 1)
    chosen[...] = jnp.where(row == (col // 64) * 256 + me * 64 + col % 64, 1.0, 0.0).astype(BF16)
    read_lengths(slot_ref, length_ref, lens_ref, (2 * d + y) * 4)
    singles = (vec_query, vec_out, vec_gain, vec_shift, vec_outer, vec_gain2, vec_shift2, vec_value)
    vec_all[y, 0:8] = jnp.concatenate([single[...].astype(F32).reshape(1, 512) for single in singles], 0)
    inner_rows = vec_inner[...].astype(F32).reshape(4, 512)
    vec_all[y, 8:16] = jnp.concatenate((inner_rows, jnp.zeros((4, 512), F32)), 0)
    pl.semaphore_wait(barrier, 6)

    first = slots.take(4)
    state_x = lambda s: remote(states.at[s], st_all.at[2, s], first + s, to_x)
    second = slots.take(4)
    state_core = lambda s: remote(states.at[s], st_all.at[1, s], second + s, to_core)
    third = slots.take(4)
    state_far = lambda s: remote(st_all.at[2, s], st_all.at[3, s], third + s, to_core)
    p = d % 2
    wq_slot = slots.take(2)

    def wq_copy(k):
        here = wq_all.at[pl.ds(pl.multiple_of(y * 512 + p * 256 + k * 128, 128), 128)]
        return remote(here, here, wq_slot + k, to_y)

    wq_pass_slot = slots.take(2)

    def wq_pass(k):
        here = wq_all.at[pl.ds(pl.multiple_of((1 - y) * 512 + p * 256 + k * 128, 128), 128)]
        return remote(here, here, wq_pass_slot + k, to_z)

    vec_slot = slots.take()
    vec_copy = remote(vec_all.at[y], vec_all.at[y], vec_slot, to_y)
    for s in range(4):
        state_x(s).start()
    vec_copy.start()
    for s in range(4):
        state_core(s).start()
    at_end(4, state_x)
    at_end(4, state_core)
    at_end(4, state_far)
    at_end(2, wq_copy)
    at_end(2, wq_pass)
    at_end(1, lambda _: vec_copy)

    wo_slot = slots.take(2)

    def wo_copy(side):
        src = wo_own.at[pl.ds(pl.multiple_of(p * 256 + side * 128 + c * 64, 64), 64)]
        return remote(src, w_out.at[x if side == 0 else 1 - x, 2 * y + p], wo_slot + side, to_y)

    wo_pass_slot = slots.take(2)

    def wo_pass(side):
        here = w_out.at[x if side == 0 else 1 - x, 2 * (1 - y) + p]
        return remote(here, here, wo_pass_slot + side, to_z)

    wi_slot = slots.take(8)

    def wi_copy(b):
        src = wi_own.at[
            pl.ds(pl.multiple_of(x * 256, 256), 256), pl.ds(pl.multiple_of((2 * b + c) * 256, 256), 256)
        ]
        dst = w_in.at[
            pl.ds(pl.multiple_of(y * 512 + x * 256, 256), 256), pl.ds(pl.multiple_of(b * 256, 256), 256)
        ]
        return remote(src, dst, wi_slot + b, to_y)

    wi_pass_slot = slots.take(8)

    def wi_pass(b):
        here = w_in.at[
            pl.ds(pl.multiple_of((1 - y) * 512 + x * 256, 256), 256),
            pl.ds(pl.multiple_of(b * 256, 256), 256),
        ]
        return remote(here, here, wi_pass_slot + b, to_x)

    wu_slot = slots.take(4)

    def wu_copy(k):
        side, half = k // 2, k % 2
        start, rows = (0, 128) if half == 0 else (128 + x * 64, 64)
        src = wu_own.at[pl.ds(pl.multiple_of((p * 4 + side * 2 + c) * 256 + start, 64), rows)]
        dst = w_ou.at[pl.ds(pl.multiple_of((4 * y + 2 * p + side) * 256 + start, 64), rows)]
        return remote(src, dst, wu_slot + k, to_y)

    wu_side_slot = slots.take(2)

    def wu_side(side):
        start = (4 * (1 - y) + 2 * p + side) * 256 + 128 + x * 64
        here = w_ou.at[pl.ds(pl.multiple_of(start, 64), 64)]
        return remote(here, here, wu_side_slot + side, to_x)

    wu_pass_slot = slots.take(4)

    def wu_pass(k):
        side, half = k // 2, k % 2
        here = w_ou.at[
            pl.ds(pl.multiple_of((4 * (1 - y) + 2 * p + side) * 256 + half * 128, 128), 128)
        ]
        return remote(here, here, wu_pass_slot + k, to_z)

    for side in range(2):
        wo_copy(side).start()
    for place in range(3):
        three[place].wait()
        made = matmul(own_three[place], chosen[...]).astype(BF16)
        wq_all[pl.ds(pl.multiple_of(y * 512, 512), 512), place * 256 : place * 256 + 256] = made
    for k in range(2):
        wq_copy(k).start()
    for b in range(8):
        wi_copy(b).start()
    for k in range(4):
        wu_copy(k).start()
    for count, make in ((2, wo_copy), (2, wo_pass), (8, wi_copy), (8, wi_pass), (4, wu_copy), (2, wu_side), (4, wu_pass)):
        at_end(count, make)

    own_early = [
        fetch(states, st_all.at[0]),
    ]
    own_out = []
    for half in range(2):
        for side in range(2):
            src = wo_own.at[pl.ds(pl.multiple_of(half * 256 + side * 128 + c * 64, 64), 64)]
            own_out.append(fetch(src, w_out.at[x if side == 0 else 1 - x, 2 * y + half]))
    own_late = []
    for b in range(8):
        src = wi_own.at[:, pl.ds(pl.multiple_of((2 * b + c) * 256, 256), 256)]
        dst = w_in.at[pl.ds(pl.multiple_of(y * 512, 512), 512), pl.ds(b * 256, 256)]
        own_late.append(fetch(src, dst))
    for half in range(2):
        for side in range(2):
            src = wu_own.at[pl.ds(pl.multiple_of((half * 4 + side * 2 + c) * 256, 256), 256)]
            dst = w_ou.at[pl.ds(pl.multiple_of((4 * y + 2 * half + side) * 256, 256), 256)]
            own_late.append(fetch(src, dst))

    state_x(0).wait_recv()
    state_far(0).start()
    for k in range(2):
        wq_copy(k).wait_recv()
        wq_pass(k).start()
    state_x(1).wait_recv()
    state_far(1).start()
    for copy in own_early:
        copy.wait()
    vec_copy.wait_recv()
    vecs[:, :512] = vec_all[0]
    vecs[:, 512:] = vec_all[1]
    for side in range(2):
        wo_copy(side).wait_recv()
        wo_pass(side).start()
    for k in range(2):
        wq_pass(k).wait_recv()

    att_slot = slots.take(8)

    def att_copy(s, j):
        rows = pl.ds(pl.multiple_of(j * 512 + s * 128, 128), 128)
        return remote(att_far.at[j, s], att.at[rows, 256:512], att_slot + 2 * s + j, to_x)

    at_end(8, lambda k: att_copy(k // 2, k % 2))
    biases = matmul(vecs[0:8, :].astype(BF16), chosen[...])
    q_bias, v_bias = biases[0:1], biases[7:8]

    def key_flags(s):
        pieces = []
        for j in range(4):
            position = lax.broadcasted_iota(jnp.int32, (128, 128), 0)
            place = me + 1 - 2 * c if j == 1 else me
            place = (place + 2) % 4 if j == 2 else place
            place = 3 - me if j == 3 else place
            pieces.append(jnp.where(position + place * 128 < lens_ref[s], 0.0, MASKED))
        return jnp.concatenate(pieces, 0).astype(BF16)

    def pass_inner(b):
        wi_copy(b).wait_recv()
        wi_pass(b).start()

    def attention(s):
        @pl.when(s < 2)
        def _():
            state_x(s + 2).wait_recv()
            state_far(s + 2).start()

        @pl.when((s == 1) | (s == 2))
        def _():
            for k in range(2):
                pass_inner(2 * (s - 1) + k)

        @pl.when(s == 3)
        def _():
            pass_inner(4)

        state_core(s).wait_recv()
        state_far(s).wait_recv()
        rows = st_all[:, s].reshape(512, 1024)
        for place in range(3):
            made = matmul(rows, wq_all[:, place * 256 : place * 256 + 256])
            made = made + q_bias if place == 0 else made
            made = made + v_bias if place == 2 else made
            qkv[:, s, :, place * 256 : place * 256 + 256] = made.astype(BF16).reshape(4, 128, 256)
        bias = key_flags(s)
        lane = lax.broadcasted_iota(jnp.int32, (512, 128), 1)
        one = jnp.ones((512, 128), BF16)
        totals = jnp.zeros((512, 128), F32)
        for pair in range(2):
            base = pair * 128
            query = qkv[:, s, :, base : base + 128].reshape(512, 128)
            key = qkv[:, s, :, 256 + base : 384 + base].reshape(512, 128)
            value = qkv[:, s, :, 512 + base : 640 + base].reshape(512, 128)
            query = (query.astype(F32) * 0.125).astype(BF16)
            mixed = []
            for which in range(2):
                scores = matmul_nt(with_flag(query, one, which), with_flag(key, bias, which))
                top = jnp.max(scores, axis=-1, keepdims=True)
                weight = jnp.exp(scores - top)
                total = jnp.sum(weight, axis=-1, keepdims=True)
                mixed.append(matmul(weight.astype(BF16), value) * (1.0 / total))
                totals = jnp.where(lane == 2 * pair + which, top + jnp.log(total), totals)
            joined = jnp.where(lane < 64, mixed[0], mixed[1]).astype(BF16)
            for j in range(2):
                rows_j = pl.ds(pl.multiple_of(j * 512 + s * 128, 128), 128)
                att[rows_j, base : base + 128] = joined[j * 128 : j * 128 + 128]
                att_far[j, s, :, base : base + 128] = joined[256 + j * 128 : 384 + j * 128]
        for j in range(2):
            att_copy(s, j).start()
        lse[s] = jnp.transpose(totals)[:8]

    repeat(4, attention)
    for src, dst in ((st_all, o_states), (wq_all, o_wq), (vecs, o_vecs), (qkv, o_qkv), (lse, o_lse)):
        keep(src, dst)

    for b in range(5, 7):
        pass_inner(b)
    for copy in own_out:
        copy.wait()
    for side in range(2):
        wo_pass(side).wait_recv()
    for s in range(4):
        for j in range(2):
            att_copy(s, j).wait_recv()
    keep(att, o_att)
    keep(w_out, o_wout)
    out_slot = slots.take(4)

    def out_copy(n):
        return remote(part_far.at[n], part_in.at[n], out_slot + n, to_core)

    at_end(4, out_copy)
    for n in range(4):
        right = w_out[:, :, :, n * 256 : n * 256 + 256].reshape(512, 256)
        part_far[n] = matmul(att[512:], right).astype(BF16)
        out_copy(n).start()
    pass_inner(7)
    for n in range(4):
        right = w_out[:, :, :, n * 256 : n * 256 + 256].reshape(512, 256)
        made = matmul(att[:512], right) + vecs[1:2, n * 256 : n * 256 + 256]
        made = made + st_all[0, :, :, n * 256 : n * 256 + 256].astype(F32).reshape(512, 256)
        out_copy(n).wait_recv()
        first_norm[:, n * 256 : n * 256 + 256] = made + part_in[n].astype(F32)

    low_slot = slots.take(4)

    def low_copy(k):
        src = low2.at[pl.ds(pl.multiple_of(k * 128, 128), 128)]
        dst = low2.at[pl.ds(pl.multiple_of(512 + k * 128, 128), 128)]
        return remote(src, dst, low_slot + k, to_core)

    at_end(4, low_copy)

    def norm_first(k):
        for half in range(2):
            rows = pl.ds(pl.multiple_of(k * 128 + half * 64, 64), 64)
            made, normed, inverse = norm_rows(first_norm[rows, :], vecs[2:3, :], vecs[3:4, :])
            first_norm[rows, :] = normed
            first_inv[rows, :] = jnp.broadcast_to(inverse, (64, 128))
            first_out[rows, :] = made
            low2[rows, :] = made.astype(BF16)
        low_copy(k).start()

    repeat(4, norm_first)

    def share_outer(k):
        wu_copy(k).wait_recv()
        wu_side(k // 2).start()

    def pass_outer(k):
        if k % 2:
            wu_side(k // 2).wait_recv()
        else:
            wu_copy(k).wait_recv()
        wu_pass(k).start()

    pass_outer(0)
    for k in range(4):
        low_copy(k).wait_recv()
    for copy in own_late:
        copy.wait()
    for src, dst in ((first_norm, o_norm), (first_inv, o_inv), (low2, o_low)):
        keep(src, dst)

    def unit_block(b):
        for step, action, k in ((1, share_outer, 1), (3, pass_outer, 1), (4, pass_outer, 2), (6, share_outer, 3)):

            @pl.when(b == step)
            def _():
                action(k)

        wi_pass(b).wait_recv()
        here = pl.ds(pl.multiple_of(b * 256, 256), 256)
        spot = pl.ds(pl.multiple_of((b // 4) * 512 + c * 256, 256), 256)
        row = vecs[pl.ds(8 + b % 4, 1), spot]
        for m in range(2):
            hidden = matmul(low2[m * 512 : m * 512 + 512, :], w_in[:, here]) + row
            below = 0.5 * (1.0 + lax.erf(hidden * math.sqrt(0.5)))
            bell = jnp.exp(-0.5 * hidden * hidden) * (1.0 / math.sqrt(2 * math.pi))
            act[m * 512 : m * 512 + 512, here] = (hidden * below).astype(BF16)
            slope[m * 512 : m * 512 + 512, here] = (below + hidden * bell).astype(BF16)

    repeat(8, unit_block)
    for src, dst in ((act, o_act), (slope, o_slope), (w_in, o_win)):
        keep(src, dst)
    mine = pl.ds(pl.multiple_of(y * 1024, 1024), 1024)
    theirs = pl.ds(pl.multiple_of((1 - y) * 1024, 1024), 1024)
    pass_outer(3)

    def outer_own(n):
        here = pl.ds(pl.multiple_of(n * 256, 256), 256)
        for m in range(2):
            acc[m * 512 : m * 512 + 512, here] = matmul(
                act[m * 512 : m * 512 + 512, mine], w_ou[mine, here]
            )

    repeat(4, outer_own)
    for k in range(4):
        wu_pass(k).wait_recv()
    keep(w_ou, o_wou)
    sum_slot = slots.take(4)

    def sum_copy(n):
        return remote(part_far2.at[n], part_in2.at[n], sum_slot + n, to_core)

    at_end(4, sum_copy)

    def outer_far(n):
        here = pl.ds(pl.multiple_of(n * 256, 256), 256)
        made = acc[512:, here] + matmul(act[512:, theirs], w_ou[theirs, here])
        part_far2[n] = made.astype(BF16)
        sum_copy(n).start()

    repeat(4, outer_far)

    def outer_near(n):
        here = pl.ds(pl.multiple_of(n * 256, 256), 256)
        made = acc[:512, here] + matmul(act[:512, theirs], w_ou[theirs, here])
        made = made + first_out[:, here] + vecs[4:5, here]
        sum_copy(n).wait_recv()
        acc[:512, here] = made + part_in2[n].astype(F32)

    repeat(4, outer_near)

    def norm_second(k):
        valid_place = lax.broadcasted_iota(jnp.int32, (128, 1), 0) + me * 128
        valid = jnp.where(valid_place < lens_ref[k], 1.0, 0.0)
        for half in range(2):
            rows = pl.ds(pl.multiple_of(k * 128 + half * 64, 64), 64)
            made, normed, inverse = norm_rows(acc[rows, :], vecs[5:6, :], vecs[6:7, :])
            encoded_out[rows, :] = (made * valid[half * 64 : half * 64 + 64]).astype(BF16)
            acc[rows, :] = normed
            second_inv[rows, :] = jnp.broadcast_to(inverse, (64, 128))

    repeat(4, norm_second)
    keep(acc.at[:512], o_norm2)
    keep(second_inv, o_inv2)
    for copy in kept:
        copy.wait()
    for count, make in pending:
        for k in range(count):
            make(k).wait_send()


def layer_call(arrays):
    any_space = pl.BlockSpec(memory_space=pl.ANY)
    v = pltpu.VMEM
    return pl.pallas_call(
        layer_kernel,
        in_specs=[pl.BlockSpec(memory_space=pltpu.SMEM)] * 2
        + [any_space] * 4
        + [pl.BlockSpec(memory_space=pltpu.VMEM)] * 9
        + [any_space] * 3,
        out_specs=[pl.BlockSpec(memory_space=pltpu.VMEM)] + [any_space] * 16 + [pl.BlockSpec(memory_space=pltpu.SMEM)],
        out_shape=[
            jax.ShapeDtypeStruct(shape, kind)
            for shape, kind in (
                ((512, 1024), BF16),
                ((4, 4, 128, 1024), BF16),
                ((1024, 768), BF16),
                ((2, 4, 64, 1024), BF16),
                ((1024, 2048), BF16),
                ((2048, 1024), BF16),
                ((16, 1024), F32),
                ((4, 4, 128, 768), BF16),
                ((4, 8, 512), F32),
                ((1024, 512), BF16),
                ((512, 1024), F32),
                ((512, 128), F32),
                ((1024, 1024), BF16),
                ((1024, 2048), BF16),
                ((1024, 2048), BF16),
                ((512, 1024), F32),
                ((512, 128), F32),
                ((4,), jnp.int32),
            )
        ],
        scratch_shapes=[
            v((4, 4, 128, 1024), BF16),
            v((1024, 768), BF16),
            v((2, 16, 512), F32),
            v((2, 4, 64, 1024), BF16),
            v((1024, 2048), BF16),
            v((2048, 1024), BF16),
            v((16, 1024), F32),
            v((4, 4, 128, 768), BF16),
            v((4, 8, 512), F32),
            v((1024, 512), BF16),
            v((2, 4, 128, 256), BF16),
            v((4, 512, 256), BF16),
            v((4, 512, 256), BF16),
            v((4, 512, 256), BF16),
            v((4, 512, 256), BF16),
            v((512, 1024), F32),
            v((512, 128), F32),
            v((512, 1024), F32),
            v((1024, 1024), BF16),
            v((1024, 2048), BF16),
            v((1024, 2048), BF16),
            v((1024, 1024), F32),
            v((512, 128), F32),
            v((1024, 256), BF16),
            v((3, 512, 1024), BF16),
            pltpu.SemaphoreType.DMA((80,)),
            pltpu.SemaphoreType.DMA((80,)),
            pltpu.SemaphoreType.DMA((64,)),
        ],
        compiler_params=pltpu.CompilerParams(
            collective_id=0, has_side_effects=True, vmem_limit_bytes=64 * 1024 * 1024 - 65536
        ),
    )(*arrays)


def accumulate(dst, src, lead, rows):
    steps = rows // 32
    total = math.prod(lead) * steps

    def body(index):
        place = []
        rest = index // steps
        for size in reversed(lead):
            place.insert(0, rest % size)
            rest = rest // size
        here = tuple(place) + (pl.ds(pl.multiple_of((index % steps) * 32, 32), 32),)
        dst[here] = add_low(dst[here], src[here])

    repeat(total, body)


def back_kernel(
    lens_ref,
    i_cot,
    i_n2,
    i_i2,
    i_vecs,
    i_w_ou,
    i_act,
    i_slope,
    i_low,
    i_w_in,
    i_n1,
    i_i1,
    i_att,
    i_w_out,
    i_qkv,
    i_lse,
    i_wq,
    i_states,
    grad_out,
    ou_out,
    in_out,
    out_out,
    qkv_out,
    vec_out,
    cot,
    n2,
    i2,
    vecs,
    w_ou,
    act,
    slope,
    low,
    w_in,
    n1,
    i1,
    att,
    w_out,
    qkv,
    lse,
    wq,
    outer2,
    part_in,
    branch2,
    mix_all,
    mix_far,
    g_ou,
    a_ou,
    b_ou,
    z_ou,
    zz_ou,
    az_ou,
    azz_ou,
    ax_ou,
    ay_ou,
    a_in,
    b_in,
    z_in,
    zz_in,
    az_in,
    azz_in,
    ax_in,
    ay_in,
    f_in,
    c_in,
    g_o,
    z_o,
    zz_o,
    x_o,
    y_o,
    g_q,
    y_q,
    z_q,
    zz_q,
    s_q,
    r_q,
    bias_q,
    vb,
    vr,
    send,
    recv,
    local,
):
    d, me, y = lax.axis_index("dp"), lax.axis_index("ctx"), lax.axis_index("fsdp")
    x, c = me // 2, me % 2
    p, q = d % 2, d // 2
    to_core = {"ctx": me + 1 - 2 * c}
    to_x = {"ctx": (me + 2) % 4}
    to_y = {"fsdp": 1 - y}
    to_z = {"dp": d + 1 - 2 * (d % 2)}
    to_zz = {"dp": (d + 2) % 4}
    to_far = {"ctx": 3 - me}
    slots = Slots()
    local_slots = Slots()
    pending = []

    def remotes(count, parts):
        first = slots.take(count)

        def make(k):
            src, dst, device = parts(k)
            return pltpu.make_async_remote_copy(
                src_ref=src,
                dst_ref=dst,
                send_sem=send.at[first + k],
                recv_sem=recv.at[first + k],
                device_id=device,
                device_id_type=MESH,
            )

        pending.append((count, make))
        return make

    def fetch(src, dst):
        copy = pltpu.make_async_copy(src, dst, local.at[local_slots.take()])
        copy.start()
        return copy

    early = [fetch(i_cot, cot), fetch(i_n2, n2), fetch(i_i2, i2), fetch(i_vecs, vecs)]
    barrier = pltpu.get_barrier_semaphore()
    for device in (to_core, to_x, to_y, to_z, to_zz, to_far):
        pl.semaphore_signal(barrier, inc=1, device_id=device, device_id_type=MESH)
    vb[0] = jnp.zeros((24, 1024), F32)
    bias_q[...] = jnp.zeros((8, 768), F32)
    for copy in early:
        copy.wait()
    got_act, got_w_ou = fetch(i_act, act), fetch(i_w_ou, w_ou)
    pl.semaphore_wait(barrier, 6)

    def chunk_of(buffer):
        def parts(k):
            src = buffer.at[pl.ds(pl.multiple_of(k * 128, 128), 128)]
            dst = buffer.at[pl.ds(pl.multiple_of(512 + k * 128, 128), 128)]
            return src, dst, to_core

        return parts

    outer_copy = remotes(4, chunk_of(outer2))
    branch_copy = remotes(4, chunk_of(branch2))

    def count_in(row, values):
        vb[0, row : row + 1, :] += jnp.sum(values, axis=0, keepdims=True)

    def norm_second(k):
        place = lax.broadcasted_iota(jnp.int32, (128, 1), 0) + me * 128
        valid = jnp.where(place < lens_ref[k], 1.0, 0.0)
        for half in range(2):
            rows = pl.ds(pl.multiple_of(k * 128 + half * 64, 64), 64)
            upstream = cot[k, half * 64 : half * 64 + 64].astype(F32) * valid[half * 64 : half * 64 + 64]
            normed = n2[rows, :]
            count_in(0, upstream * normed)
            count_in(1, upstream)
            made = norm_back(upstream, normed, i2[rows, 0:1], vecs[5:6, :])
            n2[rows, :] = made
            made = made.astype(BF16)
            outer2[rows, :] = made
            count_in(2, made.astype(F32))
        outer_copy(k).start()

    repeat(4, norm_second)
    late = [fetch(i_slope, slope), fetch(i_w_in, w_in)]
    got_act.wait()
    for k in range(4):
        outer_copy(k).wait_recv()

    low_ou, top_ou = pl.ds(0, 256), pl.ds(256, 768)
    low_in, top_in = pl.ds(0, 512), pl.ds(512, 1536)

    def ou_first(k, x_first):
        if x_first:
            return g_ou.at[k, 1 - x, :, :, top_ou], a_ou.at[k], to_x
        return g_ou.at[k, :, 1 - y, :, top_ou], a_ou.at[k], to_y

    ou_a_x = remotes(2, lambda k: ou_first(k, True))
    ou_a_y = remotes(2, lambda k: ou_first(k + 2, False))
    ou_b_y = remotes(2, lambda k: (a_ou.at[k, 1 - y], b_ou.at[k], to_y))
    ou_b_x = remotes(2, lambda k: (a_ou.at[k + 2, 1 - x], b_ou.at[k + 2], to_x))
    ou_z = remotes(2, lambda k: (b_ou.at[2 * k + 1 - p], z_ou.at[k], to_z))
    ou_zz = remotes(1, lambda k: (z_ou.at[1 - q], zz_ou, to_zz))
    low_ou_z = remotes(2, lambda k: (g_ou.at[2 * k + 1 - p, :, :, :, low_ou], az_ou.at[k], to_z))
    low_ou_zz = remotes(1, lambda k: (az_ou.at[1 - q], azz_ou, to_zz))
    low_ou_x = remotes(1, lambda k: (azz_ou.at[1 - x], ax_ou, to_x))
    low_ou_y = remotes(1, lambda k: (ax_ou.at[1 - y], ay_ou, to_y))

    def ou_add_a(k):
        if k < 2:
            ou_a_x(k).wait_recv()
            accumulate(a_ou.at[k], g_ou.at[k, x, :, :, top_ou], (2,), 128)
            ou_b_y(k).start()
        else:
            ou_a_y(k - 2).wait_recv()
            accumulate(a_ou.at[k], g_ou.at[k, :, y, :, top_ou], (2,), 128)
            ou_b_x(k - 2).start()

    def ou_add_b(k):
        if k < 2:
            ou_b_y(k).wait_recv()
            accumulate(b_ou.at[k], a_ou.at[k, y], (), 128)
        else:
            ou_b_x(k - 2).wait_recv()
            accumulate(b_ou.at[k], a_ou.at[k, x], (), 128)

    def ou_add_z():
        for k in range(2):
            ou_z(k).wait_recv()
            accumulate(z_ou.at[k], b_ou.at[2 * k + p], (), 128)
        ou_zz(0).start()

    def low_ou_add_z():
        for k in range(2):
            low_ou_z(k).wait_recv()
            accumulate(az_ou.at[k], g_ou.at[2 * k + p, :, :, :, low_ou], (2, 2), 128)
        low_ou_zz(0).start()

    def low_ou_add_zz():
        low_ou_zz(0).wait_recv()
        accumulate(azz_ou, az_ou.at[q], (2, 2), 128)
        low_ou_x(0).start()

    def low_ou_add_x():
        low_ou_x(0).wait_recv()
        accumulate(ax_ou, azz_ou.at[x], (2,), 128)
        low_ou_y(0).start()

    def ou_last():
        ou_zz(0).wait_recv()
        low_ou_y(0).wait_recv()

        def body(i):
            rows = pl.ds(pl.multiple_of(i * 32, 32), 32)
            ou_out[rows, 256:] = z_ou[q, rows, :].astype(F32) + zz_ou[rows, :].astype(F32)
            ou_out[rows, :256] = ax_ou[y, rows, :].astype(F32) + ay_ou[rows, :].astype(F32)

        repeat(4, body)

    in_a = remotes(4, lambda k: (act.at[k, :, :, 1 - y, :, top_in], a_in.at[k], to_y))
    in_b = remotes(4, lambda k: (a_in.at[k, 1 - x], b_in.at[k], to_x))
    in_z = remotes(2, lambda k: (b_in.at[2 * k + 1 - p], z_in.at[k], to_z))
    in_zz = remotes(1, lambda k: (z_in.at[1 - q], zz_in, to_zz))
    in_core = remotes(1, lambda k: (f_in.at[1 - c], c_in, to_core))
    low_in_z = remotes(2, lambda k: (act.at[2 * k + 1 - p, :, :, :, :, low_in], az_in.at[k], to_z))
    low_in_zz = remotes(1, lambda k: (az_in.at[1 - q], azz_in, to_zz))
    low_in_x = remotes(1, lambda k: (azz_in.at[1 - x], ax_in, to_x))
    low_in_y = remotes(1, lambda k: (ax_in.at[:, 1 - y], ay_in, to_y))

    def in_add_a(k):
        in_a(k).wait_recv()
        accumulate(a_in.at[k], act.at[k, :, :, y, :, top_in], (2, 2), 32)
        in_b(k).start()

    def in_add_b(k):
        in_b(k).wait_recv()
        accumulate(b_in.at[k], a_in.at[k, x], (2,), 32)

    def in_add_z():
        for k in range(2):
            in_z(k).wait_recv()
            accumulate(z_in.at[k], b_in.at[2 * k + p], (2,), 32)
        in_zz(0).start()

    def low_in_add_z():
        for k in range(2):
            low_in_z(k).wait_recv()
            accumulate(az_in.at[k], act.at[2 * k + p, :, :, :, :, low_in], (2, 2, 2), 32)
        low_in_zz(0).start()

    def low_in_add_zz():
        low_in_zz(0).wait_recv()
        accumulate(azz_in, az_in.at[q], (2, 2, 2), 32)
        low_in_x(0).start()

    def low_in_add_x():
        low_in_x(0).wait_recv()
        accumulate(ax_in, azz_in.at[x], (2, 2), 32)
        low_in_y(0).start()

    def in_sum():
        in_zz(0).wait_recv()
        low_in_y(0).wait_recv()
        for k in range(2):
            f_in[k, :, 512:] = z_in[q, k].astype(F32) + zz_in[k].astype(F32)
            f_in[k, :, :512] = ax_in[k, y].astype(F32) + ay_in[k].astype(F32)
        in_core(0).start()

    def in_last():
        def place(b, own):
            return pl.ds(pl.multiple_of((2 * b + (c if own else 1 - c)) * 256, 256), 256)

        for b in range(8):
            in_out[:, place(b, True)] = f_in[c, :, b * 256 : b * 256 + 256]
        in_core(0).wait_recv()
        for b in range(8):
            in_out[:, place(b, False)] = c_in[:, b * 256 : b * 256 + 256]

    o_z = remotes(1, lambda k: (g_o.at[:, :, 1 - p], z_o, to_z))
    o_zz = remotes(1, lambda k: (z_o.at[:, 1 - q], zz_o, to_zz))
    o_x = remotes(1, lambda k: (zz_o.at[1], x_o, to_x))
    o_y = remotes(1, lambda k: (x_o.at[1 - y], y_o, to_y))

    def o_add_z():
        o_z(0).wait_recv()
        accumulate(z_o, g_o.at[:, :, p], (2, 2, 2), 32)
        o_zz(0).start()

    def o_add_zz():
        o_zz(0).wait_recv()
        accumulate(zz_o, z_o.at[:, q], (2, 2), 32)
        o_x(0).start()

    def o_add_x():
        o_x(0).wait_recv()
        accumulate(x_o, zz_o.at[0], (2,), 32)
        o_y(0).start()

    def o_last():
        o_y(0).wait_recv()
        out_out[...] = x_o[y].astype(F32) + y_o[...].astype(F32)

    q_y = remotes(4, lambda k: (g_q.at[k, :, 1 - y], y_q.at[k], to_y))
    q_z = remotes(2, lambda k: (y_q.at[2 * k + 1 - p], z_q.at[k], to_z))
    q_zz = remotes(1, lambda k: (z_q.at[1 - q], zz_q, to_zz))
    others = ((me + 1 - 2 * c, to_core), ((me + 2) % 4, to_x), (3 - me, to_far))
    q_all = [
        remotes(1, lambda k, j=j: (s_q.at[others[j][0]], r_q.at[j], others[j][1])) for j in range(3)
    ]

    def q_add_y(k):
        q_y(k).wait_recv()
        accumulate(y_q.at[k], g_q.at[k, :, y], (4,), 32)

    def q_add_z():
        for k in range(2):
            q_z(k).wait_recv()
            accumulate(z_q.at[k], y_q.at[2 * k + p], (4,), 32)
        q_zz(0).start()

    def q_sum():
        q_zz(0).wait_recv()
        for k in range(4):
            s_q[k] = z_q[q, k].astype(F32) + zz_q[k].astype(F32)
        for j in range(3):
            q_all[j](0).start()

    def q_last():
        qkv_out[me] = s_q[me]
        for j in range(3):
            q_all[j](0).wait_recv()
            qkv_out[others[j][0]] = r_q[j]

    v_core = remotes(1, lambda k: (vb.at[0, pl.ds(0, 8)], vr.at[0, pl.ds(0, 8)], to_core))
    v_x = remotes(1, lambda k: (vb.at[1, pl.ds(0, 16)], vr.at[1, pl.ds(0, 16)], to_x))
    v_y = remotes(1, lambda k: (vb.at[2], vr.at[2], to_y))
    v_z = remotes(1, lambda k: (vb.at[3], vr.at[3], to_z))
    v_zz = remotes(1, lambda k: (vb.at[4], vr.at[4], to_zz))

    def outer_grad(i):
        k = (i % 2) * 2 + i // 2
        for half in range(2):
            spot = pl.ds(pl.multiple_of((2 * k + half) * 256, 256), 256)
            left = act[:, :, :, :, :, spot].reshape(1024, 256)
            made = matmul_tn(left, outer2[...])
            g_ou[k, half] = made.astype(BF16).reshape(2, 128, 1024)

        @pl.when(i % 2 == 0)
        def _():
            ou_a_x(k).start()

        @pl.when(i % 2 == 1)
        def _():
            ou_a_y(k - 2).start()

        @pl.when(i >= 2)
        def _():
            low_ou_z(i - 2).start()

    repeat(4, outer_grad)
    got_w_ou.wait()
    for copy in late:
        copy.wait()
    late = [fetch(i_n1, n1), fetch(i_i1, i1), fetch(i_low, low), fetch(i_att, att), fetch(i_w_out, w_out)]
    late += [fetch(i_qkv, qkv), fetch(i_lse, lse), fetch(i_wq, wq)]

    def hidden_grad(b):
        here = pl.ds(pl.multiple_of(b * 256, 256), 256)
        total = jnp.zeros((1, 256), F32)
        for m in range(2):
            made = matmul_nt(outer2[m * 512 : m * 512 + 512, :], w_ou[here, :])
            made = (made * slope[m * 512 : m * 512 + 512, here].astype(F32)).astype(BF16)
            slope[m * 512 : m * 512 + 512, here] = made
            total = total + jnp.sum(made.astype(F32), axis=0, keepdims=True)
        vb[0, pl.ds(8 + b, 1), 0:256] = total

    repeat(8, hidden_grad)

    def part_copy_parts(n):
        spot = pl.ds(pl.multiple_of(n * 256, 256), 256)
        return w_ou.at[pl.ds(1536, 512), spot], part_in.at[n], to_core

    part_copy = remotes(4, part_copy_parts)

    def first_far(n):
        here = pl.ds(pl.multiple_of(n * 256, 256), 256)
        w_ou[1536:2048, here] = matmul_nt(slope[512:, :], w_in[here, :]).astype(BF16)
        part_copy(n).start()

    repeat(4, first_far)
    ou_add_a(0)
    ou_add_a(2)
    low_ou_add_z()

    def first_near(n):
        here = pl.ds(pl.multiple_of(n * 256, 256), 256)
        made = n2[:, here] + matmul_nt(slope[:512, :], w_in[here, :])
        part_copy(n).wait_recv()
        n2[:, here] = made + part_in[n].astype(F32)

    repeat(4, first_near)
    for copy in late:
        copy.wait()

    def norm_first(k):
        for half in range(2):
            rows = pl.ds(pl.multiple_of(k * 128 + half * 64, 64), 64)
            upstream = n2[rows, :]
            normed = n1[rows, :]
            count_in(3, upstream * normed)
            count_in(4, upstream)
            made = norm_back(upstream, normed, i1[rows, 0:1], vecs[2:3, :])
            n2[rows, :] = made
            made = made.astype(BF16)
            branch2[rows, :] = made
            count_in(5, made.astype(F32))
        branch_copy(k).start()

    repeat(4, norm_first)
    v_core(0).start()
    ou_add_a(1)
    ou_add_a(3)
    for k in range(4):
        branch_copy(k).wait_recv()

    mix_copy = remotes(4, lambda s: (mix_far.at[:, s], mix_all.at[pl.ds(2, 2), s], to_x))
    mix_far[...] = matmul_nt(branch2[...], w_out[1].reshape(256, 1024)).astype(BF16).reshape(2, 4, 128, 256)
    for s in range(4):
        mix_copy(s).start()
    mix_all[0:2] = matmul_nt(branch2[...], w_out[0].reshape(256, 1024)).astype(BF16).reshape(2, 4, 128, 256)

    for half in range(2):
        made = matmul_tn(att[:, half * 256 : half * 256 + 256], branch2[...])
        g_o[half] = made.astype(BF16).reshape(2, 2, 2, 32, 1024)
    o_z(0).start()
    v_core(0).wait_recv()
    vb[1, 0:8] = vb[0, 0:8] + vr[0, 0:8]
    vb[1, 8:16] = vb[0, 8:16]
    v_x(0).start()

    def inner_grad(k):
        left = low[:, pl.ds(pl.multiple_of(k * 256, 256), 256)]
        for half in range(4):
            made = matmul_tn(left, slope[:, half * 512 : half * 512 + 512]).astype(BF16)
            act[k, :, :, :, :, half * 512 : half * 512 + 512] = made.reshape(2, 2, 2, 32, 512)

        in_a(k).start()

        @pl.when(k % 2 == 1)
        def _():
            low_in_z(k // 2).start()

    repeat(4, inner_grad)
    got_states = []
    for j in range(4):
        for s in range(4):
            rows = pl.ds((j // 2) * 512 + s * 128, 128)
            got_states.append(fetch(i_states.at[j, s], slope.at[rows, pl.ds((j % 2) * 1024, 1024)]))

    def key_flags(s):
        pieces = []
        for j in range(4):
            position = lax.broadcasted_iota(jnp.int32, (128, 128), 0)
            place = me + 1 - 2 * c if j == 1 else me
            place = (place + 2) % 4 if j == 2 else place
            place = 3 - me if j == 3 else place
            pieces.append(jnp.where(position + place * 128 < lens_ref[s], 0.0, MASKED))
        return jnp.concatenate(pieces, 0).astype(BF16)

    def piece_copy_parts(k):
        rows = pl.ds(pl.multiple_of((k % 2) * 512 + (k // 2) * 128, 128), 128)
        return w_ou.at[rows], w_in.at[rows, pl.ds(0, 1024)], to_core

    piece_copy = remotes(8, piece_copy_parts)

    def pass_copy_parts(s):
        src = w_ou.at[pl.ds(pl.multiple_of(1024 + s * 128, 128), 128)]
        dst = w_in.at[pl.ds(pl.multiple_of(s * 128, 128), 128), pl.ds(1024, 1024)]
        return src, dst, to_x

    pass_copy = remotes(4, pass_copy_parts)

    def far_pieces(s):
        for which in range(2):
            rows = pl.ds(pl.multiple_of(512 * which + s * 128, 128), 128)
            w_ou[rows, :] = matmul_nt(qkv[1 + 2 * which, s], wq[...]).astype(BF16)
        for which in range(2):
            piece_copy(2 * s + which).start()

    def passed(s):
        made = matmul_nt(qkv[2, s], wq[...])
        piece_copy(2 * s + 1).wait_recv()
        rows = pl.ds(pl.multiple_of(512 + s * 128, 128), 128)
        made = made + w_in[rows, 0:1024].astype(F32)
        w_ou[pl.ds(pl.multiple_of(1024 + s * 128, 128), 128), :] = made.astype(BF16)
        pass_copy(s).start()

    hooks = {
        0: [lambda: ou_add_b(0), lambda: ou_add_b(2), low_ou_add_zz],
        1: [lambda: ou_add_b(1), lambda: ou_add_b(3), lambda: ou_z(0).start(), lambda: ou_z(1).start(), o_add_z],
        2: [lambda: in_add_a(0)],
        3: [lambda: in_add_a(1)],
    }

    def attention(s):
        for step, actions in hooks.items():

            @pl.when(s == step)
            def _():
                for action in actions:
                    action()

        mix_copy(s).wait_recv()
        bias = key_flags(s)
        lane = lax.broadcasted_iota(jnp.int32, (512, 128), 1)
        one = jnp.ones((512, 128), BF16)
        for pair in range(2):
            base = pair * 128
            query = qkv[:, s, :, base : base + 128].reshape(512, 128)
            key = qkv[:, s, :, 256 + base : 384 + base].reshape(512, 128)
            value = qkv[:, s, :, 512 + base : 640 + base].reshape(512, 128)
            grad = mix_all[:, s, :, base : base + 128].reshape(512, 128)
            query = (query.astype(F32) * 0.125).astype(BF16)
            query_parts, key_parts, value_parts = [], [], []
            for which in range(2):
                spot = 2 * pair + which
                log_total = lse[s, spot : spot + 1, :]
                scores = matmul_nt(with_flag(key, bias, which), with_flag(query, one, which))
                probs = jnp.exp(scores - log_total)
                probs_grad = matmul_nt(value, half_lanes(grad, which))
                value_parts.append(matmul(probs.astype(BF16), grad))
                row_dot = jnp.sum(probs * probs_grad, axis=0, keepdims=True)
                score_grad = (probs * (probs_grad - row_dot)).astype(BF16)
                key_parts.append(matmul(score_grad, query))
                query_parts.append(matmul_tn(score_grad, key) * 0.125)
            for place, parts in enumerate((query_parts, key_parts, value_parts)):
                joined = jnp.where(lane < 64, parts[0], parts[1]).astype(BF16)
                start = place * 256 + base
                qkv[:, s, :, start : start + 128] = joined.reshape(4, 128, 128)
                bias_q[0:1, start : start + 128] += jnp.sum(joined.astype(F32), axis=0, keepdims=True)
        far_pieces(s)

        @pl.when(s > 0)
        def _():
            passed(s - 1)

    repeat(4, attention)
    passed(3)

    v_x(0).wait_recv()
    vb[2, 0:16] = vb[1, 0:16] + vr[1, 0:16]
    vb[2, 16:24] = jnp.concatenate((bias_q[...], jnp.zeros((8, 256), F32)), 1)
    v_y(0).start()
    for copy in got_states:
        copy.wait()

    def projection_grad(k):
        made = jnp.zeros((256, 768), F32)
        for j in range(4):
            spot = pl.ds(pl.multiple_of((j % 2) * 1024 + k * 256, 256), 256)
            left = slope[(j // 2) * 512 : (j // 2) * 512 + 512, spot]
            made = made + matmul_tn(left, qkv[j].reshape(512, 768))
        g_q[k] = made.astype(BF16).reshape(4, 2, 32, 768)
        q_y(k).start()

    repeat(4, projection_grad)
    in_add_a(2)
    low_in_add_z()
    ou_add_z()
    v_y(0).wait_recv()
    vb[3] = vb[2] + vr[2]
    v_z(0).start()
    o_add_zz()
    in_add_a(3)
    for k in range(2):
        in_add_b(k)
    in_z(0).start()

    def near_piece(s):
        rows = pl.ds(pl.multiple_of(s * 128, 128), 128)
        made = n2[rows, :] + matmul_nt(qkv[0, s], wq[...])
        piece_copy(2 * s).wait_recv()
        n2[rows, :] = made + w_in[rows, 0:1024].astype(F32)

    repeat(4, near_piece)
    low_ou_add_x()
    for k in range(2):
        q_add_y(k)
    q_z(0).start()
    low_in_add_zz()
    for k in range(2, 4):
        q_add_y(k)
    q_z(1).start()
    v_z(0).wait_recv()
    vb[4] = vb[3] + vr[3]
    v_zz(0).start()
    for k in range(2, 4):
        in_add_b(k)
    in_z(1).start()
    q_add_z()
    o_add_x()
    low_in_add_x()
    in_add_z()

    def last_piece(s):
        rows = pl.ds(pl.multiple_of(s * 128, 128), 128)
        pass_copy(s).wait_recv()
        grad_out[rows, :] = (n2[rows, :] + w_in[rows, 1024:2048].astype(F32)).astype(BF16)

    repeat(4, last_piece)
    ou_last()
    o_last()
    v_zz(0).wait_recv()
    vec_out[...] = vb[4] + vr[4]
    q_sum()
    in_sum()
    q_last()
    in_last()
    for count, make in pending:
        for k in range(count):
            make(k).wait_send()


def back_call(arrays):
    any_space = pl.BlockSpec(memory_space=pl.ANY)
    outs = (
        ((512, 1024), BF16),
        ((128, 1024), F32),
        ((32, 4096), F32),
        ((32, 1024), F32),
        ((4, 32, 768), F32),
        ((24, 1024), F32),
    )
    scratch = (
        ((4, 128, 1024), BF16),
        ((512, 1024), F32),
        ((512, 128), F32),
        ((16, 1024), F32),
        ((2048, 1024), BF16),
        ((4, 2, 2, 2, 32, 2048), BF16),
        ((1024, 2048), BF16),
        ((1024, 1024), BF16),
        ((1024, 2048), BF16),
        ((512, 1024), F32),
        ((512, 128), F32),
        ((1024, 512), BF16),
        ((2, 4, 64, 1024), BF16),
        ((4, 4, 128, 768), BF16),
        ((4, 8, 512), F32),
        ((1024, 768), BF16),
        ((1024, 1024), BF16),
        ((4, 512, 256), BF16),
        ((1024, 1024), BF16),
        ((4, 4, 128, 256), BF16),
        ((2, 4, 128, 256), BF16),
        ((4, 2, 2, 128, 1024), BF16),
        ((4, 2, 128, 768), BF16),
        ((4, 128, 768), BF16),
        ((2, 128, 768), BF16),
        ((128, 768), BF16),
        ((2, 2, 2, 128, 256), BF16),
        ((2, 2, 128, 256), BF16),
        ((2, 128, 256), BF16),
        ((128, 256), BF16),
        ((4, 2, 2, 32, 1536), BF16),
        ((4, 2, 32, 1536), BF16),
        ((2, 2, 32, 1536), BF16),
        ((2, 32, 1536), BF16),
        ((2, 2, 2, 2, 32, 512), BF16),
        ((2, 2, 2, 32, 512), BF16),
        ((2, 2, 32, 512), BF16),
        ((2, 32, 512), BF16),
        ((2, 32, 2048), F32),
        ((32, 2048), F32),
        ((2, 2, 2, 2, 32, 1024), BF16),
        ((2, 2, 2, 32, 1024), BF16),
        ((2, 2, 32, 1024), BF16),
        ((2, 32, 1024), BF16),
        ((32, 1024), BF16),
        ((4, 4, 2, 32, 768), BF16),
        ((4, 4, 32, 768), BF16),
        ((2, 4, 32, 768), BF16),
        ((4, 32, 768), BF16),
        ((4, 32, 768), F32),
        ((3, 32, 768), F32),
        ((8, 768), F32),
        ((5, 24, 1024), F32),
        ((5, 24, 1024), F32),
    )
    return pl.pallas_call(
        back_kernel,
        in_specs=[pl.BlockSpec(memory_space=pltpu.SMEM)] + [any_space] * 17,
        out_specs=[pl.BlockSpec(memory_space=pltpu.VMEM)] * len(outs),
        out_shape=[jax.ShapeDtypeStruct(shape, kind) for shape, kind in outs],
        scratch_shapes=[pltpu.VMEM(shape, kind) for shape, kind in scratch]
        + [
            pltpu.SemaphoreType.DMA((96,)),
            pltpu.SemaphoreType.DMA((96,)),
            pltpu.SemaphoreType.DMA((48,)),
        ],
        compiler_params=pltpu.CompilerParams(
            collective_id=1, has_side_effects=True, vmem_limit_bytes=64 * 1024 * 1024 - 65536
        ),
    )(*arrays)


def finish_kernel(sums_ref, qkv_ref, *refs):
    count = 5
    sources, targets = refs[:count], refs[count : 2 * count]
    rows_out, inner_out, query_out, value_out = refs[2 * count : 2 * count + 6], *refs[2 * count + 6 : 2 * count + 9]
    projections = refs[2 * count + 9 : 2 * count + 12]
    stages, sems = refs[2 * count + 12 : 3 * count + 12], refs[3 * count + 12]
    d, me, y = lax.axis_index("dp"), lax.axis_index("ctx"), lax.axis_index("fsdp")
    copies_in = [pltpu.make_async_copy(sources[i], stages[i], sems.at[i]) for i in range(count)]
    copies_out = [pltpu.make_async_copy(stages[i], targets[i], sems.at[count + i]) for i in range(count)]
    for copy in copies_in:
        copy.start()

    def from_lane(values, lane):
        return pltpu.roll(values, (1024 - lane) % 1024, 1)

    own = from_lane(sums_ref[0:8, :], ((d * 4 + me) * 2 + y) * 32)
    for i in range(6):
        rows_out[i][...] = own[i, 0:32]
    row = lax.broadcasted_iota(jnp.int32, (8, 256), 0)
    inner = jnp.sum(jnp.where(row == 2 * d + me // 2, sums_ref[8:16, 0:256], 0.0), axis=0, keepdims=True)
    inner_out[...] = jnp.where(y == 0, inner[:, 0:128], inner[:, 128:256])[0]
    for start, out in ((0, query_out), (512, value_out)):
        out[...] = from_lane(sums_ref[16:24, :], start + d * 64 + y * 32)[0, 0:32]
    for place, out in enumerate(projections):
        for g in range(4):
            start = place * 256 + g * 64
            parts = [qkv_ref[i, :, start : start + 64] for i in range(4)]
            out[:, g * 256 : g * 256 + 256] = jnp.concatenate(parts, 1)
    for i in range(count):
        copies_in[i].wait()
        copies_out[i].start()
    for copy in copies_out:
        copy.wait()


def finish_call(sums, qkv_sum, arrays):
    any_space = pl.BlockSpec(memory_space=pl.ANY)
    vmem = pl.BlockSpec(memory_space=pltpu.VMEM)
    short = jax.ShapeDtypeStruct((32,), F32)
    return pl.pallas_call(
        finish_kernel,
        in_specs=[vmem] * 2 + [any_space] * 5,
        out_specs=[any_space] * 5 + [vmem] * 12,
        out_shape=[jax.ShapeDtypeStruct(a.shape, a.dtype) for a in arrays]
        + [short] * 6
        + [jax.ShapeDtypeStruct((128,), F32), short, short]
        + [jax.ShapeDtypeStruct((32, 1024), F32)] * 3,
        scratch_shapes=[pltpu.VMEM(a.shape, a.dtype) for a in arrays] + [pltpu.SemaphoreType.DMA((16,))],
    )(sums, qkv_sum, *arrays)


def shards(
    states,
    cotangent,
    lengths,
    slot_source,
    query_weight,
    query_bias,
    key_weight,
    value_weight,
    value_bias,
    output_weight,
    output_bias,
    first_gain,
    first_shift,
    inner_weight,
    inner_bias,
    outer_weight,
    outer_bias,
    final_gain,
    final_shift,
):
    seq_dev, block_len, width = states.shape
    n_dp, n_ctx, n_fsdp = (lax.axis_size(name) for name in OWNERS)
    assert (n_ctx, n_fsdp) == (4, 2)
    head_size = width // HEADS
    units = inner_weight.shape[1]
    tokens = seq_dev * block_len
    d, me, y = (lax.axis_index(name) for name in OWNERS)
    x, c = me // 2, me % 2
    own_heads = HEADS // n_ctx
    cols = own_heads * head_size
    aligned = n_dp == own_heads

    def other_half(local):
        return swap(local, "fsdp", 1)

    def ordered(own, other, axis=0):
        return jnp.where(
            y == 0, jnp.concatenate((own, other), axis), jnp.concatenate((other, own), axis)
        )

    def gathered(local, axis=0):
        return ordered(local, other_half(local), axis)

    def head_cols(matrix):
        parts = matrix.reshape(matrix.shape[:-1] + (own_heads, n_ctx, head_size))
        return pick(parts, me, parts.ndim - 2).reshape(matrix.shape[:-1] + (cols,))

    my_seqs = (d * n_fsdp + y) * seq_dev + jnp.arange(seq_dev, dtype=jnp.int32)
    seq_len = jnp.sum(jnp.where(slot_source[None, :] == my_seqs[:, None], lengths[None, :], 0), axis=1)
    places = (me ^ jnp.arange(n_ctx, dtype=jnp.int32))[:, None] * block_len + jnp.arange(
        block_len, dtype=jnp.int32
    )
    key_ok = places.reshape(1, -1) < seq_len[:, None]
    key_bias = jnp.where(key_ok, 0.0, MASKED).astype(BF16)
    key_bias = jnp.broadcast_to(key_bias[:, :, None], key_bias.shape + (128,))
    valid_rows = (places[0][None, :] < seq_len[:, None]).astype(F32).reshape(-1, 1)
    full_len = n_ctx * block_len
    score_flops = 2 * seq_dev * own_heads * full_len * full_len * 128
    block = units // (4 * n_dp)
    wq_own = jnp.concatenate((head_cols(query_weight), head_cols(key_weight), head_cols(value_weight)), 1)

    def share(own):
        return jnp.concatenate((own, swap(own, "ctx", 1)), axis=0)

    def collect(both_rows):
        return both_rows[:tokens] + swap(both_rows[tokens:].astype(BF16), "ctx", 1).astype(F32)

    if aligned:
        (
            encoded,
            flat_all,
            w_qkv,
            w_out,
            w_inner,
            w_outer,
            vecs,
            qkv,
            log_total,
            attended,
            first_norm,
            first_inverse,
            first_low,
            activated,
            slope,
            second_norm,
            second_inverse,
            own_lengths,
        ) = layer_call(
            (
                lengths,
                slot_source,
                states,
                query_weight,
                key_weight,
                value_weight,
                query_bias,
                output_bias,
                first_gain,
                first_shift,
                outer_bias,
                final_gain,
                final_shift,
                value_bias,
                inner_bias,
                output_weight,
                inner_weight,
                outer_weight,
            )
        )
        input_grad, outer_weight_own, inner_weight_own, output_weight_own, qkv_sum, sums = back_call(
            (
                own_lengths,
                cotangent,
                second_norm,
                second_inverse,
                vecs,
                w_outer,
                activated.reshape(4, 2, 2, 2, 32, units // 2),
                slope,
                first_low,
                w_inner,
                first_norm,
                first_inverse,
                attended,
                w_out,
                qkv,
                log_total,
                w_qkv,
                flat_all,
            )
        )
        finished = finish_call(
            sums, qkv_sum, (encoded, input_grad, outer_weight_own, inner_weight_own, output_weight_own)
        )
        encoded, input_grad, outer_weight_own, inner_weight_own, output_weight_own = finished[:5]
        final_gain_own, final_shift_own, outer_bias_own, first_gain_own, first_shift_own, output_bias_own = finished[5:11]
        inner_bias_own, query_bias_own, value_bias_own, query_own, key_own, value_own = finished[11:]
        return (
            encoded.reshape(states.shape),
            input_grad.reshape(states.shape),
            query_own,
            query_bias_own,
            key_own,
            value_own,
            value_bias_own,
            output_weight_own,
            output_bias_own,
            first_gain_own,
            first_shift_own,
            inner_weight_own,
            inner_bias_own,
            outer_weight_own,
            outer_bias_own,
            final_gain_own,
            final_shift_own,
        )

    def other_half(local):
        return swap(local, "fsdp", 1)

    def ordered(own, other, axis=0):
        return jnp.where(
            y == 0, jnp.concatenate((own, other), axis), jnp.concatenate((other, own), axis)
        )

    def gathered(local, axis=0):
        return ordered(local, other_half(local), axis)

    wide = (query_bias, value_bias, output_bias, first_gain, first_shift, outer_bias, final_gain, final_shift)
    packed = jnp.concatenate([v.reshape(1, -1) for v in wide] + [inner_bias.reshape(-1, width // 2)])
    other_packed = other_half(packed)
    both = jnp.where(y == 0, jnp.stack((packed, other_packed)), jnp.stack((other_packed, packed)))
    b_query, b_value, b_out, g_first, s_first, b_outer, g_final, s_final = (
        both[:, i].reshape(width).astype(F32) for i in range(8)
    )
    b_inner = both[:, 8:].reshape(2 * n_dp, 2, -1)
    b_inner = pick(b_inner, c, 1).reshape(-1).astype(F32)
    w_qkv = gathered(wq_own)
    b_qkv = jnp.concatenate((head_cols(b_query), jnp.zeros((cols,), F32), head_cols(b_value)))

    from_x = swap(states, "ctx", 2)
    from_core = swap(states, "ctx", 1)
    from_far = swap(from_x, "ctx", 1)
    flat_all = jnp.stack((states, from_core, from_x, from_far)).reshape(-1, width)

    w_out = gathered(pick(output_weight.reshape(-1, 2, 2, head_size, width), c, 2))
    w_out = jnp.concatenate((pick(w_out, x, 1), pick(w_out, 1 - x, 1)), 0).reshape(-1, width)
    w_inner = gathered(
        pick(inner_weight.reshape(width // 2, 2 * n_dp, 2, block), c, 2).reshape(width // 2, -1)
    )
    w_outer = gathered(pick(outer_weight.reshape(n_dp, 2, block, width), c, 1).reshape(-1, width))

    qkv = (matmul(flat_all, w_qkv) + b_qkv).astype(BF16)
    qkv = qkv.reshape(n_ctx, seq_dev, block_len, 3 * cols)
    attended_all, log_total = attention_call(
        attend_kernel,
        (qkv, key_bias),
        (
            jax.ShapeDtypeStruct((n_ctx, seq_dev, block_len, cols), BF16),
            jax.ShapeDtypeStruct((seq_dev, 8, full_len), F32),
        ),
        2 * score_flops,
    )
    near = attended_all[:2].reshape(-1, cols)
    far = swap(attended_all[2:], "ctx", 2).reshape(-1, cols)
    attended = jnp.concatenate((near, far), axis=1)
    first_sum = states.reshape(-1, width).astype(F32) + collect(matmul(attended, w_out)) + b_out
    first_out, first_norm, first_inverse = norm_rows(first_sum, g_first, s_first)
    first_low = share(first_out.astype(BF16))
    hidden = matmul(first_low, w_inner) + b_inner
    below = 0.5 * (1.0 + lax.erf(hidden * math.sqrt(0.5)))
    bell = jnp.exp(-0.5 * hidden * hidden) * (1.0 / math.sqrt(2 * math.pi))
    slope = (below + hidden * bell).astype(BF16)
    activated = (hidden * below).astype(BF16)
    second_sum = first_out + collect(matmul(activated, w_outer)) + b_outer
    second_out, second_norm, second_inverse = norm_rows(second_sum, g_final, s_final)
    encoded = (second_out * valid_rows).astype(BF16).reshape(states.shape)

    out_grad = cotangent.reshape(-1, width).astype(F32) * valid_rows
    final_gain_part = jnp.sum(out_grad * second_norm, axis=0)
    final_shift_part = jnp.sum(out_grad, axis=0)
    second_grad = norm_back(out_grad, second_norm, second_inverse, g_final)
    outer_round_own = second_grad.astype(BF16)
    outer_bias_part = col_sum(outer_round_own)
    outer_round = share(outer_round_own)
    outer_weight_part = matmul_tn(activated, outer_round).astype(BF16)
    hidden_grad = (matmul_nt(outer_round, w_outer) * slope.astype(F32)).astype(BF16)
    inner_bias_part = col_sum(hidden_grad)
    inner_weight_part = matmul_tn(first_low, hidden_grad).astype(BF16)
    first_grad = second_grad + collect(matmul_nt(hidden_grad, w_inner))
    first_gain_part = jnp.sum(first_grad * first_norm, axis=0)
    first_shift_part = jnp.sum(first_grad, axis=0)
    sum_grad = norm_back(first_grad, first_norm, first_inverse, g_first)
    branch_own = sum_grad.astype(BF16)
    output_bias_part = col_sum(branch_own)
    branch_grad = share(branch_own)
    output_weight_part = matmul_tn(attended, branch_grad).astype(BF16)
    attended_grad = matmul_nt(branch_grad, w_out).astype(BF16)
    near_grad = attended_grad[:, :cols]
    far_grad = swap(attended_grad[:, cols:], "ctx", 2)
    attended_grad_all = jnp.concatenate((near_grad, far_grad), 0).reshape(n_ctx, seq_dev, block_len, cols)
    (qkv_grad,) = attention_call(
        attend_back_kernel,
        (qkv, key_bias, log_total, attended_grad_all),
        (jax.ShapeDtypeStruct(qkv.shape, BF16),),
        5 * score_flops,
    )
    flat_grad = qkv_grad.reshape(-1, 3 * cols)
    bias_part = col_sum(flat_grad)
    qkv_weight_part = matmul_tn(flat_all, flat_grad).astype(BF16)
    input_part = matmul_nt(flat_grad, w_qkv).reshape(n_ctx, tokens, width)
    to_core = swap(jnp.stack((input_part[1], input_part[3])).astype(BF16), "ctx", 1)
    to_x = swap((input_part[2] + to_core[1].astype(F32)).astype(BF16), "ctx", 2)
    input_grad = sum_grad + input_part[0] + to_core[0].astype(F32) + to_x.astype(F32)
    input_grad = input_grad.astype(BF16).reshape(states.shape)

    token_sums = jnp.stack(
        (final_gain_part, final_shift_part, outer_bias_part, first_gain_part, first_shift_part, output_bias_part)
    )
    def placed_heads(part):
        whole = jnp.zeros(part.shape[:-1] + (own_heads, n_ctx, head_size), part.dtype)
        part = part.reshape(part.shape[:-1] + (own_heads, 1, head_size))
        return lax.dynamic_update_slice_in_dim(whole, part, me, part.ndim - 2).reshape(
            part.shape[:-3] + (width,)
        )

    def placed_units(part, axis):
        split = part.shape[:axis] + (2 * n_dp, 1, block) + part.shape[axis + 1 :]
        whole = jnp.zeros(split[: axis + 1] + (2,) + split[axis + 2 :], part.dtype)
        whole = lax.dynamic_update_slice_in_dim(whole, part.reshape(split), c, axis + 1)
        return whole.reshape(part.shape[:axis] + (units,) + part.shape[axis + 1 :])

    def placed_rows(part):
        part = part.reshape(2, own_heads, 1, 1, head_size, width)
        whole = jnp.zeros((own_heads, 2, 2, head_size, width), part.dtype)
        whole = lax.dynamic_update_slice(whole, part[0], (0, x, c, 0, 0))
        whole = lax.dynamic_update_slice(whole, part[1], (0, 1 - x, c, 0, 0))
        return whole.reshape(width, width)

    def owned(part):
        return lax.psum_scatter(part, OWNERS, scatter_dimension=0, tiled=True).astype(F32)

    qkv_weights = [owned(placed_heads(qkv_weight_part[:, i * cols : (i + 1) * cols])) for i in range(3)]
    query_bias_own = owned(placed_heads(bias_part[:cols]))
    value_bias_own = owned(placed_heads(bias_part[2 * cols :]))
    output_weight_own = owned(placed_rows(output_weight_part))
    inner_weight_own = owned(placed_units(inner_weight_part, 1))
    inner_bias_own = owned(placed_units(inner_bias_part, 0))
    outer_weight_own = owned(placed_units(outer_weight_part, 0))
    sums = [owned(token_sums[i]) for i in range(6)]

    return (
        encoded,
        input_grad,
        qkv_weights[0],
        query_bias_own,
        qkv_weights[1],
        qkv_weights[2],
        value_bias_own,
        output_weight_own,
        sums[5],
        sums[3],
        sums[4],
        inner_weight_own,
        inner_bias_own,
        outer_weight_own,
        sums[2],
        sums[0],
        sums[1],
    )


def solution(mesh):
    tokens = P(("dp", "fsdp"), "ctx", None)
    matrix, vector = P("fsdp", None), P("fsdp")
    own_matrix, own_vector = P(OWNERS, None), P(OWNERS)
    return jax.shard_map(
        shards,
        mesh=mesh,
        in_specs=(
            tokens,
            tokens,
            P(),
            P(),
            matrix,
            vector,
            matrix,
            matrix,
            vector,
            matrix,
            vector,
            vector,
            vector,
            matrix,
            vector,
            matrix,
            vector,
            vector,
            vector,
        ),
        out_specs=(
            tokens,
            tokens,
            own_matrix,
            own_vector,
            own_matrix,
            own_matrix,
            own_vector,
            own_matrix,
            own_vector,
            own_vector,
            own_vector,
            own_matrix,
            own_vector,
            own_matrix,
            own_vector,
            own_vector,
            own_vector,
        ),
        check_vma=False,
    )
```

```python
import functools
import math

import jax
import jax.numpy as jnp
from jax import lax
from jax.experimental import pallas as pl
from jax.experimental.pallas import tpu as pltpu
from jax.sharding import PartitionSpec as P

HEADS = 16
EPS = 1e-12
MASKED = -1e30
F32 = jnp.float32
BF16 = jnp.bfloat16
OWNERS = ("dp", "ctx", "fsdp")


def swap(value, axis, mask):
    pairs = [(source, source ^ mask) for source in range(lax.axis_size(axis))]
    return lax.ppermute(value, axis, pairs)


def pick(array, index, axis):
    return lax.dynamic_index_in_dim(array, index, axis, keepdims=False)


def add_low(left, right):
    return (left.astype(F32) + right.astype(F32)).astype(BF16)


def matmul(left, right):
    return jnp.dot(left, right, preferred_element_type=F32)


def matmul_tn(left, right):
    return lax.dot_general(left, right, (((0,), (0,)), ((), ())), preferred_element_type=F32)


def matmul_nt(left, right):
    return lax.dot_general(left, right, (((1,), (1,)), ((), ())), preferred_element_type=F32)


def col_sum(matrix):
    return jnp.sum(matrix.astype(F32), axis=0)


def norm_rows(summed, scale_vec, shift_vec):
    row_mean = jnp.mean(summed, axis=-1, keepdims=True)
    centered = summed - row_mean
    inverse = lax.rsqrt(jnp.mean(centered * centered, axis=-1, keepdims=True) + EPS)
    normed = centered * inverse
    return (normed * scale_vec + shift_vec, normed, inverse)


def norm_back(upstream, normed, inverse, scale_vec):
    scaled = upstream * scale_vec
    return inverse * (
        scaled
        - jnp.mean(scaled, axis=-1, keepdims=True)
        - normed * jnp.mean(scaled * normed, axis=-1, keepdims=True)
    )


def half_lanes(pair, which):
    lane = lax.broadcasted_iota(jnp.int32, pair.shape, 1)
    keep = lane < 64 if which == 0 else lane >= 64
    return jnp.where(keep, pair, jnp.zeros_like(pair))


def with_flag(pair, flag, which):
    lane = lax.broadcasted_iota(jnp.int32, pair.shape, 1)
    keep = lane < 64 if which == 0 else lane >= 64
    spot = lane == (64 if which == 0 else 0)
    return jnp.where(keep, pair, jnp.where(spot, flag, jnp.zeros_like(pair)))


def attend_kernel(qkv_ref, bias_ref, out_ref, lse_ref):
    width = out_ref.shape[-1]
    rows = out_ref.shape[0] * out_ref.shape[2]
    bias = bias_ref[0]
    lane = lax.broadcasted_iota(jnp.int32, (rows, 128), 1)
    one = jnp.ones((rows, 128), BF16)
    totals = jnp.zeros((rows, 128), F32)
    for pair_index in range(width // 128):
        first = pair_index * 128
        query = qkv_ref[:, 0, :, first : first + 128].reshape(rows, 128)
        key = qkv_ref[:, 0, :, width + first : width + first + 128].reshape(rows, 128)
        value = qkv_ref[:, 0, :, 2 * width + first : 2 * width + first + 128].reshape(rows, 128)
        query = (query.astype(F32) * 0.125).astype(BF16)
        mixed = []
        for which in range(2):
            scores = matmul_nt(with_flag(query, one, which), with_flag(key, bias, which))
            top = jnp.max(scores, axis=-1, keepdims=True)
            weight = jnp.exp(scores - top)
            total = jnp.sum(weight, axis=-1, keepdims=True)
            mixed.append(matmul(weight.astype(BF16), value) * (1.0 / total))
            totals = jnp.where(lane == 2 * pair_index + which, top + jnp.log(total), totals)
        joined = jnp.where(lane < 64, mixed[0], mixed[1]).astype(BF16)
        out_ref[:, 0, :, first : first + 128] = joined.reshape(out_ref.shape[0], out_ref.shape[2], 128)
    lse_ref[0] = jnp.transpose(totals)[:8]


def attend_back_kernel(qkv_ref, bias_ref, lse_ref, grad_ref, out_ref):
    width = grad_ref.shape[-1]
    shape = (grad_ref.shape[0], grad_ref.shape[2], 128)
    rows = shape[0] * shape[1]
    bias = bias_ref[0]
    lane = lax.broadcasted_iota(jnp.int32, (rows, 128), 1)
    one = jnp.ones((rows, 128), BF16)
    for pair_index in range(width // 128):
        first = pair_index * 128
        query = qkv_ref[:, 0, :, first : first + 128].reshape(rows, 128)
        key = qkv_ref[:, 0, :, width + first : width + first + 128].reshape(rows, 128)
        value = qkv_ref[:, 0, :, 2 * width + first : 2 * width + first + 128].reshape(rows, 128)
        grad = grad_ref[:, 0, :, first : first + 128].reshape(rows, 128)
        query = (query.astype(F32) * 0.125).astype(BF16)
        query_parts, key_parts, value_parts = [], [], []
        for which in range(2):
            spot = 2 * pair_index + which
            log_total = lse_ref[0, spot : spot + 1, :]
            scores = matmul_nt(with_flag(key, bias, which), with_flag(query, one, which))
            probs = jnp.exp(scores - log_total)
            probs_grad = matmul_nt(value, half_lanes(grad, which))
            value_parts.append(matmul(probs.astype(BF16), grad))
            row_dot = jnp.sum(probs * probs_grad, axis=0, keepdims=True)
            score_grad = (probs * (probs_grad - row_dot)).astype(BF16)
            key_parts.append(matmul(score_grad, query))
            query_parts.append(matmul_tn(score_grad, key) * 0.125)
        for place, parts in enumerate((query_parts, key_parts, value_parts)):
            joined = jnp.where(lane < 64, parts[0], parts[1]).astype(BF16)
            start = place * width + first
            out_ref[:, 0, :, start : start + 128] = joined.reshape(shape)


def attention_call(kernel, arrays, outs, flops):
    def whole(array):
        shape = array.shape
        if len(shape) == 4:
            return pl.BlockSpec((shape[0], 1) + shape[2:], lambda s: (0, s, 0, 0))
        return pl.BlockSpec((1,) + shape[1:], lambda s: (s, 0, 0))

    return pl.pallas_call(
        kernel,
        grid=(arrays[0].shape[1],),
        in_specs=[whole(array) for array in arrays],
        out_specs=[whole(out) for out in outs],
        out_shape=outs,
        compiler_params=pltpu.CompilerParams(vmem_limit_bytes=40 * 1024 * 1024),
        cost_estimate=pl.CostEstimate(flops=flops, bytes_accessed=8 << 20, transcendentals=0),
    )(*arrays)


MESH = pl.DeviceIdType.MESH


def repeat(count, body):
    def step(index, carry):
        body(index)
        return carry

    lax.fori_loop(0, count, step, 0)


class Slots:
    def __init__(self):
        self.total = 0

    def take(self, count=1):
        first = self.total
        self.total += count
        return first


def read_lengths(slot_ref, length_ref, lens_ref, first):
    def step(t, totals):
        source, count = slot_ref[t], length_ref[t]
        return tuple(total + jnp.where(source == first + i, count, 0) for i, total in enumerate(totals))

    totals = lax.fori_loop(0, slot_ref.shape[0], step, (jnp.int32(0),) * 4)
    for i in range(4):
        lens_ref[i] = totals[i]


def layer_kernel(
    length_ref,
    slot_ref,
    states,
    query_own,
    key_own,
    value_own,
    vec_query,
    vec_out,
    vec_gain,
    vec_shift,
    vec_outer,
    vec_gain2,
    vec_shift2,
    vec_value,
    vec_inner,
    wo_own,
    wi_own,
    wu_own,
    encoded_out,
    o_states,
    o_wq,
    o_wout,
    o_win,
    o_wou,
    o_vecs,
    o_qkv,
    o_lse,
    o_att,
    o_norm,
    o_inv,
    o_low,
    o_act,
    o_slope,
    o_norm2,
    o_inv2,
    lens_ref,
    st_all,
    wq_all,
    vec_all,
    w_out,
    w_in,
    w_ou,
    vecs,
    qkv,
    lse,
    att,
    att_far,
    part_far,
    part_in,
    part_far2,
    part_in2,
    first_norm,
    first_inv,
    first_out,
    low2,
    act,
    slope,
    acc,
    second_inv,
    chosen,
    own_three,
    send,
    recv,
    local,
):
    d, me, y = lax.axis_index("dp"), lax.axis_index("ctx"), lax.axis_index("fsdp")
    x, c = me // 2, me % 2
    to_core = {"ctx": me + 1 - 2 * c}
    to_x = {"ctx": (me + 2) % 4}
    to_y = {"fsdp": 1 - y}
    to_z = {"dp": d + 1 - 2 * (d % 2)}
    to_zz = {"dp": (d + 2) % 4}
    to_far = {"ctx": 3 - me}
    slots = Slots()
    pending = []

    def remote(src, dst, slot, device):
        return pltpu.make_async_remote_copy(
            src_ref=src,
            dst_ref=dst,
            send_sem=send.at[slot],
            recv_sem=recv.at[slot],
            device_id=device,
            device_id_type=MESH,
        )

    def at_end(count, make):
        pending.append((count, make))

    local_slots = Slots()

    def fetch(src, dst):
        copy = pltpu.make_async_copy(src, dst, local.at[local_slots.take()])
        copy.start()
        return copy

    kept = []

    def keep(src, dst):
        kept.append(fetch(src, dst))

    three = [fetch(src, own_three.at[i]) for i, src in enumerate((query_own, key_own, value_own))]
    barrier = pltpu.get_barrier_semaphore()
    for device in (to_core, to_x, to_y, to_z, to_zz, to_far):
        pl.semaphore_signal(barrier, inc=1, device_id=device, device_id_type=MESH)
    row = lax.broadcasted_iota(jnp.int32, (1024, 256), 0)
    col = lax.broadcasted_iota(jnp.int32, (1024, 256), 1)
    chosen[...] = jnp.where(row == (col // 64) * 256 + me * 64 + col % 64, 1.0, 0.0).astype(BF16)
    read_lengths(slot_ref, length_ref, lens_ref, (2 * d + y) * 4)
    singles = (vec_query, vec_out, vec_gain, vec_shift, vec_outer, vec_gain2, vec_shift2, vec_value)
    vec_all[y, 0:8] = jnp.concatenate([single[...].astype(F32).reshape(1, 512) for single in singles], 0)
    inner_rows = vec_inner[...].astype(F32).reshape(4, 512)
    vec_all[y, 8:16] = jnp.concatenate((inner_rows, jnp.zeros((4, 512), F32)), 0)
    pl.semaphore_wait(barrier, 6)

    first = slots.take(4)
    state_x = lambda s: remote(states.at[s], st_all.at[2, s], first + s, to_x)
    second = slots.take(4)
    state_core = lambda s: remote(states.at[s], st_all.at[1, s], second + s, to_core)
    third = slots.take(4)
    state_far = lambda s: remote(st_all.at[2, s], st_all.at[3, s], third + s, to_core)
    p = d % 2
    wq_slot = slots.take(2)

    def wq_copy(k):
        here = wq_all.at[pl.ds(pl.multiple_of(y * 512 + p * 256 + k * 128, 128), 128)]
        return remote(here, here, wq_slot + k, to_y)

    wq_pass_slot = slots.take(2)

    def wq_pass(k):
        here = wq_all.at[pl.ds(pl.multiple_of((1 - y) * 512 + p * 256 + k * 128, 128), 128)]
        return remote(here, here, wq_pass_slot + k, to_z)

    vec_slot = slots.take()
    vec_copy = remote(vec_all.at[y], vec_all.at[y], vec_slot, to_y)
    for s in range(4):
        state_x(s).start()
    vec_copy.start()
    for s in range(4):
        state_core(s).start()
    at_end(4, state_x)
    at_end(4, state_core)
    at_end(4, state_far)
    at_end(2, wq_copy)
    at_end(2, wq_pass)
    at_end(1, lambda _: vec_copy)

    wo_slot = slots.take(2)

    def wo_copy(side):
        src = wo_own.at[pl.ds(pl.multiple_of(p * 256 + side * 128 + c * 64, 64), 64)]
        return remote(src, w_out.at[x if side == 0 else 1 - x, 2 * y + p], wo_slot + side, to_y)

    wo_pass_slot = slots.take(2)

    def wo_pass(side):
        here = w_out.at[x if side == 0 else 1 - x, 2 * (1 - y) + p]
        return remote(here, here, wo_pass_slot + side, to_z)

    wi_slot = slots.take(8)

    def wi_copy(b):
        src = wi_own.at[
            pl.ds(pl.multiple_of(x * 256, 256), 256), pl.ds(pl.multiple_of((2 * b + c) * 256, 256), 256)
        ]
        dst = w_in.at[
            pl.ds(pl.multiple_of(y * 512 + x * 256, 256), 256), pl.ds(pl.multiple_of(b * 256, 256), 256)
        ]
        return remote(src, dst, wi_slot + b, to_y)

    wi_pass_slot = slots.take(8)

    def wi_pass(b):
        here = w_in.at[
            pl.ds(pl.multiple_of((1 - y) * 512 + x * 256, 256), 256),
            pl.ds(pl.multiple_of(b * 256, 256), 256),
        ]
        return remote(here, here, wi_pass_slot + b, to_x)

    wu_slot = slots.take(4)

    def wu_copy(k):
        side, half = k // 2, k % 2
        start, rows = (0, 128) if half == 0 else (128 + x * 64, 64)
        src = wu_own.at[pl.ds(pl.multiple_of((p * 4 + side * 2 + c) * 256 + start, 64), rows)]
        dst = w_ou.at[pl.ds(pl.multiple_of((4 * y + 2 * p + side) * 256 + start, 64), rows)]
        return remote(src, dst, wu_slot + k, to_y)

    wu_side_slot = slots.take(2)

    def wu_side(side):
        start = (4 * (1 - y) + 2 * p + side) * 256 + 128 + x * 64
        here = w_ou.at[pl.ds(pl.multiple_of(start, 64), 64)]
        return remote(here, here, wu_side_slot + side, to_x)

    wu_pass_slot = slots.take(4)

    def wu_pass(k):
        side, half = k // 2, k % 2
        here = w_ou.at[
            pl.ds(pl.multiple_of((4 * (1 - y) + 2 * p + side) * 256 + half * 128, 128), 128)
        ]
        return remote(here, here, wu_pass_slot + k, to_z)

    for place in range(3):
        three[place].wait()
        made = matmul(own_three[place], chosen[...]).astype(BF16)
        wq_all[pl.ds(pl.multiple_of(y * 512, 512), 512), place * 256 : place * 256 + 256] = made
    for k in range(2):
        wq_copy(k).start()
    for side in range(2):
        wo_copy(side).start()
    for b in range(8):
        wi_copy(b).start()
    for k in range(4):
        wu_copy(k).start()
    for count, make in ((2, wo_copy), (2, wo_pass), (8, wi_copy), (8, wi_pass), (4, wu_copy), (2, wu_side), (4, wu_pass)):
        at_end(count, make)

    own_early = [
        fetch(states, st_all.at[0]),
    ]
    own_out = []
    for half in range(2):
        for side in range(2):
            src = wo_own.at[pl.ds(pl.multiple_of(half * 256 + side * 128 + c * 64, 64), 64)]
            own_out.append(fetch(src, w_out.at[x if side == 0 else 1 - x, 2 * y + half]))
    own_late = []
    for b in range(8):
        src = wi_own.at[:, pl.ds(pl.multiple_of((2 * b + c) * 256, 256), 256)]
        dst = w_in.at[pl.ds(pl.multiple_of(y * 512, 512), 512), pl.ds(b * 256, 256)]
        own_late.append(fetch(src, dst))
    for half in range(2):
        for side in range(2):
            src = wu_own.at[pl.ds(pl.multiple_of((half * 4 + side * 2 + c) * 256, 256), 256)]
            dst = w_ou.at[pl.ds(pl.multiple_of((4 * y + 2 * half + side) * 256, 256), 256)]
            own_late.append(fetch(src, dst))

    state_x(0).wait_recv()
    state_far(0).start()
    for k in range(2):
        wq_copy(k).wait_recv()
        wq_pass(k).start()
    state_x(1).wait_recv()
    state_far(1).start()
    for copy in own_early:
        copy.wait()
    vec_copy.wait_recv()
    vecs[:, :512] = vec_all[0]
    vecs[:, 512:] = vec_all[1]
    for k in range(2):
        wq_pass(k).wait_recv()

    att_slot = slots.take(8)

    def att_copy(s, j):
        rows = pl.ds(pl.multiple_of(j * 512 + s * 128, 128), 128)
        return remote(att_far.at[j, s], att.at[rows, 256:512], att_slot + 2 * s + j, to_x)

    at_end(8, lambda k: att_copy(k // 2, k % 2))
    biases = matmul(vecs[0:8, :].astype(BF16), chosen[...])
    q_bias, v_bias = biases[0:1], biases[7:8]

    def key_flags(s):
        pieces = []
        for j in range(4):
            position = lax.broadcasted_iota(jnp.int32, (128, 128), 0)
            place = me + 1 - 2 * c if j == 1 else me
            place = (place + 2) % 4 if j == 2 else place
            place = 3 - me if j == 3 else place
            pieces.append(jnp.where(position + place * 128 < lens_ref[s], 0.0, MASKED))
        return jnp.concatenate(pieces, 0).astype(BF16)

    def pass_inner(b):
        wi_copy(b).wait_recv()
        wi_pass(b).start()

    def attention(s):
        @pl.when(s < 2)
        def _():
            state_x(s + 2).wait_recv()
            state_far(s + 2).start()

        @pl.when(s == 1)
        def _():
            for side in range(2):
                wo_copy(side).wait_recv()
                wo_pass(side).start()

        @pl.when((s == 1) | (s == 2))
        def _():
            for k in range(2):
                pass_inner(2 * (s - 1) + k)

        @pl.when(s == 3)
        def _():
            pass_inner(4)

        state_core(s).wait_recv()
        state_far(s).wait_recv()
        rows = st_all[:, s].reshape(512, 1024)
        for place in range(3):
            made = matmul(rows, wq_all[:, place * 256 : place * 256 + 256])
            made = made + q_bias if place == 0 else made
            made = made + v_bias if place == 2 else made
            qkv[:, s, :, place * 256 : place * 256 + 256] = made.astype(BF16).reshape(4, 128, 256)
        bias = key_flags(s)
        lane = lax.broadcasted_iota(jnp.int32, (512, 128), 1)
        one = jnp.ones((512, 128), BF16)
        totals = jnp.zeros((512, 128), F32)
        for pair in range(2):
            base = pair * 128
            query = qkv[:, s, :, base : base + 128].reshape(512, 128)
            key = qkv[:, s, :, 256 + base : 384 + base].reshape(512, 128)
            value = qkv[:, s, :, 512 + base : 640 + base].reshape(512, 128)
            query = (query.astype(F32) * 0.125).astype(BF16)
            mixed = []
            for which in range(2):
                scores = matmul_nt(with_flag(query, one, which), with_flag(key, bias, which))
                top = jnp.max(scores, axis=-1, keepdims=True)
                weight = jnp.exp(scores - top)
                total = jnp.sum(weight, axis=-1, keepdims=True)
                mixed.append(matmul(weight.astype(BF16), value) * (1.0 / total))
                totals = jnp.where(lane == 2 * pair + which, top + jnp.log(total), totals)
            joined = jnp.where(lane < 64, mixed[0], mixed[1]).astype(BF16)
            for j in range(2):
                rows_j = pl.ds(pl.multiple_of(j * 512 + s * 128, 128), 128)
                att[rows_j, base : base + 128] = joined[j * 128 : j * 128 + 128]
                att_far[j, s, :, base : base + 128] = joined[256 + j * 128 : 384 + j * 128]
        for j in range(2):
            att_copy(s, j).start()
        lse[s] = jnp.transpose(totals)[:8]

    repeat(4, attention)
    for src, dst in ((st_all, o_states), (wq_all, o_wq), (vecs, o_vecs), (qkv, o_qkv), (lse, o_lse)):
        keep(src, dst)

    for b in range(5, 7):
        pass_inner(b)
    for copy in own_out:
        copy.wait()
    for side in range(2):
        wo_pass(side).wait_recv()
    for s in range(4):
        for j in range(2):
            att_copy(s, j).wait_recv()
    keep(att, o_att)
    keep(w_out, o_wout)
    out_slot = slots.take(4)

    def out_copy(n):
        return remote(part_far.at[n], part_in.at[n], out_slot + n, to_core)

    at_end(4, out_copy)
    for n in range(4):
        right = w_out[:, :, :, n * 256 : n * 256 + 256].reshape(512, 256)
        part_far[n] = matmul(att[512:], right).astype(BF16)
        out_copy(n).start()
    pass_inner(7)
    for n in range(4):
        right = w_out[:, :, :, n * 256 : n * 256 + 256].reshape(512, 256)
        made = matmul(att[:512], right) + vecs[1:2, n * 256 : n * 256 + 256]
        made = made + st_all[0, :, :, n * 256 : n * 256 + 256].astype(F32).reshape(512, 256)
        out_copy(n).wait_recv()
        first_norm[:, n * 256 : n * 256 + 256] = made + part_in[n].astype(F32)

    low_slot = slots.take(4)

    def low_copy(k):
        src = low2.at[pl.ds(pl.multiple_of(k * 128, 128), 128)]
        dst = low2.at[pl.ds(pl.multiple_of(512 + k * 128, 128), 128)]
        return remote(src, dst, low_slot + k, to_core)

    at_end(4, low_copy)

    def norm_first(k):
        for half in range(2):
            rows = pl.ds(pl.multiple_of(k * 128 + half * 64, 64), 64)
            made, normed, inverse = norm_rows(first_norm[rows, :], vecs[2:3, :], vecs[3:4, :])
            first_norm[rows, :] = normed
            first_inv[rows, :] = jnp.broadcast_to(inverse, (64, 128))
            first_out[rows, :] = made
            low2[rows, :] = made.astype(BF16)
        low_copy(k).start()

    repeat(4, norm_first)

    def share_outer(k):
        wu_copy(k).wait_recv()
        wu_side(k // 2).start()

    def pass_outer(k):
        if k % 2:
            wu_side(k // 2).wait_recv()
        else:
            wu_copy(k).wait_recv()
        wu_pass(k).start()

    pass_outer(0)
    for k in range(4):
        low_copy(k).wait_recv()
    for copy in own_late:
        copy.wait()
    for src, dst in ((first_norm, o_norm), (first_inv, o_inv), (low2, o_low)):
        keep(src, dst)

    def unit_block(b):
        for step, action, k in ((1, share_outer, 1), (3, pass_outer, 1), (4, pass_outer, 2), (6, share_outer, 3)):

            @pl.when(b == step)
            def _():
                action(k)

        wi_pass(b).wait_recv()
        here = pl.ds(pl.multiple_of(b * 256, 256), 256)
        spot = pl.ds(pl.multiple_of((b // 4) * 512 + c * 256, 256), 256)
        row = vecs[pl.ds(8 + b % 4, 1), spot]
        for m in range(2):
            hidden = matmul(low2[m * 512 : m * 512 + 512, :], w_in[:, here]) + row
            below = 0.5 * (1.0 + lax.erf(hidden * math.sqrt(0.5)))
            bell = jnp.exp(-0.5 * hidden * hidden) * (1.0 / math.sqrt(2 * math.pi))
            act[m * 512 : m * 512 + 512, here] = (hidden * below).astype(BF16)
            slope[m * 512 : m * 512 + 512, here] = (below + hidden * bell).astype(BF16)

    repeat(8, unit_block)
    for src, dst in ((act, o_act), (slope, o_slope), (w_in, o_win)):
        keep(src, dst)
    mine = pl.ds(pl.multiple_of(y * 1024, 1024), 1024)
    theirs = pl.ds(pl.multiple_of((1 - y) * 1024, 1024), 1024)
    pass_outer(3)

    def outer_own(n):
        here = pl.ds(pl.multiple_of(n * 256, 256), 256)
        for m in range(2):
            acc[m * 512 : m * 512 + 512, here] = matmul(
                act[m * 512 : m * 512 + 512, mine], w_ou[mine, here]
            )

    repeat(4, outer_own)
    for k in range(4):
        wu_pass(k).wait_recv()
    keep(w_ou, o_wou)
    sum_slot = slots.take(4)

    def sum_copy(n):
        return remote(part_far2.at[n], part_in2.at[n], sum_slot + n, to_core)

    at_end(4, sum_copy)

    def outer_far(n):
        here = pl.ds(pl.multiple_of(n * 256, 256), 256)
        made = acc[512:, here] + matmul(act[512:, theirs], w_ou[theirs, here])
        part_far2[n] = made.astype(BF16)
        sum_copy(n).start()

    repeat(4, outer_far)

    def outer_near(n):
        here = pl.ds(pl.multiple_of(n * 256, 256), 256)
        made = acc[:512, here] + matmul(act[:512, theirs], w_ou[theirs, here])
        made = made + first_out[:, here] + vecs[4:5, here]
        sum_copy(n).wait_recv()
        acc[:512, here] = made + part_in2[n].astype(F32)

    repeat(4, outer_near)

    def norm_second(k):
        valid_place = lax.broadcasted_iota(jnp.int32, (128, 1), 0) + me * 128
        valid = jnp.where(valid_place < lens_ref[k], 1.0, 0.0)
        for half in range(2):
            rows = pl.ds(pl.multiple_of(k * 128 + half * 64, 64), 64)
            made, normed, inverse = norm_rows(acc[rows, :], vecs[5:6, :], vecs[6:7, :])
            encoded_out[rows, :] = (made * valid[half * 64 : half * 64 + 64]).astype(BF16)
            acc[rows, :] = normed
            second_inv[rows, :] = jnp.broadcast_to(inverse, (64, 128))

    repeat(4, norm_second)
    keep(acc.at[:512], o_norm2)
    keep(second_inv, o_inv2)
    for copy in kept:
        copy.wait()
    for count, make in pending:
        for k in range(count):
            make(k).wait_send()


def layer_call(arrays):
    any_space = pl.BlockSpec(memory_space=pl.ANY)
    v = pltpu.VMEM
    return pl.pallas_call(
        layer_kernel,
        in_specs=[pl.BlockSpec(memory_space=pltpu.SMEM)] * 2
        + [any_space] * 4
        + [pl.BlockSpec(memory_space=pltpu.VMEM)] * 9
        + [any_space] * 3,
        out_specs=[pl.BlockSpec(memory_space=pltpu.VMEM)] + [any_space] * 16 + [pl.BlockSpec(memory_space=pltpu.SMEM)],
        out_shape=[
            jax.ShapeDtypeStruct(shape, kind)
            for shape, kind in (
                ((512, 1024), BF16),
                ((4, 4, 128, 1024), BF16),
                ((1024, 768), BF16),
                ((2, 4, 64, 1024), BF16),
                ((1024, 2048), BF16),
                ((2048, 1024), BF16),
                ((16, 1024), F32),
                ((4, 4, 128, 768), BF16),
                ((4, 8, 512), F32),
                ((1024, 512), BF16),
                ((512, 1024), F32),
                ((512, 128), F32),
                ((1024, 1024), BF16),
                ((1024, 2048), BF16),
                ((1024, 2048), BF16),
                ((512, 1024), F32),
                ((512, 128), F32),
                ((4,), jnp.int32),
            )
        ],
        scratch_shapes=[
            v((4, 4, 128, 1024), BF16),
            v((1024, 768), BF16),
            v((2, 16, 512), F32),
            v((2, 4, 64, 1024), BF16),
            v((1024, 2048), BF16),
            v((2048, 1024), BF16),
            v((16, 1024), F32),
            v((4, 4, 128, 768), BF16),
            v((4, 8, 512), F32),
            v((1024, 512), BF16),
            v((2, 4, 128, 256), BF16),
            v((4, 512, 256), BF16),
            v((4, 512, 256), BF16),
            v((4, 512, 256), BF16),
            v((4, 512, 256), BF16),
            v((512, 1024), F32),
            v((512, 128), F32),
            v((512, 1024), F32),
            v((1024, 1024), BF16),
            v((1024, 2048), BF16),
            v((1024, 2048), BF16),
            v((1024, 1024), F32),
            v((512, 128), F32),
            v((1024, 256), BF16),
            v((3, 512, 1024), BF16),
            pltpu.SemaphoreType.DMA((80,)),
            pltpu.SemaphoreType.DMA((80,)),
            pltpu.SemaphoreType.DMA((64,)),
        ],
        compiler_params=pltpu.CompilerParams(
            collective_id=0, has_side_effects=True, vmem_limit_bytes=64 * 1024 * 1024 - 65536
        ),
    )(*arrays)


def accumulate(dst, src, lead, rows):
    steps = rows // 32
    total = math.prod(lead) * steps

    def body(index):
        place = []
        rest = index // steps
        for size in reversed(lead):
            place.insert(0, rest % size)
            rest = rest // size
        here = tuple(place) + (pl.ds(pl.multiple_of((index % steps) * 32, 32), 32),)
        dst[here] = add_low(dst[here], src[here])

    repeat(total, body)


def back_kernel(
    lens_ref,
    i_cot,
    i_n2,
    i_i2,
    i_vecs,
    i_w_ou,
    i_act,
    i_slope,
    i_low,
    i_w_in,
    i_n1,
    i_i1,
    i_att,
    i_w_out,
    i_qkv,
    i_lse,
    i_wq,
    i_states,
    grad_out,
    ou_out,
    in_out,
    out_out,
    qkv_out,
    vec_out,
    cot,
    n2,
    i2,
    vecs,
    w_ou,
    act,
    slope,
    low,
    w_in,
    n1,
    i1,
    att,
    w_out,
    qkv,
    lse,
    wq,
    outer2,
    part_in,
    branch2,
    mix_all,
    mix_far,
    g_ou,
    a_ou,
    b_ou,
    z_ou,
    zz_ou,
    az_ou,
    azz_ou,
    ax_ou,
    ay_ou,
    a_in,
    b_in,
    z_in,
    zz_in,
    az_in,
    azz_in,
    ax_in,
    ay_in,
    f_in,
    c_in,
    g_o,
    z_o,
    zz_o,
    x_o,
    y_o,
    g_q,
    y_q,
    z_q,
    zz_q,
    s_q,
    r_q,
    bias_q,
    vb,
    vr,
    send,
    recv,
    local,
):
    d, me, y = lax.axis_index("dp"), lax.axis_index("ctx"), lax.axis_index("fsdp")
    x, c = me // 2, me % 2
    p, q = d % 2, d // 2
    to_core = {"ctx": me + 1 - 2 * c}
    to_x = {"ctx": (me + 2) % 4}
    to_y = {"fsdp": 1 - y}
    to_z = {"dp": d + 1 - 2 * (d % 2)}
    to_zz = {"dp": (d + 2) % 4}
    to_far = {"ctx": 3 - me}
    slots = Slots()
    local_slots = Slots()
    pending = []

    def remotes(count, parts):
        first = slots.take(count)

        def make(k):
            src, dst, device = parts(k)
            return pltpu.make_async_remote_copy(
                src_ref=src,
                dst_ref=dst,
                send_sem=send.at[first + k],
                recv_sem=recv.at[first + k],
                device_id=device,
                device_id_type=MESH,
            )

        pending.append((count, make))
        return make

    def fetch(src, dst):
        copy = pltpu.make_async_copy(src, dst, local.at[local_slots.take()])
        copy.start()
        return copy

    early = [fetch(i_cot, cot), fetch(i_n2, n2), fetch(i_i2, i2), fetch(i_vecs, vecs)]
    barrier = pltpu.get_barrier_semaphore()
    for device in (to_core, to_x, to_y, to_z, to_zz, to_far):
        pl.semaphore_signal(barrier, inc=1, device_id=device, device_id_type=MESH)
    vb[0] = jnp.zeros((24, 1024), F32)
    bias_q[...] = jnp.zeros((8, 768), F32)
    for copy in early:
        copy.wait()
    got_act, got_w_ou = fetch(i_act, act), fetch(i_w_ou, w_ou)
    pl.semaphore_wait(barrier, 6)

    def chunk_of(buffer):
        def parts(k):
            src = buffer.at[pl.ds(pl.multiple_of(k * 128, 128), 128)]
            dst = buffer.at[pl.ds(pl.multiple_of(512 + k * 128, 128), 128)]
            return src, dst, to_core

        return parts

    outer_copy = remotes(4, chunk_of(outer2))
    branch_copy = remotes(4, chunk_of(branch2))

    def count_in(row, values):
        vb[0, row : row + 1, :] += jnp.sum(values, axis=0, keepdims=True)

    def norm_second(k):
        place = lax.broadcasted_iota(jnp.int32, (128, 1), 0) + me * 128
        valid = jnp.where(place < lens_ref[k], 1.0, 0.0)
        for half in range(2):
            rows = pl.ds(pl.multiple_of(k * 128 + half * 64, 64), 64)
            upstream = cot[k, half * 64 : half * 64 + 64].astype(F32) * valid[half * 64 : half * 64 + 64]
            normed = n2[rows, :]
            count_in(0, upstream * normed)
            count_in(1, upstream)
            made = norm_back(upstream, normed, i2[rows, 0:1], vecs[5:6, :])
            n2[rows, :] = made
            made = made.astype(BF16)
            outer2[rows, :] = made
            count_in(2, made.astype(F32))
        outer_copy(k).start()

    repeat(4, norm_second)
    late = [fetch(i_slope, slope), fetch(i_w_in, w_in)]
    got_act.wait()
    for k in range(4):
        outer_copy(k).wait_recv()

    low_ou, top_ou = pl.ds(0, 256), pl.ds(256, 768)
    low_in, top_in = pl.ds(0, 512), pl.ds(512, 1536)

    def ou_first(k, x_first):
        if x_first:
            return g_ou.at[k, 1 - x, :, :, top_ou], a_ou.at[k], to_x
        return g_ou.at[k, :, 1 - y, :, top_ou], a_ou.at[k], to_y

    ou_a_x = remotes(2, lambda k: ou_first(k, True))
    ou_a_y = remotes(2, lambda k: ou_first(k + 2, False))
    ou_b_y = remotes(2, lambda k: (a_ou.at[k, 1 - y], b_ou.at[k], to_y))
    ou_b_x = remotes(2, lambda k: (a_ou.at[k + 2, 1 - x], b_ou.at[k + 2], to_x))
    ou_z = remotes(2, lambda k: (b_ou.at[2 * k + 1 - p], z_ou.at[k], to_z))
    ou_zz = remotes(1, lambda k: (z_ou.at[1 - q], zz_ou, to_zz))
    low_ou_z = remotes(2, lambda k: (g_ou.at[2 * k + 1 - p, :, :, :, low_ou], az_ou.at[k], to_z))
    low_ou_zz = remotes(1, lambda k: (az_ou.at[1 - q], azz_ou, to_zz))
    low_ou_x = remotes(1, lambda k: (azz_ou.at[1 - x], ax_ou, to_x))
    low_ou_y = remotes(1, lambda k: (ax_ou.at[1 - y], ay_ou, to_y))

    def ou_add_a(k):
        if k < 2:
            ou_a_x(k).wait_recv()
            accumulate(a_ou.at[k], g_ou.at[k, x, :, :, top_ou], (2,), 128)
            ou_b_y(k).start()
        else:
            ou_a_y(k - 2).wait_recv()
            accumulate(a_ou.at[k], g_ou.at[k, :, y, :, top_ou], (2,), 128)
            ou_b_x(k - 2).start()

    def ou_add_b(k):
        if k < 2:
            ou_b_y(k).wait_recv()
            accumulate(b_ou.at[k], a_ou.at[k, y], (), 128)
        else:
            ou_b_x(k - 2).wait_recv()
            accumulate(b_ou.at[k], a_ou.at[k, x], (), 128)

    def ou_add_z():
        for k in range(2):
            ou_z(k).wait_recv()
            accumulate(z_ou.at[k], b_ou.at[2 * k + p], (), 128)
        ou_zz(0).start()

    def low_ou_add_z():
        for k in range(2):
            low_ou_z(k).wait_recv()
            accumulate(az_ou.at[k], g_ou.at[2 * k + p, :, :, :, low_ou], (2, 2), 128)
        low_ou_zz(0).start()

    def low_ou_add_zz():
        low_ou_zz(0).wait_recv()
        accumulate(azz_ou, az_ou.at[q], (2, 2), 128)
        low_ou_x(0).start()

    def low_ou_add_x():
        low_ou_x(0).wait_recv()
        accumulate(ax_ou, azz_ou.at[x], (2,), 128)
        low_ou_y(0).start()

    def ou_last():
        ou_zz(0).wait_recv()
        low_ou_y(0).wait_recv()

        def body(i):
            rows = pl.ds(pl.multiple_of(i * 32, 32), 32)
            ou_out[rows, 256:] = z_ou[q, rows, :].astype(F32) + zz_ou[rows, :].astype(F32)
            ou_out[rows, :256] = ax_ou[y, rows, :].astype(F32) + ay_ou[rows, :].astype(F32)

        repeat(4, body)

    in_a = remotes(4, lambda k: (act.at[k, :, :, 1 - y, :, top_in], a_in.at[k], to_y))
    in_b = remotes(4, lambda k: (a_in.at[k, 1 - x], b_in.at[k], to_x))
    in_z = remotes(2, lambda k: (b_in.at[2 * k + 1 - p], z_in.at[k], to_z))
    in_zz = remotes(1, lambda k: (z_in.at[1 - q], zz_in, to_zz))
    in_core = remotes(1, lambda k: (f_in.at[1 - c], c_in, to_core))
    low_in_z = remotes(2, lambda k: (act.at[2 * k + 1 - p, :, :, :, :, low_in], az_in.at[k], to_z))
    low_in_zz = remotes(1, lambda k: (az_in.at[1 - q], azz_in, to_zz))
    low_in_x = remotes(1, lambda k: (azz_in.at[1 - x], ax_in, to_x))
    low_in_y = remotes(1, lambda k: (ax_in.at[:, 1 - y], ay_in, to_y))

    def in_add_a(k):
        in_a(k).wait_recv()
        accumulate(a_in.at[k], act.at[k, :, :, y, :, top_in], (2, 2), 32)
        in_b(k).start()

    def in_add_b(k):
        in_b(k).wait_recv()
        accumulate(b_in.at[k], a_in.at[k, x], (2,), 32)

    def in_add_z():
        for k in range(2):
            in_z(k).wait_recv()
            accumulate(z_in.at[k], b_in.at[2 * k + p], (2,), 32)
        in_zz(0).start()

    def low_in_add_z():
        for k in range(2):
            low_in_z(k).wait_recv()
            accumulate(az_in.at[k], act.at[2 * k + p, :, :, :, :, low_in], (2, 2, 2), 32)
        low_in_zz(0).start()

    def low_in_add_zz():
        low_in_zz(0).wait_recv()
        accumulate(azz_in, az_in.at[q], (2, 2, 2), 32)
        low_in_x(0).start()

    def low_in_add_x():
        low_in_x(0).wait_recv()
        accumulate(ax_in, azz_in.at[x], (2, 2), 32)
        low_in_y(0).start()

    def in_sum():
        in_zz(0).wait_recv()
        low_in_y(0).wait_recv()
        for k in range(2):
            f_in[k, :, 512:] = z_in[q, k].astype(F32) + zz_in[k].astype(F32)
            f_in[k, :, :512] = ax_in[k, y].astype(F32) + ay_in[k].astype(F32)
        in_core(0).start()

    def in_last():
        def place(b, own):
            return pl.ds(pl.multiple_of((2 * b + (c if own else 1 - c)) * 256, 256), 256)

        for b in range(8):
            in_out[:, place(b, True)] = f_in[c, :, b * 256 : b * 256 + 256]
        in_core(0).wait_recv()
        for b in range(8):
            in_out[:, place(b, False)] = c_in[:, b * 256 : b * 256 + 256]

    o_z = remotes(1, lambda k: (g_o.at[:, :, 1 - p], z_o, to_z))
    o_zz = remotes(1, lambda k: (z_o.at[:, 1 - q], zz_o, to_zz))
    o_x = remotes(1, lambda k: (zz_o.at[1], x_o, to_x))
    o_y = remotes(1, lambda k: (x_o.at[1 - y], y_o, to_y))

    def o_add_z():
        o_z(0).wait_recv()
        accumulate(z_o, g_o.at[:, :, p], (2, 2, 2), 32)
        o_zz(0).start()

    def o_add_zz():
        o_zz(0).wait_recv()
        accumulate(zz_o, z_o.at[:, q], (2, 2), 32)
        o_x(0).start()

    def o_add_x():
        o_x(0).wait_recv()
        accumulate(x_o, zz_o.at[0], (2,), 32)
        o_y(0).start()

    def o_last():
        o_y(0).wait_recv()
        out_out[...] = x_o[y].astype(F32) + y_o[...].astype(F32)

    q_y = remotes(4, lambda k: (g_q.at[k, :, 1 - y], y_q.at[k], to_y))
    q_z = remotes(2, lambda k: (y_q.at[2 * k + 1 - p], z_q.at[k], to_z))
    q_zz = remotes(1, lambda k: (z_q.at[1 - q], zz_q, to_zz))
    others = ((me + 1 - 2 * c, to_core), ((me + 2) % 4, to_x), (3 - me, to_far))
    q_all = [
        remotes(1, lambda k, j=j: (s_q.at[others[j][0]], r_q.at[j], others[j][1])) for j in range(3)
    ]

    def q_add_y(k):
        q_y(k).wait_recv()
        accumulate(y_q.at[k], g_q.at[k, :, y], (4,), 32)

    def q_add_z():
        for k in range(2):
            q_z(k).wait_recv()
            accumulate(z_q.at[k], y_q.at[2 * k + p], (4,), 32)
        q_zz(0).start()

    def q_sum():
        q_zz(0).wait_recv()
        for k in range(4):
            s_q[k] = z_q[q, k].astype(F32) + zz_q[k].astype(F32)
        for j in range(3):
            q_all[j](0).start()

    def q_last():
        qkv_out[me] = s_q[me]
        for j in range(3):
            q_all[j](0).wait_recv()
            qkv_out[others[j][0]] = r_q[j]

    v_core = remotes(1, lambda k: (vb.at[0, pl.ds(0, 8)], vr.at[0, pl.ds(0, 8)], to_core))
    v_x = remotes(1, lambda k: (vb.at[1, pl.ds(0, 16)], vr.at[1, pl.ds(0, 16)], to_x))
    v_y = remotes(1, lambda k: (vb.at[2], vr.at[2], to_y))
    v_z = remotes(1, lambda k: (vb.at[3], vr.at[3], to_z))
    v_zz = remotes(1, lambda k: (vb.at[4], vr.at[4], to_zz))

    def outer_grad(i):
        k = (i % 2) * 2 + i // 2
        for half in range(2):
            spot = pl.ds(pl.multiple_of((2 * k + half) * 256, 256), 256)
            left = act[:, :, :, :, :, spot].reshape(1024, 256)
            made = matmul_tn(left, outer2[...])
            g_ou[k, half] = made.astype(BF16).reshape(2, 128, 1024)

        @pl.when(i % 2 == 0)
        def _():
            ou_a_x(k).start()

        @pl.when(i % 2 == 1)
        def _():
            ou_a_y(k - 2).start()

        @pl.when(i >= 2)
        def _():
            low_ou_z(i - 2).start()

    repeat(4, outer_grad)
    got_w_ou.wait()
    for copy in late:
        copy.wait()
    late = [fetch(i_n1, n1), fetch(i_i1, i1), fetch(i_low, low), fetch(i_att, att), fetch(i_w_out, w_out)]
    late += [fetch(i_qkv, qkv), fetch(i_lse, lse), fetch(i_wq, wq)]

    def hidden_grad(b):
        here = pl.ds(pl.multiple_of(b * 256, 256), 256)
        total = jnp.zeros((1, 256), F32)
        for m in range(2):
            made = matmul_nt(outer2[m * 512 : m * 512 + 512, :], w_ou[here, :])
            made = (made * slope[m * 512 : m * 512 + 512, here].astype(F32)).astype(BF16)
            slope[m * 512 : m * 512 + 512, here] = made
            total = total + jnp.sum(made.astype(F32), axis=0, keepdims=True)
        vb[0, pl.ds(8 + b, 1), 0:256] = total

    repeat(8, hidden_grad)

    def part_copy_parts(n):
        spot = pl.ds(pl.multiple_of(n * 256, 256), 256)
        return w_ou.at[pl.ds(1536, 512), spot], part_in.at[n], to_core

    part_copy = remotes(4, part_copy_parts)

    def first_far(n):
        here = pl.ds(pl.multiple_of(n * 256, 256), 256)
        w_ou[1536:2048, here] = matmul_nt(slope[512:, :], w_in[here, :]).astype(BF16)
        part_copy(n).start()

    repeat(4, first_far)
    ou_add_a(0)
    ou_add_a(2)
    low_ou_add_z()

    def first_near(n):
        here = pl.ds(pl.multiple_of(n * 256, 256), 256)
        made = n2[:, here] + matmul_nt(slope[:512, :], w_in[here, :])
        part_copy(n).wait_recv()
        n2[:, here] = made + part_in[n].astype(F32)

    repeat(4, first_near)
    for copy in late:
        copy.wait()

    def norm_first(k):
        for half in range(2):
            rows = pl.ds(pl.multiple_of(k * 128 + half * 64, 64), 64)
            upstream = n2[rows, :]
            normed = n1[rows, :]
            count_in(3, upstream * normed)
            count_in(4, upstream)
            made = norm_back(upstream, normed, i1[rows, 0:1], vecs[2:3, :])
            n2[rows, :] = made
            made = made.astype(BF16)
            branch2[rows, :] = made
            count_in(5, made.astype(F32))
        branch_copy(k).start()

    repeat(4, norm_first)
    v_core(0).start()
    ou_add_a(1)
    ou_add_a(3)
    for k in range(4):
        branch_copy(k).wait_recv()

    mix_copy = remotes(4, lambda s: (mix_far.at[:, s], mix_all.at[pl.ds(2, 2), s], to_x))
    mix_far[...] = matmul_nt(branch2[...], w_out[1].reshape(256, 1024)).astype(BF16).reshape(2, 4, 128, 256)
    for s in range(4):
        mix_copy(s).start()
    mix_all[0:2] = matmul_nt(branch2[...], w_out[0].reshape(256, 1024)).astype(BF16).reshape(2, 4, 128, 256)

    for half in range(2):
        made = matmul_tn(att[:, half * 256 : half * 256 + 256], branch2[...])
        g_o[half] = made.astype(BF16).reshape(2, 2, 2, 32, 1024)
    o_z(0).start()
    v_core(0).wait_recv()
    vb[1, 0:8] = vb[0, 0:8] + vr[0, 0:8]
    vb[1, 8:16] = vb[0, 8:16]
    v_x(0).start()

    def inner_grad(k):
        left = low[:, pl.ds(pl.multiple_of(k * 256, 256), 256)]
        for half in range(4):
            made = matmul_tn(left, slope[:, half * 512 : half * 512 + 512]).astype(BF16)
            act[k, :, :, :, :, half * 512 : half * 512 + 512] = made.reshape(2, 2, 2, 32, 512)

        in_a(k).start()

        @pl.when(k % 2 == 1)
        def _():
            low_in_z(k // 2).start()

    repeat(4, inner_grad)
    got_states = []
    for j in range(4):
        for s in range(4):
            rows = pl.ds((j // 2) * 512 + s * 128, 128)
            got_states.append(fetch(i_states.at[j, s], slope.at[rows, pl.ds((j % 2) * 1024, 1024)]))

    def key_flags(s):
        pieces = []
        for j in range(4):
            position = lax.broadcasted_iota(jnp.int32, (128, 128), 0)
            place = me + 1 - 2 * c if j == 1 else me
            place = (place + 2) % 4 if j == 2 else place
            place = 3 - me if j == 3 else place
            pieces.append(jnp.where(position + place * 128 < lens_ref[s], 0.0, MASKED))
        return jnp.concatenate(pieces, 0).astype(BF16)

    def piece_copy_parts(k):
        rows = pl.ds(pl.multiple_of((k % 2) * 512 + (k // 2) * 128, 128), 128)
        return w_ou.at[rows], w_in.at[rows, pl.ds(0, 1024)], to_core

    piece_copy = remotes(8, piece_copy_parts)

    def pass_copy_parts(s):
        src = w_ou.at[pl.ds(pl.multiple_of(1024 + s * 128, 128), 128)]
        dst = w_in.at[pl.ds(pl.multiple_of(s * 128, 128), 128), pl.ds(1024, 1024)]
        return src, dst, to_x

    pass_copy = remotes(4, pass_copy_parts)

    def far_pieces(s):
        for which in range(2):
            rows = pl.ds(pl.multiple_of(512 * which + s * 128, 128), 128)
            w_ou[rows, :] = matmul_nt(qkv[1 + 2 * which, s], wq[...]).astype(BF16)
        for which in range(2):
            piece_copy(2 * s + which).start()

    def passed(s):
        made = matmul_nt(qkv[2, s], wq[...])
        piece_copy(2 * s + 1).wait_recv()
        rows = pl.ds(pl.multiple_of(512 + s * 128, 128), 128)
        made = made + w_in[rows, 0:1024].astype(F32)
        w_ou[pl.ds(pl.multiple_of(1024 + s * 128, 128), 128), :] = made.astype(BF16)
        pass_copy(s).start()

    hooks = {
        0: [lambda: ou_add_b(0), lambda: ou_add_b(2), low_ou_add_zz],
        1: [lambda: ou_add_b(1), lambda: ou_add_b(3), lambda: ou_z(0).start(), lambda: ou_z(1).start(), o_add_z],
        2: [lambda: in_add_a(0)],
        3: [lambda: in_add_a(1)],
    }

    def attention(s):
        for step, actions in hooks.items():

            @pl.when(s == step)
            def _():
                for action in actions:
                    action()

        mix_copy(s).wait_recv()
        bias = key_flags(s)
        lane = lax.broadcasted_iota(jnp.int32, (512, 128), 1)
        one = jnp.ones((512, 128), BF16)
        for pair in range(2):
            base = pair * 128
            query = qkv[:, s, :, base : base + 128].reshape(512, 128)
            key = qkv[:, s, :, 256 + base : 384 + base].reshape(512, 128)
            value = qkv[:, s, :, 512 + base : 640 + base].reshape(512, 128)
            grad = mix_all[:, s, :, base : base + 128].reshape(512, 128)
            query = (query.astype(F32) * 0.125).astype(BF16)
            query_parts, key_parts, value_parts = [], [], []
            for which in range(2):
                spot = 2 * pair + which
                log_total = lse[s, spot : spot + 1, :]
                scores = matmul_nt(with_flag(key, bias, which), with_flag(query, one, which))
                probs = jnp.exp(scores - log_total)
                probs_grad = matmul_nt(value, half_lanes(grad, which))
                value_parts.append(matmul(probs.astype(BF16), grad))
                row_dot = jnp.sum(probs * probs_grad, axis=0, keepdims=True)
                score_grad = (probs * (probs_grad - row_dot)).astype(BF16)
                key_parts.append(matmul(score_grad, query))
                query_parts.append(matmul_tn(score_grad, key) * 0.125)
            for place, parts in enumerate((query_parts, key_parts, value_parts)):
                joined = jnp.where(lane < 64, parts[0], parts[1]).astype(BF16)
                start = place * 256 + base
                qkv[:, s, :, start : start + 128] = joined.reshape(4, 128, 128)
                bias_q[0:1, start : start + 128] += jnp.sum(joined.astype(F32), axis=0, keepdims=True)
        far_pieces(s)

        @pl.when(s > 0)
        def _():
            passed(s - 1)

    repeat(4, attention)
    passed(3)

    v_x(0).wait_recv()
    vb[2, 0:16] = vb[1, 0:16] + vr[1, 0:16]
    vb[2, 16:24] = jnp.concatenate((bias_q[...], jnp.zeros((8, 256), F32)), 1)
    v_y(0).start()
    for copy in got_states:
        copy.wait()

    def projection_grad(k):
        made = jnp.zeros((256, 768), F32)
        for j in range(4):
            spot = pl.ds(pl.multiple_of((j % 2) * 1024 + k * 256, 256), 256)
            left = slope[(j // 2) * 512 : (j // 2) * 512 + 512, spot]
            made = made + matmul_tn(left, qkv[j].reshape(512, 768))
        g_q[k] = made.astype(BF16).reshape(4, 2, 32, 768)
        q_y(k).start()

    repeat(4, projection_grad)
    in_add_a(2)
    low_in_add_z()
    ou_add_z()
    v_y(0).wait_recv()
    vb[3] = vb[2] + vr[2]
    v_z(0).start()
    o_add_zz()
    in_add_a(3)
    for k in range(2):
        in_add_b(k)
    in_z(0).start()

    def near_piece(s):
        rows = pl.ds(pl.multiple_of(s * 128, 128), 128)
        made = n2[rows, :] + matmul_nt(qkv[0, s], wq[...])
        piece_copy(2 * s).wait_recv()
        n2[rows, :] = made + w_in[rows, 0:1024].astype(F32)

    repeat(4, near_piece)
    low_ou_add_x()
    for k in range(2):
        q_add_y(k)
    q_z(0).start()
    low_in_add_zz()
    for k in range(2, 4):
        q_add_y(k)
    q_z(1).start()
    v_z(0).wait_recv()
    vb[4] = vb[3] + vr[3]
    v_zz(0).start()
    for k in range(2, 4):
        in_add_b(k)
    in_z(1).start()
    q_add_z()
    o_add_x()
    low_in_add_x()
    in_add_z()

    def last_piece(s):
        rows = pl.ds(pl.multiple_of(s * 128, 128), 128)
        pass_copy(s).wait_recv()
        grad_out[rows, :] = (n2[rows, :] + w_in[rows, 1024:2048].astype(F32)).astype(BF16)

    repeat(4, last_piece)
    ou_last()
    o_last()
    v_zz(0).wait_recv()
    vec_out[...] = vb[4] + vr[4]
    q_sum()
    in_sum()
    q_last()
    in_last()
    for count, make in pending:
        for k in range(count):
            make(k).wait_send()


def back_call(arrays):
    any_space = pl.BlockSpec(memory_space=pl.ANY)
    outs = (
        ((512, 1024), BF16),
        ((128, 1024), F32),
        ((32, 4096), F32),
        ((32, 1024), F32),
        ((4, 32, 768), F32),
        ((24, 1024), F32),
    )
    scratch = (
        ((4, 128, 1024), BF16),
        ((512, 1024), F32),
        ((512, 128), F32),
        ((16, 1024), F32),
        ((2048, 1024), BF16),
        ((4, 2, 2, 2, 32, 2048), BF16),
        ((1024, 2048), BF16),
        ((1024, 1024), BF16),
        ((1024, 2048), BF16),
        ((512, 1024), F32),
        ((512, 128), F32),
        ((1024, 512), BF16),
        ((2, 4, 64, 1024), BF16),
        ((4, 4, 128, 768), BF16),
        ((4, 8, 512), F32),
        ((1024, 768), BF16),
        ((1024, 1024), BF16),
        ((4, 512, 256), BF16),
        ((1024, 1024), BF16),
        ((4, 4, 128, 256), BF16),
        ((2, 4, 128, 256), BF16),
        ((4, 2, 2, 128, 1024), BF16),
        ((4, 2, 128, 768), BF16),
        ((4, 128, 768), BF16),
        ((2, 128, 768), BF16),
        ((128, 768), BF16),
        ((2, 2, 2, 128, 256), BF16),
        ((2, 2, 128, 256), BF16),
        ((2, 128, 256), BF16),
        ((128, 256), BF16),
        ((4, 2, 2, 32, 1536), BF16),
        ((4, 2, 32, 1536), BF16),
        ((2, 2, 32, 1536), BF16),
        ((2, 32, 1536), BF16),
        ((2, 2, 2, 2, 32, 512), BF16),
        ((2, 2, 2, 32, 512), BF16),
        ((2, 2, 32, 512), BF16),
        ((2, 32, 512), BF16),
        ((2, 32, 2048), F32),
        ((32, 2048), F32),
        ((2, 2, 2, 2, 32, 1024), BF16),
        ((2, 2, 2, 32, 1024), BF16),
        ((2, 2, 32, 1024), BF16),
        ((2, 32, 1024), BF16),
        ((32, 1024), BF16),
        ((4, 4, 2, 32, 768), BF16),
        ((4, 4, 32, 768), BF16),
        ((2, 4, 32, 768), BF16),
        ((4, 32, 768), BF16),
        ((4, 32, 768), F32),
        ((3, 32, 768), F32),
        ((8, 768), F32),
        ((5, 24, 1024), F32),
        ((5, 24, 1024), F32),
    )
    return pl.pallas_call(
        back_kernel,
        in_specs=[pl.BlockSpec(memory_space=pltpu.SMEM)] + [any_space] * 17,
        out_specs=[pl.BlockSpec(memory_space=pltpu.VMEM)] * len(outs),
        out_shape=[jax.ShapeDtypeStruct(shape, kind) for shape, kind in outs],
        scratch_shapes=[pltpu.VMEM(shape, kind) for shape, kind in scratch]
        + [
            pltpu.SemaphoreType.DMA((96,)),
            pltpu.SemaphoreType.DMA((96,)),
            pltpu.SemaphoreType.DMA((48,)),
        ],
        compiler_params=pltpu.CompilerParams(
            collective_id=1, has_side_effects=True, vmem_limit_bytes=64 * 1024 * 1024 - 65536
        ),
    )(*arrays)


def finish_kernel(sums_ref, qkv_ref, *refs):
    count = 5
    sources, targets = refs[:count], refs[count : 2 * count]
    rows_out, inner_out, query_out, value_out = refs[2 * count : 2 * count + 6], *refs[2 * count + 6 : 2 * count + 9]
    projections = refs[2 * count + 9 : 2 * count + 12]
    stages, sems = refs[2 * count + 12 : 3 * count + 12], refs[3 * count + 12]
    d, me, y = lax.axis_index("dp"), lax.axis_index("ctx"), lax.axis_index("fsdp")
    copies_in = [pltpu.make_async_copy(sources[i], stages[i], sems.at[i]) for i in range(count)]
    copies_out = [pltpu.make_async_copy(stages[i], targets[i], sems.at[count + i]) for i in range(count)]
    for copy in copies_in:
        copy.start()

    def from_lane(values, lane):
        return pltpu.roll(values, (1024 - lane) % 1024, 1)

    own = from_lane(sums_ref[0:8, :], ((d * 4 + me) * 2 + y) * 32)
    for i in range(6):
        rows_out[i][...] = own[i, 0:32]
    row = lax.broadcasted_iota(jnp.int32, (8, 256), 0)
    inner = jnp.sum(jnp.where(row == 2 * d + me // 2, sums_ref[8:16, 0:256], 0.0), axis=0, keepdims=True)
    inner_out[...] = jnp.where(y == 0, inner[:, 0:128], inner[:, 128:256])[0]
    for start, out in ((0, query_out), (512, value_out)):
        out[...] = from_lane(sums_ref[16:24, :], start + d * 64 + y * 32)[0, 0:32]
    for place, out in enumerate(projections):
        for g in range(4):
            start = place * 256 + g * 64
            parts = [qkv_ref[i, :, start : start + 64] for i in range(4)]
            out[:, g * 256 : g * 256 + 256] = jnp.concatenate(parts, 1)
    for i in range(count):
        copies_in[i].wait()
        copies_out[i].start()
    for copy in copies_out:
        copy.wait()


def finish_call(sums, qkv_sum, arrays):
    any_space = pl.BlockSpec(memory_space=pl.ANY)
    vmem = pl.BlockSpec(memory_space=pltpu.VMEM)
    short = jax.ShapeDtypeStruct((32,), F32)
    return pl.pallas_call(
        finish_kernel,
        in_specs=[vmem] * 2 + [any_space] * 5,
        out_specs=[any_space] * 5 + [vmem] * 12,
        out_shape=[jax.ShapeDtypeStruct(a.shape, a.dtype) for a in arrays]
        + [short] * 6
        + [jax.ShapeDtypeStruct((128,), F32), short, short]
        + [jax.ShapeDtypeStruct((32, 1024), F32)] * 3,
        scratch_shapes=[pltpu.VMEM(a.shape, a.dtype) for a in arrays] + [pltpu.SemaphoreType.DMA((16,))],
    )(sums, qkv_sum, *arrays)


def shards(
    states,
    cotangent,
    lengths,
    slot_source,
    query_weight,
    query_bias,
    key_weight,
    value_weight,
    value_bias,
    output_weight,
    output_bias,
    first_gain,
    first_shift,
    inner_weight,
    inner_bias,
    outer_weight,
    outer_bias,
    final_gain,
    final_shift,
):
    seq_dev, block_len, width = states.shape
    n_dp, n_ctx, n_fsdp = (lax.axis_size(name) for name in OWNERS)
    assert (n_ctx, n_fsdp) == (4, 2)
    head_size = width // HEADS
    units = inner_weight.shape[1]
    tokens = seq_dev * block_len
    d, me, y = (lax.axis_index(name) for name in OWNERS)
    x, c = me // 2, me % 2
    own_heads = HEADS // n_ctx
    cols = own_heads * head_size
    aligned = n_dp == own_heads

    def other_half(local):
        return swap(local, "fsdp", 1)

    def ordered(own, other, axis=0):
        return jnp.where(
            y == 0, jnp.concatenate((own, other), axis), jnp.concatenate((other, own), axis)
        )

    def gathered(local, axis=0):
        return ordered(local, other_half(local), axis)

    def head_cols(matrix):
        parts = matrix.reshape(matrix.shape[:-1] + (own_heads, n_ctx, head_size))
        return pick(parts, me, parts.ndim - 2).reshape(matrix.shape[:-1] + (cols,))

    my_seqs = (d * n_fsdp + y) * seq_dev + jnp.arange(seq_dev, dtype=jnp.int32)
    seq_len = jnp.sum(jnp.where(slot_source[None, :] == my_seqs[:, None], lengths[None, :], 0), axis=1)
    places = (me ^ jnp.arange(n_ctx, dtype=jnp.int32))[:, None] * block_len + jnp.arange(
        block_len, dtype=jnp.int32
    )
    key_ok = places.reshape(1, -1) < seq_len[:, None]
    key_bias = jnp.where(key_ok, 0.0, MASKED).astype(BF16)
    key_bias = jnp.broadcast_to(key_bias[:, :, None], key_bias.shape + (128,))
    valid_rows = (places[0][None, :] < seq_len[:, None]).astype(F32).reshape(-1, 1)
    full_len = n_ctx * block_len
    score_flops = 2 * seq_dev * own_heads * full_len * full_len * 128
    block = units // (4 * n_dp)
    wq_own = jnp.concatenate((head_cols(query_weight), head_cols(key_weight), head_cols(value_weight)), 1)

    def share(own):
        return jnp.concatenate((own, swap(own, "ctx", 1)), axis=0)

    def collect(both_rows):
        return both_rows[:tokens] + swap(both_rows[tokens:].astype(BF16), "ctx", 1).astype(F32)

    if aligned:
        (
            encoded,
            flat_all,
            w_qkv,
            w_out,
            w_inner,
            w_outer,
            vecs,
            qkv,
            log_total,
            attended,
            first_norm,
            first_inverse,
            first_low,
            activated,
            slope,
            second_norm,
            second_inverse,
            own_lengths,
        ) = layer_call(
            (
                lengths,
                slot_source,
                states,
                query_weight,
                key_weight,
                value_weight,
                query_bias,
                output_bias,
                first_gain,
                first_shift,
                outer_bias,
                final_gain,
                final_shift,
                value_bias,
                inner_bias,
                output_weight,
                inner_weight,
                outer_weight,
            )
        )
        input_grad, outer_weight_own, inner_weight_own, output_weight_own, qkv_sum, sums = back_call(
            (
                own_lengths,
                cotangent,
                second_norm,
                second_inverse,
                vecs,
                w_outer,
                activated.reshape(4, 2, 2, 2, 32, units // 2),
                slope,
                first_low,
                w_inner,
                first_norm,
                first_inverse,
                attended,
                w_out,
                qkv,
                log_total,
                w_qkv,
                flat_all,
            )
        )
        finished = finish_call(
            sums, qkv_sum, (encoded, input_grad, outer_weight_own, inner_weight_own, output_weight_own)
        )
        encoded, input_grad, outer_weight_own, inner_weight_own, output_weight_own = finished[:5]
        final_gain_own, final_shift_own, outer_bias_own, first_gain_own, first_shift_own, output_bias_own = finished[5:11]
        inner_bias_own, query_bias_own, value_bias_own, query_own, key_own, value_own = finished[11:]
        return (
            encoded.reshape(states.shape),
            input_grad.reshape(states.shape),
            query_own,
            query_bias_own,
            key_own,
            value_own,
            value_bias_own,
            output_weight_own,
            output_bias_own,
            first_gain_own,
            first_shift_own,
            inner_weight_own,
            inner_bias_own,
            outer_weight_own,
            outer_bias_own,
            final_gain_own,
            final_shift_own,
        )

    def other_half(local):
        return swap(local, "fsdp", 1)

    def ordered(own, other, axis=0):
        return jnp.where(
            y == 0, jnp.concatenate((own, other), axis), jnp.concatenate((other, own), axis)
        )

    def gathered(local, axis=0):
        return ordered(local, other_half(local), axis)

    wide = (query_bias, value_bias, output_bias, first_gain, first_shift, outer_bias, final_gain, final_shift)
    packed = jnp.concatenate([v.reshape(1, -1) for v in wide] + [inner_bias.reshape(-1, width // 2)])
    other_packed = other_half(packed)
    both = jnp.where(y == 0, jnp.stack((packed, other_packed)), jnp.stack((other_packed, packed)))
    b_query, b_value, b_out, g_first, s_first, b_outer, g_final, s_final = (
        both[:, i].reshape(width).astype(F32) for i in range(8)
    )
    b_inner = both[:, 8:].reshape(2 * n_dp, 2, -1)
    b_inner = pick(b_inner, c, 1).reshape(-1).astype(F32)
    w_qkv = gathered(wq_own)
    b_qkv = jnp.concatenate((head_cols(b_query), jnp.zeros((cols,), F32), head_cols(b_value)))

    from_x = swap(states, "ctx", 2)
    from_core = swap(states, "ctx", 1)
    from_far = swap(from_x, "ctx", 1)
    flat_all = jnp.stack((states, from_core, from_x, from_far)).reshape(-1, width)

    w_out = gathered(pick(output_weight.reshape(-1, 2, 2, head_size, width), c, 2))
    w_out = jnp.concatenate((pick(w_out, x, 1), pick(w_out, 1 - x, 1)), 0).reshape(-1, width)
    w_inner = gathered(
        pick(inner_weight.reshape(width // 2, 2 * n_dp, 2, block), c, 2).reshape(width // 2, -1)
    )
    w_outer = gathered(pick(outer_weight.reshape(n_dp, 2, block, width), c, 1).reshape(-1, width))

    qkv = (matmul(flat_all, w_qkv) + b_qkv).astype(BF16)
    qkv = qkv.reshape(n_ctx, seq_dev, block_len, 3 * cols)
    attended_all, log_total = attention_call(
        attend_kernel,
        (qkv, key_bias),
        (
            jax.ShapeDtypeStruct((n_ctx, seq_dev, block_len, cols), BF16),
            jax.ShapeDtypeStruct((seq_dev, 8, full_len), F32),
        ),
        2 * score_flops,
    )
    near = attended_all[:2].reshape(-1, cols)
    far = swap(attended_all[2:], "ctx", 2).reshape(-1, cols)
    attended = jnp.concatenate((near, far), axis=1)
    first_sum = states.reshape(-1, width).astype(F32) + collect(matmul(attended, w_out)) + b_out
    first_out, first_norm, first_inverse = norm_rows(first_sum, g_first, s_first)
    first_low = share(first_out.astype(BF16))
    hidden = matmul(first_low, w_inner) + b_inner
    below = 0.5 * (1.0 + lax.erf(hidden * math.sqrt(0.5)))
    bell = jnp.exp(-0.5 * hidden * hidden) * (1.0 / math.sqrt(2 * math.pi))
    slope = (below + hidden * bell).astype(BF16)
    activated = (hidden * below).astype(BF16)
    second_sum = first_out + collect(matmul(activated, w_outer)) + b_outer
    second_out, second_norm, second_inverse = norm_rows(second_sum, g_final, s_final)
    encoded = (second_out * valid_rows).astype(BF16).reshape(states.shape)

    out_grad = cotangent.reshape(-1, width).astype(F32) * valid_rows
    final_gain_part = jnp.sum(out_grad * second_norm, axis=0)
    final_shift_part = jnp.sum(out_grad, axis=0)
    second_grad = norm_back(out_grad, second_norm, second_inverse, g_final)
    outer_round_own = second_grad.astype(BF16)
    outer_bias_part = col_sum(outer_round_own)
    outer_round = share(outer_round_own)
    outer_weight_part = matmul_tn(activated, outer_round).astype(BF16)
    hidden_grad = (matmul_nt(outer_round, w_outer) * slope.astype(F32)).astype(BF16)
    inner_bias_part = col_sum(hidden_grad)
    inner_weight_part = matmul_tn(first_low, hidden_grad).astype(BF16)
    first_grad = second_grad + collect(matmul_nt(hidden_grad, w_inner))
    first_gain_part = jnp.sum(first_grad * first_norm, axis=0)
    first_shift_part = jnp.sum(first_grad, axis=0)
    sum_grad = norm_back(first_grad, first_norm, first_inverse, g_first)
    branch_own = sum_grad.astype(BF16)
    output_bias_part = col_sum(branch_own)
    branch_grad = share(branch_own)
    output_weight_part = matmul_tn(attended, branch_grad).astype(BF16)
    attended_grad = matmul_nt(branch_grad, w_out).astype(BF16)
    near_grad = attended_grad[:, :cols]
    far_grad = swap(attended_grad[:, cols:], "ctx", 2)
    attended_grad_all = jnp.concatenate((near_grad, far_grad), 0).reshape(n_ctx, seq_dev, block_len, cols)
    (qkv_grad,) = attention_call(
        attend_back_kernel,
        (qkv, key_bias, log_total, attended_grad_all),
        (jax.ShapeDtypeStruct(qkv.shape, BF16),),
        5 * score_flops,
    )
    flat_grad = qkv_grad.reshape(-1, 3 * cols)
    bias_part = col_sum(flat_grad)
    qkv_weight_part = matmul_tn(flat_all, flat_grad).astype(BF16)
    input_part = matmul_nt(flat_grad, w_qkv).reshape(n_ctx, tokens, width)
    to_core = swap(jnp.stack((input_part[1], input_part[3])).astype(BF16), "ctx", 1)
    to_x = swap((input_part[2] + to_core[1].astype(F32)).astype(BF16), "ctx", 2)
    input_grad = sum_grad + input_part[0] + to_core[0].astype(F32) + to_x.astype(F32)
    input_grad = input_grad.astype(BF16).reshape(states.shape)

    token_sums = jnp.stack(
        (final_gain_part, final_shift_part, outer_bias_part, first_gain_part, first_shift_part, output_bias_part)
    )
    def placed_heads(part):
        whole = jnp.zeros(part.shape[:-1] + (own_heads, n_ctx, head_size), part.dtype)
        part = part.reshape(part.shape[:-1] + (own_heads, 1, head_size))
        return lax.dynamic_update_slice_in_dim(whole, part, me, part.ndim - 2).reshape(
            part.shape[:-3] + (width,)
        )

    def placed_units(part, axis):
        split = part.shape[:axis] + (2 * n_dp, 1, block) + part.shape[axis + 1 :]
        whole = jnp.zeros(split[: axis + 1] + (2,) + split[axis + 2 :], part.dtype)
        whole = lax.dynamic_update_slice_in_dim(whole, part.reshape(split), c, axis + 1)
        return whole.reshape(part.shape[:axis] + (units,) + part.shape[axis + 1 :])

    def placed_rows(part):
        part = part.reshape(2, own_heads, 1, 1, head_size, width)
        whole = jnp.zeros((own_heads, 2, 2, head_size, width), part.dtype)
        whole = lax.dynamic_update_slice(whole, part[0], (0, x, c, 0, 0))
        whole = lax.dynamic_update_slice(whole, part[1], (0, 1 - x, c, 0, 0))
        return whole.reshape(width, width)

    def owned(part):
        return lax.psum_scatter(part, OWNERS, scatter_dimension=0, tiled=True).astype(F32)

    qkv_weights = [owned(placed_heads(qkv_weight_part[:, i * cols : (i + 1) * cols])) for i in range(3)]
    query_bias_own = owned(placed_heads(bias_part[:cols]))
    value_bias_own = owned(placed_heads(bias_part[2 * cols :]))
    output_weight_own = owned(placed_rows(output_weight_part))
    inner_weight_own = owned(placed_units(inner_weight_part, 1))
    inner_bias_own = owned(placed_units(inner_bias_part, 0))
    outer_weight_own = owned(placed_units(outer_weight_part, 0))
    sums = [owned(token_sums[i]) for i in range(6)]

    return (
        encoded,
        input_grad,
        qkv_weights[0],
        query_bias_own,
        qkv_weights[1],
        qkv_weights[2],
        value_bias_own,
        output_weight_own,
        sums[5],
        sums[3],
        sums[4],
        inner_weight_own,
        inner_bias_own,
        outer_weight_own,
        sums[2],
        sums[0],
        sums[1],
    )


def solution(mesh):
    tokens = P(("dp", "fsdp"), "ctx", None)
    matrix, vector = P("fsdp", None), P("fsdp")
    own_matrix, own_vector = P(OWNERS, None), P(OWNERS)
    return jax.shard_map(
        shards,
        mesh=mesh,
        in_specs=(
            tokens,
            tokens,
            P(),
            P(),
            matrix,
            vector,
            matrix,
            matrix,
            vector,
            matrix,
            vector,
            vector,
            vector,
            matrix,
            vector,
            matrix,
            vector,
            vector,
            vector,
        ),
        out_specs=(
            tokens,
            tokens,
            own_matrix,
            own_vector,
            own_matrix,
            own_matrix,
            own_vector,
            own_matrix,
            own_vector,
            own_vector,
            own_vector,
            own_matrix,
            own_vector,
            own_matrix,
            own_vector,
            own_vector,
            own_vector,
        ),
        check_vma=False,
    )
```
